32 devices in a mesh: req: 4 (over z), mlp: 8 (over y, x, core).
Axes of the slice: x: 2, y: 2, z: 4, core: 2. Of those that a mesh axis runs over, the one named last changes fastest.
Arguments:
- tokens: bfloat16 [1024, 5120], P(('req', 'mlp')), may hold values from -6 to 6
- modulation: float32 [16, 6, 5120], P('req'), may hold values from -3 to 3
- lengths: int32 [4, 4], P('req'), may hold values from 1 to 160, 256 in all within a row
- request_adapter: int32 [16], P('req'), may hold values from 0 to 31
- adapter_storage: int32 [32], replicated, may hold values from 0 to 31, each once
- adapter_down_weight: bfloat16 [32, 5120, 32], P('mlp'), may hold values from -0.078125 to 0.078125
- adapter_up_maps: bfloat16 [32, 2, 16, 4096], P('mlp'), may hold values from -1.5 to 1.5
- input_projection: bfloat16 [4, 5120, 4096], P(None, None, 'mlp'), may hold values from -0.078125 to 0.078125
- query_key_gains: float32 [3, 4096], P(None, 'mlp'), may hold values from 0.1 to 1.9
- positions: int32 [3, 1024], P(None, 'req'), may hold values from 0 to 63
- block_page_lookup: int32 [4, 16], P('req'), may hold values from 0 to 15, each once within a row
- output_projection: bfloat16 [2, 4096, 5120], P(None, 'mlp'), may hold values from -0.09375 to 0.09375
- cross_norm_gain: float32 [5120], replicated, may hold values from 0.1 to 1.9
- text_token_cache: bfloat16 [2, 16, 512, 4096], P(None, 'req', None, 'mlp'), may hold values from -3 to 3
- feedforward_up: bfloat16 [5120, 8192], P('req', 'mlp'), may hold values from -0.078125 to 0.078125
- feedforward_down: bfloat16 [8192, 5120], P('mlp', 'req'), may hold values from -0.0625 to 0.0625
Outputs:
- layer_out: bfloat16 [1024, 5120], P(('req', 'mlp'))
- kv_pages: bfloat16 [2, 64, 16, 4096], P(None, 'req', None, 'mlp')
The draws below stay inside these ranges and needn't reach their ends.
Inputs may be any that keep to these rules, and one draw needn't show every extreme that they name: `lengths`: row g lists the token counts of the 4 requests of group g in order; they fill the group's 256 positions, and the largest is 160. A permutation: adapter a is stored at index adapter_storage[a] of adapter_down_weight and adapter_up_maps. `block_page_lookup`: each row is a permutation of a group's 16 pages.
All inputs are finite; a program needn't handle non-finite values.
Results may differ from the reference program's by a relative error of at most 0.017.
Values may be sent and summed in bfloat16 or wider, within the bound.
A program may use at most 192 MiB of HBM per device.

```python
import math
import jax
import jax.numpy as jnp
import numpy as np
from jax import lax

MODEL_DIM = 5120
HD = 128
TXT = 512
H = 32
FF = 8192
ADAPTER_RANK = 16
RQ = 4
PAGE = 16
GT = 256
QUERY_HEAD_WIDTH = 4096
LONGEST = 160
TOKENS = 1024
REQS = 16
ADAPTER_TOTAL = 32
PAGES_G = 16
N_REQ = 4


def with_ends(drawn, own_key, low, top_value):
    spot = [jax.random.randint(jax.random.fold_in(own_key, axis), (), 0, length) for axis, length in enumerate(drawn.shape)]
    widest = drawn.shape.index(max(drawn.shape))
    beside = spot[:widest] + [(spot[widest] + 1) % drawn.shape[widest]] + spot[widest + 1:]
    return drawn.at[tuple(spot)].set(low).at[tuple(beside)].set(top_value)


def steps_of(stream_key, dims, shards, least, top_value):
    gain, own = 1.0, jax.random.fold_in(stream_key, 6)
    for dim, parts in shards:
        heights = jnp.exp(jax.random.uniform(jax.random.fold_in(own, dim), (parts,), jnp.float32, least / len(shards), top_value / len(shards)))
        gain = gain * jnp.repeat(heights, dims[dim] // parts).reshape([-1 if axis == dim else 1 for axis in range(len(dims))])
    return gain


def split_up(amount, total, reach, slope):
    loads = [(1 << 20) // math.isqrt(rank ** slope) + 1 for rank in range(2, amount + 1)]
    surplus, given = total - reach - (amount - 1), [1] * (amount - 1)
    while surplus > 0:
        free = [i for i in range(amount - 1) if given[i] < reach]
        mass, left = sum([loads[i] for i in free]), surplus
        for i in free:
            addition = min(reach - given[i], max(1, left * loads[i] // mass), surplus)
            given[i] = given[i] + addition
            surplus = surplus - addition
    return np.array([reach] + given)


def uneven_parts(key, amount, total, bound, skew):
    if amount == 2:
        one = jax.random.randint(key, (), max(1, total - bound), min(bound, total - 1) + 1)
        return jnp.stack([one, total - one])
    sizes = jnp.asarray(split_up(amount, total, bound, skew), jnp.int32)
    twos = (amount - 1) // 2
    giver, taker = sizes[1:1 + 2 * twos:2], sizes[2:2 + 2 * twos:2]
    room = jnp.minimum(giver - 1, bound - taker)
    shifted = jax.random.randint(jax.random.fold_in(key, 1), (twos,), 0, 1 << 20) % (room + 1)
    sizes = sizes.at[1:1 + 2 * twos:2].set(giver - shifted).at[2:2 + 2 * twos:2].set(taker + shifted)
    return sizes[jax.random.permutation(jax.random.fold_in(key, 2), amount)]


def centred(stream_key, extent, scale, most, pieces=(), kind=jnp.bfloat16):
    entries = jax.random.normal(stream_key, extent, jnp.float32) * scale
    if len(pieces) > 0:
        entries = steps_of(stream_key, extent, pieces, -0.22, 0.18) * entries
    return jnp.clip(entries, min=-most, max=most).astype(kind)


def setup_inputs(seed: int = 0) -> dict:
    key_of = jax.random.split(jax.random.key(seed), 17)
    return {
        "tokens": centred(key_of[0], (TOKENS, MODEL_DIM), 1.0, 6.0, ((0, 32),)),
        "modulation": centred(key_of[1], (REQS, 6, MODEL_DIM), 0.5, 3.0, ((0, 4),), jnp.float32),
        "lengths": jax.vmap(lambda own: uneven_parts(own, RQ, GT, LONGEST, 2))(jax.random.split(key_of[2], N_REQ)).reshape((N_REQ, RQ)).astype(jnp.int32),
        "request_adapter": with_ends(jax.random.randint(key_of[3], (REQS,), 0, ADAPTER_TOTAL), jax.random.fold_in(key_of[3], 1), 0, ADAPTER_TOTAL - 1).astype(jnp.int32),
        "adapter_storage": jax.random.permutation(key_of[4], ADAPTER_TOTAL).astype(jnp.int32),
        "adapter_down_weight": centred(key_of[5], (ADAPTER_TOTAL, MODEL_DIM, 2 * ADAPTER_RANK), MODEL_DIM ** -0.5, 0.078125, ((0, 8),)),
        "adapter_up_maps": centred(key_of[6], (ADAPTER_TOTAL, 2, ADAPTER_RANK, QUERY_HEAD_WIDTH), ADAPTER_RANK ** -0.5, 1.5, ((0, 8),)),
        "input_projection": centred(key_of[7], (4, MODEL_DIM, QUERY_HEAD_WIDTH), MODEL_DIM ** -0.5, 0.078125, ((2, 8),)),
        "query_key_gains": jnp.clip(1.0 + 0.18 * jax.random.normal(key_of[8], (3, QUERY_HEAD_WIDTH), jnp.float32), 0.1, 1.9),
        "positions": with_ends(jax.random.randint(key_of[9], (3, TOKENS), 0, 64), jax.random.fold_in(key_of[9], 1), 0, 63).astype(jnp.int32),
        "block_page_lookup": jax.vmap(lambda own: jax.random.permutation(own, PAGES_G))(jax.random.split(key_of[10], N_REQ)).reshape((N_REQ, PAGES_G)).astype(jnp.int32),
        "output_projection": centred(key_of[11], (2, QUERY_HEAD_WIDTH, MODEL_DIM), QUERY_HEAD_WIDTH ** -0.5, 0.09375, ((1, 8),)),
        "cross_norm_gain": jnp.clip(1.0 + 0.18 * jax.random.normal(key_of[12], (MODEL_DIM,), jnp.float32), 0.1, 1.9),
        "text_token_cache": centred(key_of[13], (2, REQS, TXT, QUERY_HEAD_WIDTH), 1.0, 3.0, ((1, 4), (3, 8))),
        "feedforward_up": centred(key_of[14], (MODEL_DIM, FF), MODEL_DIM ** -0.5, 0.078125, ((0, 4), (1, 8))),
        "feedforward_down": centred(key_of[15], (FF, MODEL_DIM), FF ** -0.5, 0.0625, ((0, 8), (1, 4))),
    }


EPSILON = 1e-06

def layer_norm(values):
    center = values - lax.optimization_barrier(jnp.mean(values, axis=-1, keepdims=True))
    spread = lax.optimization_barrier(jnp.mean(center * center, axis=-1, keepdims=True))
    return center * lax.rsqrt(spread + EPSILON)

def rotary_tables(grid):
    half_dim = HD // 2
    spatial = half_dim // 3
    temporal = half_dim - 2 * spatial
    column = jnp.arange(half_dim, dtype=jnp.int32)
    which_axis = jnp.where(column < temporal, 0, jnp.where(column < temporal + spatial, 1, 2)).astype(jnp.int32)
    offset = jnp.where(which_axis == 0, 0, jnp.where(which_axis == 1, temporal, temporal + spatial)).astype(jnp.int32)
    span_size = jnp.where(which_axis == 0, temporal, spatial).astype(jnp.float32)
    frequency = jnp.exp(-(column - offset).astype(jnp.float32) / span_size * math.log(10000.0))
    coordinate = grid.astype(jnp.float32)[which_axis, :].T
    angles = coordinate * frequency[None, :]
    return (jnp.cos(angles), jnp.sin(angles))

def rotate(values, cosine, sine_part):
    half_dim = HD // 2
    front_half = values[..., :half_dim]
    back_half = values[..., half_dim:]
    cosine = cosine[:, None, :]
    sine_part = sine_part[:, None, :]
    return jnp.concatenate([front_half * cosine - back_half * sine_part, back_half * cosine + front_half * sine_part], axis=-1)

def attend(queries, key_rows, value_rows, allowed):
    scores = jnp.einsum('thd,shd->hts', queries.astype(jnp.float32), key_rows.astype(jnp.float32)) / math.sqrt(HD)
    scores = jnp.where(allowed[None], scores, -1e+30)
    weights = jnp.exp(scores)
    weights = (weights / lax.optimization_barrier(jnp.sum(weights, axis=-1, keepdims=True))).astype(jnp.bfloat16)
    return jnp.einsum('hts,shd->thd', weights.astype(jnp.float32), value_rows.astype(jnp.float32)).astype(jnp.bfloat16)

def reference(tokens, modulation, lengths, request_adapter, adapter_storage, adapter_down_weight, adapter_up_maps, input_projection, query_key_gains, positions, block_page_lookup, output_projection, cross_norm_gain, text_token_cache, feedforward_up, feedforward_down):
    entire_width = H * HD
    bounds = jnp.cumsum(lengths, axis=1)
    position = jnp.arange(GT, dtype=jnp.int32)
    segment = lax.optimization_barrier(jnp.sum((position[None, :, None] >= bounds[:, None, :]).astype(jnp.int32), axis=2))
    request = (jnp.arange(N_REQ, dtype=jnp.int32)[:, None] * RQ + segment).reshape(TOKENS)
    token_f32 = tokens.astype(jnp.float32)
    normed_in = (layer_norm(token_f32) * (1.0 + modulation[request, 1]) + modulation[request, 0]).astype(jnp.bfloat16)
    token_slot = adapter_storage[request_adapter[request]]
    down_combined = jnp.transpose(adapter_down_weight, (1, 0, 2)).reshape(MODEL_DIM, ADAPTER_TOTAL * 2 * ADAPTER_RANK)
    codes_all = jnp.dot(normed_in, down_combined, preferred_element_type=jnp.float32).reshape(TOKENS, ADAPTER_TOTAL, 2 * ADAPTER_RANK)
    everywhere = (token_slot[:, None] == jnp.arange(ADAPTER_TOTAL, dtype=jnp.int32)[None, :]).astype(jnp.float32)
    codes = lax.optimization_barrier(jnp.sum(everywhere[:, :, None] * codes_all, axis=1)).astype(jnp.bfloat16)

    def spread(code_part):
        return (everywhere[:, :, None] * code_part[:, None, :].astype(jnp.float32)).reshape(TOKENS, ADAPTER_TOTAL * ADAPTER_RANK).astype(jnp.bfloat16)
    query_up_weight = adapter_up_maps[:, 0].reshape(ADAPTER_TOTAL * ADAPTER_RANK, entire_width)
    value_up_weight = adapter_up_maps[:, 1].reshape(ADAPTER_TOTAL * ADAPTER_RANK, entire_width)
    query_linear = jnp.dot(normed_in, input_projection[0], preferred_element_type=jnp.float32) + jnp.dot(spread(codes[:, :ADAPTER_RANK]), query_up_weight, preferred_element_type=jnp.float32)
    key_linear = jnp.dot(normed_in, input_projection[1], preferred_element_type=jnp.float32)
    value_rows = (jnp.dot(normed_in, input_projection[2], preferred_element_type=jnp.float32) + jnp.dot(spread(codes[:, ADAPTER_RANK:]), value_up_weight, preferred_element_type=jnp.float32)).astype(jnp.bfloat16)
    query_norm = query_linear * lax.rsqrt(lax.optimization_barrier(jnp.mean(query_linear * query_linear, axis=1)) + EPSILON)[:, None] * query_key_gains[0]
    key_norm = key_linear * lax.rsqrt(lax.optimization_barrier(jnp.mean(key_linear * key_linear, axis=1)) + EPSILON)[:, None] * query_key_gains[1]
    cosine, sine_part = rotary_tables(positions)
    query_rot = rotate(query_norm.reshape(TOKENS, H, HD), cosine, sine_part).astype(jnp.bfloat16)
    key_rot = rotate(key_norm.reshape(TOKENS, H, HD), cosine, sine_part).astype(jnp.bfloat16)
    value_heads = value_rows.reshape(TOKENS, H, HD)
    stacked = jnp.stack([key_rot.reshape(N_REQ, PAGES_G, PAGE, entire_width), value_rows.reshape(N_REQ, PAGES_G, PAGE, entire_width)])
    group_index = jnp.arange(N_REQ, dtype=jnp.int32)[:, None]
    kv_pages = jnp.zeros_like(stacked).at[:, group_index, block_page_lookup].set(stacked).reshape(2, N_REQ * PAGES_G, PAGE, entire_width)
    attended_parts = []
    for group in range(N_REQ):
        rows_here = slice(group * GT, (group + 1) * GT)
        allowed = segment[group][:, None] == segment[group][None, :]
        attended_parts.append(attend(query_rot[rows_here], key_rot[rows_here], value_heads[rows_here], allowed).reshape(GT, entire_width))
    attended = jnp.concatenate(attended_parts, axis=0)
    first_res = (token_f32 + modulation[request, 2] * jnp.dot(attended, output_projection[0], preferred_element_type=jnp.float32)).astype(jnp.bfloat16)
    cross_in = (layer_norm(first_res.astype(jnp.float32)) * cross_norm_gain).astype(jnp.bfloat16)
    cross_linear = jnp.dot(cross_in, input_projection[3], preferred_element_type=jnp.float32)
    cross_query = (cross_linear * lax.rsqrt(lax.optimization_barrier(jnp.mean(cross_linear * cross_linear, axis=1)) + EPSILON)[:, None] * query_key_gains[2]).astype(jnp.bfloat16)
    text_owner = jnp.arange(RQ * TXT, dtype=jnp.int32) // TXT
    cross_parts = []
    for group in range(N_REQ):
        rows_here = slice(group * GT, (group + 1) * GT)
        text_keys = text_token_cache[0, group * RQ:(group + 1) * RQ].reshape(RQ * TXT, H, HD)
        text_values = text_token_cache[1, group * RQ:(group + 1) * RQ].reshape(RQ * TXT, H, HD)
        allowed = segment[group][:, None] == text_owner[None, :]
        cross_parts.append(attend(cross_query[rows_here].reshape(GT, H, HD), text_keys, text_values, allowed).reshape(GT, entire_width))
    cross_out = jnp.concatenate(cross_parts, axis=0)
    second_res = (first_res.astype(jnp.float32) + jnp.dot(cross_out, output_projection[1], preferred_element_type=jnp.float32)).astype(jnp.bfloat16)
    mlp_in = (layer_norm(second_res.astype(jnp.float32)) * (1.0 + modulation[request, 4]) + modulation[request, 3]).astype(jnp.bfloat16)
    hidden = jax.nn.gelu(jnp.dot(mlp_in, feedforward_up, preferred_element_type=jnp.float32), approximate=True).astype(jnp.bfloat16)
    layer_out = (second_res.astype(jnp.float32) + modulation[request, 5] * jnp.dot(hidden, feedforward_down, preferred_element_type=jnp.float32)).astype(jnp.bfloat16)
    return (layer_out, kv_pages)
```

```python
import functools
import math

import jax
import jax.numpy as jnp
from jax import lax
from jax.experimental import pallas as pl
from jax.experimental.pallas import tpu as pltpu
from jax.sharding import PartitionSpec as P

HD = 128
PAGE = 16


EPSILON = 1e-06


PAIR = 2
MESH = pl.DeviceIdType.MESH
ANY = pl.BlockSpec(memory_space=pl.ANY)
VM = pl.BlockSpec(memory_space=pltpu.VMEM)


def comm_call(kernel, out_shape, in_specs, out_specs, scratch, ident, room=4):
    return pl.pallas_call(
        kernel,
        out_shape=out_shape,
        in_specs=in_specs,
        out_specs=out_specs,
        scratch_shapes=scratch,
        compiler_params=pltpu.CompilerParams(
            collective_id=ident, has_side_effects=True, vmem_limit_bytes=room << 20
        ),
    )


def remote(source, target, send_sem, recv_sem, axis, place):
    return pltpu.make_async_remote_copy(
        src_ref=source,
        dst_ref=target,
        send_sem=send_sem,
        recv_sem=recv_sem,
        device_id={axis: place},
        device_id_type=MESH,
    )


def shift(me, step, count):
    return lax.rem(me + (step + count) % count, count)


def greet(peers):
    barrier = pltpu.get_barrier_semaphore()
    for axis, place in peers:
        pl.semaphore_signal(barrier, inc=1, device_id={axis: place}, device_id_type=MESH)
    pl.semaphore_wait(barrier, len(peers))


def pair_places(count):
    me = lax.axis_index("mlp")
    outer, core = lax.div(me, PAIR), lax.rem(me, PAIR)
    sibling = outer * PAIR + (PAIR - 1 - core)
    peers = [
        shift(outer, k, count // PAIR) * PAIR + core for k in range(count // PAIR)
    ]
    sources = [
        shift(outer, -k, count // PAIR) * PAIR + core for k in range(count // PAIR)
    ]
    return me, core, sibling, peers, sources


def gather_sems(count):
    steps = count // PAIR
    return [pltpu.SemaphoreType.DMA(())] + [pltpu.SemaphoreType.DMA((steps,))] * 4


def gather_rows(count, places, own_ref, out_ref, own_sem, send_sem, recv_sem, pass_send, pass_recv):
    me, core, sibling, peers, sources = places
    own = pltpu.make_async_copy(own_ref, out_ref.at[me], own_sem)
    sends = [
        remote(own_ref, out_ref.at[me], send_sem.at[k], recv_sem.at[k], "mlp", peers[k])
        for k in range(1, count // PAIR)
    ]
    for copy in sends:
        copy.start()
    passes = [remote(own_ref, out_ref.at[me], pass_send.at[0], pass_recv.at[0], "mlp", sibling)]
    passes[0].start()
    own.start()
    for k in range(1, count // PAIR):
        sends[k - 1].wait_recv()
        block = out_ref.at[sources[k]]
        passes.append(remote(block, block, pass_send.at[k], pass_recv.at[k], "mlp", sibling))
        passes[-1].start()
    for copy in sends:
        copy.wait_send()
    for copy in passes:
        copy.wait()
    own.wait()


def entry_kernel(count, tok_ref, scale_ref, shift_ref, maps_ref, out_ref, up_ref, norm, map_own, map_send, map_recv, *sems):
    places = pair_places(count)
    me = places[0]
    slots, width = maps_ref.shape[0], up_ref.shape[-1]
    others = [shift(me, k, count) for k in range(1, count)]
    greet([("mlp", place) for place in others])

    def columns(place):
        return maps_ref.at[:, :, :, pl.ds(pl.multiple_of(place * width, 128), width)]

    target = up_ref.at[pl.ds(me * slots, slots)]
    own = pltpu.make_async_copy(columns(me), target, map_own)
    own.start()
    copies = [
        remote(columns(place), target, map_send.at[k], map_recv.at[k], "mlp", place)
        for k, place in enumerate(others)
    ]
    norm[...] = (
        layer_norm(tok_ref[...].astype(jnp.float32)) * (1.0 + scale_ref[...]) + shift_ref[...]
    ).astype(jnp.bfloat16)
    for copy in copies:
        copy.start()
    gather_rows(count, places, norm, out_ref, *sems)
    for copy in copies:
        copy.wait()
    own.wait()


def entry_rows(tokens, scale, shift_rows, maps, count):
    rows, width = tokens.shape
    slots, two, rank, total = maps.shape
    dma = pltpu.SemaphoreType.DMA
    gathered, up = comm_call(
        functools.partial(entry_kernel, count),
        (
            jax.ShapeDtypeStruct((count, rows, width), jnp.bfloat16),
            jax.ShapeDtypeStruct((count * slots, two, rank, total // count), maps.dtype),
        ),
        [VM, VM, VM, ANY],
        (ANY, ANY),
        [pltpu.VMEM((rows, width), jnp.bfloat16), dma(()), dma((count - 1,)), dma((count - 1,))]
        + gather_sems(count),
        0,
        8,
    )(tokens, scale, shift_rows, maps)
    return gathered.reshape(count * rows, width), up


def sum_blocks(count, places, block_of, near, mid, far, ns, nr, fs, fr):
    me, core, sibling, peers, sources = places
    steps = count // PAIR
    order = list(range(1, steps)) + [0]
    pairs = {}
    for k in order:
        other = peers[k] + (PAIR - 1 - 2 * core)
        pairs[k] = remote(block_of(other), near.at[k], ns.at[k], nr.at[k], "mlp", sibling)
        pairs[k].start()
    sends = []
    for k in range(1, steps):
        pairs[k].wait_recv()
        mid[k] = (
            block_of(peers[k])[...].astype(jnp.float32) + near[k].astype(jnp.float32)
        ).astype(jnp.bfloat16)
        sends.append(remote(mid.at[k], far.at[k], fs.at[k], fr.at[k], "mlp", peers[k]))
        sends[-1].start()
    pairs[0].wait_recv()
    total = block_of(me)[...].astype(jnp.float32) + near[0].astype(jnp.float32)
    for k in range(1, steps):
        sends[k - 1].wait_recv()
        total = total + far[k].astype(jnp.float32)
    for k in order:
        pairs[k].wait_send()
    for copy in sends:
        copy.wait_send()
    return total


def sum_scratch(count, extent):
    steps = count // PAIR
    return [pltpu.VMEM((steps,) + extent, jnp.bfloat16)] * 3 + [
        pltpu.SemaphoreType.DMA((steps,))
    ] * 4


def middle_kernel(count, part_ref, base_ref, gate_ref, scale_ref, shift_ref, res_ref, out_ref, near, mid, far, norm, ns, nr, fs, fr, *sems):
    places = pair_places(count)
    greet([("mlp", places[2])] + [("mlp", place) for place in places[3][1:]])
    total = sum_blocks(
        count, places, lambda place: part_ref.at[place], near, mid, far, ns, nr, fs, fr
    )
    res = (base_ref[...].astype(jnp.float32) + gate_ref[...] * total).astype(jnp.bfloat16)
    res_ref[...] = res
    norm[...] = (layer_norm(res.astype(jnp.float32)) * scale_ref[...] + shift_ref[...]).astype(
        jnp.bfloat16
    )
    gather_rows(count, places, norm, out_ref, *sems)


def middle_rows(part, base, gate, scale, shift_rows, count, ident):
    rows, width = base.shape
    scratch = sum_scratch(count, (rows, width))
    res, gathered = comm_call(
        functools.partial(middle_kernel, count),
        (
            jax.ShapeDtypeStruct((rows, width), jnp.bfloat16),
            jax.ShapeDtypeStruct((count, rows, width), jnp.bfloat16),
        ),
        [VM] * 5,
        (VM, ANY),
        scratch[:3] + [pltpu.VMEM((rows, width), jnp.bfloat16)] + scratch[3:] + gather_sems(count),
        ident,
        24,
    )(part.reshape(count, rows, width), base, gate, scale, shift_rows)
    return res, gathered.reshape(count * rows, width)


def small_kernel(count, own_ref, out_ref, slots, send_sem, recv_sem):
    me = lax.axis_index("mlp")
    others = [shift(me, k, count) for k in range(1, count)]
    greet([("mlp", place) for place in others])
    copies = [
        remote(own_ref, slots.at[k], send_sem.at[k], recv_sem.at[k], "mlp", place)
        for k, place in enumerate(others)
    ]
    for copy in copies:
        copy.start()
    total = own_ref[...].astype(jnp.float32)
    for k, copy in enumerate(copies):
        copy.wait_recv()
        total = total + slots[k].astype(jnp.float32)
    out_ref[...] = total
    for copy in copies:
        copy.wait_send()


def small_sum(own, count, ident):
    dma = pltpu.SemaphoreType.DMA((count - 1,))
    return comm_call(
        functools.partial(small_kernel, count),
        jax.ShapeDtypeStruct(own.shape, jnp.float32),
        [VM],
        VM,
        [pltpu.VMEM((count - 1,) + own.shape, own.dtype), dma, dma],
        ident,
    )(own)


def line_kernel(count, own_ref, out_ref, own_sem, rs, rr, ls, lr):
    me = lax.axis_index("req")
    right, left = shift(me, 1, count), shift(me, -1, count)
    greet([("req", right), ("req", left)])
    own = pltpu.make_async_copy(own_ref, out_ref.at[me], own_sem)
    own.start()

    pieces = rs.shape[1]
    rows = own_ref.shape[0] // pieces

    def hop(step, piece, sign):
        block = jnp.clip(me - sign * step, 0, count - 1)
        part = pl.ds(piece * rows, rows)
        source = own_ref.at[part] if step == 0 else out_ref.at[block, part]
        send, recv, place = (rs, rr, right) if sign > 0 else (ls, lr, left)
        return remote(
            source,
            out_ref.at[block, part],
            send.at[step, piece],
            recv.at[step, piece],
            "req",
            place,
        )

    def each(step, work):
        for piece in range(pieces):
            work(step, piece)

    def advance(step, piece):
        if step > 0:

            @pl.when(me >= step)
            def _():
                hop(step - 1, piece, 1).wait_recv()

            @pl.when(me + step < count)
            def _():
                hop(step - 1, piece, -1).wait_recv()

        @pl.when((me >= step) & (me < count - 1))
        def _():
            hop(step, piece, 1).start()

        @pl.when((me + step < count) & (me > 0))
        def _():
            hop(step, piece, -1).start()

    def finish(step, piece):
        @pl.when(me >= count - 1)
        def _():
            hop(step, piece, 1).wait_recv()

        @pl.when(me < 1)
        def _():
            hop(step, piece, -1).wait_recv()

    def drain(step, piece):
        @pl.when((me >= step) & (me < count - 1))
        def _():
            hop(step, piece, 1).wait_send()

        @pl.when((me + step < count) & (me > 0))
        def _():
            hop(step, piece, -1).wait_send()

    for step in range(count - 1):
        each(step, advance)
    each(count - 2, finish)
    for step in range(count - 1):
        each(step, drain)
    own.wait()


def line_gather(own, count, ident):
    dma = pltpu.SemaphoreType.DMA
    return comm_call(
        functools.partial(line_kernel, count),
        jax.ShapeDtypeStruct((count,) + own.shape, own.dtype),
        [ANY],
        ANY,
        [dma(())] + [dma((count - 1, 4))] * 4,
        ident,
    )(own)


def exit_kernel(count, lines, part_ref, out_ref, near, mid, far, final, ns, nr, fs, fr, own_sem, send_sem, recv_sem):
    places = pair_places(count)
    me, core, sibling, peers, _ = places
    steps = count // PAIR
    line = lax.axis_index("req")
    groups = [shift(line, k + 1, lines) for k in range(lines)]
    greet(
        [("mlp", sibling)]
        + [("mlp", place) for place in peers[1:]]
        + [("req", place) for place in groups[:-1]]
    )
    order = list(range(1, steps)) + [0]
    pairs, sends, copies = {}, [], []
    for i, group in enumerate(groups):
        for k in order:
            other = peers[k] + (PAIR - 1 - 2 * core)
            pairs[i, k] = remote(
                part_ref.at[group, other], near.at[i, k], ns.at[i, k], nr.at[i, k], "mlp", sibling
            )
            pairs[i, k].start()
    for i, group in enumerate(groups):
        for k in range(1, steps):
            pairs[i, k].wait_recv()
            mid[i, k] = (
                part_ref[group, peers[k]].astype(jnp.float32) + near[i, k].astype(jnp.float32)
            ).astype(jnp.bfloat16)
            sends.append(
                remote(mid.at[i, k], far.at[i, k], fs.at[i, k], fr.at[i, k], "mlp", peers[k])
            )
            sends[-1].start()
    width = final.shape[-1]
    target = out_ref.at[:, pl.ds(pl.multiple_of(line * width, 128), width)]
    for i, group in enumerate(groups):
        pairs[i, 0].wait_recv()
        total = part_ref[group, me].astype(jnp.float32) + near[i, 0].astype(jnp.float32)
        for k in range(1, steps):
            sends[i * (steps - 1) + k - 1].wait_recv()
            total = total + far[i, k].astype(jnp.float32)
        final[i] = total.astype(jnp.bfloat16)
        if i < lines - 1:
            copies.append(
                remote(final.at[i], target, send_sem.at[i], recv_sem.at[i], "req", group)
            )
        else:
            copies.append(pltpu.make_async_copy(final.at[i], target, own_sem))
        copies[-1].start()
    for copy in list(pairs.values()) + sends:
        copy.wait_send()
    for copy in copies:
        copy.wait()


def exit_rows(part, count, lines, ident):
    groups, _, rows, width = part.shape
    steps = count // PAIR
    dma = pltpu.SemaphoreType.DMA
    return comm_call(
        functools.partial(exit_kernel, count, lines),
        jax.ShapeDtypeStruct((rows, lines * width), jnp.bfloat16),
        [VM],
        VM,
        [pltpu.VMEM((groups, steps, rows, width), jnp.bfloat16)] * 3
        + [pltpu.VMEM((groups, rows, width), jnp.bfloat16)]
        + [dma((groups, steps))] * 4
        + [dma(()), dma((lines - 1,)), dma((lines - 1,))],
        ident,
        24,
    )(part)


def lines_order(lines):
    middle = lines // 2
    return [middle - 1, middle] + [g for g in range(lines) if g not in (middle - 1, middle)]


def dot_tiles(x, w_ref, out_ref, put, tile):
    width = w_ref.shape[1]

    @pl.loop(0, width // tile)
    def _(i):
        columns = pl.ds(pl.multiple_of(i * tile, tile), tile)
        put(columns, jnp.dot(x, w_ref[:, columns], preferred_element_type=jnp.float32))


def ff_kernel(count, lines, part_ref, base_ref, scale_ref, shift_ref, gate_ref, up_hbm, down_hbm, out_ref,
              near, mid, far, ns, nr, fs, fr,
              up_ref, down_ref, w_sem, norm, res, act, a_send, a_recv, g_send, g_recv, p_send, p_recv,
              pbuf, from_outer, from_partner, staged, hid, es, er, ts, tr, ho_s, hp_s, h_r,
              dn, near2, mid2, far2, ns2, nr2, fs2, fr2, final, back, bs, br):
    places = pair_places(count)
    me, core, sibling, peers, sources = places
    steps = count // PAIR
    line = lax.axis_index("req")
    order = lines_order(lines)
    is_mid = (line == 1) | (line == 2)
    outer = jnp.where(line == 1, 0, 3)
    partner = 3 - line
    inner = jnp.where(line == 0, 1, 2)
    greet(
        [("mlp", sibling)]
        + [("mlp", place) for place in peers[1:]]
        + [("req", shift(line, k, lines)) for k in range(1, lines)]
    )
    weights = [
        pltpu.make_async_copy(up_hbm, up_ref, w_sem.at[0]),
        pltpu.make_async_copy(down_hbm, down_ref, w_sem.at[1]),
    ]
    for copy in weights:
        copy.start()
    total = sum_blocks(count, places, lambda place: part_ref.at[place], near, mid, far, ns, nr, fs, fr)
    res[...] = (base_ref[...].astype(jnp.float32) + total).astype(jnp.bfloat16)
    norm[...] = (
        layer_norm(res[...].astype(jnp.float32)) * scale_ref[...] + shift_ref[...]
    ).astype(jnp.bfloat16)

    rows, width = norm.shape
    part_width = width // lines

    def slice_of(place):
        return pl.ds(pl.multiple_of(place * part_width, 128), part_width)

    def spread_to(k):
        return remote(
            norm.at[:, slice_of(shift(line, k, lines))], act.at[line, me],
            a_send.at[k], a_recv.at[line], "req", shift(line, k, lines),
        )

    for k in range(1, lines):
        spread_to(k).start()
    act[line, me] = norm[:, slice_of(line)]

    def across(g, k):
        return remote(act.at[g, me], act.at[g, me], g_send.at[g, k], g_recv.at[g, k], "mlp", peers[k])

    def passed(g, k):
        block = act.at[g, sources[k]]
        return remote(block, block, p_send.at[g, k], p_recv.at[g, k], "mlp", sibling)

    def from_sibling(g, k):
        block = act.at[g, sources[k] + PAIR - 1 - 2 * core]
        return remote(block, block, p_send.at[g, k], p_recv.at[g, k], "mlp", sibling)

    for g in order:
        @pl.when(line != g)
        def _():
            remote(norm.at[:, slice_of(g)], act.at[g, me], a_send.at[0], a_recv.at[g], "req", g).wait_recv()

        for k in range(1, steps):
            across(g, k).start()
        passed(g, 0).start()

    tall = count * rows
    chunks = 4
    some = tall // chunks

    def chunk(j):
        return pl.ds(pl.multiple_of(j * some, some), some)

    def to_inner(g, j):
        return remote(pbuf.at[g, chunk(j)], from_outer.at[g, j], es.at[g, j], er.at[g, j], "req", inner)

    def to_partner(g, j):
        return remote(staged.at[g, j], from_partner.at[g, j], ts.at[g, j], tr.at[g, j], "req", partner)

    def out_to(g, j, place, sem):
        block = hid.at[g, chunk(j)]
        return remote(block, block, sem.at[g, j], h_r.at[g, j], "req", place)

    def gathered(g):
        for k in range(1, steps):
            remote(act.at[g, me], act.at[g, sources[k]], g_send.at[g, k], g_recv.at[g, k], "mlp", peers[k]).wait_recv()
            passed(g, k).start()
        for k in range(steps):
            from_sibling(g, k).wait_recv()

    def first_product(g):
        def put(columns, value):
            pbuf[g, :, columns] = value.astype(jnp.bfloat16)

        dot_tiles(act[g].reshape(tall, part_width), up_ref, pbuf, put, 256)

        @pl.when(jnp.logical_not(is_mid))
        def _():
            for j in range(chunks):
                to_inner(g, j).start()

    def theirs(g, i):
        j = 2 * i + 2 - line
        to_inner(g, j).wait_recv()
        staged[g, j] = (
            pbuf[g, chunk(j)].astype(jnp.float32) + from_outer[g, j].astype(jnp.float32)
        ).astype(jnp.bfloat16)
        to_partner(g, j).start()

    def mine(g, i):
        j = 2 * i + line - 1
        to_inner(g, j).wait_recv()
        to_partner(g, j).wait_recv()
        value = (
            pbuf[g, chunk(j)].astype(jnp.float32)
            + from_outer[g, j].astype(jnp.float32)
            + from_partner[g, j].astype(jnp.float32)
        )
        hid[g, chunk(j)] = jax.nn.gelu(value, approximate=True).astype(jnp.bfloat16)
        out_to(g, j, partner, hp_s).start()
        out_to(g, j, outer, ho_s).start()

    def forward(g, i):
        j = 2 * i + 2 - line
        out_to(g, j, partner, hp_s).wait_recv()
        out_to(g, j, outer, ho_s).start()

    def middle(p):
        @pl.when(is_mid)
        def _():
            g = order[p]
            theirs(g, 0)
            theirs(g, 1)
            if p > 0:
                forward(order[p - 1], 0)
            mine(g, 0)
            if p > 0:
                forward(order[p - 1], 1)
            mine(g, 1)

    def all_hidden(p):
        g = order[p]
        if p == lines - 1:
            @pl.when(is_mid)
            def _():
                forward(g, 0)
                forward(g, 1)

        @pl.when(jnp.logical_not(is_mid))
        def _():
            for j in range(chunks):
                out_to(g, j, inner, ho_s).wait_recv()

    def pair_copy(g, k):
        other = peers[k] + (PAIR - 1 - 2 * core)
        return remote(dn.at[g, other], near2.at[g, k], ns2.at[g, k], nr2.at[g, k], "mlp", sibling)

    def far_copy(g, k):
        return remote(mid2.at[g, k], far2.at[g, k], fs2.at[g, k], fr2.at[g, k], "mlp", peers[k])

    k_order = list(range(1, steps)) + [0]

    def second_product(p):
        g = order[p]

        def put(columns, value):
            dn[g, :, :, columns] = value.astype(jnp.bfloat16).reshape(count, rows, 256)

        dot_tiles(hid[g], down_ref, dn, put, 256)
        for k in k_order:
            pair_copy(g, k).start()
        for k in range(1, steps):
            pair_copy(g, k).wait_recv()
            mid2[g, k] = (
                dn[g, peers[k]].astype(jnp.float32) + near2[g, k].astype(jnp.float32)
            ).astype(jnp.bfloat16)
            far_copy(g, k).start()

    def home(g):
        return remote(final.at[g], back.at[line], bs.at[g], br.at[line], "req", g)

    def finish(p):
        g = order[p]
        pair_copy(g, 0).wait_recv()
        value = dn[g, me].astype(jnp.float32) + near2[g, 0].astype(jnp.float32)
        for k in range(1, steps):
            far_copy(g, k).wait_recv()
            value = value + far2[g, k].astype(jnp.float32)
        final[g] = value.astype(jnp.bfloat16)

        @pl.when(line == g)
        def _():
            back[g] = final[g]

        @pl.when(line != g)
        def _():
            home(g).start()

    gathered(order[0])
    weights[0].wait()
    first_product(order[0])
    gathered(order[1])
    first_product(order[1])
    middle(0)
    gathered(order[2])
    first_product(order[2])
    middle(1)
    gathered(order[3])
    first_product(order[3])
    weights[1].wait()
    all_hidden(0)
    second_product(0)
    middle(2)
    finish(0)
    all_hidden(1)
    second_product(1)
    middle(3)
    finish(1)
    all_hidden(2)
    second_product(2)
    finish(2)
    all_hidden(3)
    second_product(3)
    finish(3)

    for q in range(lines):
        columns = slice(q * part_width, (q + 1) * part_width)

        @pl.when(line != q)
        def _():
            remote(final.at[q], back.at[q], bs.at[q], br.at[q], "req", q).wait_recv()

        out_ref[:, columns] = (
            res[:, columns].astype(jnp.float32) + gate_ref[:, columns] * back[q].astype(jnp.float32)
        ).astype(jnp.bfloat16)

    for k in range(1, lines):
        spread_to(k).wait_send()
    for g in order:
        for k in range(1, steps):
            across(g, k).wait_send()
            far_copy(g, k).wait_send()
        for k in range(steps):
            passed(g, k).wait_send()
            pair_copy(g, k).wait_send()

        @pl.when(line != g)
        def _():
            home(g).wait_send()

        @pl.when(is_mid)
        def _():
            for i in range(chunks // 2):
                to_partner(g, 2 * i + 2 - line).wait_send()
                out_to(g, 2 * i + line - 1, partner, hp_s).wait_send()
            for j in range(chunks):
                out_to(g, j, outer, ho_s).wait_send()

        @pl.when(jnp.logical_not(is_mid))
        def _():
            for j in range(chunks):
                to_inner(g, j).wait_send()


def feed_forward(part, base, scale, shift_rows, gate, up, down, count, lines, ident):
    rows, width = base.shape
    steps = count // PAIR
    depth, units = up.shape
    tall = rows * count
    dma = pltpu.SemaphoreType.DMA
    vm = lambda *extent: pltpu.VMEM(extent, jnp.bfloat16)
    scratch = (
        sum_scratch(count, (rows, width))
        + [vm(depth, units), vm(units, depth), dma((2,)), vm(rows, width), vm(rows, width)]
        + [vm(lines, count, rows, depth), dma((lines,)), dma((lines,))]
        + [dma((lines, steps))] * 4
        + [vm(lines, tall, units), vm(lines, 4, tall // 4, units), vm(lines, 4, tall // 4, units)]
        + [vm(lines, 4, tall // 4, units), vm(lines, tall, units)]
        + [dma((lines, 4))] * 7
        + [vm(lines, count, rows, depth)]
        + [vm(lines, steps, rows, depth)] * 3
        + [dma((lines, steps))] * 4
        + [vm(lines, rows, depth)] * 2
        + [dma((lines,))] * 2
    )
    return comm_call(
        functools.partial(ff_kernel, count, lines),
        jax.ShapeDtypeStruct((rows, width), jnp.bfloat16),
        [VM] * 5 + [ANY] * 2,
        VM,
        scratch,
        ident,
        56,
    )(part.reshape(count, rows, width), base, scale, shift_rows, gate, up, down)


def layer_norm(values):
    center = values - jnp.mean(values, axis=-1, keepdims=True)
    spread = jnp.mean(center * center, axis=-1, keepdims=True)
    return center * lax.rsqrt(spread + EPSILON)


def rotary_tables(grid):
    half_dim = HD // 2
    spatial = half_dim // 3
    temporal = half_dim - 2 * spatial
    column = jnp.arange(HD, dtype=jnp.int32)
    sign = jnp.where(column < half_dim, -1.0, 1.0).astype(jnp.float32)
    column = column % half_dim
    which_axis = jnp.where(
        column < temporal, 0, jnp.where(column < temporal + spatial, 1, 2)
    ).astype(jnp.int32)
    offset = jnp.where(
        which_axis == 0, 0, jnp.where(which_axis == 1, temporal, temporal + spatial)
    ).astype(jnp.int32)
    span_size = jnp.where(which_axis == 0, temporal, spatial).astype(jnp.float32)
    frequency = jnp.exp(-(column - offset).astype(jnp.float32) / span_size * math.log(10000.0))
    grid = grid.astype(jnp.float32)[:, :, None]
    coordinate = jnp.where(
        which_axis == 0, grid[0], jnp.where(which_axis == 1, grid[1], grid[2])
    )
    angles = coordinate * frequency[None, :]
    return (jnp.cos(angles), jnp.sin(angles) * sign[None, :])


def attend(queries, key_rows, value_rows, allowed):
    scores = lax.dot_general(
        queries, key_rows, (((1,), (1,)), ((), ())), preferred_element_type=jnp.float32
    ) * (1.0 / math.sqrt(HD))
    weights = jnp.exp(jnp.where(allowed, scores, -1e30))
    weights = weights * (1.0 / jnp.sum(weights, axis=-1, keepdims=True))
    return jnp.dot(
        weights.astype(jnp.bfloat16), value_rows, preferred_element_type=jnp.float32
    ).astype(jnp.bfloat16)


def self_kernel(page_ref, q_ref, k_ref, v_ref, qs_ref, ks_ref, gain_ref, cos_ref, sin_ref, seg_ref, segs_ref, out_ref, kv_ref):
    cosine, sine = cos_ref[...], sin_ref[...]
    allowed = seg_ref[...] == segs_ref[...]

    def turned(ref, scale, gain, columns):
        rows = ref[:, columns] * scale * gain_ref[gain : gain + 1, columns]
        return (rows * cosine + pltpu.roll(rows, HD // 2, 1) * sine).astype(jnp.bfloat16)

    for head in range(q_ref.shape[1] // HD):
        columns = slice(head * HD, (head + 1) * HD)
        query = turned(q_ref, qs_ref[...], 0, columns)
        key = turned(k_ref, ks_ref[...], 1, columns)
        value = v_ref[:, columns]
        out_ref[:, columns] = attend(query, key, value, allowed)
        for block in range(kv_ref.shape[1]):
            page = page_ref[block]
            rows = slice(block * PAGE, (block + 1) * PAGE)
            kv_ref[0, page, :, columns] = key[rows]
            kv_ref[1, page, :, columns] = value[rows]


def self_attention(pages, query, key, value, query_scale, key_scale, gains, cosine, sine, segment):
    rows, width = query.shape
    return pl.pallas_call(
        self_kernel,
        out_shape=(
            jax.ShapeDtypeStruct((rows, width), jnp.bfloat16),
            jax.ShapeDtypeStruct((2, pages.shape[0], PAGE, width), jnp.bfloat16),
        ),
        in_specs=[pl.BlockSpec(memory_space=pltpu.SMEM)] + [VM] * 10,
        out_specs=(VM, VM),
        compiler_params=pltpu.CompilerParams(vmem_limit_bytes=16 << 20),
    )(
        pages,
        query,
        key,
        value,
        query_scale[:, None],
        key_scale[:, None],
        gains,
        cosine,
        sine,
        segment[:, None],
        segment[None, :],
    )


def cross_kernel(q_ref, k_ref, v_ref, seg_ref, owner_ref, out_ref):
    out_ref[...] = attend(q_ref[...], k_ref[0], v_ref[0], seg_ref[...] == owner_ref[...])


def cross_attention(query, cache, segment, owner):
    rows, width = query.shape
    texts = cache.shape[1]
    head = pl.BlockSpec((rows, HD), lambda h: (0, h))
    return pl.pallas_call(
        cross_kernel,
        out_shape=jax.ShapeDtypeStruct((rows, width), jnp.bfloat16),
        grid=(width // HD,),
        in_specs=[
            head,
            pl.BlockSpec((1, texts, HD), lambda h: (0, 0, h)),
            pl.BlockSpec((1, texts, HD), lambda h: (1, 0, h)),
            pl.BlockSpec((rows, 1), lambda h: (0, 0)),
            pl.BlockSpec((1, texts), lambda h: (0, 0)),
        ],
        out_specs=head,
        compiler_params=pltpu.CompilerParams(vmem_limit_bytes=24 << 20),
    )(query, cache, cache, segment[:, None], owner[None, :])


def product_kernel(act, x_ref, w_ref, out_ref):
    out_ref[0] = act(
        jnp.dot(x_ref[...], w_ref[0], preferred_element_type=jnp.float32)
    ).astype(out_ref.dtype)


def product(rows_in, maps, first, amount, tile, dtype, act=lambda part: part):
    rows, depth = rows_in.shape
    width = maps.shape[2]
    tile = min(tile, width)
    return pl.pallas_call(
        functools.partial(product_kernel, act),
        out_shape=jax.ShapeDtypeStruct((amount, rows, width), dtype),
        grid=(amount, width // tile),
        in_specs=[
            pl.BlockSpec((rows, depth), lambda i, j: (0, 0)),
            pl.BlockSpec((1, depth, tile), lambda i, j: (first + i, 0, j)),
        ],
        out_specs=pl.BlockSpec((1, rows, tile), lambda i, j: (i, 0, j)),
        compiler_params=pltpu.CompilerParams(vmem_limit_bytes=24 << 20),
    )(rows_in, pltpu.with_memory_space_constraint(maps, pltpu.HBM))


def choose_rows(table, segment):
    chosen = jnp.zeros((segment.shape[0],) + table.shape[1:], table.dtype)
    for request in range(table.shape[0]):
        picked = (segment == request).reshape((-1,) + (1,) * (table.ndim - 1))
        chosen = jnp.where(picked, table[request][None], chosen)
    return chosen


def body(
    tokens,
    modulation,
    lengths,
    request_adapter,
    adapter_storage,
    adapter_down_weight,
    adapter_up_maps,
    input_projection,
    query_key_gains,
    positions,
    block_page_lookup,
    output_projection,
    cross_norm_gain,
    text_token_cache,
    feedforward_up,
    feedforward_down,
):
    mlp_count = lax.axis_size("mlp")
    my_index = lax.axis_index("mlp")
    own_count = tokens.shape[0]
    group_rows = own_count * mlp_count
    local_width = input_projection.shape[2]
    entire_width = local_width * mlp_count
    resident_slots = adapter_down_weight.shape[0]
    doubled_rank = adapter_down_weight.shape[2]
    rank_once = doubled_rank // 2

    req_count = lax.axis_size("req")
    slot_total = resident_slots * mlp_count
    tuned = mlp_count == 8 and req_count == 4
    counts = lengths[0]
    index = jnp.arange(counts.shape[0], dtype=jnp.int32)
    bounds = jnp.sum(jnp.where(index[:, None] >= index[None, :], counts[None, :], 0), axis=1)
    position = jnp.arange(group_rows, dtype=jnp.int32)
    segment = jnp.sum((position[:, None] >= bounds[None, :]).astype(jnp.int32), axis=1)
    own_start = my_index * own_count
    own_segment = lax.dynamic_slice_in_dim(segment, own_start, own_count)
    per_token = [choose_rows(modulation[:, which_row, :], own_segment) for which_row in range(6)]
    token_f32 = tokens.astype(jnp.float32)
    rows_in, adapter_up_weight = entry_rows(
        tokens, per_token[1], per_token[0], adapter_up_maps, mlp_count
    )
    request_slot = adapter_storage[request_adapter]
    token_slot = jnp.sum(
        jnp.where(
            segment[:, None] == jnp.arange(request_slot.shape[0], dtype=jnp.int32)[None, :],
            request_slot[None, :],
            0,
        ),
        axis=1,
    )
    resident = my_index * resident_slots + jnp.arange(resident_slots, dtype=jnp.int32)
    held = (token_slot[None, :] == resident[:, None]).astype(jnp.float32)
    code_block = lax.dot_general(
        adapter_down_weight.transpose(0, 2, 1).reshape(resident_slots * doubled_rank, -1),
        rows_in,
        (((1,), (1,)), ((), ())),
        preferred_element_type=jnp.float32,
    ).reshape(resident_slots, doubled_rank, group_rows)
    my_codes = jnp.sum(held[:, None, :] * code_block, axis=0).astype(jnp.bfloat16)
    codes = small_sum(my_codes, mlp_count, 1).astype(jnp.bfloat16)
    slots = jnp.arange(slot_total, dtype=jnp.int32)
    everywhere = token_slot[None, :] == slots[:, None]

    def spread(code_part):
        return jnp.where(everywhere[:, None, :], code_part[None], jnp.bfloat16(0)).reshape(
            slot_total * rank_once, group_rows
        )

    def adapted(code_part, which_map):
        return lax.dot_general(
            spread(code_part),
            adapter_up_weight[:, which_map].reshape(slot_total * rank_once, local_width),
            (((0,), (0,)), ((), ())),
            preferred_element_type=jnp.float32,
        )

    projected = product(rows_in, input_projection, 0, 3, 256, jnp.float32)
    query_linear = projected[0] + adapted(codes[:rank_once], 0)
    key_linear = projected[1]
    value_rows = (projected[2] + adapted(codes[rank_once:], 1)).astype(jnp.bfloat16)
    squares = small_sum(
        jnp.stack(
            [jnp.sum(query_linear * query_linear, axis=1), jnp.sum(key_linear * key_linear, axis=1)]
        ),
        mlp_count,
        2,
    )
    query_square, key_square = squares[0], squares[1]
    cosine, sine = rotary_tables(positions)
    attended, kv_pages = self_attention(
        block_page_lookup[0],
        query_linear,
        key_linear,
        value_rows,
        lax.rsqrt(query_square / entire_width + EPSILON),
        lax.rsqrt(key_square / entire_width + EPSILON),
        query_key_gains,
        cosine,
        sine,
        segment,
    )
    text_owner = (
        jnp.arange(text_token_cache.shape[1] * text_token_cache.shape[2], dtype=jnp.int32)
        // text_token_cache.shape[2]
    )

    def out_rows(rows, which_map):
        return product(rows, output_projection, which_map, 1, 1280, jnp.bfloat16)[0]

    first_res, cross_in = middle_rows(
        out_rows(attended, 0),
        tokens,
        per_token[2],
        cross_norm_gain[None, :],
        jnp.zeros((1, tokens.shape[1]), jnp.float32),
        mlp_count,
        3,
    )
    cross_linear = product(cross_in, input_projection, 3, 1, 256, jnp.float32)[0]
    cross_square = small_sum(
        jnp.sum(cross_linear * cross_linear, axis=1)[None, :], mlp_count, 4
    )[0]
    cross_query = (
        cross_linear
        * lax.rsqrt(cross_square / entire_width + EPSILON)[:, None]
        * query_key_gains[2]
    ).astype(jnp.bfloat16)
    cross_out = cross_attention(
        cross_query,
        text_token_cache.reshape(2, text_owner.shape[0], local_width),
        segment,
        text_owner,
    )
    if tuned:
        layer_out = feed_forward(
            out_rows(cross_out, 1),
            first_res,
            1.0 + per_token[4],
            per_token[3],
            per_token[5],
            feedforward_up,
            feedforward_down,
            mlp_count,
            req_count,
            5,
        )
        return (layer_out, kv_pages)
    up_full = lax.all_gather(feedforward_up, "req", axis=0, tiled=True)
    second_res, mlp_in = middle_rows(
        out_rows(cross_out, 1),
        first_res,
        jnp.ones((1, tokens.shape[1]), jnp.float32),
        1.0 + per_token[4],
        per_token[3],
        mlp_count,
        5,
    )
    hidden = product(
        mlp_in,
        up_full[None],
        0,
        1,
        256,
        jnp.bfloat16,
        functools.partial(jax.nn.gelu, approximate=True),
    )[0]
    hidden_all = line_gather(hidden, req_count, 6)
    units, columns = feedforward_down.shape
    down_part = jnp.dot(
        hidden_all.reshape(req_count * group_rows, units),
        feedforward_down,
        preferred_element_type=jnp.float32,
    ).astype(jnp.bfloat16)
    down_own = exit_rows(
        down_part.reshape(req_count, mlp_count, own_count, columns), mlp_count, req_count, 7
    )
    layer_out = (
        second_res.astype(jnp.float32) + per_token[5] * down_own.astype(jnp.float32)
    ).astype(jnp.bfloat16)
    return (layer_out, kv_pages)


def solution(mesh):
    return jax.shard_map(
        body,
        mesh=mesh,
        in_specs=(
            P(("req", "mlp"), None),
            P("req", None, None),
            P("req", None),
            P("req"),
            P(),
            P("mlp", None, None),
            P("mlp", None, None, None),
            P(None, None, "mlp"),
            P(None, "mlp"),
            P(None, "req"),
            P("req", None),
            P(None, "mlp", None),
            P(),
            P(None, "req", None, "mlp"),
            P("req", "mlp"),
            P("mlp", "req"),
        ),
        out_specs=(P(("req", "mlp"), None), P(None, "req", None, "mlp")),
        check_vma=False,
    )
```

```python
import functools
import math

import jax
import jax.numpy as jnp
from jax import lax
from jax.experimental import pallas as pl
from jax.experimental.pallas import tpu as pltpu
from jax.sharding import PartitionSpec as P

HD = 128
PAGE = 16


EPSILON = 1e-06


PAIR = 2
MESH = pl.DeviceIdType.MESH
ANY = pl.BlockSpec(memory_space=pl.ANY)
VM = pl.BlockSpec(memory_space=pltpu.VMEM)


def comm_call(kernel, out_shape, in_specs, out_specs, scratch, ident, room=4):
    return pl.pallas_call(
        kernel,
        out_shape=out_shape,
        in_specs=in_specs,
        out_specs=out_specs,
        scratch_shapes=scratch,
        compiler_params=pltpu.CompilerParams(
            collective_id=ident, has_side_effects=True, vmem_limit_bytes=room << 20
        ),
    )


def remote(source, target, send_sem, recv_sem, axis, place):
    return pltpu.make_async_remote_copy(
        src_ref=source,
        dst_ref=target,
        send_sem=send_sem,
        recv_sem=recv_sem,
        device_id={axis: place},
        device_id_type=MESH,
    )


def shift(me, step, count):
    return lax.rem(me + (step + count) % count, count)


def greet(peers):
    barrier = pltpu.get_barrier_semaphore()
    for axis, place in peers:
        pl.semaphore_signal(barrier, inc=1, device_id={axis: place}, device_id_type=MESH)
    pl.semaphore_wait(barrier, len(peers))


def pair_places(count):
    me = lax.axis_index("mlp")
    outer, core = lax.div(me, PAIR), lax.rem(me, PAIR)
    sibling = outer * PAIR + (PAIR - 1 - core)
    peers = [
        shift(outer, k, count // PAIR) * PAIR + core for k in range(count // PAIR)
    ]
    sources = [
        shift(outer, -k, count // PAIR) * PAIR + core for k in range(count // PAIR)
    ]
    return me, core, sibling, peers, sources


def gather_sems(count):
    steps = count // PAIR
    return [pltpu.SemaphoreType.DMA(())] + [pltpu.SemaphoreType.DMA((steps,))] * 4


def gather_rows(count, places, own_ref, out_ref, own_sem, send_sem, recv_sem, pass_send, pass_recv):
    me, core, sibling, peers, sources = places
    own = pltpu.make_async_copy(own_ref, out_ref.at[me], own_sem)
    sends = [
        remote(own_ref, out_ref.at[me], send_sem.at[k], recv_sem.at[k], "mlp", peers[k])
        for k in range(1, count // PAIR)
    ]
    for copy in sends:
        copy.start()
    passes = [remote(own_ref, out_ref.at[me], pass_send.at[0], pass_recv.at[0], "mlp", sibling)]
    passes[0].start()
    own.start()
    for k in range(1, count // PAIR):
        sends[k - 1].wait_recv()
        block = out_ref.at[sources[k]]
        passes.append(remote(block, block, pass_send.at[k], pass_recv.at[k], "mlp", sibling))
        passes[-1].start()
    for copy in sends:
        copy.wait_send()
    for copy in passes:
        copy.wait()
    own.wait()


def entry_kernel(count, tok_ref, scale_ref, shift_ref, maps_ref, out_ref, up_ref, norm, map_own, map_send, map_recv, *sems):
    places = pair_places(count)
    me = places[0]
    slots, width = maps_ref.shape[0], up_ref.shape[-1]
    others = [shift(me, k, count) for k in range(1, count)]
    greet([("mlp", place) for place in others])

    def columns(place):
        return maps_ref.at[:, :, :, pl.ds(pl.multiple_of(place * width, 128), width)]

    target = up_ref.at[pl.ds(me * slots, slots)]
    own = pltpu.make_async_copy(columns(me), target, map_own)
    own.start()
    copies = [
        remote(columns(place), target, map_send.at[k], map_recv.at[k], "mlp", place)
        for k, place in enumerate(others)
    ]
    norm[...] = (
        layer_norm(tok_ref[...].astype(jnp.float32)) * (1.0 + scale_ref[...]) + shift_ref[...]
    ).astype(jnp.bfloat16)
    for copy in copies:
        copy.start()
    gather_rows(count, places, norm, out_ref, *sems)
    for copy in copies:
        copy.wait()
    own.wait()


def entry_rows(tokens, scale, shift_rows, maps, count):
    rows, width = tokens.shape
    slots, two, rank, total = maps.shape
    dma = pltpu.SemaphoreType.DMA
    gathered, up = comm_call(
        functools.partial(entry_kernel, count),
        (
            jax.ShapeDtypeStruct((count, rows, width), jnp.bfloat16),
            jax.ShapeDtypeStruct((count * slots, two, rank, total // count), maps.dtype),
        ),
        [VM, VM, VM, ANY],
        (ANY, ANY),
        [pltpu.VMEM((rows, width), jnp.bfloat16), dma(()), dma((count - 1,)), dma((count - 1,))]
        + gather_sems(count),
        0,
        8,
    )(tokens, scale, shift_rows, maps)
    return gathered.reshape(count * rows, width), up


def sum_blocks(count, places, block_of, near, mid, far, ns, nr, fs, fr):
    me, core, sibling, peers, sources = places
    steps = count // PAIR
    order = list(range(1, steps)) + [0]
    pairs = {}
    for k in order:
        other = peers[k] + (PAIR - 1 - 2 * core)
        pairs[k] = remote(block_of(other), near.at[k], ns.at[k], nr.at[k], "mlp", sibling)
        pairs[k].start()
    sends = []
    for k in range(1, steps):
        pairs[k].wait_recv()
        mid[k] = (
            block_of(peers[k])[...].astype(jnp.float32) + near[k].astype(jnp.float32)
        ).astype(jnp.bfloat16)
        sends.append(remote(mid.at[k], far.at[k], fs.at[k], fr.at[k], "mlp", peers[k]))
        sends[-1].start()
    pairs[0].wait_recv()
    total = block_of(me)[...].astype(jnp.float32) + near[0].astype(jnp.float32)
    for k in range(1, steps):
        sends[k - 1].wait_recv()
        total = total + far[k].astype(jnp.float32)
    for k in order:
        pairs[k].wait_send()
    for copy in sends:
        copy.wait_send()
    return total


def sum_scratch(count, extent):
    steps = count // PAIR
    return [pltpu.VMEM((steps,) + extent, jnp.bfloat16)] * 3 + [
        pltpu.SemaphoreType.DMA((steps,))
    ] * 4


def middle_kernel(count, part_ref, base_ref, gate_ref, scale_ref, shift_ref, res_ref, out_ref, near, mid, far, norm, ns, nr, fs, fr, *sems):
    places = pair_places(count)
    greet([("mlp", places[2])] + [("mlp", place) for place in places[3][1:]])
    total = sum_blocks(
        count, places, lambda place: part_ref.at[place], near, mid, far, ns, nr, fs, fr
    )
    res = (base_ref[...].astype(jnp.float32) + gate_ref[...] * total).astype(jnp.bfloat16)
    res_ref[...] = res
    norm[...] = (layer_norm(res.astype(jnp.float32)) * scale_ref[...] + shift_ref[...]).astype(
        jnp.bfloat16
    )
    gather_rows(count, places, norm, out_ref, *sems)


def middle_rows(part, base, gate, scale, shift_rows, count, ident):
    rows, width = base.shape
    scratch = sum_scratch(count, (rows, width))
    res, gathered = comm_call(
        functools.partial(middle_kernel, count),
        (
            jax.ShapeDtypeStruct((rows, width), jnp.bfloat16),
            jax.ShapeDtypeStruct((count, rows, width), jnp.bfloat16),
        ),
        [VM] * 5,
        (VM, ANY),
        scratch[:3] + [pltpu.VMEM((rows, width), jnp.bfloat16)] + scratch[3:] + gather_sems(count),
        ident,
        24,
    )(part.reshape(count, rows, width), base, gate, scale, shift_rows)
    return res, gathered.reshape(count * rows, width)


def small_kernel(count, own_ref, out_ref, slots, send_sem, recv_sem):
    me = lax.axis_index("mlp")
    others = [shift(me, k, count) for k in range(1, count)]
    greet([("mlp", place) for place in others])
    copies = [
        remote(own_ref, slots.at[k], send_sem.at[k], recv_sem.at[k], "mlp", place)
        for k, place in enumerate(others)
    ]
    for copy in copies:
        copy.start()
    total = own_ref[...].astype(jnp.float32)
    for k, copy in enumerate(copies):
        copy.wait_recv()
        total = total + slots[k].astype(jnp.float32)
    out_ref[...] = total
    for copy in copies:
        copy.wait_send()


def small_sum(own, count, ident):
    dma = pltpu.SemaphoreType.DMA((count - 1,))
    return comm_call(
        functools.partial(small_kernel, count),
        jax.ShapeDtypeStruct(own.shape, jnp.float32),
        [VM],
        VM,
        [pltpu.VMEM((count - 1,) + own.shape, own.dtype), dma, dma],
        ident,
    )(own)


def line_kernel(count, own_ref, out_ref, own_sem, rs, rr, ls, lr):
    me = lax.axis_index("req")
    right, left = shift(me, 1, count), shift(me, -1, count)
    greet([("req", right), ("req", left)])
    own = pltpu.make_async_copy(own_ref, out_ref.at[me], own_sem)
    own.start()

    pieces = rs.shape[1]
    rows = own_ref.shape[0] // pieces

    def hop(step, piece, sign):
        block = jnp.clip(me - sign * step, 0, count - 1)
        part = pl.ds(piece * rows, rows)
        source = own_ref.at[part] if step == 0 else out_ref.at[block, part]
        send, recv, place = (rs, rr, right) if sign > 0 else (ls, lr, left)
        return remote(
            source,
            out_ref.at[block, part],
            send.at[step, piece],
            recv.at[step, piece],
            "req",
            place,
        )

    def each(step, work):
        for piece in range(pieces):
            work(step, piece)

    def advance(step, piece):
        if step > 0:

            @pl.when(me >= step)
            def _():
                hop(step - 1, piece, 1).wait_recv()

            @pl.when(me + step < count)
            def _():
                hop(step - 1, piece, -1).wait_recv()

        @pl.when((me >= step) & (me < count - 1))
        def _():
            hop(step, piece, 1).start()

        @pl.when((me + step < count) & (me > 0))
        def _():
            hop(step, piece, -1).start()

    def finish(step, piece):
        @pl.when(me >= count - 1)
        def _():
            hop(step, piece, 1).wait_recv()

        @pl.when(me < 1)
        def _():
            hop(step, piece, -1).wait_recv()

    def drain(step, piece):
        @pl.when((me >= step) & (me < count - 1))
        def _():
            hop(step, piece, 1).wait_send()

        @pl.when((me + step < count) & (me > 0))
        def _():
            hop(step, piece, -1).wait_send()

    for step in range(count - 1):
        each(step, advance)
    each(count - 2, finish)
    for step in range(count - 1):
        each(step, drain)
    own.wait()


def line_gather(own, count, ident):
    dma = pltpu.SemaphoreType.DMA
    return comm_call(
        functools.partial(line_kernel, count),
        jax.ShapeDtypeStruct((count,) + own.shape, own.dtype),
        [ANY],
        ANY,
        [dma(())] + [dma((count - 1, 4))] * 4,
        ident,
    )(own)


def exit_kernel(count, lines, part_ref, out_ref, near, mid, far, final, ns, nr, fs, fr, own_sem, send_sem, recv_sem):
    places = pair_places(count)
    me, core, sibling, peers, _ = places
    steps = count // PAIR
    line = lax.axis_index("req")
    groups = [shift(line, k + 1, lines) for k in range(lines)]
    greet(
        [("mlp", sibling)]
        + [("mlp", place) for place in peers[1:]]
        + [("req", place) for place in groups[:-1]]
    )
    order = list(range(1, steps)) + [0]
    pairs, sends, copies = {}, [], []
    for i, group in enumerate(groups):
        for k in order:
            other = peers[k] + (PAIR - 1 - 2 * core)
            pairs[i, k] = remote(
                part_ref.at[group, other], near.at[i, k], ns.at[i, k], nr.at[i, k], "mlp", sibling
            )
            pairs[i, k].start()
    for i, group in enumerate(groups):
        for k in range(1, steps):
            pairs[i, k].wait_recv()
            mid[i, k] = (
                part_ref[group, peers[k]].astype(jnp.float32) + near[i, k].astype(jnp.float32)
            ).astype(jnp.bfloat16)
            sends.append(
                remote(mid.at[i, k], far.at[i, k], fs.at[i, k], fr.at[i, k], "mlp", peers[k])
            )
            sends[-1].start()
    width = final.shape[-1]
    target = out_ref.at[:, pl.ds(pl.multiple_of(line * width, 128), width)]
    for i, group in enumerate(groups):
        pairs[i, 0].wait_recv()
        total = part_ref[group, me].astype(jnp.float32) + near[i, 0].astype(jnp.float32)
        for k in range(1, steps):
            sends[i * (steps - 1) + k - 1].wait_recv()
            total = total + far[i, k].astype(jnp.float32)
        final[i] = total.astype(jnp.bfloat16)
        if i < lines - 1:
            copies.append(
                remote(final.at[i], target, send_sem.at[i], recv_sem.at[i], "req", group)
            )
        else:
            copies.append(pltpu.make_async_copy(final.at[i], target, own_sem))
        copies[-1].start()
    for copy in list(pairs.values()) + sends:
        copy.wait_send()
    for copy in copies:
        copy.wait()


def exit_rows(part, count, lines, ident):
    groups, _, rows, width = part.shape
    steps = count // PAIR
    dma = pltpu.SemaphoreType.DMA
    return comm_call(
        functools.partial(exit_kernel, count, lines),
        jax.ShapeDtypeStruct((rows, lines * width), jnp.bfloat16),
        [VM],
        VM,
        [pltpu.VMEM((groups, steps, rows, width), jnp.bfloat16)] * 3
        + [pltpu.VMEM((groups, rows, width), jnp.bfloat16)]
        + [dma((groups, steps))] * 4
        + [dma(()), dma((lines - 1,)), dma((lines - 1,))],
        ident,
        24,
    )(part)


def lines_order(lines):
    middle = lines // 2
    return [middle - 1, middle] + [g for g in range(lines) if g not in (middle - 1, middle)]


def dot_tiles(x, w_ref, out_ref, put, tile):
    width = w_ref.shape[1]

    @pl.loop(0, width // tile)
    def _(i):
        columns = pl.ds(pl.multiple_of(i * tile, tile), tile)
        put(columns, jnp.dot(x, w_ref[:, columns], preferred_element_type=jnp.float32))


def ff_kernel(count, lines, part_ref, base_ref, scale_ref, shift_ref, gate_ref, up_hbm, down_hbm, out_ref,
              near, mid, far, ns, nr, fs, fr,
              up_ref, down_ref, w_sem, norm, res, act, a_send, a_recv, g_send, g_recv, p_send, p_recv,
              pbuf, from_outer, from_partner, staged, hid, es, er, ts, tr, ho_s, hp_s, h_r,
              dn, near2, mid2, far2, ns2, nr2, fs2, fr2, final, back, bs, br):
    places = pair_places(count)
    me, core, sibling, peers, sources = places
    steps = count // PAIR
    line = lax.axis_index("req")
    order = lines_order(lines)
    is_mid = (line == 1) | (line == 2)
    outer = jnp.where(line == 1, 0, 3)
    partner = 3 - line
    inner = jnp.where(line == 0, 1, 2)
    greet(
        [("mlp", sibling)]
        + [("mlp", place) for place in peers[1:]]
        + [("req", shift(line, k, lines)) for k in range(1, lines)]
    )
    weights = [
        pltpu.make_async_copy(up_hbm, up_ref, w_sem.at[0]),
        pltpu.make_async_copy(down_hbm, down_ref, w_sem.at[1]),
    ]
    for copy in weights:
        copy.start()
    total = sum_blocks(count, places, lambda place: part_ref.at[place], near, mid, far, ns, nr, fs, fr)
    res[...] = (base_ref[...].astype(jnp.float32) + total).astype(jnp.bfloat16)
    norm[...] = (
        layer_norm(res[...].astype(jnp.float32)) * scale_ref[...] + shift_ref[...]
    ).astype(jnp.bfloat16)

    rows, width = norm.shape
    part_width = width // lines

    def slice_of(place):
        return pl.ds(pl.multiple_of(place * part_width, 128), part_width)

    def spread_to(k):
        place = lax.rem(line + k, lines)
        return remote(
            norm.at[:, slice_of(place)], act.at[line, me], a_send.at[k], a_recv.at[line], "req", place
        )

    act[line, me] = norm[:, slice_of(line)]

    @pl.when(is_mid)
    def _():
        for k in (2, 1, 3):
            spread_to(k).start()

    def across(g, k):
        return remote(act.at[g, me], act.at[g, me], g_send.at[g, k], g_recv.at[g, k], "mlp", peers[k])

    def passed(g, k):
        block = act.at[g, sources[k]]
        return remote(block, block, p_send.at[g, k], p_recv.at[g, k], "mlp", sibling)

    def from_sibling(g, k):
        block = act.at[g, sources[k] + PAIR - 1 - 2 * core]
        return remote(block, block, p_send.at[g, k], p_recv.at[g, k], "mlp", sibling)

    def landed(p):
        g = order[p]

        @pl.when(line != g)
        def _():
            remote(norm.at[:, slice_of(g)], act.at[g, me], a_send.at[0], a_recv.at[g], "req", g).wait_recv()

    def opened(p):
        if p < lines:
            g = order[p]
            if p > 1:
                landed(p)
            for k in range(1, steps):
                across(g, k).start()
            passed(g, 0).start()

    tall = count * rows
    chunks = from_outer.shape[1]
    some = tall // chunks

    def chunk(j):
        return pl.ds(pl.multiple_of(j * some, some), some)

    def to_inner(g, j):
        return remote(pbuf.at[g, chunk(j)], from_outer.at[g, j], es.at[g, j], er.at[g, j], "req", inner)

    def to_partner(g, j):
        return remote(staged.at[g, j], from_partner.at[g, j], ts.at[g, j], tr.at[g, j], "req", partner)

    def out_to(g, j, place, sem):
        block = hid.at[g, chunk(j)]
        return remote(block, block, sem.at[g, j], h_r.at[g, j], "req", place)

    def gathered(p):
        g = order[p]
        for k in range(1, steps):
            remote(act.at[g, me], act.at[g, sources[k]], g_send.at[g, k], g_recv.at[g, k], "mlp", peers[k]).wait_recv()
            passed(g, k).start()
        opened(p + 1)
        for k in range(steps):
            from_sibling(g, k).wait_recv()

    def first_product(p):
        g = order[p]

        def put(columns, value):
            pbuf[g, :, columns] = value.astype(jnp.bfloat16)

        dot_tiles(act[g].reshape(tall, part_width), up_ref, pbuf, put, 256)

        @pl.when(jnp.logical_not(is_mid))
        def _():
            for j in range(chunks):
                to_inner(g, j).start()

    def theirs(g, i):
        j = 2 * i + 2 - line
        to_inner(g, j).wait_recv()
        staged[g, j] = (
            pbuf[g, chunk(j)].astype(jnp.float32) + from_outer[g, j].astype(jnp.float32)
        ).astype(jnp.bfloat16)
        to_partner(g, j).start()

    def mine(g, i):
        j = 2 * i + line - 1
        to_inner(g, j).wait_recv()
        to_partner(g, j).wait_recv()
        value = (
            pbuf[g, chunk(j)].astype(jnp.float32)
            + from_outer[g, j].astype(jnp.float32)
            + from_partner[g, j].astype(jnp.float32)
        )
        hid[g, chunk(j)] = jax.nn.gelu(value, approximate=True).astype(jnp.bfloat16)
        out_to(g, j, partner, hp_s).start()
        out_to(g, j, outer, ho_s).start()

    def forward(g, i):
        j = 2 * i + 2 - line
        out_to(g, j, partner, hp_s).wait_recv()
        out_to(g, j, outer, ho_s).start()

    def middle(p):
        @pl.when(is_mid)
        def _():
            g = order[p]
            pairs = chunks // 2
            theirs(g, 0)
            if p > 0:
                forward(order[p - 1], pairs - 1)
            for i in range(pairs):
                if i + 1 < pairs:
                    theirs(g, i + 1)
                mine(g, i)
                if i > 0:
                    forward(g, i - 1)

    def all_hidden(p):
        g = order[p]
        if p == lines - 1:
            @pl.when(is_mid)
            def _():
                forward(g, chunks // 2 - 1)

        @pl.when(jnp.logical_not(is_mid))
        def _():
            for j in range(chunks):
                out_to(g, j, inner, ho_s).wait_recv()

    def pair_copy(g, k):
        other = peers[k] + (PAIR - 1 - 2 * core)
        return remote(dn.at[g, other], near2.at[g, k], ns2.at[g, k], nr2.at[g, k], "mlp", sibling)

    def far_copy(g, k):
        return remote(mid2.at[g, k], far2.at[g, k], fs2.at[g, k], fr2.at[g, k], "mlp", peers[k])

    k_order = list(range(1, steps)) + [0]

    def second_product(p):
        g = order[p]

        def put(columns, value):
            dn[g, :, :, columns] = value.astype(jnp.bfloat16).reshape(count, rows, 256)

        dot_tiles(hid[g], down_ref, dn, put, 256)
        for k in k_order:
            pair_copy(g, k).start()

    def relay(p):
        g = order[p]
        for k in range(1, steps):
            pair_copy(g, k).wait_recv()
            mid2[g, k] = (
                dn[g, peers[k]].astype(jnp.float32) + near2[g, k].astype(jnp.float32)
            ).astype(jnp.bfloat16)
            far_copy(g, k).start()

    def home(g):
        return remote(final.at[g], back.at[line], bs.at[g], br.at[line], "req", g)

    def finish(p):
        g = order[p]
        pair_copy(g, 0).wait_recv()
        value = dn[g, me].astype(jnp.float32) + near2[g, 0].astype(jnp.float32)
        for k in range(1, steps):
            far_copy(g, k).wait_recv()
            value = value + far2[g, k].astype(jnp.float32)
        final[g] = value.astype(jnp.bfloat16)

        @pl.when(line == g)
        def _():
            back[g] = final[g]

        @pl.when(line != g)
        def _():
            home(g).start()

    landed(0)
    opened(0)
    landed(1)

    @pl.when(jnp.logical_not(is_mid))
    def _():
        for far_place in (3, 2, 1):
            spread_to(jnp.where(line == 0, far_place, 4 - far_place)).start()

    weights[0].wait()
    gathered(0)
    first_product(0)
    gathered(1)
    first_product(1)
    middle(0)
    gathered(2)
    first_product(2)
    gathered(3)
    first_product(3)
    weights[1].wait()
    middle(1)
    all_hidden(0)
    second_product(0)
    relay(0)
    middle(2)
    all_hidden(1)
    second_product(1)
    finish(0)
    relay(1)
    middle(3)
    all_hidden(2)
    second_product(2)
    finish(1)
    relay(2)
    all_hidden(3)
    second_product(3)
    finish(2)
    relay(3)
    finish(3)

    for q in range(lines):
        columns = slice(q * part_width, (q + 1) * part_width)

        @pl.when(line != q)
        def _():
            remote(final.at[q], back.at[q], bs.at[q], br.at[q], "req", q).wait_recv()

        out_ref[:, columns] = (
            res[:, columns].astype(jnp.float32) + gate_ref[:, columns] * back[q].astype(jnp.float32)
        ).astype(jnp.bfloat16)

    for k in range(1, lines):
        spread_to(k).wait_send()
    for g in order:
        for k in range(1, steps):
            across(g, k).wait_send()
            far_copy(g, k).wait_send()
        for k in range(steps):
            passed(g, k).wait_send()
            pair_copy(g, k).wait_send()

        @pl.when(line != g)
        def _():
            home(g).wait_send()

        @pl.when(is_mid)
        def _():
            for i in range(chunks // 2):
                to_partner(g, 2 * i + 2 - line).wait_send()
                out_to(g, 2 * i + line - 1, partner, hp_s).wait_send()
            for j in range(chunks):
                out_to(g, j, outer, ho_s).wait_send()

        @pl.when(jnp.logical_not(is_mid))
        def _():
            for j in range(chunks):
                to_inner(g, j).wait_send()


def feed_forward(part, base, scale, shift_rows, gate, up, down, count, lines, ident):
    rows, width = base.shape
    steps = count // PAIR
    depth, units = up.shape
    tall = rows * count
    chunks = 4
    dma = pltpu.SemaphoreType.DMA
    vm = lambda *extent: pltpu.VMEM(extent, jnp.bfloat16)
    scratch = (
        sum_scratch(count, (rows, width))
        + [vm(depth, units), vm(units, depth), dma((2,)), vm(rows, width), vm(rows, width)]
        + [vm(lines, count, rows, depth), dma((lines,)), dma((lines,))]
        + [dma((lines, steps))] * 4
        + [vm(lines, tall, units), vm(lines, chunks, tall // chunks, units)]
        + [vm(lines, chunks, tall // chunks, units)] * 2
        + [vm(lines, tall, units)]
        + [dma((lines, chunks))] * 7
        + [vm(lines, count, rows, depth)]
        + [vm(lines, steps, rows, depth)] * 3
        + [dma((lines, steps))] * 4
        + [vm(lines, rows, depth)] * 2
        + [dma((lines,))] * 2
    )
    return comm_call(
        functools.partial(ff_kernel, count, lines),
        jax.ShapeDtypeStruct((rows, width), jnp.bfloat16),
        [VM] * 5 + [ANY] * 2,
        VM,
        scratch,
        ident,
        56,
    )(part.reshape(count, rows, width), base, scale, shift_rows, gate, up, down)


def layer_norm(values):
    center = values - jnp.mean(values, axis=-1, keepdims=True)
    spread = jnp.mean(center * center, axis=-1, keepdims=True)
    return center * lax.rsqrt(spread + EPSILON)


def rotary_tables(grid):
    half_dim = HD // 2
    spatial = half_dim // 3
    temporal = half_dim - 2 * spatial
    column = jnp.arange(HD, dtype=jnp.int32)
    sign = jnp.where(column < half_dim, -1.0, 1.0).astype(jnp.float32)
    column = column % half_dim
    which_axis = jnp.where(
        column < temporal, 0, jnp.where(column < temporal + spatial, 1, 2)
    ).astype(jnp.int32)
    offset = jnp.where(
        which_axis == 0, 0, jnp.where(which_axis == 1, temporal, temporal + spatial)
    ).astype(jnp.int32)
    span_size = jnp.where(which_axis == 0, temporal, spatial).astype(jnp.float32)
    frequency = jnp.exp(-(column - offset).astype(jnp.float32) / span_size * math.log(10000.0))
    grid = grid.astype(jnp.float32)[:, :, None]
    coordinate = jnp.where(
        which_axis == 0, grid[0], jnp.where(which_axis == 1, grid[1], grid[2])
    )
    angles = coordinate * frequency[None, :]
    return (jnp.cos(angles), jnp.sin(angles) * sign[None, :])


def attend(queries, key_rows, value_rows, allowed):
    scores = lax.dot_general(
        queries, key_rows, (((1,), (1,)), ((), ())), preferred_element_type=jnp.float32
    ) * (1.0 / math.sqrt(HD))
    weights = jnp.exp(jnp.where(allowed, scores, -1e30))
    weights = weights * (1.0 / jnp.sum(weights, axis=-1, keepdims=True))
    return jnp.dot(
        weights.astype(jnp.bfloat16), value_rows, preferred_element_type=jnp.float32
    ).astype(jnp.bfloat16)


def quad():
    me = lax.axis_index("mlp")
    core, x, y = lax.rem(me, 2), lax.rem(lax.div(me, 2), 2), lax.div(me, 4)

    def at(row, column, which):
        return (row * 2 + column) * 2 + which

    return me, at(y, x, 1 - core), at(y, 1 - x, core), at(1 - y, x, core), at(1 - y, 1 - x, core)


def part_columns(width, parts, c):
    return slice(c * (width // parts), (c + 1) * (width // parts))


class QuadGather:
    def __init__(self, parts, own_ref, out_ref, own_sem, xs, xr, ys, yr, fs, fr, ss, sr):
        self.parts, self.own_ref, self.out_ref = parts, own_ref, out_ref
        self.me, self.sib, self.xn, self.yn, self.dg = quad()
        self.sems = (xs, xr, ys, yr, fs, fr, ss, sr)
        self.half = parts // 2
        self.own = pltpu.make_async_copy(own_ref, out_ref.at[self.me], own_sem)
        self.x_order = list(range(parts))
        self.y_order = list(range(self.half, parts)) + list(range(self.half))
        self.order = [c for two in zip(range(self.half), range(self.half, parts)) for c in two]
        self.across, self.up, self.onward, self.passes = {}, {}, {}, {}

    def piece(self, place, c):
        return self.out_ref.at[place, :, part_columns(self.own_ref.shape[1], self.parts, c)]

    def mine(self, c):
        return self.own_ref.at[:, part_columns(self.own_ref.shape[1], self.parts, c)]

    def hand(self, kind, place, c):
        send, recv = self.sems[6].at[kind, c], self.sems[7].at[kind, c]
        source = self.piece(place, c) if kind else self.mine(c)
        self.passes[kind, c] = remote(source, self.piece(place, c), send, recv, "mlp", self.sib)
        self.passes[kind, c].start()

    def start(self):
        xs, xr, ys, yr = self.sems[:4]
        self.own.start()
        for i in range(self.parts):
            c = self.x_order[i]
            self.across[c] = remote(self.mine(c), self.piece(self.me, c), xs.at[c], xr.at[c], "mlp", self.xn)
            self.across[c].start()
            c = self.y_order[i]
            self.up[c] = remote(self.mine(c), self.piece(self.me, c), ys.at[c], yr.at[c], "mlp", self.yn)
            self.up[c].start()
        for c in self.order:
            self.hand(0, self.me, c)

    def send_on(self, place, c, to):
        fs, fr = self.sems[4:6]
        block = self.piece(place, c)
        self.onward[c] = remote(block, block, fs.at[c], fr.at[c], "mlp", to)
        self.onward[c].start()

    def step(self, i):
        c = self.x_order[i]
        self.across[c].wait_recv()
        if c < self.half:
            self.send_on(self.xn, c, self.yn)
        self.hand(1, self.xn, c)
        c = self.y_order[i]
        self.up[c].wait_recv()
        if c >= self.half:
            self.send_on(self.yn, c, self.xn)
        self.hand(2, self.yn, c)

    def corner(self, c):
        self.onward[c].wait_recv()
        self.hand(3, self.dg, c)

    def whole(self, c):
        for kind in range(4):
            self.passes[kind, c].wait_recv()

    def drain(self):
        for group in (self.across, self.up, self.onward, self.passes):
            for copy in group.values():
                copy.wait_send()


def quad_sems(parts):
    dma = pltpu.SemaphoreType.DMA
    return [dma(())] + [dma((parts,))] * 6 + [dma((4, parts))] * 2


def share(own_ref, slots_ref, send_sem, recv_sem, count):
    me = lax.axis_index("mlp")
    copies = [
        remote(own_ref, slots_ref.at[k], send_sem.at[k], recv_sem.at[k], "mlp", shift(me, k, count))
        for k in range(1, count)
    ]
    for copy in copies:
        copy.start()
    return copies


def pick_rows(mod_ref, which, owner):
    chosen = mod_ref[0, which : which + 1, :]
    for request in range(1, mod_ref.shape[0]):
        chosen = jnp.where(owner == request, mod_ref[request, which : which + 1, :], chosen)
    return chosen


def row_to_column(row, lanes=128):
    return jnp.transpose(jnp.broadcast_to(row, (lanes, row.shape[1])))


def column_to_rows(column, lanes=128):
    return jnp.transpose(jnp.broadcast_to(column, (column.shape[0], lanes)))[0:8]


def enter_kernel(count, parts, tok_ref, mod_ref, owner_ref, seg_ref, pick_ref, down_ref, maps_ref, w_hbm,
                 lin_ref, value_ref, scale_ref,
                 norm, rows_all, w_ref, w_sem, acc, code_acc, code_own, code_slots, cs, cr,
                 chosen, near, mid, far, us, ur, vs, vr, sq_own, sq_slots, qs, qr, *sems):
    me, sib, xn, yn, dg = quad()
    core = lax.rem(me, PAIR)
    flip = 1 - 2 * core
    greet([("mlp", shift(me, k, count)) for k in range(1, count)])
    rows, width = tok_ref.shape
    depth = width // parts
    tall = rows * count
    heads = acc.shape[2]
    owner = owner_ref[...]
    norm[...] = (
        layer_norm(tok_ref[...].astype(jnp.float32)) * (1.0 + pick_rows(mod_ref, 1, owner))
        + pick_rows(mod_ref, 0, owner)
    ).astype(jnp.bfloat16)
    gather = QuadGather(parts, norm, rows_all, *sems)
    gather.start()
    loads = {}
    for c in gather.order:
        block = pl.ds(c * depth, depth)
        loads[c] = pltpu.make_async_copy(w_hbm.at[0:3, block], w_ref.at[:, block], w_sem.at[c])
        loads[c].start()

    slots = maps_ref.shape[0]
    requests = mod_ref.shape[0]
    rank = maps_ref.shape[2]
    for j in range(2):
        for r in range(requests):
            for place in range(count):
                columns = slice(place * heads, (place + 1) * heads)
                total = jnp.zeros((rank, heads), jnp.float32)
                for s in range(slots):
                    total = total + maps_ref[s, j, :, columns].astype(jnp.float32) * pick_ref[
                        r * slots + s : r * slots + s + 1, 0:1
                    ]
                chosen[place, j, r * rank : (r + 1) * rank] = total.astype(jnp.bfloat16)

    dest = [me, xn, yn, dg]
    pair = [
        remote(chosen.at[dest[t] + flip], near.at[t], us.at[t], ur.at[t], "mlp", sib) for t in range(4)
    ]
    out = {
        t: remote(mid.at[t], far.at[t], vs.at[t], vr.at[t], "mlp", dest[t]) for t in (1, 2, 3)
    }

    def code_part(c):
        x = rows_all[:, :, part_columns(width, parts, c)].reshape(tall, depth)
        code_acc[...] += lax.dot_general(
            down_ref[:, part_columns(width, parts, c)], x, (((1,), (1,)), ((), ())),
            preferred_element_type=jnp.float32,
        )

    def product_part(c, fresh):
        loads[c].wait()

        @pl.loop(0, 3)
        def _(i):
            x = rows_all[:, :, part_columns(width, parts, c)].reshape(tall, depth)
            value = jnp.dot(x, w_ref[i, c * depth : (c + 1) * depth], preferred_element_type=jnp.float32)
            acc[i] = value if fresh else acc[i] + value

    code_acc[...] = jnp.zeros_like(code_acc)
    order = gather.order
    for i in range(parts):
        gather.step(i)
    for copy in pair:
        copy.start()
    for c in order[:2]:
        gather.corner(c)
    for t in (3, 1, 2):
        pair[t].wait_recv()
        mid[t] = chosen[dest[t]] + near[t]
        out[t].start()
    gather.own.wait()
    for c in order[:2]:
        gather.whole(c)
        code_part(c)
        product_part(c, c == order[0])
    for k in range(2, parts, 2):
        for c in order[k : k + 2]:
            gather.corner(c)
        for c in order[k : k + 2]:
            gather.whole(c)
            code_part(c)
            if c != order[-1]:
                product_part(c, False)
    segment = seg_ref[...]
    doubled = 2 * rank
    code = jnp.zeros((doubled, tall), jnp.float32)
    for s in range(slots):
        held = jnp.zeros((1, tall), jnp.float32)
        for r in range(requests):
            held = held + jnp.where(segment == r, pick_ref[r * slots + s : r * slots + s + 1, 0:1], 0.0)
        code = code + held * code_acc[s * doubled : (s + 1) * doubled]
    code_own[...] = code.astype(jnp.bfloat16)
    shared = share(code_own, code_slots, cs, cr, count)
    product_part(order[-1], False)
    pair[0].wait_recv()
    up = chosen[me].astype(jnp.float32) + near[0].astype(jnp.float32)
    for t in (1, 2, 3):
        out[t].wait_recv()
        up = up + far[t].astype(jnp.float32)
    up = up.astype(jnp.bfloat16)
    code = code_own[...].astype(jnp.float32)
    for k, copy in enumerate(shared):
        copy.wait_recv()
        code = code + code_slots[k + 1].astype(jnp.float32)

    def adapted(j):
        spread = jnp.concatenate(
            [jnp.where(segment == r, code[j * rank : (j + 1) * rank], 0.0) for r in range(requests)], axis=0
        )
        return jnp.dot(jnp.transpose(spread).astype(jnp.bfloat16), up[j], preferred_element_type=jnp.float32)

    query = acc[0] + adapted(0)
    key = acc[1]
    sq_own[0] = column_to_rows(jnp.sum(query * query, axis=1, keepdims=True))
    sq_own[1] = column_to_rows(jnp.sum(key * key, axis=1, keepdims=True))
    squares = share(sq_own, sq_slots, qs, qr, count)
    lin_ref[0] = query
    lin_ref[1] = key
    value_ref[...] = (acc[2] + adapted(1)).astype(jnp.bfloat16)
    total = sq_own[...]
    for k, copy in enumerate(squares):
        copy.wait_recv()
        total = total + sq_slots[k + 1]
    scale = lax.rsqrt(total / (heads * count) + EPSILON)
    for i in range(2):
        scale_ref[i] = row_to_column(scale[i, 0:1])
    gather.drain()
    for copy in shared + squares + pair + list(out.values()):
        copy.wait_send()


def enter(tokens, modulation, owner, segment, pick, down, maps, weights, count):
    rows, width = tokens.shape
    parts = 4
    heads = weights.shape[2]
    tall = rows * count
    slots, two, rank, _ = maps.shape
    requests = modulation.shape[0]
    dma = pltpu.SemaphoreType.DMA
    vm = lambda *extent: pltpu.VMEM(extent, jnp.bfloat16)
    vf = lambda *extent: pltpu.VMEM(extent, jnp.float32)
    up = (two, requests * rank, heads)
    scratch = (
        [vm(rows, width), vm(count, rows, width), vm(3, width, heads), dma((parts,)), vf(3, tall, heads)]
        + [vf(slots * two * rank, tall), vm(two * rank, tall), vm(count, two * rank, tall), dma((count,)), dma((count,))]
        + [vm(count, *up), vm(4, *up), vm(4, *up), vm(4, *up)]
        + [dma((4,))] * 4
        + [vf(2, 8, tall), vf(count, 2, 8, tall), dma((count,)), dma((count,))]
        + quad_sems(parts)
    )
    return comm_call(
        functools.partial(enter_kernel, count, parts),
        (
            jax.ShapeDtypeStruct((2, tall, heads), jnp.float32),
            jax.ShapeDtypeStruct((tall, heads), jnp.bfloat16),
            jax.ShapeDtypeStruct((2, tall, 128), jnp.float32),
        ),
        [VM] * 7 + [ANY],
        (VM, VM, VM),
        scratch,
        0,
        48,
    )(tokens, modulation, owner, segment, pick, down, maps, weights)


def self_kernel(page_ref, q_ref, k_ref, v_ref, qs_ref, ks_ref, gain_ref, cos_ref, sin_ref, seg_ref, segs_ref, out_ref, kv_ref):
    cosine, sine = cos_ref[...], sin_ref[...]
    allowed = seg_ref[...] == segs_ref[...]

    def turned(ref, scale, gain, columns):
        rows = ref[:, columns] * scale * gain_ref[gain : gain + 1, columns]
        return (rows * cosine + pltpu.roll(rows, HD // 2, 1) * sine).astype(jnp.bfloat16)

    for head in range(q_ref.shape[1] // HD):
        columns = slice(head * HD, (head + 1) * HD)
        query = turned(q_ref, qs_ref[...], 0, columns)
        key = turned(k_ref, ks_ref[...], 1, columns)
        value = v_ref[:, columns]
        out_ref[:, columns] = attend(query, key, value, allowed)
        for block in range(kv_ref.shape[1]):
            page = page_ref[block]
            rows = slice(block * PAGE, (block + 1) * PAGE)
            kv_ref[0, page, :, columns] = key[rows]
            kv_ref[1, page, :, columns] = value[rows]


def self_attention(pages, query, key, value, query_scale, key_scale, gains, cosine, sine, segment):
    rows, width = query.shape
    return pl.pallas_call(
        self_kernel,
        out_shape=(
            jax.ShapeDtypeStruct((rows, width), jnp.bfloat16),
            jax.ShapeDtypeStruct((2, pages.shape[0], PAGE, width), jnp.bfloat16),
        ),
        in_specs=[pl.BlockSpec(memory_space=pltpu.SMEM)] + [VM] * 10,
        out_specs=(VM, VM),
        compiler_params=pltpu.CompilerParams(vmem_limit_bytes=16 << 20),
    )(
        pages,
        query,
        key,
        value,
        query_scale[:, None],
        key_scale[:, None],
        gains,
        cosine,
        sine,
        segment[:, None],
        segment[None, :],
    )


def cross_kernel(q_ref, k_ref, v_ref, seg_ref, owner_ref, out_ref):
    out_ref[...] = attend(q_ref[...], k_ref[0], v_ref[0], seg_ref[...] == owner_ref[...])


def cross_attention(query, cache, segment, owner):
    rows, width = query.shape
    texts = cache.shape[1]
    head = pl.BlockSpec((rows, HD), lambda h: (0, h))
    return pl.pallas_call(
        cross_kernel,
        out_shape=jax.ShapeDtypeStruct((rows, width), jnp.bfloat16),
        grid=(width // HD,),
        in_specs=[
            head,
            pl.BlockSpec((1, texts, HD), lambda h: (0, 0, h)),
            pl.BlockSpec((1, texts, HD), lambda h: (1, 0, h)),
            pl.BlockSpec((rows, 1), lambda h: (0, 0)),
            pl.BlockSpec((1, texts), lambda h: (0, 0)),
        ],
        out_specs=head,
        compiler_params=pltpu.CompilerParams(vmem_limit_bytes=24 << 20),
    )(query, cache, cache, segment[:, None], owner[None, :])


def product_kernel(act, x_ref, w_ref, out_ref):
    out_ref[0] = act(
        jnp.dot(x_ref[...], w_ref[0], preferred_element_type=jnp.float32)
    ).astype(out_ref.dtype)


def product(rows_in, maps, first, amount, tile, dtype, act=lambda part: part):
    rows, depth = rows_in.shape
    width = maps.shape[2]
    tile = min(tile, width)
    return pl.pallas_call(
        functools.partial(product_kernel, act),
        out_shape=jax.ShapeDtypeStruct((amount, rows, width), dtype),
        grid=(amount, width // tile),
        in_specs=[
            pl.BlockSpec((rows, depth), lambda i, j: (0, 0)),
            pl.BlockSpec((1, depth, tile), lambda i, j: (first + i, 0, j)),
        ],
        out_specs=pl.BlockSpec((1, rows, tile), lambda i, j: (i, 0, j)),
        compiler_params=pltpu.CompilerParams(vmem_limit_bytes=24 << 20),
    )(rows_in, pltpu.with_memory_space_constraint(maps, pltpu.HBM))


def choose_rows(table, segment):
    chosen = jnp.zeros((segment.shape[0],) + table.shape[1:], table.dtype)
    for request in range(table.shape[0]):
        picked = (segment == request).reshape((-1,) + (1,) * (table.ndim - 1))
        chosen = jnp.where(picked, table[request][None], chosen)
    return chosen


def body(
    tokens,
    modulation,
    lengths,
    request_adapter,
    adapter_storage,
    adapter_down_weight,
    adapter_up_maps,
    input_projection,
    query_key_gains,
    positions,
    block_page_lookup,
    output_projection,
    cross_norm_gain,
    text_token_cache,
    feedforward_up,
    feedforward_down,
):
    mlp_count = lax.axis_size("mlp")
    my_index = lax.axis_index("mlp")
    own_count = tokens.shape[0]
    group_rows = own_count * mlp_count
    local_width = input_projection.shape[2]
    entire_width = local_width * mlp_count
    resident_slots = adapter_down_weight.shape[0]
    doubled_rank = adapter_down_weight.shape[2]
    rank_once = doubled_rank // 2

    req_count = lax.axis_size("req")
    slot_total = resident_slots * mlp_count
    tuned = mlp_count == 8 and req_count == 4
    counts = lengths[0]
    index = jnp.arange(counts.shape[0], dtype=jnp.int32)
    bounds = jnp.sum(jnp.where(index[:, None] >= index[None, :], counts[None, :], 0), axis=1)
    position = jnp.arange(group_rows, dtype=jnp.int32)
    segment = jnp.sum((position[:, None] >= bounds[None, :]).astype(jnp.int32), axis=1)
    own_start = my_index * own_count
    own_segment = lax.dynamic_slice_in_dim(segment, own_start, own_count)
    if tuned:
        storage = jnp.arange(adapter_storage.shape[0], dtype=jnp.int32)
        request_slot = jnp.sum(
            jnp.where(request_adapter[:, None] == storage[None, :], adapter_storage[None, :], 0), axis=1
        )
        resident = my_index * resident_slots + jnp.arange(resident_slots, dtype=jnp.int32)
        pick = (request_slot[:, None] == resident[None, :]).astype(jnp.float32).reshape(-1, 1)
        linear, value_rows, scales = enter(
            tokens,
            modulation,
            own_segment[:, None],
            segment[None, :],
            jnp.broadcast_to(pick, (pick.shape[0], 128)),
            adapter_down_weight.transpose(0, 2, 1).reshape(resident_slots * doubled_rank, -1),
            adapter_up_maps,
            input_projection,
            mlp_count,
        )
        query_linear, key_linear = linear[0], linear[1]
        query_scale, key_scale = scales[0, :, 0], scales[1, :, 0]
        per_token = [choose_rows(modulation[:, which_row, :], own_segment) for which_row in range(6)]
    else:
        per_token = [choose_rows(modulation[:, which_row, :], own_segment) for which_row in range(6)]
        token_f32 = tokens.astype(jnp.float32)
        rows_in, adapter_up_weight = entry_rows(
            tokens, per_token[1], per_token[0], adapter_up_maps, mlp_count
        )
        request_slot = adapter_storage[request_adapter]
        token_slot = jnp.sum(
            jnp.where(
                segment[:, None] == jnp.arange(request_slot.shape[0], dtype=jnp.int32)[None, :],
                request_slot[None, :],
                0,
            ),
            axis=1,
        )
        resident = my_index * resident_slots + jnp.arange(resident_slots, dtype=jnp.int32)
        held = (token_slot[None, :] == resident[:, None]).astype(jnp.float32)
        code_block = lax.dot_general(
            adapter_down_weight.transpose(0, 2, 1).reshape(resident_slots * doubled_rank, -1),
            rows_in,
            (((1,), (1,)), ((), ())),
            preferred_element_type=jnp.float32,
        ).reshape(resident_slots, doubled_rank, group_rows)
        my_codes = jnp.sum(held[:, None, :] * code_block, axis=0).astype(jnp.bfloat16)
        codes = small_sum(my_codes, mlp_count, 1).astype(jnp.bfloat16)
        slots = jnp.arange(slot_total, dtype=jnp.int32)
        everywhere = token_slot[None, :] == slots[:, None]

        def spread(code_part):
            return jnp.where(everywhere[:, None, :], code_part[None], jnp.bfloat16(0)).reshape(
                slot_total * rank_once, group_rows
            )

        def adapted(code_part, which_map):
            return lax.dot_general(
                spread(code_part),
                adapter_up_weight[:, which_map].reshape(slot_total * rank_once, local_width),
                (((0,), (0,)), ((), ())),
                preferred_element_type=jnp.float32,
            )

        projected = product(rows_in, input_projection, 0, 3, 256, jnp.float32)
        query_linear = projected[0] + adapted(codes[:rank_once], 0)
        key_linear = projected[1]
        value_rows = (projected[2] + adapted(codes[rank_once:], 1)).astype(jnp.bfloat16)
        squares = small_sum(
            jnp.stack(
                [jnp.sum(query_linear * query_linear, axis=1), jnp.sum(key_linear * key_linear, axis=1)]
            ),
            mlp_count,
            2,
        )
        query_square, key_square = squares[0], squares[1]
        query_scale = lax.rsqrt(query_square / entire_width + EPSILON)
        key_scale = lax.rsqrt(key_square / entire_width + EPSILON)
    cosine, sine = rotary_tables(positions)
    attended, kv_pages = self_attention(
        block_page_lookup[0],
        query_linear,
        key_linear,
        value_rows,
        query_scale,
        key_scale,
        query_key_gains,
        cosine,
        sine,
        segment,
    )
    text_owner = (
        jnp.arange(text_token_cache.shape[1] * text_token_cache.shape[2], dtype=jnp.int32)
        // text_token_cache.shape[2]
    )

    def out_rows(rows, which_map):
        return product(rows, output_projection, which_map, 1, 1280, jnp.bfloat16)[0]

    first_res, cross_in = middle_rows(
        out_rows(attended, 0),
        tokens,
        per_token[2],
        cross_norm_gain[None, :],
        jnp.zeros((1, tokens.shape[1]), jnp.float32),
        mlp_count,
        3,
    )
    cross_linear = product(cross_in, input_projection, 3, 1, 256, jnp.float32)[0]
    cross_square = small_sum(
        jnp.sum(cross_linear * cross_linear, axis=1)[None, :], mlp_count, 4
    )[0]
    cross_query = (
        cross_linear
        * lax.rsqrt(cross_square / entire_width + EPSILON)[:, None]
        * query_key_gains[2]
    ).astype(jnp.bfloat16)
    cross_out = cross_attention(
        cross_query,
        text_token_cache.reshape(2, text_owner.shape[0], local_width),
        segment,
        text_owner,
    )
    if tuned:
        layer_out = feed_forward(
            out_rows(cross_out, 1),
            first_res,
            1.0 + per_token[4],
            per_token[3],
            per_token[5],
            feedforward_up,
            feedforward_down,
            mlp_count,
            req_count,
            5,
        )
        return (layer_out, kv_pages)
    up_full = lax.all_gather(feedforward_up, "req", axis=0, tiled=True)
    second_res, mlp_in = middle_rows(
        out_rows(cross_out, 1),
        first_res,
        jnp.ones((1, tokens.shape[1]), jnp.float32),
        1.0 + per_token[4],
        per_token[3],
        mlp_count,
        5,
    )
    hidden = product(
        mlp_in,
        up_full[None],
        0,
        1,
        256,
        jnp.bfloat16,
        functools.partial(jax.nn.gelu, approximate=True),
    )[0]
    hidden_all = line_gather(hidden, req_count, 6)
    units, columns = feedforward_down.shape
    down_part = jnp.dot(
        hidden_all.reshape(req_count * group_rows, units),
        feedforward_down,
        preferred_element_type=jnp.float32,
    ).astype(jnp.bfloat16)
    down_own = exit_rows(
        down_part.reshape(req_count, mlp_count, own_count, columns), mlp_count, req_count, 7
    )
    layer_out = (
        second_res.astype(jnp.float32) + per_token[5] * down_own.astype(jnp.float32)
    ).astype(jnp.bfloat16)
    return (layer_out, kv_pages)


def solution(mesh):
    return jax.shard_map(
        body,
        mesh=mesh,
        in_specs=(
            P(("req", "mlp"), None),
            P("req", None, None),
            P("req", None),
            P("req"),
            P(),
            P("mlp", None, None),
            P("mlp", None, None, None),
            P(None, None, "mlp"),
            P(None, "mlp"),
            P(None, "req"),
            P("req", None),
            P(None, "mlp", None),
            P(),
            P(None, "req", None, "mlp"),
            P("req", "mlp"),
            P("mlp", "req"),
        ),
        out_specs=(P(("req", "mlp"), None), P(None, "req", None, "mlp")),
        check_vma=False,
    )
```

```python
import functools
import math

import jax
import jax.numpy as jnp
from jax import lax
from jax.experimental import pallas as pl
from jax.experimental.pallas import tpu as pltpu
from jax.sharding import PartitionSpec as P

HD = 128
PAGE = 16


EPSILON = 1e-06


PAIR = 2
MESH = pl.DeviceIdType.MESH
ANY = pl.BlockSpec(memory_space=pl.ANY)
VM = pl.BlockSpec(memory_space=pltpu.VMEM)


def comm_call(kernel, out_shape, in_specs, out_specs, scratch, ident, room=4):
    return pl.pallas_call(
        kernel,
        out_shape=out_shape,
        in_specs=in_specs,
        out_specs=out_specs,
        scratch_shapes=scratch,
        compiler_params=pltpu.CompilerParams(
            collective_id=ident, has_side_effects=True, vmem_limit_bytes=room << 20
        ),
    )


def remote(source, target, send_sem, recv_sem, axis, place):
    return pltpu.make_async_remote_copy(
        src_ref=source,
        dst_ref=target,
        send_sem=send_sem,
        recv_sem=recv_sem,
        device_id={axis: place},
        device_id_type=MESH,
    )


def shift(me, step, count):
    return lax.rem(me + (step + count) % count, count)


def greet(peers):
    barrier = pltpu.get_barrier_semaphore()
    for axis, place in peers:
        pl.semaphore_signal(barrier, inc=1, device_id={axis: place}, device_id_type=MESH)
    pl.semaphore_wait(barrier, len(peers))


def pair_places(count):
    me = lax.axis_index("mlp")
    outer, core = lax.div(me, PAIR), lax.rem(me, PAIR)
    sibling = outer * PAIR + (PAIR - 1 - core)
    peers = [
        shift(outer, k, count // PAIR) * PAIR + core for k in range(count // PAIR)
    ]
    sources = [
        shift(outer, -k, count // PAIR) * PAIR + core for k in range(count // PAIR)
    ]
    return me, core, sibling, peers, sources


def gather_sems(count):
    steps = count // PAIR
    return [pltpu.SemaphoreType.DMA(())] + [pltpu.SemaphoreType.DMA((steps,))] * 4


def gather_rows(count, places, own_ref, out_ref, own_sem, send_sem, recv_sem, pass_send, pass_recv):
    me, core, sibling, peers, sources = places
    own = pltpu.make_async_copy(own_ref, out_ref.at[me], own_sem)
    sends = [
        remote(own_ref, out_ref.at[me], send_sem.at[k], recv_sem.at[k], "mlp", peers[k])
        for k in range(1, count // PAIR)
    ]
    for copy in sends:
        copy.start()
    passes = [remote(own_ref, out_ref.at[me], pass_send.at[0], pass_recv.at[0], "mlp", sibling)]
    passes[0].start()
    own.start()
    for k in range(1, count // PAIR):
        sends[k - 1].wait_recv()
        block = out_ref.at[sources[k]]
        passes.append(remote(block, block, pass_send.at[k], pass_recv.at[k], "mlp", sibling))
        passes[-1].start()
    for copy in sends:
        copy.wait_send()
    for copy in passes:
        copy.wait()
    own.wait()


def entry_kernel(count, tok_ref, scale_ref, shift_ref, maps_ref, out_ref, up_ref, norm, map_own, map_send, map_recv, *sems):
    places = pair_places(count)
    me = places[0]
    slots, width = maps_ref.shape[0], up_ref.shape[-1]
    others = [shift(me, k, count) for k in range(1, count)]
    greet([("mlp", place) for place in others])

    def columns(place):
        return maps_ref.at[:, :, :, pl.ds(pl.multiple_of(place * width, 128), width)]

    target = up_ref.at[pl.ds(me * slots, slots)]
    own = pltpu.make_async_copy(columns(me), target, map_own)
    own.start()
    copies = [
        remote(columns(place), target, map_send.at[k], map_recv.at[k], "mlp", place)
        for k, place in enumerate(others)
    ]
    norm[...] = (
        layer_norm(tok_ref[...].astype(jnp.float32)) * (1.0 + scale_ref[...]) + shift_ref[...]
    ).astype(jnp.bfloat16)
    for copy in copies:
        copy.start()
    gather_rows(count, places, norm, out_ref, *sems)
    for copy in copies:
        copy.wait()
    own.wait()


def entry_rows(tokens, scale, shift_rows, maps, count):
    rows, width = tokens.shape
    slots, two, rank, total = maps.shape
    dma = pltpu.SemaphoreType.DMA
    gathered, up = comm_call(
        functools.partial(entry_kernel, count),
        (
            jax.ShapeDtypeStruct((count, rows, width), jnp.bfloat16),
            jax.ShapeDtypeStruct((count * slots, two, rank, total // count), maps.dtype),
        ),
        [VM, VM, VM, ANY],
        (ANY, ANY),
        [pltpu.VMEM((rows, width), jnp.bfloat16), dma(()), dma((count - 1,)), dma((count - 1,))]
        + gather_sems(count),
        0,
        8,
    )(tokens, scale, shift_rows, maps)
    return gathered.reshape(count * rows, width), up


def sum_blocks(count, places, block_of, near, mid, far, ns, nr, fs, fr):
    me, core, sibling, peers, sources = places
    steps = count // PAIR
    order = list(range(1, steps)) + [0]
    pairs = {}
    for k in order:
        other = peers[k] + (PAIR - 1 - 2 * core)
        pairs[k] = remote(block_of(other), near.at[k], ns.at[k], nr.at[k], "mlp", sibling)
        pairs[k].start()
    sends = []
    for k in range(1, steps):
        pairs[k].wait_recv()
        mid[k] = (
            block_of(peers[k])[...].astype(jnp.float32) + near[k].astype(jnp.float32)
        ).astype(jnp.bfloat16)
        sends.append(remote(mid.at[k], far.at[k], fs.at[k], fr.at[k], "mlp", peers[k]))
        sends[-1].start()
    pairs[0].wait_recv()
    total = block_of(me)[...].astype(jnp.float32) + near[0].astype(jnp.float32)
    for k in range(1, steps):
        sends[k - 1].wait_recv()
        total = total + far[k].astype(jnp.float32)
    for k in order:
        pairs[k].wait_send()
    for copy in sends:
        copy.wait_send()
    return total


def sum_scratch(count, extent):
    steps = count // PAIR
    return [pltpu.VMEM((steps,) + extent, jnp.bfloat16)] * 3 + [
        pltpu.SemaphoreType.DMA((steps,))
    ] * 4


def middle_kernel(count, part_ref, base_ref, gate_ref, scale_ref, shift_ref, res_ref, out_ref, near, mid, far, norm, ns, nr, fs, fr, *sems):
    places = pair_places(count)
    greet([("mlp", places[2])] + [("mlp", place) for place in places[3][1:]])
    total = sum_blocks(
        count, places, lambda place: part_ref.at[place], near, mid, far, ns, nr, fs, fr
    )
    res = (base_ref[...].astype(jnp.float32) + gate_ref[...] * total).astype(jnp.bfloat16)
    res_ref[...] = res
    norm[...] = (layer_norm(res.astype(jnp.float32)) * scale_ref[...] + shift_ref[...]).astype(
        jnp.bfloat16
    )
    gather_rows(count, places, norm, out_ref, *sems)


def middle_rows(part, base, gate, scale, shift_rows, count, ident):
    rows, width = base.shape
    scratch = sum_scratch(count, (rows, width))
    res, gathered = comm_call(
        functools.partial(middle_kernel, count),
        (
            jax.ShapeDtypeStruct((rows, width), jnp.bfloat16),
            jax.ShapeDtypeStruct((count, rows, width), jnp.bfloat16),
        ),
        [VM] * 5,
        (VM, ANY),
        scratch[:3] + [pltpu.VMEM((rows, width), jnp.bfloat16)] + scratch[3:] + gather_sems(count),
        ident,
        24,
    )(part.reshape(count, rows, width), base, gate, scale, shift_rows)
    return res, gathered.reshape(count * rows, width)


def small_kernel(count, own_ref, out_ref, slots, send_sem, recv_sem):
    me = lax.axis_index("mlp")
    others = [shift(me, k, count) for k in range(1, count)]
    greet([("mlp", place) for place in others])
    copies = [
        remote(own_ref, slots.at[k], send_sem.at[k], recv_sem.at[k], "mlp", place)
        for k, place in enumerate(others)
    ]
    for copy in copies:
        copy.start()
    total = own_ref[...].astype(jnp.float32)
    for k, copy in enumerate(copies):
        copy.wait_recv()
        total = total + slots[k].astype(jnp.float32)
    out_ref[...] = total
    for copy in copies:
        copy.wait_send()


def small_sum(own, count, ident):
    dma = pltpu.SemaphoreType.DMA((count - 1,))
    return comm_call(
        functools.partial(small_kernel, count),
        jax.ShapeDtypeStruct(own.shape, jnp.float32),
        [VM],
        VM,
        [pltpu.VMEM((count - 1,) + own.shape, own.dtype), dma, dma],
        ident,
    )(own)


def line_kernel(count, own_ref, out_ref, own_sem, rs, rr, ls, lr):
    me = lax.axis_index("req")
    right, left = shift(me, 1, count), shift(me, -1, count)
    greet([("req", right), ("req", left)])
    own = pltpu.make_async_copy(own_ref, out_ref.at[me], own_sem)
    own.start()

    pieces = rs.shape[1]
    rows = own_ref.shape[0] // pieces

    def hop(step, piece, sign):
        block = jnp.clip(me - sign * step, 0, count - 1)
        part = pl.ds(piece * rows, rows)
        source = own_ref.at[part] if step == 0 else out_ref.at[block, part]
        send, recv, place = (rs, rr, right) if sign > 0 else (ls, lr, left)
        return remote(
            source,
            out_ref.at[block, part],
            send.at[step, piece],
            recv.at[step, piece],
            "req",
            place,
        )

    def each(step, work):
        for piece in range(pieces):
            work(step, piece)

    def advance(step, piece):
        if step > 0:

            @pl.when(me >= step)
            def _():
                hop(step - 1, piece, 1).wait_recv()

            @pl.when(me + step < count)
            def _():
                hop(step - 1, piece, -1).wait_recv()

        @pl.when((me >= step) & (me < count - 1))
        def _():
            hop(step, piece, 1).start()

        @pl.when((me + step < count) & (me > 0))
        def _():
            hop(step, piece, -1).start()

    def finish(step, piece):
        @pl.when(me >= count - 1)
        def _():
            hop(step, piece, 1).wait_recv()

        @pl.when(me < 1)
        def _():
            hop(step, piece, -1).wait_recv()

    def drain(step, piece):
        @pl.when((me >= step) & (me < count - 1))
        def _():
            hop(step, piece, 1).wait_send()

        @pl.when((me + step < count) & (me > 0))
        def _():
            hop(step, piece, -1).wait_send()

    for step in range(count - 1):
        each(step, advance)
    each(count - 2, finish)
    for step in range(count - 1):
        each(step, drain)
    own.wait()


def line_gather(own, count, ident):
    dma = pltpu.SemaphoreType.DMA
    return comm_call(
        functools.partial(line_kernel, count),
        jax.ShapeDtypeStruct((count,) + own.shape, own.dtype),
        [ANY],
        ANY,
        [dma(())] + [dma((count - 1, 4))] * 4,
        ident,
    )(own)


def exit_kernel(count, lines, part_ref, out_ref, near, mid, far, final, ns, nr, fs, fr, own_sem, send_sem, recv_sem):
    places = pair_places(count)
    me, core, sibling, peers, _ = places
    steps = count // PAIR
    line = lax.axis_index("req")
    groups = [shift(line, k + 1, lines) for k in range(lines)]
    greet(
        [("mlp", sibling)]
        + [("mlp", place) for place in peers[1:]]
        + [("req", place) for place in groups[:-1]]
    )
    order = list(range(1, steps)) + [0]
    pairs, sends, copies = {}, [], []
    for i, group in enumerate(groups):
        for k in order:
            other = peers[k] + (PAIR - 1 - 2 * core)
            pairs[i, k] = remote(
                part_ref.at[group, other], near.at[i, k], ns.at[i, k], nr.at[i, k], "mlp", sibling
            )
            pairs[i, k].start()
    for i, group in enumerate(groups):
        for k in range(1, steps):
            pairs[i, k].wait_recv()
            mid[i, k] = (
                part_ref[group, peers[k]].astype(jnp.float32) + near[i, k].astype(jnp.float32)
            ).astype(jnp.bfloat16)
            sends.append(
                remote(mid.at[i, k], far.at[i, k], fs.at[i, k], fr.at[i, k], "mlp", peers[k])
            )
            sends[-1].start()
    width = final.shape[-1]
    target = out_ref.at[:, pl.ds(pl.multiple_of(line * width, 128), width)]
    for i, group in enumerate(groups):
        pairs[i, 0].wait_recv()
        total = part_ref[group, me].astype(jnp.float32) + near[i, 0].astype(jnp.float32)
        for k in range(1, steps):
            sends[i * (steps - 1) + k - 1].wait_recv()
            total = total + far[i, k].astype(jnp.float32)
        final[i] = total.astype(jnp.bfloat16)
        if i < lines - 1:
            copies.append(
                remote(final.at[i], target, send_sem.at[i], recv_sem.at[i], "req", group)
            )
        else:
            copies.append(pltpu.make_async_copy(final.at[i], target, own_sem))
        copies[-1].start()
    for copy in list(pairs.values()) + sends:
        copy.wait_send()
    for copy in copies:
        copy.wait()


def exit_rows(part, count, lines, ident):
    groups, _, rows, width = part.shape
    steps = count // PAIR
    dma = pltpu.SemaphoreType.DMA
    return comm_call(
        functools.partial(exit_kernel, count, lines),
        jax.ShapeDtypeStruct((rows, lines * width), jnp.bfloat16),
        [VM],
        VM,
        [pltpu.VMEM((groups, steps, rows, width), jnp.bfloat16)] * 3
        + [pltpu.VMEM((groups, rows, width), jnp.bfloat16)]
        + [dma((groups, steps))] * 4
        + [dma(()), dma((lines - 1,)), dma((lines - 1,))],
        ident,
        24,
    )(part)


def lines_order(lines):
    middle = lines // 2
    return [middle - 1, middle] + [g for g in range(lines) if g not in (middle - 1, middle)]


def dot_tiles(x, w_ref, out_ref, put, tile):
    width = w_ref.shape[1]

    @pl.loop(0, width // tile)
    def _(i):
        columns = pl.ds(pl.multiple_of(i * tile, tile), tile)
        put(columns, jnp.dot(x, w_ref[:, columns], preferred_element_type=jnp.float32))


def ff_kernel(count, lines, parts, x_ref, base_ref, mod_ref, owner_ref, o_hbm, up_hbm, down_hbm, out_ref,
              o_ref, o_sem, part, near, mid, first_in, second_in, ns, nr, xs, xr, fs, fr, gate, sums,
              up_ref, down_ref, w_sem, norm, res, act, a_send, a_recv, g_send, g_recv, p_send, p_recv,
              pbuf, from_outer, from_partner, staged, hid, es, er, ts, tr, ho_s, hp_s, h_r,
              dn, near2, mid2, far2, ns2, nr2, fs2, fr2, final, back, bs, br):
    places = pair_places(count)
    me, core, sibling, peers, sources = places
    steps = count // PAIR
    line = lax.axis_index("req")
    order = lines_order(lines)
    is_mid = (line == 1) | (line == 2)
    outer = jnp.where(line == 1, 0, 3)
    partner = 3 - line
    inner = jnp.where(line == 0, 1, 2)
    adder = QuadSum(parts, part, near, mid, first_in, second_in, ns, nr, xs, xr, fs, fr)
    loads_o = {}
    for c in adder.order:
        columns = part_columns(base_ref.shape[1], parts, c)
        loads_o[c] = pltpu.make_async_copy(o_hbm.at[1, :, columns], o_ref.at[:, columns], o_sem.at[c])
        loads_o[c].start()
    greet(
        [("mlp", sibling)]
        + [("mlp", place) for place in peers[1:]]
        + [("req", shift(line, k, lines)) for k in range(1, lines)]
    )
    weights = [
        pltpu.make_async_copy(up_hbm, up_ref, w_sem.at[0]),
        pltpu.make_async_copy(down_hbm, down_ref, w_sem.at[1]),
    ]
    for copy in weights:
        copy.start()
    owner = owner_ref[...]
    gate[...] = pick_rows(mod_ref, 5, owner)

    def consume(c, total):
        columns = part_columns(base_ref.shape[1], parts, c)
        value = (base_ref[:, columns].astype(jnp.float32) + total).astype(jnp.bfloat16)
        res[:, columns] = value
        sums[:, columns] = value.astype(jnp.float32)

    adder.run(part_product(x_ref, o_ref, part, parts, loads_o), consume)
    norm[...] = (
        layer_norm(sums[...]) * (1.0 + pick_rows(mod_ref, 4, owner)) + pick_rows(mod_ref, 3, owner)
    ).astype(jnp.bfloat16)

    rows, width = norm.shape
    part_width = width // lines

    def slice_of(place):
        return pl.ds(pl.multiple_of(place * part_width, 128), part_width)

    def spread_to(k):
        place = lax.rem(line + k, lines)
        return remote(
            norm.at[:, slice_of(place)], act.at[line, me], a_send.at[k], a_recv.at[line], "req", place
        )

    act[line, me] = norm[:, slice_of(line)]

    @pl.when(is_mid)
    def _():
        for k in (2, 1, 3):
            spread_to(k).start()

    def across(g, k):
        return remote(act.at[g, me], act.at[g, me], g_send.at[g, k], g_recv.at[g, k], "mlp", peers[k])

    def passed(g, k):
        block = act.at[g, sources[k]]
        return remote(block, block, p_send.at[g, k], p_recv.at[g, k], "mlp", sibling)

    def from_sibling(g, k):
        block = act.at[g, sources[k] + PAIR - 1 - 2 * core]
        return remote(block, block, p_send.at[g, k], p_recv.at[g, k], "mlp", sibling)

    def landed(p):
        g = order[p]

        @pl.when(line != g)
        def _():
            remote(norm.at[:, slice_of(g)], act.at[g, me], a_send.at[0], a_recv.at[g], "req", g).wait_recv()

    def opened(p):
        if p < lines:
            g = order[p]
            if p > 1:
                landed(p)
            for k in range(1, steps):
                across(g, k).start()
            passed(g, 0).start()

    tall = count * rows
    chunks = from_outer.shape[1]
    some = tall // chunks

    def chunk(j):
        return pl.ds(pl.multiple_of(j * some, some), some)

    def to_inner(g, j):
        return remote(pbuf.at[g, chunk(j)], from_outer.at[g, j], es.at[g, j], er.at[g, j], "req", inner)

    def to_partner(g, j):
        return remote(staged.at[g, j], from_partner.at[g, j], ts.at[g, j], tr.at[g, j], "req", partner)

    def out_to(g, j, place, sem):
        block = hid.at[g, chunk(j)]
        return remote(block, block, sem.at[g, j], h_r.at[g, j], "req", place)

    def gathered(p):
        g = order[p]
        for k in range(1, steps):
            remote(act.at[g, me], act.at[g, sources[k]], g_send.at[g, k], g_recv.at[g, k], "mlp", peers[k]).wait_recv()
            passed(g, k).start()
        opened(p + 1)
        for k in range(steps):
            from_sibling(g, k).wait_recv()

    def first_product(p):
        g = order[p]

        def put(columns, value):
            pbuf[g, :, columns] = value.astype(jnp.bfloat16)

        dot_tiles(act[g].reshape(tall, part_width), up_ref, pbuf, put, 256)

        @pl.when(jnp.logical_not(is_mid))
        def _():
            for j in range(chunks):
                to_inner(g, j).start()

    def theirs(g, i):
        j = 2 * i + 2 - line
        to_inner(g, j).wait_recv()
        staged[g, j] = (
            pbuf[g, chunk(j)].astype(jnp.float32) + from_outer[g, j].astype(jnp.float32)
        ).astype(jnp.bfloat16)
        to_partner(g, j).start()

    def mine(g, i):
        j = 2 * i + line - 1
        to_inner(g, j).wait_recv()
        to_partner(g, j).wait_recv()
        value = (
            pbuf[g, chunk(j)].astype(jnp.float32)
            + from_outer[g, j].astype(jnp.float32)
            + from_partner[g, j].astype(jnp.float32)
        )
        hid[g, chunk(j)] = jax.nn.gelu(value, approximate=True).astype(jnp.bfloat16)
        out_to(g, j, partner, hp_s).start()
        out_to(g, j, outer, ho_s).start()

    def forward(g, i):
        j = 2 * i + 2 - line
        out_to(g, j, partner, hp_s).wait_recv()
        out_to(g, j, outer, ho_s).start()

    def middle(p):
        @pl.when(is_mid)
        def _():
            g = order[p]
            pairs = chunks // 2
            theirs(g, 0)
            if p > 0:
                forward(order[p - 1], pairs - 1)
            for i in range(pairs):
                if i + 1 < pairs:
                    theirs(g, i + 1)
                mine(g, i)
                if i > 0:
                    forward(g, i - 1)

    def all_hidden(p):
        g = order[p]
        if p == lines - 1:
            @pl.when(is_mid)
            def _():
                forward(g, chunks // 2 - 1)

        @pl.when(jnp.logical_not(is_mid))
        def _():
            for j in range(chunks):
                out_to(g, j, inner, ho_s).wait_recv()

    def pair_copy(g, k):
        other = peers[k] + (PAIR - 1 - 2 * core)
        return remote(dn.at[g, other], near2.at[g, k], ns2.at[g, k], nr2.at[g, k], "mlp", sibling)

    def far_copy(g, k):
        return remote(mid2.at[g, k], far2.at[g, k], fs2.at[g, k], fr2.at[g, k], "mlp", peers[k])

    k_order = list(range(1, steps)) + [0]

    def second_product(p):
        g = order[p]

        def put(columns, value):
            dn[g, :, :, columns] = value.astype(jnp.bfloat16).reshape(count, rows, 256)

        dot_tiles(hid[g], down_ref, dn, put, 256)
        for k in k_order:
            pair_copy(g, k).start()

    def relay(p):
        g = order[p]
        for k in range(1, steps):
            pair_copy(g, k).wait_recv()
            mid2[g, k] = (
                dn[g, peers[k]].astype(jnp.float32) + near2[g, k].astype(jnp.float32)
            ).astype(jnp.bfloat16)
            far_copy(g, k).start()

    def home(g):
        return remote(final.at[g], back.at[line], bs.at[g], br.at[line], "req", g)

    def finish(p):
        g = order[p]
        pair_copy(g, 0).wait_recv()
        value = dn[g, me].astype(jnp.float32) + near2[g, 0].astype(jnp.float32)
        for k in range(1, steps):
            far_copy(g, k).wait_recv()
            value = value + far2[g, k].astype(jnp.float32)
        final[g] = value.astype(jnp.bfloat16)

        @pl.when(line == g)
        def _():
            back[g] = final[g]

        @pl.when(line != g)
        def _():
            home(g).start()

    landed(0)
    opened(0)
    landed(1)

    @pl.when(jnp.logical_not(is_mid))
    def _():
        for far_place in (3, 2, 1):
            spread_to(jnp.where(line == 0, far_place, 4 - far_place)).start()

    weights[0].wait()
    gathered(0)
    first_product(0)
    gathered(1)
    first_product(1)
    middle(0)
    gathered(2)
    first_product(2)
    gathered(3)
    first_product(3)
    weights[1].wait()
    middle(1)
    all_hidden(0)
    second_product(0)
    relay(0)
    middle(2)
    all_hidden(1)
    second_product(1)
    finish(0)
    relay(1)
    middle(3)
    all_hidden(2)
    second_product(2)
    finish(1)
    relay(2)
    all_hidden(3)
    second_product(3)
    finish(2)
    relay(3)
    finish(3)

    for q in range(lines):
        columns = slice(q * part_width, (q + 1) * part_width)

        @pl.when(line != q)
        def _():
            remote(final.at[q], back.at[q], bs.at[q], br.at[q], "req", q).wait_recv()

        out_ref[:, columns] = (
            res[:, columns].astype(jnp.float32) + gate[:, columns] * back[q].astype(jnp.float32)
        ).astype(jnp.bfloat16)

    adder.drain()
    for k in range(1, lines):
        spread_to(k).wait_send()
    for g in order:
        for k in range(1, steps):
            across(g, k).wait_send()
            far_copy(g, k).wait_send()
        for k in range(steps):
            passed(g, k).wait_send()
            pair_copy(g, k).wait_send()

        @pl.when(line != g)
        def _():
            home(g).wait_send()

        @pl.when(is_mid)
        def _():
            for i in range(chunks // 2):
                to_partner(g, 2 * i + 2 - line).wait_send()
                out_to(g, 2 * i + line - 1, partner, hp_s).wait_send()
            for j in range(chunks):
                out_to(g, j, outer, ho_s).wait_send()

        @pl.when(jnp.logical_not(is_mid))
        def _():
            for j in range(chunks):
                to_inner(g, j).wait_send()


def feed_forward(rows_in, base, modulation, owner, out_maps, up, down, count, lines, ident):
    rows, width = base.shape
    steps = count // PAIR
    depth, units = up.shape
    tall = rows * count
    chunks = 4
    parts = 4
    dma = pltpu.SemaphoreType.DMA
    vm = lambda *extent: pltpu.VMEM(extent, jnp.bfloat16)
    scratch = (
        [vm(rows_in.shape[1], width), dma((parts,))]
        + quad_sum_scratch(parts, count, rows, width)
        + [pltpu.VMEM((rows, width), jnp.float32)] * 2
        + [vm(depth, units), vm(units, depth), dma((2,)), vm(rows, width), vm(rows, width)]
        + [vm(lines, count, rows, depth), dma((lines,)), dma((lines,))]
        + [dma((lines, steps))] * 4
        + [vm(lines, tall, units), vm(lines, chunks, tall // chunks, units)]
        + [vm(lines, chunks, tall // chunks, units)] * 2
        + [vm(lines, tall, units)]
        + [dma((lines, chunks))] * 7
        + [vm(lines, count, rows, depth)]
        + [vm(lines, steps, rows, depth)] * 3
        + [dma((lines, steps))] * 4
        + [vm(lines, rows, depth)] * 2
        + [dma((lines,))] * 2
    )
    return comm_call(
        functools.partial(ff_kernel, count, lines, parts),
        jax.ShapeDtypeStruct((rows, width), jnp.bfloat16),
        [VM] * 4 + [ANY] * 3,
        VM,
        scratch,
        ident,
        60,
    )(rows_in, base, modulation, owner, out_maps, up, down)


def layer_norm(values):
    center = values - jnp.mean(values, axis=-1, keepdims=True)
    spread = jnp.mean(center * center, axis=-1, keepdims=True)
    return center * lax.rsqrt(spread + EPSILON)


def rotary_tables(grid):
    half_dim = HD // 2
    spatial = half_dim // 3
    temporal = half_dim - 2 * spatial
    column = jnp.arange(HD, dtype=jnp.int32)
    sign = jnp.where(column < half_dim, -1.0, 1.0).astype(jnp.float32)
    column = column % half_dim
    which_axis = jnp.where(
        column < temporal, 0, jnp.where(column < temporal + spatial, 1, 2)
    ).astype(jnp.int32)
    offset = jnp.where(
        which_axis == 0, 0, jnp.where(which_axis == 1, temporal, temporal + spatial)
    ).astype(jnp.int32)
    span_size = jnp.where(which_axis == 0, temporal, spatial).astype(jnp.float32)
    frequency = jnp.exp(-(column - offset).astype(jnp.float32) / span_size * math.log(10000.0))
    grid = grid.astype(jnp.float32)[:, :, None]
    coordinate = jnp.where(
        which_axis == 0, grid[0], jnp.where(which_axis == 1, grid[1], grid[2])
    )
    angles = coordinate * frequency[None, :]
    return (jnp.cos(angles), jnp.sin(angles) * sign[None, :])


def attend(queries, key_rows, value_rows, allowed):
    scores = lax.dot_general(
        queries, key_rows, (((1,), (1,)), ((), ())), preferred_element_type=jnp.float32
    ) * (1.0 / math.sqrt(HD))
    weights = jnp.exp(jnp.where(allowed, scores, -1e30))
    weights = weights * (1.0 / jnp.sum(weights, axis=-1, keepdims=True))
    return jnp.dot(
        weights.astype(jnp.bfloat16), value_rows, preferred_element_type=jnp.float32
    ).astype(jnp.bfloat16)


def quad():
    me = lax.axis_index("mlp")
    core, x, y = lax.rem(me, 2), lax.rem(lax.div(me, 2), 2), lax.div(me, 4)

    def at(row, column, which):
        return (row * 2 + column) * 2 + which

    return me, at(y, x, 1 - core), at(y, 1 - x, core), at(1 - y, x, core), at(1 - y, 1 - x, core)


def part_columns(width, parts, c):
    return slice(c * (width // parts), (c + 1) * (width // parts))


class QuadGather:
    def __init__(self, parts, own_ref, out_ref, own_sem, xs, xr, ys, yr, fs, fr, ss, sr):
        self.parts, self.own_ref, self.out_ref = parts, own_ref, out_ref
        self.me, self.sib, self.xn, self.yn, self.dg = quad()
        self.sems = (xs, xr, ys, yr, fs, fr, ss, sr)
        self.half = parts // 2
        self.own = pltpu.make_async_copy(own_ref, out_ref.at[self.me], own_sem)
        self.x_order = list(range(parts))
        self.y_order = list(range(self.half, parts)) + list(range(self.half))
        self.order = [c for two in zip(range(self.half), range(self.half, parts)) for c in two]
        self.across, self.up, self.onward, self.passes = {}, {}, {}, {}

    def piece(self, place, c):
        return self.out_ref.at[place, :, part_columns(self.own_ref.shape[1], self.parts, c)]

    def mine(self, c):
        return self.own_ref.at[:, part_columns(self.own_ref.shape[1], self.parts, c)]

    def hand(self, kind, place, c):
        send, recv = self.sems[6].at[kind, c], self.sems[7].at[kind, c]
        source = self.piece(place, c) if kind else self.mine(c)
        self.passes[kind, c] = remote(source, self.piece(place, c), send, recv, "mlp", self.sib)
        self.passes[kind, c].start()

    def start(self):
        xs, xr, ys, yr = self.sems[:4]
        self.own.start()
        for i in range(self.parts):
            c = self.x_order[i]
            self.across[c] = remote(self.mine(c), self.piece(self.me, c), xs.at[c], xr.at[c], "mlp", self.xn)
            self.across[c].start()
            c = self.y_order[i]
            self.up[c] = remote(self.mine(c), self.piece(self.me, c), ys.at[c], yr.at[c], "mlp", self.yn)
            self.up[c].start()
        for c in self.order:
            self.hand(0, self.me, c)

    def send_on(self, place, c, to):
        fs, fr = self.sems[4:6]
        block = self.piece(place, c)
        self.onward[c] = remote(block, block, fs.at[c], fr.at[c], "mlp", to)
        self.onward[c].start()

    def step(self, i):
        c = self.x_order[i]
        self.across[c].wait_recv()
        if c < self.half:
            self.send_on(self.xn, c, self.yn)
        self.hand(1, self.xn, c)
        c = self.y_order[i]
        self.up[c].wait_recv()
        if c >= self.half:
            self.send_on(self.yn, c, self.xn)
        self.hand(2, self.yn, c)

    def corner(self, c):
        self.onward[c].wait_recv()
        self.hand(3, self.dg, c)

    def whole(self, c):
        for kind in range(4):
            self.passes[kind, c].wait_recv()

    def drain(self):
        for group in (self.across, self.up, self.onward, self.passes):
            for copy in group.values():
                copy.wait_send()


def quad_sems(parts):
    dma = pltpu.SemaphoreType.DMA
    return [dma(())] + [dma((parts,))] * 6 + [dma((4, parts))] * 2


def share(own_ref, slots_ref, send_sem, recv_sem, count):
    me = lax.axis_index("mlp")
    copies = [
        remote(own_ref, slots_ref.at[k], send_sem.at[k], recv_sem.at[k], "mlp", shift(me, k, count))
        for k in range(1, count)
    ]
    for copy in copies:
        copy.start()
    return copies


def pick_rows(mod_ref, which, owner):
    chosen = mod_ref[0, which : which + 1, :]
    for request in range(1, mod_ref.shape[0]):
        chosen = jnp.where(owner == request, mod_ref[request, which : which + 1, :], chosen)
    return chosen


def row_to_column(row, lanes=128):
    return jnp.transpose(jnp.broadcast_to(row, (lanes, row.shape[1])))


def column_to_rows(column, lanes=128):
    return jnp.transpose(jnp.broadcast_to(column, (column.shape[0], lanes)))[0:8]


def enter_kernel(count, parts, tok_ref, mod_ref, owner_ref, seg_ref, pick_ref, down_ref, maps_ref, w_hbm,
                 lin_ref, value_ref, scale_ref,
                 norm, rows_all, w_ref, w_sem, acc, code_acc, code_own, code_slots, cs, cr,
                 chosen, near, mid, far, us, ur, vs, vr, sq_own, sq_slots, qs, qr, *sems):
    me, sib, xn, yn, dg = quad()
    core = lax.rem(me, PAIR)
    flip = 1 - 2 * core
    greet([("mlp", shift(me, k, count)) for k in range(1, count)])
    rows, width = tok_ref.shape
    depth = width // parts
    tall = rows * count
    heads = acc.shape[2]
    owner = owner_ref[...]
    norm[...] = (
        layer_norm(tok_ref[...].astype(jnp.float32)) * (1.0 + pick_rows(mod_ref, 1, owner))
        + pick_rows(mod_ref, 0, owner)
    ).astype(jnp.bfloat16)
    gather = QuadGather(parts, norm, rows_all, *sems)
    gather.start()
    loads = {}
    for c in gather.order:
        block = pl.ds(c * depth, depth)
        loads[c] = pltpu.make_async_copy(w_hbm.at[0:3, block], w_ref.at[:, block], w_sem.at[c])
        loads[c].start()

    slots = maps_ref.shape[0]
    requests = mod_ref.shape[0]
    rank = maps_ref.shape[2]
    for j in range(2):
        for r in range(requests):
            for place in range(count):
                columns = slice(place * heads, (place + 1) * heads)
                total = jnp.zeros((rank, heads), jnp.float32)
                for s in range(slots):
                    total = total + maps_ref[s, j, :, columns].astype(jnp.float32) * pick_ref[
                        r * slots + s : r * slots + s + 1, 0:1
                    ]
                chosen[place, j, r * rank : (r + 1) * rank] = total.astype(jnp.bfloat16)

    dest = [me, xn, yn, dg]
    pair = [
        remote(chosen.at[dest[t] + flip], near.at[t], us.at[t], ur.at[t], "mlp", sib) for t in range(4)
    ]
    out = {
        t: remote(mid.at[t], far.at[t], vs.at[t], vr.at[t], "mlp", dest[t]) for t in (1, 2, 3)
    }

    def code_part(c):
        x = rows_all[:, :, part_columns(width, parts, c)].reshape(tall, depth)
        code_acc[...] += lax.dot_general(
            down_ref[:, part_columns(width, parts, c)], x, (((1,), (1,)), ((), ())),
            preferred_element_type=jnp.float32,
        )

    def product_part(c, fresh):
        loads[c].wait()

        @pl.loop(0, 3)
        def _(i):
            x = rows_all[:, :, part_columns(width, parts, c)].reshape(tall, depth)
            value = jnp.dot(x, w_ref[i, c * depth : (c + 1) * depth], preferred_element_type=jnp.float32)
            acc[i] = value if fresh else acc[i] + value

    code_acc[...] = jnp.zeros_like(code_acc)
    order = gather.order
    for i in range(parts):
        gather.step(i)
    for copy in pair:
        copy.start()
    for c in order[:2]:
        gather.corner(c)
    for t in (3, 1, 2):
        pair[t].wait_recv()
        mid[t] = chosen[dest[t]] + near[t]
        out[t].start()
    gather.own.wait()
    for c in order[:2]:
        gather.whole(c)
        code_part(c)
        product_part(c, c == order[0])
    for k in range(2, parts, 2):
        for c in order[k : k + 2]:
            gather.corner(c)
        for c in order[k : k + 2]:
            gather.whole(c)
            code_part(c)
            if c != order[-1]:
                product_part(c, False)
    segment = seg_ref[...]
    doubled = 2 * rank
    code = jnp.zeros((doubled, tall), jnp.float32)
    for s in range(slots):
        held = jnp.zeros((1, tall), jnp.float32)
        for r in range(requests):
            held = held + jnp.where(segment == r, pick_ref[r * slots + s : r * slots + s + 1, 0:1], 0.0)
        code = code + held * code_acc[s * doubled : (s + 1) * doubled]
    code_own[...] = code.astype(jnp.bfloat16)
    shared = share(code_own, code_slots, cs, cr, count)
    product_part(order[-1], False)
    pair[0].wait_recv()
    up = chosen[me].astype(jnp.float32) + near[0].astype(jnp.float32)
    for t in (1, 2, 3):
        out[t].wait_recv()
        up = up + far[t].astype(jnp.float32)
    up = up.astype(jnp.bfloat16)
    code = code_own[...].astype(jnp.float32)
    for k, copy in enumerate(shared):
        copy.wait_recv()
        code = code + code_slots[k + 1].astype(jnp.float32)

    def adapted(j):
        spread = jnp.concatenate(
            [jnp.where(segment == r, code[j * rank : (j + 1) * rank], 0.0) for r in range(requests)], axis=0
        )
        return jnp.dot(jnp.transpose(spread).astype(jnp.bfloat16), up[j], preferred_element_type=jnp.float32)

    query = acc[0] + adapted(0)
    key = acc[1]
    sq_own[0] = column_to_rows(jnp.sum(query * query, axis=1, keepdims=True))
    sq_own[1] = column_to_rows(jnp.sum(key * key, axis=1, keepdims=True))
    squares = share(sq_own, sq_slots, qs, qr, count)
    lin_ref[0] = query
    lin_ref[1] = key
    value_ref[...] = (acc[2] + adapted(1)).astype(jnp.bfloat16)
    total = sq_own[...]
    for k, copy in enumerate(squares):
        copy.wait_recv()
        total = total + sq_slots[k + 1]
    scale = lax.rsqrt(total / (heads * count) + EPSILON)
    for i in range(2):
        scale_ref[i] = row_to_column(scale[i, 0:1])
    gather.drain()
    for copy in shared + squares + pair + list(out.values()):
        copy.wait_send()


def enter(tokens, modulation, owner, segment, pick, down, maps, weights, count):
    rows, width = tokens.shape
    parts = 4
    heads = weights.shape[2]
    tall = rows * count
    slots, two, rank, _ = maps.shape
    requests = modulation.shape[0]
    dma = pltpu.SemaphoreType.DMA
    vm = lambda *extent: pltpu.VMEM(extent, jnp.bfloat16)
    vf = lambda *extent: pltpu.VMEM(extent, jnp.float32)
    up = (two, requests * rank, heads)
    scratch = (
        [vm(rows, width), vm(count, rows, width), vm(3, width, heads), dma((parts,)), vf(3, tall, heads)]
        + [vf(slots * two * rank, tall), vm(two * rank, tall), vm(count, two * rank, tall), dma((count,)), dma((count,))]
        + [vm(count, *up), vm(4, *up), vm(4, *up), vm(4, *up)]
        + [dma((4,))] * 4
        + [vf(2, 8, tall), vf(count, 2, 8, tall), dma((count,)), dma((count,))]
        + quad_sems(parts)
    )
    return comm_call(
        functools.partial(enter_kernel, count, parts),
        (
            jax.ShapeDtypeStruct((2, tall, heads), jnp.float32),
            jax.ShapeDtypeStruct((tall, heads), jnp.bfloat16),
            jax.ShapeDtypeStruct((2, tall, 128), jnp.float32),
        ),
        [VM] * 7 + [ANY],
        (VM, VM, VM),
        scratch,
        0,
        48,
    )(tokens, modulation, owner, segment, pick, down, maps, weights)


class QuadSum:
    def __init__(self, parts, part_ref, near, mid, first_in, second_in, ns, nr, xs, xr, fs, fr):
        self.parts, self.part_ref, self.near, self.mid = parts, part_ref, near, mid
        self.first_in, self.second_in = first_in, second_in
        self.sems = (ns, nr, xs, xr, fs, fr)
        self.me, self.sib, self.xn, self.yn, dg = quad()
        self.dest = [self.me, self.xn, self.yn, dg]
        self.flip = 1 - 2 * lax.rem(self.me, PAIR)
        self.half = parts // 2
        self.order = [c for two in zip(range(self.half), range(self.half, parts)) for c in two]
        self.pairs, self.ones, self.twos = {}, {}, {}

    def columns(self, c):
        return part_columns(self.part_ref.shape[2], self.parts, c)

    def ways(self, c):
        return (1, 2) if c < self.half else (2, 1)

    def offer(self, c):
        ns, nr = self.sems[:2]
        columns = self.columns(c)
        for t in (3, 1, 2, 0):
            self.pairs[t, c] = remote(
                self.part_ref.at[self.dest[t] + self.flip, :, columns],
                self.near.at[t, :, columns],
                ns.at[t, c],
                nr.at[t, c],
                "mlp",
                self.sib,
            )
            self.pairs[t, c].start()

    def both(self, t, columns):
        return self.part_ref[self.dest[t], :, columns].astype(jnp.float32) + self.near[
            t, :, columns
        ].astype(jnp.float32)

    def first(self, c):
        xs, xr = self.sems[2:4]
        columns = self.columns(c)
        far, _ = self.ways(c)
        for t, slot in ((3, 1), (far, 0)):
            self.pairs[t, c].wait_recv()
            self.mid[t, :, columns] = self.both(t, columns).astype(jnp.bfloat16)
            self.ones[t, c] = remote(
                self.mid.at[t, :, columns],
                self.first_in.at[slot, :, columns],
                xs.at[slot, c],
                xr.at[slot, c],
                "mlp",
                self.dest[far],
            )
            self.ones[t, c].start()

    def second(self, c):
        fs, fr = self.sems[4:6]
        columns = self.columns(c)
        _, keep = self.ways(c)
        self.pairs[keep, c].wait_recv()
        self.ones[3, c].wait_recv()
        self.mid[keep, :, columns] = (
            self.both(keep, columns) + self.first_in[1, :, columns].astype(jnp.float32)
        ).astype(jnp.bfloat16)
        self.twos[c] = remote(
            self.mid.at[keep, :, columns], self.second_in.at[:, columns], fs.at[c], fr.at[c], "mlp", self.dest[keep]
        )
        self.twos[c].start()

    def total(self, c):
        columns = self.columns(c)
        far, _ = self.ways(c)
        self.pairs[0, c].wait_recv()
        self.ones[far, c].wait_recv()
        self.twos[c].wait_recv()
        return (
            self.both(0, columns)
            + self.first_in[0, :, columns].astype(jnp.float32)
            + self.second_in[:, columns].astype(jnp.float32)
        )

    def run(self, produce, consume):
        order = self.order
        produce(order[0])
        self.offer(order[0])
        for i in range(1, self.parts):
            produce(order[i])
            self.offer(order[i])
            self.first(order[i - 1])
        self.first(order[-1])
        for c in order:
            self.second(c)
        for c in order:
            consume(c, self.total(c))

    def drain(self):
        for group in (self.pairs, self.ones, self.twos):
            for copy in group.values():
                copy.wait_send()


def quad_sum_scratch(parts, count, rows, width):
    dma = pltpu.SemaphoreType.DMA
    vm = lambda *extent: pltpu.VMEM(extent, jnp.bfloat16)
    return (
        [vm(count, rows, width), vm(4, rows, width), vm(4, rows, width), vm(2, rows, width), vm(rows, width)]
        + [dma((4, parts))] * 2
        + [dma((2, parts))] * 2
        + [dma((parts,))] * 2
    )


def part_product(x_ref, w_ref, part_ref, parts, loads):
    count, rows, width = part_ref.shape

    def produce(c):
        columns = part_columns(width, parts, c)
        loads[c].wait()
        part_ref[:, :, columns] = (
            jnp.dot(x_ref[...], w_ref[:, columns], preferred_element_type=jnp.float32)
            .astype(jnp.bfloat16)
            .reshape(count, rows, width // parts)
        )

    return produce


def cross_in_kernel(count, parts, att_ref, base_ref, mod_ref, owner_ref, gain_ref, head_gain_ref, o_hbm, q_hbm,
                    res_ref, query_ref,
                    o_ref, o_sem, q_ref, q_sem, sums, norm, rows_all, acc, sq_own, sq_slots, qs, qr, *sems):
    sum_sems, gather_sems_ = sems[:11], sems[11:]
    me = lax.axis_index("mlp")
    rows, width = base_ref.shape
    depth = width // parts
    tall = rows * count
    heads = acc.shape[1]
    adder = QuadSum(parts, *sum_sems)
    loads_o, loads_q = {}, {}
    for c in adder.order:
        columns = part_columns(width, parts, c)
        loads_o[c] = pltpu.make_async_copy(o_hbm.at[0, :, columns], o_ref.at[:, columns], o_sem.at[c])
        loads_o[c].start()
    greet([("mlp", shift(me, k, count)) for k in range(1, count)])
    for c in adder.order:
        block = pl.ds(c * depth, depth)
        loads_q[c] = pltpu.make_async_copy(q_hbm.at[3, block], q_ref.at[block], q_sem.at[c])
        loads_q[c].start()
    gate = pick_rows(mod_ref, 2, owner_ref[...])

    def consume(c, total):
        columns = part_columns(width, parts, c)
        res = (base_ref[:, columns].astype(jnp.float32) + gate[:, columns] * total).astype(jnp.bfloat16)
        res_ref[:, columns] = res
        sums[:, columns] = res.astype(jnp.float32)

    adder.run(part_product(att_ref, o_ref, sum_sems[0], parts, loads_o), consume)
    norm[...] = (layer_norm(sums[...]) * gain_ref[...]).astype(jnp.bfloat16)
    gather = QuadGather(parts, norm, rows_all, *gather_sems_)
    gather.start()
    order = gather.order

    def product_part(c):
        x = rows_all[:, :, part_columns(width, parts, c)].reshape(tall, depth)
        loads_q[c].wait()
        value = jnp.dot(x, q_ref[c * depth : (c + 1) * depth], preferred_element_type=jnp.float32)
        acc[...] = value if c == order[0] else acc[...] + value

    for i in range(parts):
        gather.step(i)
    gather.own.wait()
    for k in range(0, parts, 2):
        for c in order[k : k + 2]:
            gather.corner(c)
        for c in order[k : k + 2]:
            gather.whole(c)
            product_part(c)
    query = acc[...]
    sq_own[...] = column_to_rows(jnp.sum(query * query, axis=1, keepdims=True))
    squares = share(sq_own, sq_slots, qs, qr, count)
    total = sq_own[...]
    for k, copy in enumerate(squares):
        copy.wait_recv()
        total = total + sq_slots[k + 1]
    scale = row_to_column(lax.rsqrt(total / (heads * count) + EPSILON)[0:1])[:, 0:1]
    query_ref[...] = (acc[...] * scale * head_gain_ref[...]).astype(jnp.bfloat16)
    adder.drain()
    gather.drain()
    for copy in squares:
        copy.wait_send()


def cross_in(attended, base, modulation, owner, gain, head_gain, out_maps, in_maps, count):
    rows, width = base.shape
    parts = 4
    tall, heads = attended.shape
    dma = pltpu.SemaphoreType.DMA
    vm = lambda *extent: pltpu.VMEM(extent, jnp.bfloat16)
    vf = lambda *extent: pltpu.VMEM(extent, jnp.float32)
    scratch = (
        [vm(heads, width), dma((parts,)), vm(width, heads), dma((parts,))]
        + [vf(rows, width), vm(rows, width), vm(count, rows, width), vf(tall, heads)]
        + [vf(8, tall), vf(count, 8, tall), dma((count,)), dma((count,))]
        + quad_sum_scratch(parts, count, rows, width)
        + quad_sems(parts)
    )
    return comm_call(
        functools.partial(cross_in_kernel, count, parts),
        (
            jax.ShapeDtypeStruct((rows, width), jnp.bfloat16),
            jax.ShapeDtypeStruct((tall, heads), jnp.bfloat16),
        ),
        [VM] * 6 + [ANY] * 2,
        (VM, VM),
        scratch,
        3,
        48,
    )(attended, base, modulation, owner, gain, head_gain, out_maps, in_maps)


def self_kernel(page_ref, q_ref, k_ref, v_ref, qs_ref, ks_ref, gain_ref, cos_ref, sin_ref, seg_ref, segs_ref, out_ref, kv_ref):
    cosine, sine = cos_ref[...], sin_ref[...]
    allowed = seg_ref[...] == segs_ref[...]

    def turned(ref, scale, gain, columns):
        rows = ref[:, columns] * scale * gain_ref[gain : gain + 1, columns]
        return (rows * cosine + pltpu.roll(rows, HD // 2, 1) * sine).astype(jnp.bfloat16)

    for head in range(q_ref.shape[1] // HD):
        columns = slice(head * HD, (head + 1) * HD)
        query = turned(q_ref, qs_ref[...], 0, columns)
        key = turned(k_ref, ks_ref[...], 1, columns)
        value = v_ref[:, columns]
        out_ref[:, columns] = attend(query, key, value, allowed)
        for block in range(kv_ref.shape[1]):
            page = page_ref[block]
            rows = slice(block * PAGE, (block + 1) * PAGE)
            kv_ref[0, page, :, columns] = key[rows]
            kv_ref[1, page, :, columns] = value[rows]


def self_attention(pages, query, key, value, query_scale, key_scale, gains, cosine, sine, segment):
    rows, width = query.shape
    return pl.pallas_call(
        self_kernel,
        out_shape=(
            jax.ShapeDtypeStruct((rows, width), jnp.bfloat16),
            jax.ShapeDtypeStruct((2, pages.shape[0], PAGE, width), jnp.bfloat16),
        ),
        in_specs=[pl.BlockSpec(memory_space=pltpu.SMEM)] + [VM] * 10,
        out_specs=(VM, VM),
        compiler_params=pltpu.CompilerParams(vmem_limit_bytes=16 << 20),
    )(
        pages,
        query,
        key,
        value,
        query_scale[:, None],
        key_scale[:, None],
        gains,
        cosine,
        sine,
        segment[:, None],
        segment[None, :],
    )


def cross_kernel(q_ref, k_ref, v_ref, seg_ref, owner_ref, out_ref):
    out_ref[...] = attend(q_ref[...], k_ref[0], v_ref[0], seg_ref[...] == owner_ref[...])


def cross_attention(query, cache, segment, owner):
    rows, width = query.shape
    texts = cache.shape[1]
    head = pl.BlockSpec((rows, HD), lambda h: (0, h))
    return pl.pallas_call(
        cross_kernel,
        out_shape=jax.ShapeDtypeStruct((rows, width), jnp.bfloat16),
        grid=(width // HD,),
        in_specs=[
            head,
            pl.BlockSpec((1, texts, HD), lambda h: (0, 0, h)),
            pl.BlockSpec((1, texts, HD), lambda h: (1, 0, h)),
            pl.BlockSpec((rows, 1), lambda h: (0, 0)),
            pl.BlockSpec((1, texts), lambda h: (0, 0)),
        ],
        out_specs=head,
        compiler_params=pltpu.CompilerParams(vmem_limit_bytes=24 << 20),
    )(query, cache, cache, segment[:, None], owner[None, :])


def product_kernel(act, x_ref, w_ref, out_ref):
    out_ref[0] = act(
        jnp.dot(x_ref[...], w_ref[0], preferred_element_type=jnp.float32)
    ).astype(out_ref.dtype)


def product(rows_in, maps, first, amount, tile, dtype, act=lambda part: part):
    rows, depth = rows_in.shape
    width = maps.shape[2]
    tile = min(tile, width)
    return pl.pallas_call(
        functools.partial(product_kernel, act),
        out_shape=jax.ShapeDtypeStruct((amount, rows, width), dtype),
        grid=(amount, width // tile),
        in_specs=[
            pl.BlockSpec((rows, depth), lambda i, j: (0, 0)),
            pl.BlockSpec((1, depth, tile), lambda i, j: (first + i, 0, j)),
        ],
        out_specs=pl.BlockSpec((1, rows, tile), lambda i, j: (i, 0, j)),
        compiler_params=pltpu.CompilerParams(vmem_limit_bytes=24 << 20),
    )(rows_in, pltpu.with_memory_space_constraint(maps, pltpu.HBM))


def choose_rows(table, segment):
    chosen = jnp.zeros((segment.shape[0],) + table.shape[1:], table.dtype)
    for request in range(table.shape[0]):
        picked = (segment == request).reshape((-1,) + (1,) * (table.ndim - 1))
        chosen = jnp.where(picked, table[request][None], chosen)
    return chosen


def body(
    tokens,
    modulation,
    lengths,
    request_adapter,
    adapter_storage,
    adapter_down_weight,
    adapter_up_maps,
    input_projection,
    query_key_gains,
    positions,
    block_page_lookup,
    output_projection,
    cross_norm_gain,
    text_token_cache,
    feedforward_up,
    feedforward_down,
):
    mlp_count = lax.axis_size("mlp")
    my_index = lax.axis_index("mlp")
    own_count = tokens.shape[0]
    group_rows = own_count * mlp_count
    local_width = input_projection.shape[2]
    entire_width = local_width * mlp_count
    resident_slots = adapter_down_weight.shape[0]
    doubled_rank = adapter_down_weight.shape[2]
    rank_once = doubled_rank // 2

    req_count = lax.axis_size("req")
    slot_total = resident_slots * mlp_count
    tuned = mlp_count == 8 and req_count == 4
    counts = lengths[0]
    index = jnp.arange(counts.shape[0], dtype=jnp.int32)
    bounds = jnp.sum(jnp.where(index[:, None] >= index[None, :], counts[None, :], 0), axis=1)
    position = jnp.arange(group_rows, dtype=jnp.int32)
    segment = jnp.sum((position[:, None] >= bounds[None, :]).astype(jnp.int32), axis=1)
    own_start = my_index * own_count
    own_segment = lax.dynamic_slice_in_dim(segment, own_start, own_count)
    if tuned:
        storage = jnp.arange(adapter_storage.shape[0], dtype=jnp.int32)
        request_slot = jnp.sum(
            jnp.where(request_adapter[:, None] == storage[None, :], adapter_storage[None, :], 0), axis=1
        )
        resident = my_index * resident_slots + jnp.arange(resident_slots, dtype=jnp.int32)
        pick = (request_slot[:, None] == resident[None, :]).astype(jnp.float32).reshape(-1, 1)
        linear, value_rows, scales = enter(
            tokens,
            modulation,
            own_segment[:, None],
            segment[None, :],
            jnp.broadcast_to(pick, (pick.shape[0], 128)),
            adapter_down_weight.transpose(0, 2, 1).reshape(resident_slots * doubled_rank, -1),
            adapter_up_maps,
            input_projection,
            mlp_count,
        )
        query_linear, key_linear = linear[0], linear[1]
        query_scale, key_scale = scales[0, :, 0], scales[1, :, 0]
    else:
        per_token = [choose_rows(modulation[:, which_row, :], own_segment) for which_row in range(6)]
        token_f32 = tokens.astype(jnp.float32)
        rows_in, adapter_up_weight = entry_rows(
            tokens, per_token[1], per_token[0], adapter_up_maps, mlp_count
        )
        request_slot = adapter_storage[request_adapter]
        token_slot = jnp.sum(
            jnp.where(
                segment[:, None] == jnp.arange(request_slot.shape[0], dtype=jnp.int32)[None, :],
                request_slot[None, :],
                0,
            ),
            axis=1,
        )
        resident = my_index * resident_slots + jnp.arange(resident_slots, dtype=jnp.int32)
        held = (token_slot[None, :] == resident[:, None]).astype(jnp.float32)
        code_block = lax.dot_general(
            adapter_down_weight.transpose(0, 2, 1).reshape(resident_slots * doubled_rank, -1),
            rows_in,
            (((1,), (1,)), ((), ())),
            preferred_element_type=jnp.float32,
        ).reshape(resident_slots, doubled_rank, group_rows)
        my_codes = jnp.sum(held[:, None, :] * code_block, axis=0).astype(jnp.bfloat16)
        codes = small_sum(my_codes, mlp_count, 1).astype(jnp.bfloat16)
        slots = jnp.arange(slot_total, dtype=jnp.int32)
        everywhere = token_slot[None, :] == slots[:, None]

        def spread(code_part):
            return jnp.where(everywhere[:, None, :], code_part[None], jnp.bfloat16(0)).reshape(
                slot_total * rank_once, group_rows
            )

        def adapted(code_part, which_map):
            return lax.dot_general(
                spread(code_part),
                adapter_up_weight[:, which_map].reshape(slot_total * rank_once, local_width),
                (((0,), (0,)), ((), ())),
                preferred_element_type=jnp.float32,
            )

        projected = product(rows_in, input_projection, 0, 3, 256, jnp.float32)
        query_linear = projected[0] + adapted(codes[:rank_once], 0)
        key_linear = projected[1]
        value_rows = (projected[2] + adapted(codes[rank_once:], 1)).astype(jnp.bfloat16)
        squares = small_sum(
            jnp.stack(
                [jnp.sum(query_linear * query_linear, axis=1), jnp.sum(key_linear * key_linear, axis=1)]
            ),
            mlp_count,
            2,
        )
        query_square, key_square = squares[0], squares[1]
        query_scale = lax.rsqrt(query_square / entire_width + EPSILON)
        key_scale = lax.rsqrt(key_square / entire_width + EPSILON)
    cosine, sine = rotary_tables(positions)
    attended, kv_pages = self_attention(
        block_page_lookup[0],
        query_linear,
        key_linear,
        value_rows,
        query_scale,
        key_scale,
        query_key_gains,
        cosine,
        sine,
        segment,
    )
    text_owner = (
        jnp.arange(text_token_cache.shape[1] * text_token_cache.shape[2], dtype=jnp.int32)
        // text_token_cache.shape[2]
    )

    def out_rows(rows, which_map):
        return product(rows, output_projection, which_map, 1, 1280, jnp.bfloat16)[0]

    if tuned:
        first_res, cross_query = cross_in(
            attended,
            tokens,
            modulation,
            own_segment[:, None],
            cross_norm_gain[None, :],
            query_key_gains[2:3],
            output_projection,
            input_projection,
            mlp_count,
        )
    else:
        first_res, cross_rows = middle_rows(
            out_rows(attended, 0),
            tokens,
            per_token[2],
            cross_norm_gain[None, :],
            jnp.zeros((1, tokens.shape[1]), jnp.float32),
            mlp_count,
            3,
        )
        cross_linear = product(cross_rows, input_projection, 3, 1, 256, jnp.float32)[0]
        cross_square = small_sum(
            jnp.sum(cross_linear * cross_linear, axis=1)[None, :], mlp_count, 4
        )[0]
        cross_query = (
            cross_linear
            * lax.rsqrt(cross_square / entire_width + EPSILON)[:, None]
            * query_key_gains[2]
        ).astype(jnp.bfloat16)
    cross_out = cross_attention(
        cross_query,
        text_token_cache.reshape(2, text_owner.shape[0], local_width),
        segment,
        text_owner,
    )
    if tuned:
        layer_out = feed_forward(
            cross_out,
            first_res,
            modulation,
            own_segment[:, None],
            output_projection,
            feedforward_up,
            feedforward_down,
            mlp_count,
            req_count,
            5,
        )
        return (layer_out, kv_pages)
    up_full = lax.all_gather(feedforward_up, "req", axis=0, tiled=True)
    second_res, mlp_in = middle_rows(
        out_rows(cross_out, 1),
        first_res,
        jnp.ones((1, tokens.shape[1]), jnp.float32),
        1.0 + per_token[4],
        per_token[3],
        mlp_count,
        5,
    )
    hidden = product(
        mlp_in,
        up_full[None],
        0,
        1,
        256,
        jnp.bfloat16,
        functools.partial(jax.nn.gelu, approximate=True),
    )[0]
    hidden_all = line_gather(hidden, req_count, 6)
    units, columns = feedforward_down.shape
    down_part = jnp.dot(
        hidden_all.reshape(req_count * group_rows, units),
        feedforward_down,
        preferred_element_type=jnp.float32,
    ).astype(jnp.bfloat16)
    down_own = exit_rows(
        down_part.reshape(req_count, mlp_count, own_count, columns), mlp_count, req_count, 7
    )
    layer_out = (
        second_res.astype(jnp.float32) + per_token[5] * down_own.astype(jnp.float32)
    ).astype(jnp.bfloat16)
    return (layer_out, kv_pages)


def solution(mesh):
    return jax.shard_map(
        body,
        mesh=mesh,
        in_specs=(
            P(("req", "mlp"), None),
            P("req", None, None),
            P("req", None),
            P("req"),
            P(),
            P("mlp", None, None),
            P("mlp", None, None, None),
            P(None, None, "mlp"),
            P(None, "mlp"),
            P(None, "req"),
            P("req", None),
            P(None, "mlp", None),
            P(),
            P(None, "req", None, "mlp"),
            P("req", "mlp"),
            P("mlp", "req"),
        ),
        out_specs=(P(("req", "mlp"), None), P(None, "req", None, "mlp")),
        check_vma=False,
    )
```

```python
import functools
import math

import jax
import jax.numpy as jnp
from jax import lax
from jax.experimental import pallas as pl
from jax.experimental.pallas import tpu as pltpu
from jax.sharding import PartitionSpec as P

HD = 128
PAGE = 16


EPSILON = 1e-06


PAIR = 2
MESH = pl.DeviceIdType.MESH
ANY = pl.BlockSpec(memory_space=pl.ANY)
VM = pl.BlockSpec(memory_space=pltpu.VMEM)
HBM = pl.BlockSpec(memory_space=pltpu.HBM)


def comm_call(kernel, out_shape, in_specs, out_specs, scratch, ident, room=4):
    return pl.pallas_call(
        kernel,
        out_shape=out_shape,
        in_specs=in_specs,
        out_specs=out_specs,
        scratch_shapes=scratch,
        compiler_params=pltpu.CompilerParams(
            collective_id=ident, has_side_effects=True, vmem_limit_bytes=room << 20
        ),
    )


def remote(source, target, send_sem, recv_sem, axis, place):
    return pltpu.make_async_remote_copy(
        src_ref=source,
        dst_ref=target,
        send_sem=send_sem,
        recv_sem=recv_sem,
        device_id={axis: place},
        device_id_type=MESH,
    )


def shift(me, step, count):
    return lax.rem(me + (step + count) % count, count)


def greet(peers):
    barrier = pltpu.get_barrier_semaphore()
    for axis, place in peers:
        pl.semaphore_signal(barrier, inc=1, device_id={axis: place}, device_id_type=MESH)
    pl.semaphore_wait(barrier, len(peers))


def hello(peers):
    barrier = pltpu.get_barrier_semaphore()
    for axis, place in peers:
        pl.semaphore_signal(barrier, inc=1, device_id={axis: place}, device_id_type=MESH)


def heard(peers):
    pl.semaphore_wait(pltpu.get_barrier_semaphore(), len(peers))


def in_hbm(*arrays):
    return [pltpu.with_memory_space_constraint(array, pltpu.HBM) for array in arrays]


def pair_places(count):
    me = lax.axis_index("mlp")
    outer, core = lax.div(me, PAIR), lax.rem(me, PAIR)
    sibling = outer * PAIR + (PAIR - 1 - core)
    peers = [
        shift(outer, k, count // PAIR) * PAIR + core for k in range(count // PAIR)
    ]
    sources = [
        shift(outer, -k, count // PAIR) * PAIR + core for k in range(count // PAIR)
    ]
    return me, core, sibling, peers, sources


def gather_sems(count):
    steps = count // PAIR
    return [pltpu.SemaphoreType.DMA(())] + [pltpu.SemaphoreType.DMA((steps,))] * 4


def gather_rows(count, places, own_ref, out_ref, own_sem, send_sem, recv_sem, pass_send, pass_recv):
    me, core, sibling, peers, sources = places
    own = pltpu.make_async_copy(own_ref, out_ref.at[me], own_sem)
    sends = [
        remote(own_ref, out_ref.at[me], send_sem.at[k], recv_sem.at[k], "mlp", peers[k])
        for k in range(1, count // PAIR)
    ]
    for copy in sends:
        copy.start()
    passes = [remote(own_ref, out_ref.at[me], pass_send.at[0], pass_recv.at[0], "mlp", sibling)]
    passes[0].start()
    own.start()
    for k in range(1, count // PAIR):
        sends[k - 1].wait_recv()
        block = out_ref.at[sources[k]]
        passes.append(remote(block, block, pass_send.at[k], pass_recv.at[k], "mlp", sibling))
        passes[-1].start()
    for copy in sends:
        copy.wait_send()
    for copy in passes:
        copy.wait()
    own.wait()


def entry_kernel(count, tok_ref, scale_ref, shift_ref, maps_ref, out_ref, up_ref, norm, map_own, map_send, map_recv, *sems):
    places = pair_places(count)
    me = places[0]
    slots, width = maps_ref.shape[0], up_ref.shape[-1]
    others = [shift(me, k, count) for k in range(1, count)]
    greet([("mlp", place) for place in others])

    def columns(place):
        return maps_ref.at[:, :, :, pl.ds(pl.multiple_of(place * width, 128), width)]

    target = up_ref.at[pl.ds(me * slots, slots)]
    own = pltpu.make_async_copy(columns(me), target, map_own)
    own.start()
    copies = [
        remote(columns(place), target, map_send.at[k], map_recv.at[k], "mlp", place)
        for k, place in enumerate(others)
    ]
    norm[...] = (
        layer_norm(tok_ref[...].astype(jnp.float32)) * (1.0 + scale_ref[...]) + shift_ref[...]
    ).astype(jnp.bfloat16)
    for copy in copies:
        copy.start()
    gather_rows(count, places, norm, out_ref, *sems)
    for copy in copies:
        copy.wait()
    own.wait()


def entry_rows(tokens, scale, shift_rows, maps, count):
    rows, width = tokens.shape
    slots, two, rank, total = maps.shape
    dma = pltpu.SemaphoreType.DMA
    gathered, up = comm_call(
        functools.partial(entry_kernel, count),
        (
            jax.ShapeDtypeStruct((count, rows, width), jnp.bfloat16),
            jax.ShapeDtypeStruct((count * slots, two, rank, total // count), maps.dtype),
        ),
        [VM, VM, VM, ANY],
        (ANY, ANY),
        [pltpu.VMEM((rows, width), jnp.bfloat16), dma(()), dma((count - 1,)), dma((count - 1,))]
        + gather_sems(count),
        0,
        8,
    )(tokens, scale, shift_rows, maps)
    return gathered.reshape(count * rows, width), up


def sum_blocks(count, places, block_of, near, mid, far, ns, nr, fs, fr):
    me, core, sibling, peers, sources = places
    steps = count // PAIR
    order = list(range(1, steps)) + [0]
    pairs = {}
    for k in order:
        other = peers[k] + (PAIR - 1 - 2 * core)
        pairs[k] = remote(block_of(other), near.at[k], ns.at[k], nr.at[k], "mlp", sibling)
        pairs[k].start()
    sends = []
    for k in range(1, steps):
        pairs[k].wait_recv()
        mid[k] = (
            block_of(peers[k])[...].astype(jnp.float32) + near[k].astype(jnp.float32)
        ).astype(jnp.bfloat16)
        sends.append(remote(mid.at[k], far.at[k], fs.at[k], fr.at[k], "mlp", peers[k]))
        sends[-1].start()
    pairs[0].wait_recv()
    total = block_of(me)[...].astype(jnp.float32) + near[0].astype(jnp.float32)
    for k in range(1, steps):
        sends[k - 1].wait_recv()
        total = total + far[k].astype(jnp.float32)
    for k in order:
        pairs[k].wait_send()
    for copy in sends:
        copy.wait_send()
    return total


def sum_scratch(count, extent):
    steps = count // PAIR
    return [pltpu.VMEM((steps,) + extent, jnp.bfloat16)] * 3 + [
        pltpu.SemaphoreType.DMA((steps,))
    ] * 4


def middle_kernel(count, part_ref, base_ref, gate_ref, scale_ref, shift_ref, res_ref, out_ref, near, mid, far, norm, ns, nr, fs, fr, *sems):
    places = pair_places(count)
    greet([("mlp", places[2])] + [("mlp", place) for place in places[3][1:]])
    total = sum_blocks(
        count, places, lambda place: part_ref.at[place], near, mid, far, ns, nr, fs, fr
    )
    res = (base_ref[...].astype(jnp.float32) + gate_ref[...] * total).astype(jnp.bfloat16)
    res_ref[...] = res
    norm[...] = (layer_norm(res.astype(jnp.float32)) * scale_ref[...] + shift_ref[...]).astype(
        jnp.bfloat16
    )
    gather_rows(count, places, norm, out_ref, *sems)


def middle_rows(part, base, gate, scale, shift_rows, count, ident):
    rows, width = base.shape
    scratch = sum_scratch(count, (rows, width))
    res, gathered = comm_call(
        functools.partial(middle_kernel, count),
        (
            jax.ShapeDtypeStruct((rows, width), jnp.bfloat16),
            jax.ShapeDtypeStruct((count, rows, width), jnp.bfloat16),
        ),
        [VM] * 5,
        (VM, ANY),
        scratch[:3] + [pltpu.VMEM((rows, width), jnp.bfloat16)] + scratch[3:] + gather_sems(count),
        ident,
        24,
    )(part.reshape(count, rows, width), base, gate, scale, shift_rows)
    return res, gathered.reshape(count * rows, width)


def small_kernel(count, own_ref, out_ref, slots, send_sem, recv_sem):
    me = lax.axis_index("mlp")
    others = [shift(me, k, count) for k in range(1, count)]
    greet([("mlp", place) for place in others])
    copies = [
        remote(own_ref, slots.at[k], send_sem.at[k], recv_sem.at[k], "mlp", place)
        for k, place in enumerate(others)
    ]
    for copy in copies:
        copy.start()
    total = own_ref[...].astype(jnp.float32)
    for k, copy in enumerate(copies):
        copy.wait_recv()
        total = total + slots[k].astype(jnp.float32)
    out_ref[...] = total
    for copy in copies:
        copy.wait_send()


def small_sum(own, count, ident):
    dma = pltpu.SemaphoreType.DMA((count - 1,))
    return comm_call(
        functools.partial(small_kernel, count),
        jax.ShapeDtypeStruct(own.shape, jnp.float32),
        [VM],
        VM,
        [pltpu.VMEM((count - 1,) + own.shape, own.dtype), dma, dma],
        ident,
    )(own)


def line_kernel(count, own_ref, out_ref, own_sem, rs, rr, ls, lr):
    me = lax.axis_index("req")
    right, left = shift(me, 1, count), shift(me, -1, count)
    greet([("req", right), ("req", left)])
    own = pltpu.make_async_copy(own_ref, out_ref.at[me], own_sem)
    own.start()

    pieces = rs.shape[1]
    rows = own_ref.shape[0] // pieces

    def hop(step, piece, sign):
        block = jnp.clip(me - sign * step, 0, count - 1)
        part = pl.ds(piece * rows, rows)
        source = own_ref.at[part] if step == 0 else out_ref.at[block, part]
        send, recv, place = (rs, rr, right) if sign > 0 else (ls, lr, left)
        return remote(
            source,
            out_ref.at[block, part],
            send.at[step, piece],
            recv.at[step, piece],
            "req",
            place,
        )

    def each(step, work):
        for piece in range(pieces):
            work(step, piece)

    def advance(step, piece):
        if step > 0:

            @pl.when(me >= step)
            def _():
                hop(step - 1, piece, 1).wait_recv()

            @pl.when(me + step < count)
            def _():
                hop(step - 1, piece, -1).wait_recv()

        @pl.when((me >= step) & (me < count - 1))
        def _():
            hop(step, piece, 1).start()

        @pl.when((me + step < count) & (me > 0))
        def _():
            hop(step, piece, -1).start()

    def finish(step, piece):
        @pl.when(me >= count - 1)
        def _():
            hop(step, piece, 1).wait_recv()

        @pl.when(me < 1)
        def _():
            hop(step, piece, -1).wait_recv()

    def drain(step, piece):
        @pl.when((me >= step) & (me < count - 1))
        def _():
            hop(step, piece, 1).wait_send()

        @pl.when((me + step < count) & (me > 0))
        def _():
            hop(step, piece, -1).wait_send()

    for step in range(count - 1):
        each(step, advance)
    each(count - 2, finish)
    for step in range(count - 1):
        each(step, drain)
    own.wait()


def line_gather(own, count, ident):
    dma = pltpu.SemaphoreType.DMA
    return comm_call(
        functools.partial(line_kernel, count),
        jax.ShapeDtypeStruct((count,) + own.shape, own.dtype),
        [ANY],
        ANY,
        [dma(())] + [dma((count - 1, 4))] * 4,
        ident,
    )(own)


def exit_kernel(count, lines, part_ref, out_ref, near, mid, far, final, ns, nr, fs, fr, own_sem, send_sem, recv_sem):
    places = pair_places(count)
    me, core, sibling, peers, _ = places
    steps = count // PAIR
    line = lax.axis_index("req")
    groups = [shift(line, k + 1, lines) for k in range(lines)]
    greet(
        [("mlp", sibling)]
        + [("mlp", place) for place in peers[1:]]
        + [("req", place) for place in groups[:-1]]
    )
    order = list(range(1, steps)) + [0]
    pairs, sends, copies = {}, [], []
    for i, group in enumerate(groups):
        for k in order:
            other = peers[k] + (PAIR - 1 - 2 * core)
            pairs[i, k] = remote(
                part_ref.at[group, other], near.at[i, k], ns.at[i, k], nr.at[i, k], "mlp", sibling
            )
            pairs[i, k].start()
    for i, group in enumerate(groups):
        for k in range(1, steps):
            pairs[i, k].wait_recv()
            mid[i, k] = (
                part_ref[group, peers[k]].astype(jnp.float32) + near[i, k].astype(jnp.float32)
            ).astype(jnp.bfloat16)
            sends.append(
                remote(mid.at[i, k], far.at[i, k], fs.at[i, k], fr.at[i, k], "mlp", peers[k])
            )
            sends[-1].start()
    width = final.shape[-1]
    target = out_ref.at[:, pl.ds(pl.multiple_of(line * width, 128), width)]
    for i, group in enumerate(groups):
        pairs[i, 0].wait_recv()
        total = part_ref[group, me].astype(jnp.float32) + near[i, 0].astype(jnp.float32)
        for k in range(1, steps):
            sends[i * (steps - 1) + k - 1].wait_recv()
            total = total + far[i, k].astype(jnp.float32)
        final[i] = total.astype(jnp.bfloat16)
        if i < lines - 1:
            copies.append(
                remote(final.at[i], target, send_sem.at[i], recv_sem.at[i], "req", group)
            )
        else:
            copies.append(pltpu.make_async_copy(final.at[i], target, own_sem))
        copies[-1].start()
    for copy in list(pairs.values()) + sends:
        copy.wait_send()
    for copy in copies:
        copy.wait()


def exit_rows(part, count, lines, ident):
    groups, _, rows, width = part.shape
    steps = count // PAIR
    dma = pltpu.SemaphoreType.DMA
    return comm_call(
        functools.partial(exit_kernel, count, lines),
        jax.ShapeDtypeStruct((rows, lines * width), jnp.bfloat16),
        [VM],
        VM,
        [pltpu.VMEM((groups, steps, rows, width), jnp.bfloat16)] * 3
        + [pltpu.VMEM((groups, rows, width), jnp.bfloat16)]
        + [dma((groups, steps))] * 4
        + [dma(()), dma((lines - 1,)), dma((lines - 1,))],
        ident,
        24,
    )(part)


def attend_text(queries, text_ref, columns, segment):
    requests = text_ref.shape[1]
    scores = None
    for r in range(requests):
        some = lax.dot_general(
            queries, text_ref[0, r, :, columns], (((1,), (1,)), ((), ())), preferred_element_type=jnp.float32
        )
        scores = some if r == 0 else jnp.where(segment == r, some, scores)
    weights = jnp.exp(scores * (1.0 / math.sqrt(HD)))
    weights = weights * (1.0 / jnp.sum(weights, axis=-1, keepdims=True))
    total = None
    for r in range(requests):
        mine = jnp.where(segment == r, weights, 0.0).astype(jnp.bfloat16)
        some = jnp.dot(mine, text_ref[1, r, :, columns], preferred_element_type=jnp.float32)
        total = some if r == 0 else total + some
    return total.astype(jnp.bfloat16)


def lines_order(lines):
    middle = lines // 2
    return [g for g in range(lines) if g not in (middle - 1, middle)] + [middle - 1, middle]


def dot_tiles(x, w_ref, out_ref, put, tile):
    width = w_ref.shape[1]

    @pl.loop(0, width // tile)
    def _(i):
        columns = pl.ds(pl.multiple_of(i * tile, tile), tile)
        put(columns, jnp.dot(x, w_ref[:, columns], preferred_element_type=jnp.float32))


def ff_kernel(count, lines, parts, query_ref, seg_ref, base_ref, mod_ref, owner_ref, text_hbm, o_hbm, hop_one, hop_two, up_hbm, down_hbm, out_ref,
              text_ref, text_sem, x_ref, o_ref, o_sem, part, near, mid, first_in, second_in, ns, nr, xs, xr, fs, fr, gate, sums,
              up_ref, down_ref, w_sem, norm, res, act, a_send, a_recv, g_send, g_recv, p_send, p_recv,
              pbuf, from_outer, from_partner, staged, hid, es, er, ts, tr, ho_s, hp_s, h_r,
              dn, near2, mid2, far2, ns2, nr2, fs2, fr2, final, back, bs, br,
              wide_ref, wide_sem, hs, hr, rows_all, acc, zo_s, zp_s, z_r, *sems):
    places = pair_places(count)
    me, core, sibling, peers, sources = places
    steps = count // PAIR
    line = lax.axis_index("req")
    order = lines_order(lines)
    is_mid = (line == 1) | (line == 2)
    outer = jnp.where(line == 1, 0, 3)
    partner = 3 - line
    inner = jnp.where(line == 0, 1, 2)
    adder = QuadSum(parts, part, near, mid, first_in, second_in, ns, nr, xs, xr, fs, fr)
    heads = query_ref.shape[1] // HD
    texts = {}
    for h in range(heads):
        for i in range(2):
            columns = slice(h * HD, (h + 1) * HD)
            texts[i, h] = pltpu.make_async_copy(
                text_hbm.at[i, :, :, columns], text_ref.at[i, :, :, columns], text_sem.at[i, h]
            )
            texts[i, h].start()
    loads_o = {}
    for c in adder.order:
        columns = part_columns(base_ref.shape[1], parts, c)
        loads_o[c] = pltpu.make_async_copy(o_hbm.at[1, :, columns], o_ref.at[:, columns], o_sem.at[c])
        loads_o[c].start()
    friends = (
        [("mlp", sibling)]
        + [("mlp", place) for place in peers[1:]]
        + [("req", shift(line, k, lines)) for k in range(1, lines)]
    )
    hello(friends)
    wide = wide_ref.shape[1]
    weights = [
        pltpu.make_async_copy(up_hbm.at[:, wide:], up_ref, w_sem.at[0]),
        pltpu.make_async_copy(down_hbm, down_ref, w_sem.at[1]),
    ]
    part_width = up_hbm.shape[0]

    def wide_rows(place):
        return wide_ref.at[pl.ds(pl.multiple_of(place * part_width, 128), part_width)]

    hop = LineHop(
        3, lines, hop_two.at[0], hop_two.at[1],
        lambda side, place: wide_rows(jnp.clip(place, 0, lines - 1)), hs, hr,
    )
    sources_w = [(0, up_hbm.at[:, 0:wide])]
    for distance, held in ((1, hop_one), (2, hop_two)):
        sources_w += [(distance, held.at[0]), (-distance, held.at[1])]
    for q in range(lines):
        for distance, source in sources_w:
            @pl.when(line - q == distance)
            def _():
                pltpu.make_async_copy(source, wide_rows(q), wide_sem.at[q]).start()

    def wide_ready(q):
        if q == 0:
            @pl.when(line == lines - 1)
            def _():
                hop.right.wait_recv()

        if q == lines - 1:
            @pl.when(line == 0)
            def _():
                hop.left.wait_recv()

        @pl.when(jnp.abs(line - q) < lines - 1)
        def _():
            pltpu.make_async_copy(hop_one.at[0], wide_rows(q), wide_sem.at[q]).wait()

    for copy in weights:
        copy.start()
    owner = owner_ref[...]
    gate[...] = pick_rows(mod_ref, 5, owner)

    def consume(c, total):
        columns = part_columns(base_ref.shape[1], parts, c)
        value = (base_ref[:, columns].astype(jnp.float32) + total).astype(jnp.bfloat16)
        res[:, columns] = value
        sums[:, columns] = value.astype(jnp.float32)

    segment = seg_ref[...]
    for h in range(heads):
        columns = slice(h * HD, (h + 1) * HD)
        texts[0, h].wait()
        texts[1, h].wait()
        x_ref[:, columns] = attend_text(query_ref[:, columns], text_ref, columns, segment)

    def ready():
        heard(friends)
        hop.start()

    adder.run(part_product(x_ref, o_ref, part, parts, loads_o), consume, ready)
    norm[...] = (
        layer_norm(sums[...]) * (1.0 + pick_rows(mod_ref, 4, owner)) + pick_rows(mod_ref, 3, owner)
    ).astype(jnp.bfloat16)

    rows, width = norm.shape

    def slice_of(place):
        return pl.ds(pl.multiple_of(place * part_width, 128), part_width)

    def spread_to(k):
        place = lax.rem(line + k, lines)
        return remote(
            norm.at[:, slice_of(place)], act.at[line, me], a_send.at[k], a_recv.at[line], "req", place
        )

    gather = QuadGather(parts, norm, rows_all, *sems)
    gather.start()
    for k in (2, 1, 3):
        spread_to(k).start()

    def across(g, k):
        return remote(act.at[g, me], act.at[g, me], g_send.at[g, k], g_recv.at[g, k], "mlp", peers[k])

    def passed(g, k):
        block = act.at[g, sources[k]]
        return remote(block, block, p_send.at[g, k], p_recv.at[g, k], "mlp", sibling)

    def from_sibling(g, k):
        block = act.at[g, sources[k] + PAIR - 1 - 2 * core]
        return remote(block, block, p_send.at[g, k], p_recv.at[g, k], "mlp", sibling)

    def landed(p):
        g = order[p]

        @pl.when(line != g)
        def _():
            remote(norm.at[:, slice_of(g)], act.at[g, me], a_send.at[0], a_recv.at[g], "req", g).wait_recv()

    def opened(p):
        if p < lines:
            g = order[p]
            landed(p)

            @pl.when(line != g)
            def _():
                for k in range(1, steps):
                    across(g, k).start()
                passed(g, 0).start()

    tall = count * rows
    chunks = from_outer.shape[1]
    some = tall // chunks

    def chunk(j):
        return pl.ds(pl.multiple_of(j * some, some), some)

    def to_inner(g, j):
        return remote(pbuf.at[g, chunk(j)], from_outer.at[g, j], es.at[g, j], er.at[g, j], "req", inner)

    def to_partner(g, j):
        return remote(staged.at[g, j], from_partner.at[g, j], ts.at[g, j], tr.at[g, j], "req", partner)

    def out_to(g, j, place, sem):
        block = hid.at[g, chunk(j), wide:]
        return remote(block, block, sem.at[g, j], h_r.at[g, j], "req", place)

    def gathered(p):
        g = order[p]

        @pl.when(line != g)
        def _():
            for k in range(1, steps):
                remote(act.at[g, me], act.at[g, sources[k]], g_send.at[g, k], g_recv.at[g, k], "mlp", peers[k]).wait_recv()
                passed(g, k).start()

        opened(p + 1)

        @pl.when(line != g)
        def _():
            for k in range(steps):
                from_sibling(g, k).wait_recv()

    def first_product(p):
        g = order[p]

        def put(columns, value):
            pbuf[g, :, columns] = value.astype(jnp.bfloat16)

        dot_tiles(act[g].reshape(tall, part_width), up_ref, pbuf, put, 256 if up_ref.shape[1] % 256 == 0 else up_ref.shape[1])

        @pl.when(jnp.logical_not(is_mid))
        def _():
            for j in range(chunks):
                to_inner(g, j).start()

    def theirs(g, i):
        j = 2 * i + 2 - line
        to_inner(g, j).wait_recv()
        staged[g, j] = (
            pbuf[g, chunk(j)].astype(jnp.float32) + from_outer[g, j].astype(jnp.float32)
        ).astype(jnp.bfloat16)
        to_partner(g, j).start()

    def mine(g, i):
        j = 2 * i + line - 1
        to_inner(g, j).wait_recv()
        to_partner(g, j).wait_recv()
        value = (
            pbuf[g, chunk(j)].astype(jnp.float32)
            + from_outer[g, j].astype(jnp.float32)
            + from_partner[g, j].astype(jnp.float32)
        )
        hid[g, chunk(j), wide:] = jax.nn.gelu(value, approximate=True).astype(jnp.bfloat16)
        out_to(g, j, partner, hp_s).start()
        out_to(g, j, outer, ho_s).start()

    def forward(g, i):
        j = 2 * i + 2 - line
        out_to(g, j, partner, hp_s).wait_recv()
        out_to(g, j, outer, ho_s).start()

    def middle(p):
        @pl.when(is_mid)
        def _():
            g = order[p]
            pairs = chunks // 2
            theirs(g, 0)
            if p > 0:
                forward(order[p - 1], pairs - 1)
            for i in range(pairs):
                if i + 1 < pairs:
                    theirs(g, i + 1)
                mine(g, i)
                if i > 0:
                    forward(g, i - 1)

    def all_hidden(p):
        g = order[p]
        if p == lines - 1:
            @pl.when(is_mid)
            def _():
                forward(g, chunks // 2 - 1)

        @pl.when(jnp.logical_not(is_mid))
        def _():
            for j in range(chunks):
                out_to(g, j, inner, ho_s).wait_recv()

    def pair_copy(g, k):
        other = peers[k] + (PAIR - 1 - 2 * core)
        return remote(dn.at[g, other], near2.at[g, k], ns2.at[g, k], nr2.at[g, k], "mlp", sibling)

    def far_copy(g, k):
        return remote(mid2.at[g, k], far2.at[g, k], fs2.at[g, k], fr2.at[g, k], "mlp", peers[k])

    k_order = list(range(1, steps)) + [0]

    def second_product(p):
        g = order[p]

        def put(columns, value):
            dn[g, :, :, columns] = value.astype(jnp.bfloat16).reshape(count, rows, 256)

        dot_tiles(hid[g], down_ref, dn, put, 256)
        for k in k_order:
            pair_copy(g, k).start()

    def relay(p):
        g = order[p]
        for k in range(1, steps):
            pair_copy(g, k).wait_recv()
            mid2[g, k] = (
                dn[g, peers[k]].astype(jnp.float32) + near2[g, k].astype(jnp.float32)
            ).astype(jnp.bfloat16)
            far_copy(g, k).start()

    def home(g):
        return remote(final.at[g], back.at[line], bs.at[g], br.at[line], "req", g)

    def finish(p):
        g = order[p]
        pair_copy(g, 0).wait_recv()
        value = dn[g, me].astype(jnp.float32) + near2[g, 0].astype(jnp.float32)
        for k in range(1, steps):
            far_copy(g, k).wait_recv()
            value = value + far2[g, k].astype(jnp.float32)
        final[g] = value.astype(jnp.bfloat16)

        @pl.when(line == g)
        def _():
            back[g] = final[g]

        @pl.when(line != g)
        def _():
            home(g).start()

    def along(g, place, sem):
        block = hid.at[g, :, 0:wide]
        return remote(block, block, sem.at[g], z_r.at[g], "req", place)

    def wide_part(c):
        x = rows_all[:, :, part_columns(width, parts, c)].reshape(tall, part_width)
        wide_ready(c)
        value = jnp.dot(x, wide_ref[c * part_width : (c + 1) * part_width], preferred_element_type=jnp.float32)
        acc[...] = value if c == gather.order[0] else acc[...] + value

    def pass_outer():
        @pl.when(is_mid)
        def _():
            along(outer, partner, zp_s).wait_recv()
            along(outer, partner, zp_s).start()

    def pass_partner(g):
        @pl.when(is_mid)
        def _():
            along(g, outer, zo_s).wait_recv()
            along(g, outer, zo_s).start()

    for i in range(parts):
        gather.step(i)
    gather.own.wait()
    opened(0)
    for k in range(0, parts, 2):
        for c in gather.order[k : k + 2]:
            gather.corner(c)
        for c in gather.order[k : k + 2]:
            gather.whole(c)
            wide_part(c)
    hid[line, :, 0:wide] = jax.nn.gelu(acc[...], approximate=True).astype(jnp.bfloat16)

    @pl.when(is_mid)
    def _():
        along(line, outer, zo_s).start()
        along(line, partner, zp_s).start()

    @pl.when(jnp.logical_not(is_mid))
    def _():
        along(line, inner, zo_s).start()

    act[line] = rows_all[:, :, slice_of(line)]
    weights[0].wait()
    gathered(0)
    first_product(0)
    gathered(1)
    first_product(1)
    pass_outer()
    pass_partner(partner)
    middle(0)
    gathered(2)
    first_product(2)
    gathered(3)
    first_product(3)
    weights[1].wait()
    pass_partner(3 - outer)
    middle(1)

    @pl.when(jnp.logical_not(is_mid))
    def _():
        for k in range(1, lines):
            along(lax.rem(line + k, lines), inner, zo_s).wait_recv()

    all_hidden(0)
    second_product(0)
    relay(0)
    middle(2)
    all_hidden(1)
    second_product(1)
    finish(0)
    relay(1)
    middle(3)
    all_hidden(2)
    second_product(2)
    finish(1)
    relay(2)
    all_hidden(3)
    second_product(3)
    finish(2)
    relay(3)
    finish(3)

    for q in range(lines):
        columns = slice(q * part_width, (q + 1) * part_width)

        @pl.when(line != q)
        def _():
            remote(final.at[q], back.at[q], bs.at[q], br.at[q], "req", q).wait_recv()

        out_ref[:, columns] = (
            res[:, columns].astype(jnp.float32) + gate[:, columns] * back[q].astype(jnp.float32)
        ).astype(jnp.bfloat16)

    adder.drain()
    gather.drain()
    hop.sent()
    for k in range(1, lines):
        spread_to(k).wait_send()

    @pl.when(is_mid)
    def _():
        along(outer, partner, zp_s).wait_send()
        along(line, partner, zp_s).wait_send()
        along(line, outer, zo_s).wait_send()
        along(partner, outer, zo_s).wait_send()
        along(3 - outer, outer, zo_s).wait_send()

    @pl.when(jnp.logical_not(is_mid))
    def _():
        along(line, inner, zo_s).wait_send()

    for g in order:
        for k in range(1, steps):
            far_copy(g, k).wait_send()
        for k in range(steps):
            pair_copy(g, k).wait_send()

        @pl.when(line != g)
        def _():
            for k in range(1, steps):
                across(g, k).wait_send()
            for k in range(steps):
                passed(g, k).wait_send()

        @pl.when(line != g)
        def _():
            home(g).wait_send()

        @pl.when(is_mid)
        def _():
            for i in range(chunks // 2):
                to_partner(g, 2 * i + 2 - line).wait_send()
                out_to(g, 2 * i + line - 1, partner, hp_s).wait_send()
            for j in range(chunks):
                out_to(g, j, outer, ho_s).wait_send()

        @pl.when(jnp.logical_not(is_mid))
        def _():
            for j in range(chunks):
                to_inner(g, j).wait_send()


def feed_forward(query, segment, base, modulation, owner, text, out_maps, hop_one, hop_two, up, down, count, lines, ident):
    rows, width = base.shape
    steps = count // PAIR
    depth, units = up.shape
    wide = hop_one.shape[2]
    rest = units - wide
    tall = rows * count
    chunks = 2
    parts = 4
    dma = pltpu.SemaphoreType.DMA
    vm = lambda *extent: pltpu.VMEM(extent, jnp.bfloat16)
    scratch = (
        [vm(*text.shape), dma((2, query.shape[1] // HD)), vm(*query.shape)]
        + [vm(query.shape[1], width), dma((parts,))]
        + quad_sum_scratch(parts, count, rows, width)
        + [pltpu.VMEM((rows, width), jnp.float32)] * 2
        + [vm(depth, rest), vm(units, depth), dma((2,)), vm(rows, width), vm(rows, width)]
        + [vm(lines, count, rows, depth), dma((lines,)), dma((lines,))]
        + [dma((lines, steps))] * 4
        + [vm(lines, tall, rest)]
        + [vm(lines, chunks, tall // chunks, rest)] * 3
        + [vm(lines, tall, units)]
        + [dma((lines, chunks))] * 7
        + [vm(lines, count, rows, depth)]
        + [vm(lines, steps, rows, depth)] * 3
        + [dma((lines, steps))] * 4
        + [vm(lines, rows, depth)] * 2
        + [dma((lines,))] * 2
        + [vm(width, wide), dma((parts,)), dma((2,)), dma((2,)), vm(count, rows, width), pltpu.VMEM((tall, wide), jnp.float32)]
        + [dma((lines,))] * 3
        + quad_sems(parts)
    )
    return comm_call(
        functools.partial(ff_kernel, count, lines, parts),
        jax.ShapeDtypeStruct((rows, width), jnp.bfloat16),
        [VM] * 5 + [HBM] * 6,
        VM,
        scratch,
        ident,
        60,
    )(query, segment, base, modulation, owner, *in_hbm(text, out_maps, hop_one, hop_two, up, down))


def layer_norm(values):
    center = values - jnp.mean(values, axis=-1, keepdims=True)
    spread = jnp.mean(center * center, axis=-1, keepdims=True)
    return center * lax.rsqrt(spread + EPSILON)


def rotary_tables(grid):
    half_dim = HD // 2
    spatial = half_dim // 3
    temporal = half_dim - 2 * spatial
    column = jnp.arange(HD, dtype=jnp.int32)
    sign = jnp.where(column < half_dim, -1.0, 1.0).astype(jnp.float32)
    column = column % half_dim
    which_axis = jnp.where(
        column < temporal, 0, jnp.where(column < temporal + spatial, 1, 2)
    ).astype(jnp.int32)
    offset = jnp.where(
        which_axis == 0, 0, jnp.where(which_axis == 1, temporal, temporal + spatial)
    ).astype(jnp.int32)
    span_size = jnp.where(which_axis == 0, temporal, spatial).astype(jnp.float32)
    frequency = jnp.exp(-(column - offset).astype(jnp.float32) / span_size * math.log(10000.0))
    grid = grid.astype(jnp.float32)[:, :, None]
    coordinate = jnp.where(
        which_axis == 0, grid[0], jnp.where(which_axis == 1, grid[1], grid[2])
    )
    angles = coordinate * frequency[None, :]
    return (jnp.cos(angles), jnp.sin(angles) * sign[None, :])


def attend(queries, key_rows, value_rows, allowed):
    scores = lax.dot_general(
        queries, key_rows, (((1,), (1,)), ((), ())), preferred_element_type=jnp.float32
    ) * (1.0 / math.sqrt(HD))
    weights = jnp.exp(jnp.where(allowed, scores, -1e30))
    weights = weights * (1.0 / jnp.sum(weights, axis=-1, keepdims=True))
    return jnp.dot(
        weights.astype(jnp.bfloat16), value_rows, preferred_element_type=jnp.float32
    ).astype(jnp.bfloat16)


def quad():
    me = lax.axis_index("mlp")
    core, x, y = lax.rem(me, 2), lax.rem(lax.div(me, 2), 2), lax.div(me, 4)

    def at(row, column, which):
        return (row * 2 + column) * 2 + which

    return me, at(y, x, 1 - core), at(y, 1 - x, core), at(1 - y, x, core), at(1 - y, 1 - x, core)


def part_columns(width, parts, c):
    return slice(c * (width // parts), (c + 1) * (width // parts))


class QuadGather:
    def __init__(self, parts, own_ref, out_ref, own_sem, xs, xr, ys, yr, fs, fr, ss, sr):
        self.parts, self.own_ref, self.out_ref = parts, own_ref, out_ref
        self.me, self.sib, self.xn, self.yn, self.dg = quad()
        self.sems = (xs, xr, ys, yr, fs, fr, ss, sr)
        self.half = parts // 2
        self.own = pltpu.make_async_copy(own_ref, out_ref.at[self.me], own_sem)
        self.x_order = list(range(parts))
        self.y_order = list(range(self.half, parts)) + list(range(self.half))
        self.order = [c for two in zip(range(self.half), range(self.half, parts)) for c in two]
        self.across, self.up, self.onward, self.passes = {}, {}, {}, {}

    def piece(self, place, c):
        return self.out_ref.at[place, :, part_columns(self.own_ref.shape[1], self.parts, c)]

    def mine(self, c):
        return self.own_ref.at[:, part_columns(self.own_ref.shape[1], self.parts, c)]

    def hand(self, kind, place, c):
        send, recv = self.sems[6].at[kind, c], self.sems[7].at[kind, c]
        source = self.piece(place, c) if kind else self.mine(c)
        self.passes[kind, c] = remote(source, self.piece(place, c), send, recv, "mlp", self.sib)
        self.passes[kind, c].start()

    def start(self):
        xs, xr, ys, yr = self.sems[:4]
        self.own.start()
        for i in range(self.parts):
            c = self.x_order[i]
            self.across[c] = remote(self.mine(c), self.piece(self.me, c), xs.at[c], xr.at[c], "mlp", self.xn)
            self.across[c].start()
            c = self.y_order[i]
            self.up[c] = remote(self.mine(c), self.piece(self.me, c), ys.at[c], yr.at[c], "mlp", self.yn)
            self.up[c].start()
        for c in self.order:
            self.hand(0, self.me, c)

    def send_on(self, place, c, to):
        fs, fr = self.sems[4:6]
        block = self.piece(place, c)
        self.onward[c] = remote(block, block, fs.at[c], fr.at[c], "mlp", to)
        self.onward[c].start()

    def step(self, i):
        c = self.x_order[i]
        self.across[c].wait_recv()
        if c < self.half:
            self.send_on(self.xn, c, self.yn)
        self.hand(1, self.xn, c)
        c = self.y_order[i]
        self.up[c].wait_recv()
        if c >= self.half:
            self.send_on(self.yn, c, self.xn)
        self.hand(2, self.yn, c)

    def corner(self, c):
        self.onward[c].wait_recv()
        self.hand(3, self.dg, c)

    def whole(self, c):
        for kind in range(4):
            self.passes[kind, c].wait_recv()

    def drain(self):
        for group in (self.across, self.up, self.onward, self.passes):
            for copy in group.values():
                copy.wait_send()


def quad_sems(parts):
    dma = pltpu.SemaphoreType.DMA
    return [dma(())] + [dma((parts,))] * 6 + [dma((4, parts))] * 2


def share(own_ref, slots_ref, send_sem, recv_sem, count):
    me = lax.axis_index("mlp")
    copies = [
        remote(own_ref, slots_ref.at[k], send_sem.at[k], recv_sem.at[k], "mlp", shift(me, k, count))
        for k in range(1, count)
    ]
    for copy in copies:
        copy.start()
    return copies


def pick_rows(mod_ref, which, owner):
    chosen = mod_ref[0, which : which + 1, :]
    for request in range(1, mod_ref.shape[0]):
        chosen = jnp.where(owner == request, mod_ref[request, which : which + 1, :], chosen)
    return chosen


class LineHop:
    def __init__(self, step, lines, from_left, from_right, into, send_sem, recv_sem):
        self.line = lax.axis_index("req")
        self.step, self.lines = step, lines
        right, left = jnp.minimum(self.line + 1, lines - 1), jnp.maximum(self.line - 1, 0)
        self.right = remote(from_left, into(0, self.line + 1 - step), send_sem.at[0], recv_sem.at[0], "req", right)
        self.left = remote(from_right, into(1, self.line - 1 + step), send_sem.at[1], recv_sem.at[1], "req", left)

    def sending(self, work):
        line, step, lines = self.line, self.step, self.lines

        @pl.when((line >= step - 1) & (line < lines - 1))
        def _():
            work(self.right)

        @pl.when((line + step - 1 < lines) & (line > 0))
        def _():
            work(self.left)

    def start(self):
        self.sending(lambda copy: copy.start())

    def landed(self):
        @pl.when(self.line >= self.step)
        def _():
            self.right.wait_recv()

        @pl.when(self.line + self.step < self.lines)
        def _():
            self.left.wait_recv()

    def sent(self):
        self.sending(lambda copy: copy.wait_send())


def line_peers(lines):
    line = lax.axis_index("req")
    return [("req", shift(line, 1, lines)), ("req", shift(line, -1, lines))]


def row_to_column(row, lanes=128):
    return jnp.transpose(jnp.broadcast_to(row, (lanes, row.shape[1])))


def column_to_rows(column, lanes=128):
    return jnp.transpose(jnp.broadcast_to(column, (column.shape[0], lanes)))[0:8]


def enter_kernel(count, lines, parts, tok_ref, mod_ref, owner_ref, seg_ref, pick_ref, down_hbm, maps_hbm, w_hbm, up_hbm,
                 lin_ref, value_ref, scale_ref, hop_ref,
                 down_ref, maps_ref, in_sem, norm, rows_all, w_ref, w_sem, acc, code_acc, code_own, code_slots, cs, cr,
                 chosen, near, mid, far, us, ur, vs, vr, sq_own, sq_slots, qs, qr, hs, hr, *sems):
    me, sib, xn, yn, dg = quad()
    core = lax.rem(me, PAIR)
    flip = 1 - 2 * core
    own_maps = up_hbm.at[:, 0 : hop_ref.shape[2]]
    hop = LineHop(1, lines, own_maps, own_maps, lambda side, _: hop_ref.at[side], hs, hr)
    friends = [("mlp", shift(me, k, count)) for k in range(1, count)] + line_peers(lines)
    hello(friends)
    brought = [
        pltpu.make_async_copy(maps_hbm, maps_ref, in_sem.at[0]),
        pltpu.make_async_copy(down_hbm, down_ref, in_sem.at[1]),
    ]
    for copy in brought:
        copy.start()
    rows, width = tok_ref.shape
    depth = width // parts
    tall = rows * count
    heads = acc.shape[2]
    owner = owner_ref[...]
    norm[...] = (
        layer_norm(tok_ref[...].astype(jnp.float32)) * (1.0 + pick_rows(mod_ref, 1, owner))
        + pick_rows(mod_ref, 0, owner)
    ).astype(jnp.bfloat16)
    gather = QuadGather(parts, norm, rows_all, *sems)
    heard(friends)
    gather.start()
    hop.start()
    loads = {}
    for c in gather.order:
        block = pl.ds(c * depth, depth)
        loads[c] = pltpu.make_async_copy(w_hbm.at[0:3, block], w_ref.at[:, block], w_sem.at[c])
        loads[c].start()

    slots = maps_ref.shape[0]
    requests = mod_ref.shape[0]
    rank = maps_ref.shape[2]

    def choose(r):
        for j in range(2):
            for place in range(count):
                columns = slice(place * heads, (place + 1) * heads)
                total = jnp.zeros((rank, heads), jnp.float32)
                for s in range(slots):
                    total = total + maps_ref[s, j, :, columns].astype(jnp.float32) * pick_ref[
                        r * slots + s : r * slots + s + 1, 0:1
                    ]
                chosen[place, j, r * rank : (r + 1) * rank] = total.astype(jnp.bfloat16)

    dest = [me, xn, yn, dg]
    pair = [
        remote(chosen.at[dest[t] + flip], near.at[t], us.at[t], ur.at[t], "mlp", sib) for t in range(4)
    ]
    out = {
        t: remote(mid.at[t], far.at[t], vs.at[t], vr.at[t], "mlp", dest[t]) for t in (1, 2, 3)
    }

    def code_part(c):
        x = rows_all[:, :, part_columns(width, parts, c)].reshape(tall, depth)
        code_acc[...] += lax.dot_general(
            down_ref[:, part_columns(width, parts, c)], x, (((1,), (1,)), ((), ())),
            preferred_element_type=jnp.float32,
        )

    def product_part(c, fresh):
        loads[c].wait()

        @pl.loop(0, 3)
        def _(i):
            x = rows_all[:, :, part_columns(width, parts, c)].reshape(tall, depth)
            value = jnp.dot(x, w_ref[i, c * depth : (c + 1) * depth], preferred_element_type=jnp.float32)
            acc[i] = value if fresh else acc[i] + value

    code_acc[...] = jnp.zeros_like(code_acc)
    order = gather.order
    brought[0].wait()
    for i in range(max(parts, requests)):
        if i < parts:
            gather.step(i)
        if i < requests:
            choose(i)
    brought[1].wait()
    for copy in pair:
        copy.start()
    for c in order[:2]:
        gather.corner(c)
    for t in (3, 1, 2):
        pair[t].wait_recv()
        mid[t] = chosen[dest[t]] + near[t]
        out[t].start()
    gather.own.wait()
    for c in order[:2]:
        gather.whole(c)
        code_part(c)
        product_part(c, c == order[0])
    for k in range(2, parts, 2):
        for c in order[k : k + 2]:
            gather.corner(c)
        for c in order[k : k + 2]:
            gather.whole(c)
            code_part(c)
            if c != order[-1]:
                product_part(c, False)
    segment = seg_ref[...]
    doubled = 2 * rank
    code = jnp.zeros((doubled, tall), jnp.float32)
    for s in range(slots):
        held = jnp.zeros((1, tall), jnp.float32)
        for r in range(requests):
            held = held + jnp.where(segment == r, pick_ref[r * slots + s : r * slots + s + 1, 0:1], 0.0)
        code = code + held * code_acc[s * doubled : (s + 1) * doubled]
    code_own[...] = code.astype(jnp.bfloat16)
    shared = share(code_own, code_slots, cs, cr, count)
    product_part(order[-1], False)
    pair[0].wait_recv()
    up = chosen[me].astype(jnp.float32) + near[0].astype(jnp.float32)
    for t in (1, 2, 3):
        out[t].wait_recv()
        up = up + far[t].astype(jnp.float32)
    up = up.astype(jnp.bfloat16)
    code = code_own[...].astype(jnp.float32)
    for k, copy in enumerate(shared):
        copy.wait_recv()
        code = code + code_slots[k + 1].astype(jnp.float32)

    def adapted(j):
        spread = jnp.concatenate(
            [jnp.where(segment == r, code[j * rank : (j + 1) * rank], 0.0) for r in range(requests)], axis=0
        )
        return jnp.dot(jnp.transpose(spread).astype(jnp.bfloat16), up[j], preferred_element_type=jnp.float32)

    query = acc[0] + adapted(0)
    key = acc[1]
    sq_own[0] = column_to_rows(jnp.sum(query * query, axis=1, keepdims=True))
    sq_own[1] = column_to_rows(jnp.sum(key * key, axis=1, keepdims=True))
    squares = share(sq_own, sq_slots, qs, qr, count)
    lin_ref[0] = query
    lin_ref[1] = key
    value_ref[...] = (acc[2] + adapted(1)).astype(jnp.bfloat16)
    total = sq_own[...]
    for k, copy in enumerate(squares):
        copy.wait_recv()
        total = total + sq_slots[k + 1]
    scale = lax.rsqrt(total / (heads * count) + EPSILON)
    for i in range(2):
        scale_ref[i] = row_to_column(scale[i, 0:1])
    gather.drain()
    hop.landed()
    hop.sent()
    for copy in shared + squares + pair + list(out.values()):
        copy.wait_send()


def enter(tokens, modulation, owner, segment, pick, down, maps, weights, up_maps, wide, count, lines):
    rows, width = tokens.shape
    parts = 4
    heads = weights.shape[2]
    tall = rows * count
    slots, two, rank, _ = maps.shape
    requests = modulation.shape[0]
    dma = pltpu.SemaphoreType.DMA
    vm = lambda *extent: pltpu.VMEM(extent, jnp.bfloat16)
    vf = lambda *extent: pltpu.VMEM(extent, jnp.float32)
    up = (two, requests * rank, heads)
    scratch = (
        [vm(*down.shape), vm(*maps.shape), dma((2,))]
        + [vm(rows, width), vm(count, rows, width), vm(3, width, heads), dma((parts,)), vf(3, tall, heads)]
        + [vf(slots * two * rank, tall), vm(two * rank, tall), vm(count, two * rank, tall), dma((count,)), dma((count,))]
        + [vm(count, *up), vm(4, *up), vm(4, *up), vm(4, *up)]
        + [dma((4,))] * 4
        + [vf(2, 8, tall), vf(count, 2, 8, tall), dma((count,)), dma((count,)), dma((2,)), dma((2,))]
        + quad_sems(parts)
    )
    return comm_call(
        functools.partial(enter_kernel, count, lines, parts),
        (
            jax.ShapeDtypeStruct((2, tall, heads), jnp.float32),
            jax.ShapeDtypeStruct((tall, heads), jnp.bfloat16),
            jax.ShapeDtypeStruct((2, tall, 128), jnp.float32),
            pltpu.HBM((2, up_maps.shape[0], wide), jnp.bfloat16),
        ),
        [VM] * 5 + [HBM] * 4,
        (VM, VM, VM, HBM),
        scratch,
        0,
        48,
    )(tokens, modulation, owner, segment, pick, *in_hbm(down, maps, weights, up_maps))


class QuadSum:
    def __init__(self, parts, part_ref, near, mid, first_in, second_in, ns, nr, xs, xr, fs, fr):
        self.parts, self.part_ref, self.near, self.mid = parts, part_ref, near, mid
        self.first_in, self.second_in = first_in, second_in
        self.sems = (ns, nr, xs, xr, fs, fr)
        self.me, self.sib, self.xn, self.yn, dg = quad()
        self.dest = [self.me, self.xn, self.yn, dg]
        self.flip = 1 - 2 * lax.rem(self.me, PAIR)
        self.half = parts // 2
        self.order = [c for two in zip(range(self.half), range(self.half, parts)) for c in two]
        self.pairs, self.ones, self.twos = {}, {}, {}

    def columns(self, c):
        return part_columns(self.part_ref.shape[2], self.parts, c)

    def ways(self, c):
        return (1, 2) if c < self.half else (2, 1)

    def offer(self, c):
        ns, nr = self.sems[:2]
        columns = self.columns(c)
        for t in (3, 1, 2, 0):
            self.pairs[t, c] = remote(
                self.part_ref.at[self.dest[t] + self.flip, :, columns],
                self.near.at[t, :, columns],
                ns.at[t, c],
                nr.at[t, c],
                "mlp",
                self.sib,
            )
            self.pairs[t, c].start()

    def both(self, t, columns):
        return self.part_ref[self.dest[t], :, columns].astype(jnp.float32) + self.near[
            t, :, columns
        ].astype(jnp.float32)

    def first(self, c):
        xs, xr = self.sems[2:4]
        columns = self.columns(c)
        far, _ = self.ways(c)
        for t, slot in ((3, 1), (far, 0)):
            self.pairs[t, c].wait_recv()
            self.mid[t, :, columns] = self.both(t, columns).astype(jnp.bfloat16)
            self.ones[t, c] = remote(
                self.mid.at[t, :, columns],
                self.first_in.at[slot, :, columns],
                xs.at[slot, c],
                xr.at[slot, c],
                "mlp",
                self.dest[far],
            )
            self.ones[t, c].start()

    def second(self, c):
        fs, fr = self.sems[4:6]
        columns = self.columns(c)
        _, keep = self.ways(c)
        self.pairs[keep, c].wait_recv()
        self.ones[3, c].wait_recv()
        self.mid[keep, :, columns] = (
            self.both(keep, columns) + self.first_in[1, :, columns].astype(jnp.float32)
        ).astype(jnp.bfloat16)
        self.twos[c] = remote(
            self.mid.at[keep, :, columns], self.second_in.at[:, columns], fs.at[c], fr.at[c], "mlp", self.dest[keep]
        )
        self.twos[c].start()

    def total(self, c):
        columns = self.columns(c)
        far, _ = self.ways(c)
        self.pairs[0, c].wait_recv()
        self.ones[far, c].wait_recv()
        self.twos[c].wait_recv()
        return (
            self.both(0, columns)
            + self.first_in[0, :, columns].astype(jnp.float32)
            + self.second_in[:, columns].astype(jnp.float32)
        )

    def run(self, produce, consume, ready):
        order = self.order
        produce(order[0])
        ready()
        self.offer(order[0])
        for i in range(1, self.parts):
            produce(order[i])
            self.offer(order[i])
            self.first(order[i - 1])
        self.first(order[-1])
        for c in order:
            self.second(c)
        for c in order:
            consume(c, self.total(c))

    def drain(self):
        for group in (self.pairs, self.ones, self.twos):
            for copy in group.values():
                copy.wait_send()


def quad_sum_scratch(parts, count, rows, width):
    dma = pltpu.SemaphoreType.DMA
    vm = lambda *extent: pltpu.VMEM(extent, jnp.bfloat16)
    return (
        [vm(count, rows, width), vm(4, rows, width), vm(4, rows, width), vm(2, rows, width), vm(rows, width)]
        + [dma((4, parts))] * 2
        + [dma((2, parts))] * 2
        + [dma((parts,))] * 2
    )


def part_product(x_ref, w_ref, part_ref, parts, loads):
    count, rows, width = part_ref.shape

    def produce(c):
        columns = part_columns(width, parts, c)
        loads[c].wait()
        part_ref[:, :, columns] = (
            jnp.dot(x_ref[...], w_ref[:, columns], preferred_element_type=jnp.float32)
            .astype(jnp.bfloat16)
            .reshape(count, rows, width // parts)
        )

    return produce


def cross_in_kernel(count, lines, parts, att_ref, base_ref, mod_ref, owner_ref, gain_ref, head_gain_ref, o_hbm, q_hbm, held_hbm,
                    res_ref, query_ref, hop_ref,
                    o_ref, o_sem, q_ref, q_sem, sums, norm, rows_all, acc, sq_own, sq_slots, qs, qr, hs, hr, *sems):
    sum_sems, gather_sems_ = sems[:11], sems[11:]
    me = lax.axis_index("mlp")
    rows, width = base_ref.shape
    depth = width // parts
    tall = rows * count
    heads = acc.shape[1]
    adder = QuadSum(parts, *sum_sems)
    loads_o, loads_q = {}, {}
    for c in adder.order:
        columns = part_columns(width, parts, c)
        loads_o[c] = pltpu.make_async_copy(o_hbm.at[0, :, columns], o_ref.at[:, columns], o_sem.at[c])
        loads_o[c].start()
    hop = LineHop(2, lines, held_hbm.at[0], held_hbm.at[1], lambda side, _: hop_ref.at[side], hs, hr)
    friends = [("mlp", shift(me, k, count)) for k in range(1, count)] + line_peers(lines)
    hello(friends)

    def ready():
        heard(friends)
        hop.start()

    for c in adder.order:
        block = pl.ds(c * depth, depth)
        loads_q[c] = pltpu.make_async_copy(q_hbm.at[3, block], q_ref.at[block], q_sem.at[c])
        loads_q[c].start()
    gate = pick_rows(mod_ref, 2, owner_ref[...])

    def consume(c, total):
        columns = part_columns(width, parts, c)
        res = (base_ref[:, columns].astype(jnp.float32) + gate[:, columns] * total).astype(jnp.bfloat16)
        res_ref[:, columns] = res
        sums[:, columns] = res.astype(jnp.float32)

    adder.run(part_product(att_ref, o_ref, sum_sems[0], parts, loads_o), consume, ready)
    norm[...] = (layer_norm(sums[...]) * gain_ref[...]).astype(jnp.bfloat16)
    gather = QuadGather(parts, norm, rows_all, *gather_sems_)
    gather.start()
    order = gather.order

    def product_part(c):
        x = rows_all[:, :, part_columns(width, parts, c)].reshape(tall, depth)
        loads_q[c].wait()
        value = jnp.dot(x, q_ref[c * depth : (c + 1) * depth], preferred_element_type=jnp.float32)
        acc[...] = value if c == order[0] else acc[...] + value

    for i in range(parts):
        gather.step(i)
    gather.own.wait()
    for k in range(0, parts, 2):
        for c in order[k : k + 2]:
            gather.corner(c)
        for c in order[k : k + 2]:
            gather.whole(c)
            product_part(c)
    query = acc[...]
    sq_own[...] = column_to_rows(jnp.sum(query * query, axis=1, keepdims=True))
    squares = share(sq_own, sq_slots, qs, qr, count)
    total = sq_own[...]
    for k, copy in enumerate(squares):
        copy.wait_recv()
        total = total + sq_slots[k + 1]
    scale = row_to_column(lax.rsqrt(total / (heads * count) + EPSILON)[0:1])[:, 0:1]
    query_ref[...] = (acc[...] * scale * head_gain_ref[...]).astype(jnp.bfloat16)
    adder.drain()
    gather.drain()
    hop.landed()
    hop.sent()
    for copy in squares:
        copy.wait_send()


def cross_in(attended, base, modulation, owner, gain, head_gain, out_maps, in_maps, held, count, lines):
    rows, width = base.shape
    parts = 4
    tall, heads = attended.shape
    dma = pltpu.SemaphoreType.DMA
    vm = lambda *extent: pltpu.VMEM(extent, jnp.bfloat16)
    vf = lambda *extent: pltpu.VMEM(extent, jnp.float32)
    scratch = (
        [vm(heads, width), dma((parts,)), vm(width, heads), dma((parts,))]
        + [vf(rows, width), vm(rows, width), vm(count, rows, width), vf(tall, heads)]
        + [vf(8, tall), vf(count, 8, tall), dma((count,)), dma((count,)), dma((2,)), dma((2,))]
        + quad_sum_scratch(parts, count, rows, width)
        + quad_sems(parts)
    )
    return comm_call(
        functools.partial(cross_in_kernel, count, lines, parts),
        (
            jax.ShapeDtypeStruct((rows, width), jnp.bfloat16),
            jax.ShapeDtypeStruct((tall, heads), jnp.bfloat16),
            pltpu.HBM(held.shape, held.dtype),
        ),
        [VM] * 6 + [HBM] * 3,
        (VM, VM, HBM),
        scratch,
        3,
        48,
    )(attended, base, modulation, owner, gain, head_gain, *in_hbm(out_maps, in_maps, held))


def self_kernel(page_ref, q_ref, k_ref, v_ref, qs_ref, ks_ref, gain_ref, cos_ref, sin_ref, seg_ref, segs_ref, out_ref, kv_ref):
    cosine, sine = cos_ref[...], sin_ref[...]
    allowed = seg_ref[...] == segs_ref[...]

    def turned(ref, scale, gain, columns):
        rows = ref[:, columns] * scale * gain_ref[gain : gain + 1, columns]
        return (rows * cosine + pltpu.roll(rows, HD // 2, 1) * sine).astype(jnp.bfloat16)

    for head in range(q_ref.shape[1] // HD):
        columns = slice(head * HD, (head + 1) * HD)
        query = turned(q_ref, qs_ref[...], 0, columns)
        key = turned(k_ref, ks_ref[...], 1, columns)
        value = v_ref[:, columns]
        out_ref[:, columns] = attend(query, key, value, allowed)
        for block in range(kv_ref.shape[1]):
            page = page_ref[block]
            rows = slice(block * PAGE, (block + 1) * PAGE)
            kv_ref[0, page, :, columns] = key[rows]
            kv_ref[1, page, :, columns] = value[rows]


def joint_kernel(page_ref, lin_ref, v_ref, scale_ref, gain_ref, cos_ref, sin_ref, seg_ref, segs_ref, out_ref, kv_ref):
    self_kernel(
        page_ref, lin_ref.at[0], lin_ref.at[1], v_ref, scale_ref.at[0, :, 0:1], scale_ref.at[1, :, 0:1],
        gain_ref, cos_ref, sin_ref, seg_ref, segs_ref, out_ref, kv_ref,
    )


def joint_attention(pages, linear, value, scales, gains, cosine, sine, segment):
    _, rows, width = linear.shape
    return pl.pallas_call(
        joint_kernel,
        out_shape=(
            jax.ShapeDtypeStruct((rows, width), jnp.bfloat16),
            jax.ShapeDtypeStruct((2, pages.shape[0], PAGE, width), jnp.bfloat16),
        ),
        in_specs=[pl.BlockSpec(memory_space=pltpu.SMEM)] + [VM] * 8,
        out_specs=(VM, VM),
        compiler_params=pltpu.CompilerParams(vmem_limit_bytes=16 << 20),
    )(pages, linear, value, scales, gains, cosine, sine, segment[:, None], segment[None, :])


def self_attention(pages, query, key, value, query_scale, key_scale, gains, cosine, sine, segment):
    rows, width = query.shape
    return pl.pallas_call(
        self_kernel,
        out_shape=(
            jax.ShapeDtypeStruct((rows, width), jnp.bfloat16),
            jax.ShapeDtypeStruct((2, pages.shape[0], PAGE, width), jnp.bfloat16),
        ),
        in_specs=[pl.BlockSpec(memory_space=pltpu.SMEM)] + [VM] * 10,
        out_specs=(VM, VM),
        compiler_params=pltpu.CompilerParams(vmem_limit_bytes=16 << 20),
    )(
        pages,
        query,
        key,
        value,
        query_scale[:, None],
        key_scale[:, None],
        gains,
        cosine,
        sine,
        segment[:, None],
        segment[None, :],
    )


def cross_kernel(q_ref, k_ref, v_ref, seg_ref, owner_ref, out_ref):
    out_ref[...] = attend(q_ref[...], k_ref[0], v_ref[0], seg_ref[...] == owner_ref[...])


def cross_attention(query, cache, segment, owner):
    rows, width = query.shape
    texts = cache.shape[1]
    head = pl.BlockSpec((rows, HD), lambda h: (0, h))
    return pl.pallas_call(
        cross_kernel,
        out_shape=jax.ShapeDtypeStruct((rows, width), jnp.bfloat16),
        grid=(width // HD,),
        in_specs=[
            head,
            pl.BlockSpec((1, texts, HD), lambda h: (0, 0, h)),
            pl.BlockSpec((1, texts, HD), lambda h: (1, 0, h)),
            pl.BlockSpec((rows, 1), lambda h: (0, 0)),
            pl.BlockSpec((1, texts), lambda h: (0, 0)),
        ],
        out_specs=head,
        compiler_params=pltpu.CompilerParams(vmem_limit_bytes=24 << 20),
    )(query, cache, cache, segment[:, None], owner[None, :])


def product_kernel(act, x_ref, w_ref, out_ref):
    out_ref[0] = act(
        jnp.dot(x_ref[...], w_ref[0], preferred_element_type=jnp.float32)
    ).astype(out_ref.dtype)


def product(rows_in, maps, first, amount, tile, dtype, act=lambda part: part):
    rows, depth = rows_in.shape
    width = maps.shape[2]
    tile = min(tile, width)
    return pl.pallas_call(
        functools.partial(product_kernel, act),
        out_shape=jax.ShapeDtypeStruct((amount, rows, width), dtype),
        grid=(amount, width // tile),
        in_specs=[
            pl.BlockSpec((rows, depth), lambda i, j: (0, 0)),
            pl.BlockSpec((1, depth, tile), lambda i, j: (first + i, 0, j)),
        ],
        out_specs=pl.BlockSpec((1, rows, tile), lambda i, j: (i, 0, j)),
        compiler_params=pltpu.CompilerParams(vmem_limit_bytes=24 << 20),
    )(rows_in, pltpu.with_memory_space_constraint(maps, pltpu.HBM))


def choose_rows(table, segment):
    chosen = jnp.zeros((segment.shape[0],) + table.shape[1:], table.dtype)
    for request in range(table.shape[0]):
        picked = (segment == request).reshape((-1,) + (1,) * (table.ndim - 1))
        chosen = jnp.where(picked, table[request][None], chosen)
    return chosen


def body(
    tokens,
    modulation,
    lengths,
    request_adapter,
    adapter_storage,
    adapter_down_weight,
    adapter_up_maps,
    input_projection,
    query_key_gains,
    positions,
    block_page_lookup,
    output_projection,
    cross_norm_gain,
    text_token_cache,
    feedforward_up,
    feedforward_down,
):
    mlp_count = lax.axis_size("mlp")
    my_index = lax.axis_index("mlp")
    own_count = tokens.shape[0]
    group_rows = own_count * mlp_count
    local_width = input_projection.shape[2]
    entire_width = local_width * mlp_count
    resident_slots = adapter_down_weight.shape[0]
    doubled_rank = adapter_down_weight.shape[2]
    rank_once = doubled_rank // 2

    req_count = lax.axis_size("req")
    slot_total = resident_slots * mlp_count
    tuned = mlp_count == 8 and req_count == 4
    counts = lengths[0]
    index = jnp.arange(counts.shape[0], dtype=jnp.int32)
    bounds = jnp.sum(jnp.where(index[:, None] >= index[None, :], counts[None, :], 0), axis=1)
    position = jnp.arange(group_rows, dtype=jnp.int32)
    segment = jnp.sum((position[:, None] >= bounds[None, :]).astype(jnp.int32), axis=1)
    own_start = my_index * own_count
    own_segment = lax.dynamic_slice_in_dim(segment, own_start, own_count)
    if tuned:
        storage = jnp.arange(adapter_storage.shape[0], dtype=jnp.int32)
        request_slot = jnp.sum(
            jnp.where(request_adapter[:, None] == storage[None, :], adapter_storage[None, :], 0), axis=1
        )
        resident = my_index * resident_slots + jnp.arange(resident_slots, dtype=jnp.int32)
        pick = (request_slot[:, None] == resident[None, :]).astype(jnp.float32).reshape(-1, 1)
        linear, value_rows, scales, hop_one = enter(
            tokens,
            modulation,
            own_segment[:, None],
            segment[None, :],
            jnp.broadcast_to(pick, (pick.shape[0], 128)),
            adapter_down_weight.transpose(0, 2, 1).reshape(resident_slots * doubled_rank, -1),
            adapter_up_maps,
            input_projection,
            feedforward_up,
            feedforward_up.shape[1] * 3 // 8,
            mlp_count,
            req_count,
        )
        cosine, sine = rotary_tables(positions)
        attended, kv_pages = joint_attention(
            block_page_lookup[0], linear, value_rows, scales, query_key_gains, cosine, sine, segment
        )
    else:
        per_token = [choose_rows(modulation[:, which_row, :], own_segment) for which_row in range(6)]
        token_f32 = tokens.astype(jnp.float32)
        rows_in, adapter_up_weight = entry_rows(
            tokens, per_token[1], per_token[0], adapter_up_maps, mlp_count
        )
        request_slot = adapter_storage[request_adapter]
        token_slot = jnp.sum(
            jnp.where(
                segment[:, None] == jnp.arange(request_slot.shape[0], dtype=jnp.int32)[None, :],
                request_slot[None, :],
                0,
            ),
            axis=1,
        )
        resident = my_index * resident_slots + jnp.arange(resident_slots, dtype=jnp.int32)
        held = (token_slot[None, :] == resident[:, None]).astype(jnp.float32)
        code_block = lax.dot_general(
            adapter_down_weight.transpose(0, 2, 1).reshape(resident_slots * doubled_rank, -1),
            rows_in,
            (((1,), (1,)), ((), ())),
            preferred_element_type=jnp.float32,
        ).reshape(resident_slots, doubled_rank, group_rows)
        my_codes = jnp.sum(held[:, None, :] * code_block, axis=0).astype(jnp.bfloat16)
        codes = small_sum(my_codes, mlp_count, 1).astype(jnp.bfloat16)
        slots = jnp.arange(slot_total, dtype=jnp.int32)
        everywhere = token_slot[None, :] == slots[:, None]

        def spread(code_part):
            return jnp.where(everywhere[:, None, :], code_part[None], jnp.bfloat16(0)).reshape(
                slot_total * rank_once, group_rows
            )

        def adapted(code_part, which_map):
            return lax.dot_general(
                spread(code_part),
                adapter_up_weight[:, which_map].reshape(slot_total * rank_once, local_width),
                (((0,), (0,)), ((), ())),
                preferred_element_type=jnp.float32,
            )

        projected = product(rows_in, input_projection, 0, 3, 256, jnp.float32)
        query_linear = projected[0] + adapted(codes[:rank_once], 0)
        key_linear = projected[1]
        value_rows = (projected[2] + adapted(codes[rank_once:], 1)).astype(jnp.bfloat16)
        squares = small_sum(
            jnp.stack(
                [jnp.sum(query_linear * query_linear, axis=1), jnp.sum(key_linear * key_linear, axis=1)]
            ),
            mlp_count,
            2,
        )
        query_square, key_square = squares[0], squares[1]
        query_scale = lax.rsqrt(query_square / entire_width + EPSILON)
        key_scale = lax.rsqrt(key_square / entire_width + EPSILON)
        cosine, sine = rotary_tables(positions)
        attended, kv_pages = self_attention(
            block_page_lookup[0],
            query_linear,
            key_linear,
            value_rows,
            query_scale,
            key_scale,
            query_key_gains,
            cosine,
            sine,
            segment,
        )
    text_owner = (
        jnp.arange(text_token_cache.shape[1] * text_token_cache.shape[2], dtype=jnp.int32)
        // text_token_cache.shape[2]
    )

    def out_rows(rows, which_map):
        return product(rows, output_projection, which_map, 1, 1280, jnp.bfloat16)[0]

    if tuned:
        first_res, cross_query, hop_two = cross_in(
            attended,
            tokens,
            modulation,
            own_segment[:, None],
            cross_norm_gain[None, :],
            query_key_gains[2:3],
            output_projection,
            input_projection,
            hop_one,
            mlp_count,
            req_count,
        )
    else:
        first_res, cross_rows = middle_rows(
            out_rows(attended, 0),
            tokens,
            per_token[2],
            cross_norm_gain[None, :],
            jnp.zeros((1, tokens.shape[1]), jnp.float32),
            mlp_count,
            3,
        )
        cross_linear = product(cross_rows, input_projection, 3, 1, 256, jnp.float32)[0]
        cross_square = small_sum(
            jnp.sum(cross_linear * cross_linear, axis=1)[None, :], mlp_count, 4
        )[0]
        cross_query = (
            cross_linear
            * lax.rsqrt(cross_square / entire_width + EPSILON)[:, None]
            * query_key_gains[2]
        ).astype(jnp.bfloat16)
    if tuned:
        layer_out = feed_forward(
            cross_query,
            segment[:, None],
            first_res,
            modulation,
            own_segment[:, None],
            text_token_cache,
            output_projection,
            hop_one,
            hop_two,
            feedforward_up,
            feedforward_down,
            mlp_count,
            req_count,
            5,
        )
        return (layer_out, kv_pages)
    cross_out = cross_attention(
        cross_query,
        text_token_cache.reshape(2, text_owner.shape[0], local_width),
        segment,
        text_owner,
    )
    up_full = lax.all_gather(feedforward_up, "req", axis=0, tiled=True)
    second_res, mlp_in = middle_rows(
        out_rows(cross_out, 1),
        first_res,
        jnp.ones((1, tokens.shape[1]), jnp.float32),
        1.0 + per_token[4],
        per_token[3],
        mlp_count,
        5,
    )
    hidden = product(
        mlp_in,
        up_full[None],
        0,
        1,
        256,
        jnp.bfloat16,
        functools.partial(jax.nn.gelu, approximate=True),
    )[0]
    hidden_all = line_gather(hidden, req_count, 6)
    units, columns = feedforward_down.shape
    down_part = jnp.dot(
        hidden_all.reshape(req_count * group_rows, units),
        feedforward_down,
        preferred_element_type=jnp.float32,
    ).astype(jnp.bfloat16)
    down_own = exit_rows(
        down_part.reshape(req_count, mlp_count, own_count, columns), mlp_count, req_count, 7
    )
    layer_out = (
        second_res.astype(jnp.float32) + per_token[5] * down_own.astype(jnp.float32)
    ).astype(jnp.bfloat16)
    return (layer_out, kv_pages)


def solution(mesh):
    return jax.shard_map(
        body,
        mesh=mesh,
        in_specs=(
            P(("req", "mlp"), None),
            P("req", None, None),
            P("req", None),
            P("req"),
            P(),
            P("mlp", None, None),
            P("mlp", None, None, None),
            P(None, None, "mlp"),
            P(None, "mlp"),
            P(None, "req"),
            P("req", None),
            P(None, "mlp", None),
            P(),
            P(None, "req", None, "mlp"),
            P("req", "mlp"),
            P("mlp", "req"),
        ),
        out_specs=(P(("req", "mlp"), None), P(None, "req", None, "mlp")),
        check_vma=False,
    )
```

```python
import functools
import math

import jax
import jax.numpy as jnp
from jax import lax
from jax.experimental import pallas as pl
from jax.experimental.pallas import tpu as pltpu
from jax.sharding import PartitionSpec as P

HD = 128
PAGE = 16


EPSILON = 1e-06


PAIR = 2
MESH = pl.DeviceIdType.MESH
ANY = pl.BlockSpec(memory_space=pl.ANY)
VM = pl.BlockSpec(memory_space=pltpu.VMEM)
HBM = pl.BlockSpec(memory_space=pltpu.HBM)


def comm_call(kernel, out_shape, in_specs, out_specs, scratch, ident, room=4):
    return pl.pallas_call(
        kernel,
        out_shape=out_shape,
        in_specs=in_specs,
        out_specs=out_specs,
        scratch_shapes=scratch,
        compiler_params=pltpu.CompilerParams(
            collective_id=ident, has_side_effects=True, vmem_limit_bytes=room << 20
        ),
    )


def remote(source, target, send_sem, recv_sem, axis, place):
    return pltpu.make_async_remote_copy(
        src_ref=source,
        dst_ref=target,
        send_sem=send_sem,
        recv_sem=recv_sem,
        device_id={axis: place},
        device_id_type=MESH,
    )


def shift(me, step, count):
    return lax.rem(me + (step + count) % count, count)


def greet(peers):
    barrier = pltpu.get_barrier_semaphore()
    for axis, place in peers:
        pl.semaphore_signal(barrier, inc=1, device_id={axis: place}, device_id_type=MESH)
    pl.semaphore_wait(barrier, len(peers))


def hello(peers):
    barrier = pltpu.get_barrier_semaphore()
    for axis, place in peers:
        pl.semaphore_signal(barrier, inc=1, device_id={axis: place}, device_id_type=MESH)


def heard(peers):
    pl.semaphore_wait(pltpu.get_barrier_semaphore(), len(peers))


def in_hbm(*arrays):
    return [pltpu.with_memory_space_constraint(array, pltpu.HBM) for array in arrays]


def pair_places(count):
    me = lax.axis_index("mlp")
    outer, core = lax.div(me, PAIR), lax.rem(me, PAIR)
    sibling = outer * PAIR + (PAIR - 1 - core)
    peers = [
        shift(outer, k, count // PAIR) * PAIR + core for k in range(count // PAIR)
    ]
    sources = [
        shift(outer, -k, count // PAIR) * PAIR + core for k in range(count // PAIR)
    ]
    return me, core, sibling, peers, sources


def gather_sems(count):
    steps = count // PAIR
    return [pltpu.SemaphoreType.DMA(())] + [pltpu.SemaphoreType.DMA((steps,))] * 4


def gather_rows(count, places, own_ref, out_ref, own_sem, send_sem, recv_sem, pass_send, pass_recv):
    me, core, sibling, peers, sources = places
    own = pltpu.make_async_copy(own_ref, out_ref.at[me], own_sem)
    sends = [
        remote(own_ref, out_ref.at[me], send_sem.at[k], recv_sem.at[k], "mlp", peers[k])
        for k in range(1, count // PAIR)
    ]
    for copy in sends:
        copy.start()
    passes = [remote(own_ref, out_ref.at[me], pass_send.at[0], pass_recv.at[0], "mlp", sibling)]
    passes[0].start()
    own.start()
    for k in range(1, count // PAIR):
        sends[k - 1].wait_recv()
        block = out_ref.at[sources[k]]
        passes.append(remote(block, block, pass_send.at[k], pass_recv.at[k], "mlp", sibling))
        passes[-1].start()
    for copy in sends:
        copy.wait_send()
    for copy in passes:
        copy.wait()
    own.wait()


def entry_kernel(count, tok_ref, scale_ref, shift_ref, maps_ref, out_ref, up_ref, norm, map_own, map_send, map_recv, *sems):
    places = pair_places(count)
    me = places[0]
    slots, width = maps_ref.shape[0], up_ref.shape[-1]
    others = [shift(me, k, count) for k in range(1, count)]
    greet([("mlp", place) for place in others])

    def columns(place):
        return maps_ref.at[:, :, :, pl.ds(pl.multiple_of(place * width, 128), width)]

    target = up_ref.at[pl.ds(me * slots, slots)]
    own = pltpu.make_async_copy(columns(me), target, map_own)
    own.start()
    copies = [
        remote(columns(place), target, map_send.at[k], map_recv.at[k], "mlp", place)
        for k, place in enumerate(others)
    ]
    norm[...] = (
        layer_norm(tok_ref[...].astype(jnp.float32)) * (1.0 + scale_ref[...]) + shift_ref[...]
    ).astype(jnp.bfloat16)
    for copy in copies:
        copy.start()
    gather_rows(count, places, norm, out_ref, *sems)
    for copy in copies:
        copy.wait()
    own.wait()


def entry_rows(tokens, scale, shift_rows, maps, count):
    rows, width = tokens.shape
    slots, two, rank, total = maps.shape
    dma = pltpu.SemaphoreType.DMA
    gathered, up = comm_call(
        functools.partial(entry_kernel, count),
        (
            jax.ShapeDtypeStruct((count, rows, width), jnp.bfloat16),
            jax.ShapeDtypeStruct((count * slots, two, rank, total // count), maps.dtype),
        ),
        [VM, VM, VM, ANY],
        (ANY, ANY),
        [pltpu.VMEM((rows, width), jnp.bfloat16), dma(()), dma((count - 1,)), dma((count - 1,))]
        + gather_sems(count),
        0,
        8,
    )(tokens, scale, shift_rows, maps)
    return gathered.reshape(count * rows, width), up


def sum_blocks(count, places, block_of, near, mid, far, ns, nr, fs, fr):
    me, core, sibling, peers, sources = places
    steps = count // PAIR
    order = list(range(1, steps)) + [0]
    pairs = {}
    for k in order:
        other = peers[k] + (PAIR - 1 - 2 * core)
        pairs[k] = remote(block_of(other), near.at[k], ns.at[k], nr.at[k], "mlp", sibling)
        pairs[k].start()
    sends = []
    for k in range(1, steps):
        pairs[k].wait_recv()
        mid[k] = (
            block_of(peers[k])[...].astype(jnp.float32) + near[k].astype(jnp.float32)
        ).astype(jnp.bfloat16)
        sends.append(remote(mid.at[k], far.at[k], fs.at[k], fr.at[k], "mlp", peers[k]))
        sends[-1].start()
    pairs[0].wait_recv()
    total = block_of(me)[...].astype(jnp.float32) + near[0].astype(jnp.float32)
    for k in range(1, steps):
        sends[k - 1].wait_recv()
        total = total + far[k].astype(jnp.float32)
    for k in order:
        pairs[k].wait_send()
    for copy in sends:
        copy.wait_send()
    return total


def sum_scratch(count, extent):
    steps = count // PAIR
    return [pltpu.VMEM((steps,) + extent, jnp.bfloat16)] * 3 + [
        pltpu.SemaphoreType.DMA((steps,))
    ] * 4


def middle_kernel(count, part_ref, base_ref, gate_ref, scale_ref, shift_ref, res_ref, out_ref, near, mid, far, norm, ns, nr, fs, fr, *sems):
    places = pair_places(count)
    greet([("mlp", places[2])] + [("mlp", place) for place in places[3][1:]])
    total = sum_blocks(
        count, places, lambda place: part_ref.at[place], near, mid, far, ns, nr, fs, fr
    )
    res = (base_ref[...].astype(jnp.float32) + gate_ref[...] * total).astype(jnp.bfloat16)
    res_ref[...] = res
    norm[...] = (layer_norm(res.astype(jnp.float32)) * scale_ref[...] + shift_ref[...]).astype(
        jnp.bfloat16
    )
    gather_rows(count, places, norm, out_ref, *sems)


def middle_rows(part, base, gate, scale, shift_rows, count, ident):
    rows, width = base.shape
    scratch = sum_scratch(count, (rows, width))
    res, gathered = comm_call(
        functools.partial(middle_kernel, count),
        (
            jax.ShapeDtypeStruct((rows, width), jnp.bfloat16),
            jax.ShapeDtypeStruct((count, rows, width), jnp.bfloat16),
        ),
        [VM] * 5,
        (VM, ANY),
        scratch[:3] + [pltpu.VMEM((rows, width), jnp.bfloat16)] + scratch[3:] + gather_sems(count),
        ident,
        24,
    )(part.reshape(count, rows, width), base, gate, scale, shift_rows)
    return res, gathered.reshape(count * rows, width)


def small_kernel(count, own_ref, out_ref, slots, send_sem, recv_sem):
    me = lax.axis_index("mlp")
    others = [shift(me, k, count) for k in range(1, count)]
    greet([("mlp", place) for place in others])
    copies = [
        remote(own_ref, slots.at[k], send_sem.at[k], recv_sem.at[k], "mlp", place)
        for k, place in enumerate(others)
    ]
    for copy in copies:
        copy.start()
    total = own_ref[...].astype(jnp.float32)
    for k, copy in enumerate(copies):
        copy.wait_recv()
        total = total + slots[k].astype(jnp.float32)
    out_ref[...] = total
    for copy in copies:
        copy.wait_send()


def small_sum(own, count, ident):
    dma = pltpu.SemaphoreType.DMA((count - 1,))
    return comm_call(
        functools.partial(small_kernel, count),
        jax.ShapeDtypeStruct(own.shape, jnp.float32),
        [VM],
        VM,
        [pltpu.VMEM((count - 1,) + own.shape, own.dtype), dma, dma],
        ident,
    )(own)


def line_kernel(count, own_ref, out_ref, own_sem, rs, rr, ls, lr):
    me = lax.axis_index("req")
    right, left = shift(me, 1, count), shift(me, -1, count)
    greet([("req", right), ("req", left)])
    own = pltpu.make_async_copy(own_ref, out_ref.at[me], own_sem)
    own.start()

    pieces = rs.shape[1]
    rows = own_ref.shape[0] // pieces

    def hop(step, piece, sign):
        block = jnp.clip(me - sign * step, 0, count - 1)
        part = pl.ds(piece * rows, rows)
        source = own_ref.at[part] if step == 0 else out_ref.at[block, part]
        send, recv, place = (rs, rr, right) if sign > 0 else (ls, lr, left)
        return remote(
            source,
            out_ref.at[block, part],
            send.at[step, piece],
            recv.at[step, piece],
            "req",
            place,
        )

    def each(step, work):
        for piece in range(pieces):
            work(step, piece)

    def advance(step, piece):
        if step > 0:

            @pl.when(me >= step)
            def _():
                hop(step - 1, piece, 1).wait_recv()

            @pl.when(me + step < count)
            def _():
                hop(step - 1, piece, -1).wait_recv()

        @pl.when((me >= step) & (me < count - 1))
        def _():
            hop(step, piece, 1).start()

        @pl.when((me + step < count) & (me > 0))
        def _():
            hop(step, piece, -1).start()

    def finish(step, piece):
        @pl.when(me >= count - 1)
        def _():
            hop(step, piece, 1).wait_recv()

        @pl.when(me < 1)
        def _():
            hop(step, piece, -1).wait_recv()

    def drain(step, piece):
        @pl.when((me >= step) & (me < count - 1))
        def _():
            hop(step, piece, 1).wait_send()

        @pl.when((me + step < count) & (me > 0))
        def _():
            hop(step, piece, -1).wait_send()

    for step in range(count - 1):
        each(step, advance)
    each(count - 2, finish)
    for step in range(count - 1):
        each(step, drain)
    own.wait()


def line_gather(own, count, ident):
    dma = pltpu.SemaphoreType.DMA
    return comm_call(
        functools.partial(line_kernel, count),
        jax.ShapeDtypeStruct((count,) + own.shape, own.dtype),
        [ANY],
        ANY,
        [dma(())] + [dma((count - 1, 4))] * 4,
        ident,
    )(own)


def exit_kernel(count, lines, part_ref, out_ref, near, mid, far, final, ns, nr, fs, fr, own_sem, send_sem, recv_sem):
    places = pair_places(count)
    me, core, sibling, peers, _ = places
    steps = count // PAIR
    line = lax.axis_index("req")
    groups = [shift(line, k + 1, lines) for k in range(lines)]
    greet(
        [("mlp", sibling)]
        + [("mlp", place) for place in peers[1:]]
        + [("req", place) for place in groups[:-1]]
    )
    order = list(range(1, steps)) + [0]
    pairs, sends, copies = {}, [], []
    for i, group in enumerate(groups):
        for k in order:
            other = peers[k] + (PAIR - 1 - 2 * core)
            pairs[i, k] = remote(
                part_ref.at[group, other], near.at[i, k], ns.at[i, k], nr.at[i, k], "mlp", sibling
            )
            pairs[i, k].start()
    for i, group in enumerate(groups):
        for k in range(1, steps):
            pairs[i, k].wait_recv()
            mid[i, k] = (
                part_ref[group, peers[k]].astype(jnp.float32) + near[i, k].astype(jnp.float32)
            ).astype(jnp.bfloat16)
            sends.append(
                remote(mid.at[i, k], far.at[i, k], fs.at[i, k], fr.at[i, k], "mlp", peers[k])
            )
            sends[-1].start()
    width = final.shape[-1]
    target = out_ref.at[:, pl.ds(pl.multiple_of(line * width, 128), width)]
    for i, group in enumerate(groups):
        pairs[i, 0].wait_recv()
        total = part_ref[group, me].astype(jnp.float32) + near[i, 0].astype(jnp.float32)
        for k in range(1, steps):
            sends[i * (steps - 1) + k - 1].wait_recv()
            total = total + far[i, k].astype(jnp.float32)
        final[i] = total.astype(jnp.bfloat16)
        if i < lines - 1:
            copies.append(
                remote(final.at[i], target, send_sem.at[i], recv_sem.at[i], "req", group)
            )
        else:
            copies.append(pltpu.make_async_copy(final.at[i], target, own_sem))
        copies[-1].start()
    for copy in list(pairs.values()) + sends:
        copy.wait_send()
    for copy in copies:
        copy.wait()


def exit_rows(part, count, lines, ident):
    groups, _, rows, width = part.shape
    steps = count // PAIR
    dma = pltpu.SemaphoreType.DMA
    return comm_call(
        functools.partial(exit_kernel, count, lines),
        jax.ShapeDtypeStruct((rows, lines * width), jnp.bfloat16),
        [VM],
        VM,
        [pltpu.VMEM((groups, steps, rows, width), jnp.bfloat16)] * 3
        + [pltpu.VMEM((groups, rows, width), jnp.bfloat16)]
        + [dma((groups, steps))] * 4
        + [dma(()), dma((lines - 1,)), dma((lines - 1,))],
        ident,
        24,
    )(part)


def attend_text(queries, text_ref, columns, segment):
    requests = text_ref.shape[1]
    scores = None
    for r in range(requests):
        some = lax.dot_general(
            queries, text_ref[0, r, :, columns], (((1,), (1,)), ((), ())), preferred_element_type=jnp.float32
        )
        scores = some if r == 0 else jnp.where(segment == r, some, scores)
    weights = jnp.exp(scores * (1.0 / math.sqrt(HD)))
    weights = weights * (1.0 / jnp.sum(weights, axis=-1, keepdims=True))
    total = None
    for r in range(requests):
        mine = jnp.where(segment == r, weights, 0.0).astype(jnp.bfloat16)
        some = jnp.dot(mine, text_ref[1, r, :, columns], preferred_element_type=jnp.float32)
        total = some if r == 0 else total + some
    return total.astype(jnp.bfloat16)


def lines_order(lines):
    middle = lines // 2
    return [g for g in range(lines) if g not in (middle - 1, middle)] + [middle - 1, middle]


def dot_tiles(x, w_ref, out_ref, put, tile):
    width = w_ref.shape[1]

    @pl.loop(0, width // tile)
    def _(i):
        columns = pl.ds(pl.multiple_of(i * tile, tile), tile)
        put(columns, jnp.dot(x, w_ref[:, columns], preferred_element_type=jnp.float32))


def ff_kernel(count, lines, parts, query_ref, seg_ref, base_ref, mod_ref, owner_ref, text_hbm, o_hbm, hop_one, hop_two, up_hbm, down_hbm, res, delta_ref,
              text_ref, text_sem, x_ref, o_ref, o_sem, part, near, mid, first_in, second_in, ns, nr, xs, xr, fs, fr, gate, sums,
              up_ref, down_ref, w_sem, norm, act, a_send, a_recv, g_send, g_recv, p_send, p_recv,
              pbuf, from_outer, from_partner, staged, hid, es, er, ts, tr, ho_s, hp_s, h_r,
              dn, near2, mid2, far2, ns2, nr2, fs2, fr2, final, back, bs, br,
              wide_ref, wide_sem, hs, hr, rows_all, acc, zo_s, zp_s, z_r, *sems):
    places = pair_places(count)
    me, core, sibling, peers, sources = places
    steps = count // PAIR
    line = lax.axis_index("req")
    order = lines_order(lines)
    is_mid = (line == 1) | (line == 2)
    outer = jnp.where(line == 1, 0, 3)
    partner = 3 - line
    inner = jnp.where(line == 0, 1, 2)
    adder = QuadSum(parts, part, near, mid, first_in, second_in, ns, nr, xs, xr, fs, fr)
    heads = query_ref.shape[1] // HD
    texts = {}
    for h in range(heads):
        for i in range(2):
            columns = slice(h * HD, (h + 1) * HD)
            texts[i, h] = pltpu.make_async_copy(
                text_hbm.at[i, :, :, columns], text_ref.at[i, :, :, columns], text_sem.at[i, h]
            )
            texts[i, h].start()
    loads_o = {}
    for c in adder.order:
        columns = part_columns(base_ref.shape[1], parts, c)
        loads_o[c] = pltpu.make_async_copy(o_hbm.at[1, :, columns], o_ref.at[:, columns], o_sem.at[c])
        loads_o[c].start()
    friends = (
        [("mlp", sibling)]
        + [("mlp", place) for place in peers[1:]]
        + [("req", shift(line, k, lines)) for k in range(1, lines)]
    )
    hello(friends)
    wide = wide_ref.shape[1]
    weights = [
        pltpu.make_async_copy(up_hbm.at[:, wide:], up_ref, w_sem.at[0]),
        pltpu.make_async_copy(down_hbm, down_ref, w_sem.at[1]),
    ]
    part_width = up_hbm.shape[0]

    def wide_rows(place):
        return wide_ref.at[pl.ds(pl.multiple_of(place * part_width, 128), part_width)]

    hop = LineHop(
        3, lines, hop_two.at[0], hop_two.at[1],
        lambda side, place: wide_rows(jnp.clip(place, 0, lines - 1)), hs, hr,
    )
    sources_w = [(0, up_hbm.at[:, 0:wide])]
    for distance, held in ((1, hop_one), (2, hop_two)):
        sources_w += [(distance, held.at[0]), (-distance, held.at[1])]
    for q in range(lines):
        for distance, source in sources_w:
            @pl.when(line - q == distance)
            def _():
                pltpu.make_async_copy(source, wide_rows(q), wide_sem.at[q]).start()

    def wide_ready(q):
        if q == 0:
            @pl.when(line == lines - 1)
            def _():
                hop.right.wait_recv()

        if q == lines - 1:
            @pl.when(line == 0)
            def _():
                hop.left.wait_recv()

        @pl.when(jnp.abs(line - q) < lines - 1)
        def _():
            pltpu.make_async_copy(hop_one.at[0], wide_rows(q), wide_sem.at[q]).wait()

    for copy in weights:
        copy.start()
    owner = owner_ref[...]
    gate[...] = pick_rows(mod_ref, 5, owner)

    def consume(c, total):
        columns = part_columns(base_ref.shape[1], parts, c)
        value = (base_ref[:, columns].astype(jnp.float32) + total).astype(jnp.bfloat16)
        res[:, columns] = value
        sums[:, columns] = value.astype(jnp.float32)

    segment = seg_ref[...]
    for h in range(heads):
        columns = slice(h * HD, (h + 1) * HD)
        texts[0, h].wait()
        texts[1, h].wait()
        x_ref[:, columns] = attend_text(query_ref[:, columns], text_ref, columns, segment)

    def ready():
        heard(friends)
        hop.start()

    adder.run(part_product(x_ref, o_ref, part, parts, loads_o), consume, ready)
    norm[...] = (
        layer_norm(sums[...]) * (1.0 + pick_rows(mod_ref, 4, owner)) + pick_rows(mod_ref, 3, owner)
    ).astype(jnp.bfloat16)

    rows, width = norm.shape

    def slice_of(place):
        return pl.ds(pl.multiple_of(place * part_width, 128), part_width)

    def spread_to(k):
        place = lax.rem(line + k, lines)
        return remote(
            norm.at[:, slice_of(place)], act.at[line, me], a_send.at[k], a_recv.at[line], "req", place
        )

    gather = QuadGather(parts, norm, rows_all, *sems)
    gather.start()
    for k in (2, 1, 3):
        spread_to(k).start()

    def across(g, k):
        return remote(act.at[g, me], act.at[g, me], g_send.at[g, k], g_recv.at[g, k], "mlp", peers[k])

    def passed(g, k):
        block = act.at[g, sources[k]]
        return remote(block, block, p_send.at[g, k], p_recv.at[g, k], "mlp", sibling)

    def from_sibling(g, k):
        block = act.at[g, sources[k] + PAIR - 1 - 2 * core]
        return remote(block, block, p_send.at[g, k], p_recv.at[g, k], "mlp", sibling)

    def landed(p):
        g = order[p]

        @pl.when(line != g)
        def _():
            remote(norm.at[:, slice_of(g)], act.at[g, me], a_send.at[0], a_recv.at[g], "req", g).wait_recv()

    def opened(p):
        if p < lines:
            g = order[p]
            landed(p)

            @pl.when(line != g)
            def _():
                for k in range(1, steps):
                    across(g, k).start()
                passed(g, 0).start()

    tall = count * rows
    chunks = from_outer.shape[1]
    some = tall // chunks

    def chunk(j):
        return pl.ds(pl.multiple_of(j * some, some), some)

    def to_inner(g, j):
        return remote(pbuf.at[g, chunk(j)], from_outer.at[g, j], es.at[g, j], er.at[g, j], "req", inner)

    def to_partner(g, j):
        return remote(staged.at[g, j], from_partner.at[g, j], ts.at[g, j], tr.at[g, j], "req", partner)

    def out_to(g, j, place, sem):
        block = hid.at[g, chunk(j), wide:]
        return remote(block, block, sem.at[g, j], h_r.at[g, j], "req", place)

    def gathered(p):
        g = order[p]

        @pl.when(line != g)
        def _():
            for k in range(1, steps):
                remote(act.at[g, me], act.at[g, sources[k]], g_send.at[g, k], g_recv.at[g, k], "mlp", peers[k]).wait_recv()
                passed(g, k).start()

        @pl.when(line != g)
        def _():
            for k in range(steps):
                from_sibling(g, k).wait_recv()

    def first_product(p):
        g = order[p]

        def put(columns, value):
            pbuf[g, :, columns] = value.astype(jnp.bfloat16)

        dot_tiles(act[g].reshape(tall, part_width), up_ref, pbuf, put, 256 if up_ref.shape[1] % 256 == 0 else up_ref.shape[1])

        @pl.when(jnp.logical_not(is_mid))
        def _():
            for j in range(chunks):
                to_inner(g, j).start()

    def theirs(g, i):
        j = 2 * i + 2 - line
        to_inner(g, j).wait_recv()
        staged[g, j] = (
            pbuf[g, chunk(j)].astype(jnp.float32) + from_outer[g, j].astype(jnp.float32)
        ).astype(jnp.bfloat16)
        to_partner(g, j).start()

    def mine(g, i):
        j = 2 * i + line - 1
        to_inner(g, j).wait_recv()
        to_partner(g, j).wait_recv()
        value = (
            pbuf[g, chunk(j)].astype(jnp.float32)
            + from_outer[g, j].astype(jnp.float32)
            + from_partner[g, j].astype(jnp.float32)
        )
        hid[g, chunk(j), wide:] = jax.nn.gelu(value, approximate=True).astype(jnp.bfloat16)
        out_to(g, j, partner, hp_s).start()
        out_to(g, j, outer, ho_s).start()

    def forward(g, i):
        j = 2 * i + 2 - line
        out_to(g, j, partner, hp_s).wait_recv()
        out_to(g, j, outer, ho_s).start()

    def at_middle(work, p):
        @pl.when(is_mid)
        def _():
            for i in range(chunks // 2):
                work(order[p], i)

    def all_hidden(p):
        g = order[p]
        @pl.when(jnp.logical_not(is_mid))
        def _():
            for j in range(chunks):
                out_to(g, j, inner, ho_s).wait_recv()

    def pair_copy(g, k):
        other = peers[k] + (PAIR - 1 - 2 * core)
        return remote(dn.at[g, other], near2.at[g, k], ns2.at[g, k], nr2.at[g, k], "mlp", sibling)

    def far_copy(g, k):
        return remote(mid2.at[g, k], far2.at[g, k], fs2.at[g, k], fr2.at[g, k], "mlp", peers[k])

    k_order = list(range(1, steps)) + [0]

    def second_product(p):
        g = order[p]

        def put(columns, value):
            dn[g, :, :, columns] = value.astype(jnp.bfloat16).reshape(count, rows, 256)

        dot_tiles(hid[g], down_ref, dn, put, 256)
        for k in k_order:
            pair_copy(g, k).start()

    def relay(p):
        g = order[p]
        for k in range(1, steps):
            pair_copy(g, k).wait_recv()
            mid2[g, k] = (
                dn[g, peers[k]].astype(jnp.float32) + near2[g, k].astype(jnp.float32)
            ).astype(jnp.bfloat16)
            far_copy(g, k).start()

    def home(g):
        return remote(final.at[g], back.at[line], bs.at[g], br.at[line], "req", g)

    def finish(p):
        g = order[p]
        pair_copy(g, 0).wait_recv()
        value = dn[g, me].astype(jnp.float32) + near2[g, 0].astype(jnp.float32)
        for k in range(1, steps):
            far_copy(g, k).wait_recv()
            value = value + far2[g, k].astype(jnp.float32)
        final[g] = value.astype(jnp.bfloat16)

        @pl.when(line == g)
        def _():
            back[g] = final[g]

        @pl.when(line != g)
        def _():
            home(g).start()

    def along(g, place, sem):
        block = hid.at[g, :, 0:wide]
        return remote(block, block, sem.at[g], z_r.at[g], "req", place)

    def wide_part(c):
        x = rows_all[:, :, part_columns(width, parts, c)].reshape(tall, part_width)
        wide_ready(c)
        value = jnp.dot(x, wide_ref[c * part_width : (c + 1) * part_width], preferred_element_type=jnp.float32)
        acc[...] = value if c == gather.order[0] else acc[...] + value

    def pass_outer():
        @pl.when(is_mid)
        def _():
            along(outer, partner, zp_s).wait_recv()
            along(outer, partner, zp_s).start()

    def pass_partner(g):
        @pl.when(is_mid)
        def _():
            along(g, outer, zo_s).wait_recv()
            along(g, outer, zo_s).start()

    for i in range(parts):
        gather.step(i)
    gather.own.wait()
    for p in range(lines):
        opened(p)
    for k in range(0, parts, 2):
        for c in gather.order[k : k + 2]:
            gather.corner(c)
        for c in gather.order[k : k + 2]:
            gather.whole(c)
            wide_part(c)
    hid[line, :, 0:wide] = jax.nn.gelu(acc[...], approximate=True).astype(jnp.bfloat16)

    @pl.when(is_mid)
    def _():
        along(line, outer, zo_s).start()
        along(line, partner, zp_s).start()

    @pl.when(jnp.logical_not(is_mid))
    def _():
        along(line, inner, zo_s).start()

    act[line] = rows_all[:, :, slice_of(line)]
    weights[0].wait()
    gathered(0)
    first_product(0)
    gathered(1)
    first_product(1)
    at_middle(theirs, 0)
    pass_outer()
    pass_partner(partner)
    gathered(2)
    first_product(2)
    pass_partner(3 - outer)
    at_middle(mine, 0)
    at_middle(theirs, 1)
    gathered(3)
    first_product(3)
    at_middle(forward, 0)
    at_middle(mine, 1)
    at_middle(theirs, 2)
    weights[1].wait()

    @pl.when(jnp.logical_not(is_mid))
    def _():
        for k in range(1, lines):
            along(lax.rem(line + k, lines), inner, zo_s).wait_recv()

    all_hidden(0)
    second_product(0)
    at_middle(forward, 1)
    at_middle(mine, 2)
    at_middle(theirs, 3)
    relay(0)
    all_hidden(1)
    second_product(1)
    at_middle(forward, 2)
    at_middle(mine, 3)
    finish(0)
    relay(1)
    all_hidden(2)
    second_product(2)
    at_middle(forward, 3)
    finish(1)
    relay(2)
    all_hidden(3)
    second_product(3)
    finish(2)
    relay(3)
    finish(3)

    for q in range(lines):
        columns = slice(q * part_width, (q + 1) * part_width)

        @pl.when(line != q)
        def _():
            remote(final.at[q], back.at[q], bs.at[q], br.at[q], "req", q).wait_recv()

        delta_ref[:, columns] = gate[:, columns] * back[q].astype(jnp.float32)

    adder.drain()
    gather.drain()
    hop.sent()
    for k in range(1, lines):
        spread_to(k).wait_send()

    @pl.when(is_mid)
    def _():
        along(outer, partner, zp_s).wait_send()
        along(line, partner, zp_s).wait_send()
        along(line, outer, zo_s).wait_send()
        along(partner, outer, zo_s).wait_send()
        along(3 - outer, outer, zo_s).wait_send()

    @pl.when(jnp.logical_not(is_mid))
    def _():
        along(line, inner, zo_s).wait_send()

    for g in order:
        for k in range(1, steps):
            far_copy(g, k).wait_send()
        for k in range(steps):
            pair_copy(g, k).wait_send()

        @pl.when(line != g)
        def _():
            for k in range(1, steps):
                across(g, k).wait_send()
            for k in range(steps):
                passed(g, k).wait_send()

        @pl.when(line != g)
        def _():
            home(g).wait_send()

        @pl.when(is_mid)
        def _():
            for i in range(chunks // 2):
                to_partner(g, 2 * i + 2 - line).wait_send()
                out_to(g, 2 * i + line - 1, partner, hp_s).wait_send()
            for j in range(chunks):
                out_to(g, j, outer, ho_s).wait_send()

        @pl.when(jnp.logical_not(is_mid))
        def _():
            for j in range(chunks):
                to_inner(g, j).wait_send()


def feed_forward(query, segment, base, modulation, owner, text, out_maps, hop_one, hop_two, up, down, count, lines, ident):
    rows, width = base.shape
    steps = count // PAIR
    depth, units = up.shape
    wide = hop_one.shape[2]
    rest = units - wide
    tall = rows * count
    chunks = 4
    parts = 4
    dma = pltpu.SemaphoreType.DMA
    vm = lambda *extent: pltpu.VMEM(extent, jnp.bfloat16)
    scratch = (
        [vm(*text.shape), dma((2, query.shape[1] // HD)), vm(*query.shape)]
        + [vm(query.shape[1], width), dma((parts,))]
        + quad_sum_scratch(parts, count, rows, width)
        + [pltpu.VMEM((rows, width), jnp.float32)] * 2
        + [vm(depth, rest), vm(units, depth), dma((2,)), vm(rows, width)]
        + [vm(lines, count, rows, depth), dma((lines,)), dma((lines,))]
        + [dma((lines, steps))] * 4
        + [vm(lines, tall, rest)]
        + [vm(lines, chunks, tall // chunks, rest)] * 3
        + [vm(lines, tall, units)]
        + [dma((lines, chunks))] * 7
        + [vm(lines, count, rows, depth)]
        + [vm(lines, steps, rows, depth)] * 3
        + [dma((lines, steps))] * 4
        + [vm(lines, rows, depth)] * 2
        + [dma((lines,))] * 2
        + [vm(width, wide), dma((parts,)), dma((2,)), dma((2,)), vm(count, rows, width), pltpu.VMEM((tall, wide), jnp.float32)]
        + [dma((lines,))] * 3
        + quad_sems(parts)
    )
    return comm_call(
        functools.partial(ff_kernel, count, lines, parts),
        (
            jax.ShapeDtypeStruct((rows, width), jnp.bfloat16),
            jax.ShapeDtypeStruct((rows, width), jnp.float32),
        ),
        [VM] * 5 + [HBM] * 6,
        (VM, VM),
        scratch,
        ident,
        52,
    )(query, segment, base, modulation, owner, *in_hbm(text, out_maps, hop_one, hop_two, up, down))


def layer_norm(values):
    center = values - jnp.mean(values, axis=-1, keepdims=True)
    spread = jnp.mean(center * center, axis=-1, keepdims=True)
    return center * lax.rsqrt(spread + EPSILON)


def rotary_tables(grid):
    half_dim = HD // 2
    spatial = half_dim // 3
    temporal = half_dim - 2 * spatial
    column = jnp.arange(HD, dtype=jnp.int32)
    sign = jnp.where(column < half_dim, -1.0, 1.0).astype(jnp.float32)
    column = column % half_dim
    which_axis = jnp.where(
        column < temporal, 0, jnp.where(column < temporal + spatial, 1, 2)
    ).astype(jnp.int32)
    offset = jnp.where(
        which_axis == 0, 0, jnp.where(which_axis == 1, temporal, temporal + spatial)
    ).astype(jnp.int32)
    span_size = jnp.where(which_axis == 0, temporal, spatial).astype(jnp.float32)
    frequency = jnp.exp(-(column - offset).astype(jnp.float32) / span_size * math.log(10000.0))
    grid = grid.astype(jnp.float32)[:, :, None]
    coordinate = jnp.where(
        which_axis == 0, grid[0], jnp.where(which_axis == 1, grid[1], grid[2])
    )
    angles = coordinate * frequency[None, :]
    return (jnp.cos(angles), jnp.sin(angles) * sign[None, :])


def attend(queries, key_rows, value_rows, allowed):
    scores = lax.dot_general(
        queries, key_rows, (((1,), (1,)), ((), ())), preferred_element_type=jnp.float32
    ) * (1.0 / math.sqrt(HD))
    weights = jnp.exp(jnp.where(allowed, scores, -1e30))
    weights = weights * (1.0 / jnp.sum(weights, axis=-1, keepdims=True))
    return jnp.dot(
        weights.astype(jnp.bfloat16), value_rows, preferred_element_type=jnp.float32
    ).astype(jnp.bfloat16)


def quad():
    me = lax.axis_index("mlp")
    core, x, y = lax.rem(me, 2), lax.rem(lax.div(me, 2), 2), lax.div(me, 4)

    def at(row, column, which):
        return (row * 2 + column) * 2 + which

    return me, at(y, x, 1 - core), at(y, 1 - x, core), at(1 - y, x, core), at(1 - y, 1 - x, core)


def part_columns(width, parts, c):
    return slice(c * (width // parts), (c + 1) * (width // parts))


class QuadGather:
    def __init__(self, parts, own_ref, out_ref, own_sem, xs, xr, ys, yr, fs, fr, ss, sr):
        self.parts, self.own_ref, self.out_ref = parts, own_ref, out_ref
        self.me, self.sib, self.xn, self.yn, self.dg = quad()
        self.sems = (xs, xr, ys, yr, fs, fr, ss, sr)
        self.half = parts // 2
        self.own = pltpu.make_async_copy(own_ref, out_ref.at[self.me], own_sem)
        self.x_order = list(range(parts))
        self.y_order = list(range(self.half, parts)) + list(range(self.half))
        self.order = [c for two in zip(range(self.half), range(self.half, parts)) for c in two]
        self.across, self.up, self.onward, self.passes = {}, {}, {}, {}

    def piece(self, place, c):
        return self.out_ref.at[place, :, part_columns(self.own_ref.shape[1], self.parts, c)]

    def mine(self, c):
        return self.own_ref.at[:, part_columns(self.own_ref.shape[1], self.parts, c)]

    def hand(self, kind, place, c):
        send, recv = self.sems[6].at[kind, c], self.sems[7].at[kind, c]
        source = self.piece(place, c) if kind else self.mine(c)
        self.passes[kind, c] = remote(source, self.piece(place, c), send, recv, "mlp", self.sib)
        self.passes[kind, c].start()

    def start(self):
        xs, xr, ys, yr = self.sems[:4]
        self.own.start()
        for i in range(self.parts):
            c = self.x_order[i]
            self.across[c] = remote(self.mine(c), self.piece(self.me, c), xs.at[c], xr.at[c], "mlp", self.xn)
            self.across[c].start()
            c = self.y_order[i]
            self.up[c] = remote(self.mine(c), self.piece(self.me, c), ys.at[c], yr.at[c], "mlp", self.yn)
            self.up[c].start()
        for c in self.order:
            self.hand(0, self.me, c)

    def send_on(self, place, c, to):
        fs, fr = self.sems[4:6]
        block = self.piece(place, c)
        self.onward[c] = remote(block, block, fs.at[c], fr.at[c], "mlp", to)
        self.onward[c].start()

    def step(self, i):
        c = self.x_order[i]
        self.across[c].wait_recv()
        if c < self.half:
            self.send_on(self.xn, c, self.yn)
        self.hand(1, self.xn, c)
        c = self.y_order[i]
        self.up[c].wait_recv()
        if c >= self.half:
            self.send_on(self.yn, c, self.xn)
        self.hand(2, self.yn, c)

    def corner(self, c):
        self.onward[c].wait_recv()
        self.hand(3, self.dg, c)

    def whole(self, c):
        for kind in range(4):
            self.passes[kind, c].wait_recv()

    def drain(self):
        for group in (self.across, self.up, self.onward, self.passes):
            for copy in group.values():
                copy.wait_send()


def quad_sems(parts):
    dma = pltpu.SemaphoreType.DMA
    return [dma(())] + [dma((parts,))] * 6 + [dma((4, parts))] * 2


def share(own_ref, slots_ref, send_sem, recv_sem, count):
    me = lax.axis_index("mlp")
    copies = [
        remote(own_ref, slots_ref.at[k], send_sem.at[k], recv_sem.at[k], "mlp", shift(me, k, count))
        for k in range(1, count)
    ]
    for copy in copies:
        copy.start()
    return copies


def pick_rows(mod_ref, which, owner):
    chosen = mod_ref[which, 0:1, :]
    for request in range(1, mod_ref.shape[1]):
        chosen = jnp.where(owner == request, mod_ref[which, request : request + 1, :], chosen)
    return chosen


class LineHop:
    def __init__(self, step, lines, from_left, from_right, into, send_sem, recv_sem):
        self.line = lax.axis_index("req")
        self.step, self.lines = step, lines
        right, left = jnp.minimum(self.line + 1, lines - 1), jnp.maximum(self.line - 1, 0)
        self.right = remote(from_left, into(0, self.line + 1 - step), send_sem.at[0], recv_sem.at[0], "req", right)
        self.left = remote(from_right, into(1, self.line - 1 + step), send_sem.at[1], recv_sem.at[1], "req", left)

    def sending(self, work):
        line, step, lines = self.line, self.step, self.lines

        @pl.when((line >= step - 1) & (line < lines - 1))
        def _():
            work(self.right)

        @pl.when((line + step - 1 < lines) & (line > 0))
        def _():
            work(self.left)

    def start(self):
        self.sending(lambda copy: copy.start())

    def landed(self):
        @pl.when(self.line >= self.step)
        def _():
            self.right.wait_recv()

        @pl.when(self.line + self.step < self.lines)
        def _():
            self.left.wait_recv()

    def sent(self):
        self.sending(lambda copy: copy.wait_send())


def line_peers(lines):
    line = lax.axis_index("req")
    return [("req", shift(line, 1, lines)), ("req", shift(line, -1, lines))]


def row_to_column(row, lanes=128):
    return jnp.transpose(jnp.broadcast_to(row, (lanes, row.shape[1])))


def column_to_rows(column, lanes=128):
    return jnp.transpose(jnp.broadcast_to(column, (column.shape[0], lanes)))[0:8]


def enter_kernel(count, lines, parts, tok_ref, mod_ref, owner_ref, seg_ref, pick_ref, down_hbm, maps_hbm, w_hbm, up_hbm,
                 lin_ref, value_ref, scale_ref, hop_ref,
                 down_ref, maps_ref, in_sem, norm, rows_all, w_ref, w_sem, acc, code_acc, code_own, code_slots, cs, cr,
                 chosen, near, mid, far, us, ur, vs, vr, sq_own, sq_slots, qs, qr, hs, hr, *sems):
    me, sib, xn, yn, dg = quad()
    core = lax.rem(me, PAIR)
    flip = 1 - 2 * core
    own_maps = up_hbm.at[:, 0 : hop_ref.shape[2]]
    hop = LineHop(1, lines, own_maps, own_maps, lambda side, _: hop_ref.at[side], hs, hr)
    friends = [("mlp", shift(me, k, count)) for k in range(1, count)] + line_peers(lines)
    hello(friends)
    brought = [
        pltpu.make_async_copy(maps_hbm, maps_ref, in_sem.at[0]),
        pltpu.make_async_copy(down_hbm, down_ref, in_sem.at[1]),
    ]
    for copy in brought:
        copy.start()
    rows, width = tok_ref.shape
    depth = width // parts
    tall = rows * count
    heads = acc.shape[2]
    owner = owner_ref[...]
    norm[...] = (
        layer_norm(tok_ref[...].astype(jnp.float32)) * (1.0 + pick_rows(mod_ref, 1, owner))
        + pick_rows(mod_ref, 0, owner)
    ).astype(jnp.bfloat16)
    gather = QuadGather(parts, norm, rows_all, *sems)
    heard(friends)
    gather.start()
    hop.start()
    loads = {}
    for c in gather.order:
        block = pl.ds(c * depth, depth)
        loads[c] = pltpu.make_async_copy(w_hbm.at[0:3, block], w_ref.at[:, block], w_sem.at[c])
        loads[c].start()

    slots = maps_ref.shape[0]
    requests = mod_ref.shape[1]
    rank = maps_ref.shape[2]

    def choose(r):
        for j in range(2):
            for place in range(count):
                columns = slice(place * heads, (place + 1) * heads)
                total = jnp.zeros((rank, heads), jnp.float32)
                for s in range(slots):
                    total = total + maps_ref[s, j, :, columns].astype(jnp.float32) * pick_ref[
                        r * slots + s : r * slots + s + 1, 0:1
                    ]
                chosen[place, j, r * rank : (r + 1) * rank] = total.astype(jnp.bfloat16)

    dest = [me, xn, yn, dg]
    pair = [
        remote(chosen.at[dest[t] + flip], near.at[t], us.at[t], ur.at[t], "mlp", sib) for t in range(4)
    ]
    out = {
        t: remote(mid.at[t], far.at[t], vs.at[t], vr.at[t], "mlp", dest[t]) for t in (1, 2, 3)
    }

    def code_part(c):
        x = rows_all[:, :, part_columns(width, parts, c)].reshape(tall, depth)
        code_acc[...] += lax.dot_general(
            down_ref[:, part_columns(width, parts, c)], x, (((1,), (1,)), ((), ())),
            preferred_element_type=jnp.float32,
        )

    def product_part(c, fresh):
        loads[c].wait()

        @pl.loop(0, 3)
        def _(i):
            x = rows_all[:, :, part_columns(width, parts, c)].reshape(tall, depth)
            value = jnp.dot(x, w_ref[i, c * depth : (c + 1) * depth], preferred_element_type=jnp.float32)
            acc[i] = value if fresh else acc[i] + value

    code_acc[...] = jnp.zeros_like(code_acc)
    order = gather.order
    brought[0].wait()
    for i in range(max(parts, requests)):
        if i < parts:
            gather.step(i)
        if i < requests:
            choose(i)
    brought[1].wait()
    for copy in pair:
        copy.start()
    for c in order[:2]:
        gather.corner(c)
    for t in (3, 1, 2):
        pair[t].wait_recv()
        mid[t] = chosen[dest[t]] + near[t]
        out[t].start()
    gather.own.wait()
    for c in order[:2]:
        gather.whole(c)
        code_part(c)
        product_part(c, c == order[0])
    for k in range(2, parts, 2):
        for c in order[k : k + 2]:
            gather.corner(c)
        for c in order[k : k + 2]:
            gather.whole(c)
            code_part(c)
            if c != order[-1]:
                product_part(c, False)
    segment = seg_ref[...]
    doubled = 2 * rank
    code = jnp.zeros((doubled, tall), jnp.float32)
    for s in range(slots):
        held = jnp.zeros((1, tall), jnp.float32)
        for r in range(requests):
            held = held + jnp.where(segment == r, pick_ref[r * slots + s : r * slots + s + 1, 0:1], 0.0)
        code = code + held * code_acc[s * doubled : (s + 1) * doubled]
    code_own[...] = code.astype(jnp.bfloat16)
    shared = share(code_own, code_slots, cs, cr, count)
    product_part(order[-1], False)
    pair[0].wait_recv()
    up = chosen[me].astype(jnp.float32) + near[0].astype(jnp.float32)
    for t in (1, 2, 3):
        out[t].wait_recv()
        up = up + far[t].astype(jnp.float32)
    up = up.astype(jnp.bfloat16)
    code = code_own[...].astype(jnp.float32)
    for k, copy in enumerate(shared):
        copy.wait_recv()
        code = code + code_slots[k + 1].astype(jnp.float32)

    def adapted(j):
        spread = jnp.concatenate(
            [jnp.where(segment == r, code[j * rank : (j + 1) * rank], 0.0) for r in range(requests)], axis=0
        )
        return jnp.dot(jnp.transpose(spread).astype(jnp.bfloat16), up[j], preferred_element_type=jnp.float32)

    query = acc[0] + adapted(0)
    key = acc[1]
    sq_own[0] = column_to_rows(jnp.sum(query * query, axis=1, keepdims=True))
    sq_own[1] = column_to_rows(jnp.sum(key * key, axis=1, keepdims=True))
    squares = share(sq_own, sq_slots, qs, qr, count)
    lin_ref[0] = query
    lin_ref[1] = key
    value_ref[...] = (acc[2] + adapted(1)).astype(jnp.bfloat16)
    total = sq_own[...]
    for k, copy in enumerate(squares):
        copy.wait_recv()
        total = total + sq_slots[k + 1]
    scale = lax.rsqrt(total / (heads * count) + EPSILON)
    for i in range(2):
        scale_ref[i] = row_to_column(scale[i, 0:1])
    gather.drain()
    hop.landed()
    hop.sent()
    for copy in shared + squares + pair + list(out.values()):
        copy.wait_send()


def enter(tokens, modulation, owner, segment, pick, down, maps, weights, up_maps, wide, count, lines):
    rows, width = tokens.shape
    parts = 4
    heads = weights.shape[2]
    tall = rows * count
    slots, two, rank, _ = maps.shape
    requests = modulation.shape[1]
    dma = pltpu.SemaphoreType.DMA
    vm = lambda *extent: pltpu.VMEM(extent, jnp.bfloat16)
    vf = lambda *extent: pltpu.VMEM(extent, jnp.float32)
    up = (two, requests * rank, heads)
    scratch = (
        [vm(*down.shape), vm(*maps.shape), dma((2,))]
        + [vm(rows, width), vm(count, rows, width), vm(3, width, heads), dma((parts,)), vf(3, tall, heads)]
        + [vf(slots * two * rank, tall), vm(two * rank, tall), vm(count, two * rank, tall), dma((count,)), dma((count,))]
        + [vm(count, *up), vm(4, *up), vm(4, *up), vm(4, *up)]
        + [dma((4,))] * 4
        + [vf(2, 8, tall), vf(count, 2, 8, tall), dma((count,)), dma((count,)), dma((2,)), dma((2,))]
        + quad_sems(parts)
    )
    return comm_call(
        functools.partial(enter_kernel, count, lines, parts),
        (
            jax.ShapeDtypeStruct((2, tall, heads), jnp.float32),
            jax.ShapeDtypeStruct((tall, heads), jnp.bfloat16),
            jax.ShapeDtypeStruct((2, tall, 128), jnp.float32),
            pltpu.HBM((2, up_maps.shape[0], wide), jnp.bfloat16),
        ),
        [VM] * 5 + [HBM] * 4,
        (VM, VM, VM, HBM),
        scratch,
        0,
        48,
    )(tokens, modulation, owner, segment, pick, *in_hbm(down, maps, weights, up_maps))


class QuadSum:
    def __init__(self, parts, part_ref, near, mid, first_in, second_in, ns, nr, xs, xr, fs, fr):
        self.parts, self.part_ref, self.near, self.mid = parts, part_ref, near, mid
        self.first_in, self.second_in = first_in, second_in
        self.sems = (ns, nr, xs, xr, fs, fr)
        self.me, self.sib, self.xn, self.yn, dg = quad()
        self.dest = [self.me, self.xn, self.yn, dg]
        self.flip = 1 - 2 * lax.rem(self.me, PAIR)
        self.half = parts // 2
        self.order = [c for two in zip(range(self.half), range(self.half, parts)) for c in two]
        self.pairs, self.ones, self.twos = {}, {}, {}

    def columns(self, c):
        return part_columns(self.part_ref.shape[2], self.parts, c)

    def ways(self, c):
        return (1, 2) if c < self.half else (2, 1)

    def offer(self, c):
        ns, nr = self.sems[:2]
        columns = self.columns(c)
        for t in (3, 1, 2, 0):
            self.pairs[t, c] = remote(
                self.part_ref.at[self.dest[t] + self.flip, :, columns],
                self.near.at[t, :, columns],
                ns.at[t, c],
                nr.at[t, c],
                "mlp",
                self.sib,
            )
            self.pairs[t, c].start()

    def both(self, t, columns):
        return self.part_ref[self.dest[t], :, columns].astype(jnp.float32) + self.near[
            t, :, columns
        ].astype(jnp.float32)

    def first(self, c):
        xs, xr = self.sems[2:4]
        columns = self.columns(c)
        far, _ = self.ways(c)
        for t, slot in ((3, 1), (far, 0)):
            self.pairs[t, c].wait_recv()
            self.mid[t, :, columns] = self.both(t, columns).astype(jnp.bfloat16)
            self.ones[t, c] = remote(
                self.mid.at[t, :, columns],
                self.first_in.at[slot, :, columns],
                xs.at[slot, c],
                xr.at[slot, c],
                "mlp",
                self.dest[far],
            )
            self.ones[t, c].start()

    def second(self, c):
        fs, fr = self.sems[4:6]
        columns = self.columns(c)
        _, keep = self.ways(c)
        self.pairs[keep, c].wait_recv()
        self.ones[3, c].wait_recv()
        self.mid[keep, :, columns] = (
            self.both(keep, columns) + self.first_in[1, :, columns].astype(jnp.float32)
        ).astype(jnp.bfloat16)
        self.twos[c] = remote(
            self.mid.at[keep, :, columns], self.second_in.at[:, columns], fs.at[c], fr.at[c], "mlp", self.dest[keep]
        )
        self.twos[c].start()

    def total(self, c):
        columns = self.columns(c)
        far, _ = self.ways(c)
        self.pairs[0, c].wait_recv()
        self.ones[far, c].wait_recv()
        self.twos[c].wait_recv()
        return (
            self.both(0, columns)
            + self.first_in[0, :, columns].astype(jnp.float32)
            + self.second_in[:, columns].astype(jnp.float32)
        )

    def run(self, produce, consume, ready):
        order = self.order
        produce(order[0])
        ready()
        self.offer(order[0])
        for i in range(1, self.parts):
            produce(order[i])
            self.offer(order[i])
            self.first(order[i - 1])
        self.first(order[-1])
        for c in order:
            self.second(c)
        for c in order:
            consume(c, self.total(c))

    def drain(self):
        for group in (self.pairs, self.ones, self.twos):
            for copy in group.values():
                copy.wait_send()


def quad_sum_scratch(parts, count, rows, width):
    dma = pltpu.SemaphoreType.DMA
    vm = lambda *extent: pltpu.VMEM(extent, jnp.bfloat16)
    return (
        [vm(count, rows, width), vm(4, rows, width), vm(4, rows, width), vm(2, rows, width), vm(rows, width)]
        + [dma((4, parts))] * 2
        + [dma((2, parts))] * 2
        + [dma((parts,))] * 2
    )


def part_product(x_ref, w_ref, part_ref, parts, loads):
    count, rows, width = part_ref.shape

    def produce(c):
        columns = part_columns(width, parts, c)
        loads[c].wait()
        part_ref[:, :, columns] = (
            jnp.dot(x_ref[...], w_ref[:, columns], preferred_element_type=jnp.float32)
            .astype(jnp.bfloat16)
            .reshape(count, rows, width // parts)
        )

    return produce


def cross_in_kernel(count, lines, parts, att_ref, base_ref, mod_ref, owner_ref, gain_ref, head_gain_ref, o_hbm, q_hbm, held_hbm,
                    res_ref, query_ref, hop_ref,
                    o_ref, o_sem, q_ref, q_sem, sums, norm, rows_all, acc, sq_own, sq_slots, qs, qr, hs, hr, *sems):
    sum_sems, gather_sems_ = sems[:11], sems[11:]
    me = lax.axis_index("mlp")
    rows, width = base_ref.shape
    depth = width // parts
    tall = rows * count
    heads = acc.shape[1]
    adder = QuadSum(parts, *sum_sems)
    loads_o, loads_q = {}, {}
    for c in adder.order:
        columns = part_columns(width, parts, c)
        loads_o[c] = pltpu.make_async_copy(o_hbm.at[0, :, columns], o_ref.at[:, columns], o_sem.at[c])
        loads_o[c].start()
    hop = LineHop(2, lines, held_hbm.at[0], held_hbm.at[1], lambda side, _: hop_ref.at[side], hs, hr)
    friends = [("mlp", shift(me, k, count)) for k in range(1, count)] + line_peers(lines)
    hello(friends)

    def ready():
        heard(friends)
        hop.start()

    for c in adder.order:
        block = pl.ds(c * depth, depth)
        loads_q[c] = pltpu.make_async_copy(q_hbm.at[3, block], q_ref.at[block], q_sem.at[c])
        loads_q[c].start()
    gate = pick_rows(mod_ref, 2, owner_ref[...])

    def consume(c, total):
        columns = part_columns(width, parts, c)
        res = (base_ref[:, columns].astype(jnp.float32) + gate[:, columns] * total).astype(jnp.bfloat16)
        res_ref[:, columns] = res
        sums[:, columns] = res.astype(jnp.float32)

    adder.run(part_product(att_ref, o_ref, sum_sems[0], parts, loads_o), consume, ready)
    norm[...] = (layer_norm(sums[...]) * gain_ref[...]).astype(jnp.bfloat16)
    gather = QuadGather(parts, norm, rows_all, *gather_sems_)
    gather.start()
    order = gather.order

    def product_part(c):
        x = rows_all[:, :, part_columns(width, parts, c)].reshape(tall, depth)
        loads_q[c].wait()
        value = jnp.dot(x, q_ref[c * depth : (c + 1) * depth], preferred_element_type=jnp.float32)
        acc[...] = value if c == order[0] else acc[...] + value

    for i in range(parts):
        gather.step(i)
    gather.own.wait()
    for k in range(0, parts, 2):
        for c in order[k : k + 2]:
            gather.corner(c)
        for c in order[k : k + 2]:
            gather.whole(c)
            product_part(c)
    query = acc[...]
    sq_own[...] = column_to_rows(jnp.sum(query * query, axis=1, keepdims=True))
    squares = share(sq_own, sq_slots, qs, qr, count)
    total = sq_own[...]
    for k, copy in enumerate(squares):
        copy.wait_recv()
        total = total + sq_slots[k + 1]
    scale = row_to_column(lax.rsqrt(total / (heads * count) + EPSILON)[0:1])[:, 0:1]
    query_ref[...] = (acc[...] * scale * head_gain_ref[2:3]).astype(jnp.bfloat16)
    adder.drain()
    gather.drain()
    hop.landed()
    hop.sent()
    for copy in squares:
        copy.wait_send()


def cross_in(attended, base, modulation, owner, gain, head_gain, out_maps, in_maps, held, count, lines):
    rows, width = base.shape
    parts = 4
    tall, heads = attended.shape
    dma = pltpu.SemaphoreType.DMA
    vm = lambda *extent: pltpu.VMEM(extent, jnp.bfloat16)
    vf = lambda *extent: pltpu.VMEM(extent, jnp.float32)
    scratch = (
        [vm(heads, width), dma((parts,)), vm(width, heads), dma((parts,))]
        + [vf(rows, width), vm(rows, width), vm(count, rows, width), vf(tall, heads)]
        + [vf(8, tall), vf(count, 8, tall), dma((count,)), dma((count,)), dma((2,)), dma((2,))]
        + quad_sum_scratch(parts, count, rows, width)
        + quad_sems(parts)
    )
    return comm_call(
        functools.partial(cross_in_kernel, count, lines, parts),
        (
            jax.ShapeDtypeStruct((rows, width), jnp.bfloat16),
            jax.ShapeDtypeStruct((tall, heads), jnp.bfloat16),
            pltpu.HBM(held.shape, held.dtype),
        ),
        [VM] * 6 + [HBM] * 3,
        (VM, VM, HBM),
        scratch,
        3,
        48,
    )(attended, base, modulation, owner, gain, head_gain, *in_hbm(out_maps, in_maps, held))


def self_kernel(page_ref, q_ref, k_ref, v_ref, qs_ref, ks_ref, gain_ref, cos_ref, sin_ref, seg_ref, segs_ref, out_ref, kv_ref):
    cosine, sine = cos_ref[...], sin_ref[...]
    allowed = seg_ref[...] == segs_ref[...]

    def turned(ref, scale, gain, columns):
        rows = ref[:, columns] * scale * gain_ref[gain : gain + 1, columns]
        return (rows * cosine + pltpu.roll(rows, HD // 2, 1) * sine).astype(jnp.bfloat16)

    for head in range(q_ref.shape[1] // HD):
        columns = slice(head * HD, (head + 1) * HD)
        query = turned(q_ref, qs_ref[...], 0, columns)
        key = turned(k_ref, ks_ref[...], 1, columns)
        value = v_ref[:, columns]
        out_ref[:, columns] = attend(query, key, value, allowed)
        for block in range(kv_ref.shape[1]):
            page = page_ref[block]
            rows = slice(block * PAGE, (block + 1) * PAGE)
            kv_ref[0, page, :, columns] = key[rows]
            kv_ref[1, page, :, columns] = value[rows]


def joint_kernel(page_ref, lin_ref, v_ref, scale_ref, gain_ref, cos_ref, sin_ref, seg_ref, segs_ref, out_ref, kv_ref):
    self_kernel(
        page_ref, lin_ref.at[0], lin_ref.at[1], v_ref, scale_ref.at[0, :, 0:1], scale_ref.at[1, :, 0:1],
        gain_ref, cos_ref, sin_ref, seg_ref, segs_ref, out_ref, kv_ref,
    )


def joint_attention(pages, linear, value, scales, gains, cosine, sine, segment):
    _, rows, width = linear.shape
    return pl.pallas_call(
        joint_kernel,
        out_shape=(
            jax.ShapeDtypeStruct((rows, width), jnp.bfloat16),
            jax.ShapeDtypeStruct((2, pages.shape[0], PAGE, width), jnp.bfloat16),
        ),
        in_specs=[pl.BlockSpec(memory_space=pltpu.SMEM)] + [VM] * 8,
        out_specs=(VM, VM),
        compiler_params=pltpu.CompilerParams(vmem_limit_bytes=16 << 20),
    )(pages, linear, value, scales, gains, cosine, sine, segment[:, None], segment[None, :])


def self_attention(pages, query, key, value, query_scale, key_scale, gains, cosine, sine, segment):
    rows, width = query.shape
    return pl.pallas_call(
        self_kernel,
        out_shape=(
            jax.ShapeDtypeStruct((rows, width), jnp.bfloat16),
            jax.ShapeDtypeStruct((2, pages.shape[0], PAGE, width), jnp.bfloat16),
        ),
        in_specs=[pl.BlockSpec(memory_space=pltpu.SMEM)] + [VM] * 10,
        out_specs=(VM, VM),
        compiler_params=pltpu.CompilerParams(vmem_limit_bytes=16 << 20),
    )(
        pages,
        query,
        key,
        value,
        query_scale[:, None],
        key_scale[:, None],
        gains,
        cosine,
        sine,
        segment[:, None],
        segment[None, :],
    )


def cross_kernel(q_ref, k_ref, v_ref, seg_ref, owner_ref, out_ref):
    out_ref[...] = attend(q_ref[...], k_ref[0], v_ref[0], seg_ref[...] == owner_ref[...])


def cross_attention(query, cache, segment, owner):
    rows, width = query.shape
    texts = cache.shape[1]
    head = pl.BlockSpec((rows, HD), lambda h: (0, h))
    return pl.pallas_call(
        cross_kernel,
        out_shape=jax.ShapeDtypeStruct((rows, width), jnp.bfloat16),
        grid=(width // HD,),
        in_specs=[
            head,
            pl.BlockSpec((1, texts, HD), lambda h: (0, 0, h)),
            pl.BlockSpec((1, texts, HD), lambda h: (1, 0, h)),
            pl.BlockSpec((rows, 1), lambda h: (0, 0)),
            pl.BlockSpec((1, texts), lambda h: (0, 0)),
        ],
        out_specs=head,
        compiler_params=pltpu.CompilerParams(vmem_limit_bytes=24 << 20),
    )(query, cache, cache, segment[:, None], owner[None, :])


def product_kernel(act, x_ref, w_ref, out_ref):
    out_ref[0] = act(
        jnp.dot(x_ref[...], w_ref[0], preferred_element_type=jnp.float32)
    ).astype(out_ref.dtype)


def product(rows_in, maps, first, amount, tile, dtype, act=lambda part: part):
    rows, depth = rows_in.shape
    width = maps.shape[2]
    tile = min(tile, width)
    return pl.pallas_call(
        functools.partial(product_kernel, act),
        out_shape=jax.ShapeDtypeStruct((amount, rows, width), dtype),
        grid=(amount, width // tile),
        in_specs=[
            pl.BlockSpec((rows, depth), lambda i, j: (0, 0)),
            pl.BlockSpec((1, depth, tile), lambda i, j: (first + i, 0, j)),
        ],
        out_specs=pl.BlockSpec((1, rows, tile), lambda i, j: (i, 0, j)),
        compiler_params=pltpu.CompilerParams(vmem_limit_bytes=24 << 20),
    )(rows_in, pltpu.with_memory_space_constraint(maps, pltpu.HBM))


def choose_rows(table, segment):
    chosen = jnp.zeros((segment.shape[0],) + table.shape[1:], table.dtype)
    for request in range(table.shape[0]):
        picked = (segment == request).reshape((-1,) + (1,) * (table.ndim - 1))
        chosen = jnp.where(picked, table[request][None], chosen)
    return chosen


def body(
    tokens,
    modulation,
    lengths,
    request_adapter,
    adapter_storage,
    adapter_down_weight,
    adapter_up_maps,
    input_projection,
    query_key_gains,
    positions,
    block_page_lookup,
    output_projection,
    cross_norm_gain,
    text_token_cache,
    feedforward_up,
    feedforward_down,
):
    mlp_count = lax.axis_size("mlp")
    my_index = lax.axis_index("mlp")
    own_count = tokens.shape[0]
    group_rows = own_count * mlp_count
    local_width = input_projection.shape[2]
    entire_width = local_width * mlp_count
    resident_slots = adapter_down_weight.shape[0]
    doubled_rank = adapter_down_weight.shape[2]
    rank_once = doubled_rank // 2

    req_count = lax.axis_size("req")
    slot_total = resident_slots * mlp_count
    tuned = mlp_count == 8 and req_count == 4
    counts = lengths[0]
    index = jnp.arange(counts.shape[0], dtype=jnp.int32)
    bounds = jnp.sum(jnp.where(index[:, None] >= index[None, :], counts[None, :], 0), axis=1)
    position = jnp.arange(group_rows, dtype=jnp.int32)
    segment = jnp.sum((position[:, None] >= bounds[None, :]).astype(jnp.int32), axis=1)
    own_start = my_index * own_count
    own_segment = lax.dynamic_slice_in_dim(segment, own_start, own_count)
    if tuned:
        by_kind = modulation.transpose(1, 0, 2)
        storage = jnp.arange(adapter_storage.shape[0], dtype=jnp.int32)
        request_slot = jnp.sum(
            jnp.where(request_adapter[:, None] == storage[None, :], adapter_storage[None, :], 0), axis=1
        )
        resident = my_index * resident_slots + jnp.arange(resident_slots, dtype=jnp.int32)
        pick = (request_slot[:, None] == resident[None, :]).astype(jnp.float32).reshape(-1, 1)
        linear, value_rows, scales, hop_one = enter(
            tokens,
            by_kind,
            own_segment[:, None],
            segment[None, :],
            jnp.broadcast_to(pick, (pick.shape[0], 128)),
            adapter_down_weight.transpose(0, 2, 1).reshape(resident_slots * doubled_rank, -1),
            adapter_up_maps,
            input_projection,
            feedforward_up,
            feedforward_up.shape[1] * 3 // 8,
            mlp_count,
            req_count,
        )
        cosine, sine = rotary_tables(positions)
        attended, kv_pages = joint_attention(
            block_page_lookup[0], linear, value_rows, scales, query_key_gains, cosine, sine, segment
        )
    else:
        per_token = [choose_rows(modulation[:, which_row, :], own_segment) for which_row in range(6)]
        token_f32 = tokens.astype(jnp.float32)
        rows_in, adapter_up_weight = entry_rows(
            tokens, per_token[1], per_token[0], adapter_up_maps, mlp_count
        )
        request_slot = adapter_storage[request_adapter]
        token_slot = jnp.sum(
            jnp.where(
                segment[:, None] == jnp.arange(request_slot.shape[0], dtype=jnp.int32)[None, :],
                request_slot[None, :],
                0,
            ),
            axis=1,
        )
        resident = my_index * resident_slots + jnp.arange(resident_slots, dtype=jnp.int32)
        held = (token_slot[None, :] == resident[:, None]).astype(jnp.float32)
        code_block = lax.dot_general(
            adapter_down_weight.transpose(0, 2, 1).reshape(resident_slots * doubled_rank, -1),
            rows_in,
            (((1,), (1,)), ((), ())),
            preferred_element_type=jnp.float32,
        ).reshape(resident_slots, doubled_rank, group_rows)
        my_codes = jnp.sum(held[:, None, :] * code_block, axis=0).astype(jnp.bfloat16)
        codes = small_sum(my_codes, mlp_count, 1).astype(jnp.bfloat16)
        slots = jnp.arange(slot_total, dtype=jnp.int32)
        everywhere = token_slot[None, :] == slots[:, None]

        def spread(code_part):
            return jnp.where(everywhere[:, None, :], code_part[None], jnp.bfloat16(0)).reshape(
                slot_total * rank_once, group_rows
            )

        def adapted(code_part, which_map):
            return lax.dot_general(
                spread(code_part),
                adapter_up_weight[:, which_map].reshape(slot_total * rank_once, local_width),
                (((0,), (0,)), ((), ())),
                preferred_element_type=jnp.float32,
            )

        projected = product(rows_in, input_projection, 0, 3, 256, jnp.float32)
        query_linear = projected[0] + adapted(codes[:rank_once], 0)
        key_linear = projected[1]
        value_rows = (projected[2] + adapted(codes[rank_once:], 1)).astype(jnp.bfloat16)
        squares = small_sum(
            jnp.stack(
                [jnp.sum(query_linear * query_linear, axis=1), jnp.sum(key_linear * key_linear, axis=1)]
            ),
            mlp_count,
            2,
        )
        query_square, key_square = squares[0], squares[1]
        query_scale = lax.rsqrt(query_square / entire_width + EPSILON)
        key_scale = lax.rsqrt(key_square / entire_width + EPSILON)
        cosine, sine = rotary_tables(positions)
        attended, kv_pages = self_attention(
            block_page_lookup[0],
            query_linear,
            key_linear,
            value_rows,
            query_scale,
            key_scale,
            query_key_gains,
            cosine,
            sine,
            segment,
        )
    text_owner = (
        jnp.arange(text_token_cache.shape[1] * text_token_cache.shape[2], dtype=jnp.int32)
        // text_token_cache.shape[2]
    )

    def out_rows(rows, which_map):
        return product(rows, output_projection, which_map, 1, 1280, jnp.bfloat16)[0]

    if tuned:
        first_res, cross_query, hop_two = cross_in(
            attended,
            tokens,
            by_kind,
            own_segment[:, None],
            cross_norm_gain[None, :],
            query_key_gains,
            output_projection,
            input_projection,
            hop_one,
            mlp_count,
            req_count,
        )
    else:
        first_res, cross_rows = middle_rows(
            out_rows(attended, 0),
            tokens,
            per_token[2],
            cross_norm_gain[None, :],
            jnp.zeros((1, tokens.shape[1]), jnp.float32),
            mlp_count,
            3,
        )
        cross_linear = product(cross_rows, input_projection, 3, 1, 256, jnp.float32)[0]
        cross_square = small_sum(
            jnp.sum(cross_linear * cross_linear, axis=1)[None, :], mlp_count, 4
        )[0]
        cross_query = (
            cross_linear
            * lax.rsqrt(cross_square / entire_width + EPSILON)[:, None]
            * query_key_gains[2]
        ).astype(jnp.bfloat16)
    if tuned:
        second_res, delta = feed_forward(
            cross_query,
            segment[:, None],
            first_res,
            by_kind,
            own_segment[:, None],
            text_token_cache,
            output_projection,
            hop_one,
            hop_two,
            feedforward_up,
            feedforward_down,
            mlp_count,
            req_count,
            5,
        )
        layer_out = (second_res.astype(jnp.float32) + delta).astype(jnp.bfloat16)
        return (layer_out, kv_pages)
    cross_out = cross_attention(
        cross_query,
        text_token_cache.reshape(2, text_owner.shape[0], local_width),
        segment,
        text_owner,
    )
    up_full = lax.all_gather(feedforward_up, "req", axis=0, tiled=True)
    second_res, mlp_in = middle_rows(
        out_rows(cross_out, 1),
        first_res,
        jnp.ones((1, tokens.shape[1]), jnp.float32),
        1.0 + per_token[4],
        per_token[3],
        mlp_count,
        5,
    )
    hidden = product(
        mlp_in,
        up_full[None],
        0,
        1,
        256,
        jnp.bfloat16,
        functools.partial(jax.nn.gelu, approximate=True),
    )[0]
    hidden_all = line_gather(hidden, req_count, 6)
    units, columns = feedforward_down.shape
    down_part = jnp.dot(
        hidden_all.reshape(req_count * group_rows, units),
        feedforward_down,
        preferred_element_type=jnp.float32,
    ).astype(jnp.bfloat16)
    down_own = exit_rows(
        down_part.reshape(req_count, mlp_count, own_count, columns), mlp_count, req_count, 7
    )
    layer_out = (
        second_res.astype(jnp.float32) + per_token[5] * down_own.astype(jnp.float32)
    ).astype(jnp.bfloat16)
    return (layer_out, kv_pages)


def solution(mesh):
    return jax.shard_map(
        body,
        mesh=mesh,
        in_specs=(
            P(("req", "mlp"), None),
            P("req", None, None),
            P("req", None),
            P("req"),
            P(),
            P("mlp", None, None),
            P("mlp", None, None, None),
            P(None, None, "mlp"),
            P(None, "mlp"),
            P(None, "req"),
            P("req", None),
            P(None, "mlp", None),
            P(),
            P(None, "req", None, "mlp"),
            P("req", "mlp"),
            P("mlp", "req"),
        ),
        out_specs=(P(("req", "mlp"), None), P(None, "req", None, "mlp")),
        check_vma=False,
    )
```

```python
import functools
import math

import jax
import jax.numpy as jnp
from jax import lax
from jax.experimental import pallas as pl
from jax.experimental.pallas import tpu as pltpu
from jax.sharding import PartitionSpec as P

HD = 128
PAGE = 16


EPSILON = 1e-06


PAIR = 2
MESH = pl.DeviceIdType.MESH
ANY = pl.BlockSpec(memory_space=pl.ANY)
VM = pl.BlockSpec(memory_space=pltpu.VMEM)
HBM = pl.BlockSpec(memory_space=pltpu.HBM)


def comm_call(kernel, out_shape, in_specs, out_specs, scratch, ident, room=4):
    return pl.pallas_call(
        kernel,
        out_shape=out_shape,
        in_specs=in_specs,
        out_specs=out_specs,
        scratch_shapes=scratch,
        compiler_params=pltpu.CompilerParams(
            collective_id=ident, has_side_effects=True, vmem_limit_bytes=room << 20
        ),
    )


def remote(source, target, send_sem, recv_sem, axis, place):
    return pltpu.make_async_remote_copy(
        src_ref=source,
        dst_ref=target,
        send_sem=send_sem,
        recv_sem=recv_sem,
        device_id={axis: place},
        device_id_type=MESH,
    )


def shift(me, step, count):
    return lax.rem(me + (step + count) % count, count)


def greet(peers):
    barrier = pltpu.get_barrier_semaphore()
    for axis, place in peers:
        pl.semaphore_signal(barrier, inc=1, device_id={axis: place}, device_id_type=MESH)
    pl.semaphore_wait(barrier, len(peers))


def hello(peers):
    barrier = pltpu.get_barrier_semaphore()
    for axis, place in peers:
        pl.semaphore_signal(barrier, inc=1, device_id={axis: place}, device_id_type=MESH)


def heard(peers):
    pl.semaphore_wait(pltpu.get_barrier_semaphore(), len(peers))


def in_hbm(*arrays):
    return [pltpu.with_memory_space_constraint(array, pltpu.HBM) for array in arrays]


def pair_places(count):
    me = lax.axis_index("mlp")
    outer, core = lax.div(me, PAIR), lax.rem(me, PAIR)
    sibling = outer * PAIR + (PAIR - 1 - core)
    peers = [
        shift(outer, k, count // PAIR) * PAIR + core for k in range(count // PAIR)
    ]
    sources = [
        shift(outer, -k, count // PAIR) * PAIR + core for k in range(count // PAIR)
    ]
    return me, core, sibling, peers, sources


def gather_sems(count):
    steps = count // PAIR
    return [pltpu.SemaphoreType.DMA(())] + [pltpu.SemaphoreType.DMA((steps,))] * 4


def gather_rows(count, places, own_ref, out_ref, own_sem, send_sem, recv_sem, pass_send, pass_recv):
    me, core, sibling, peers, sources = places
    own = pltpu.make_async_copy(own_ref, out_ref.at[me], own_sem)
    sends = [
        remote(own_ref, out_ref.at[me], send_sem.at[k], recv_sem.at[k], "mlp", peers[k])
        for k in range(1, count // PAIR)
    ]
    for copy in sends:
        copy.start()
    passes = [remote(own_ref, out_ref.at[me], pass_send.at[0], pass_recv.at[0], "mlp", sibling)]
    passes[0].start()
    own.start()
    for k in range(1, count // PAIR):
        sends[k - 1].wait_recv()
        block = out_ref.at[sources[k]]
        passes.append(remote(block, block, pass_send.at[k], pass_recv.at[k], "mlp", sibling))
        passes[-1].start()
    for copy in sends:
        copy.wait_send()
    for copy in passes:
        copy.wait()
    own.wait()


def entry_kernel(count, tok_ref, scale_ref, shift_ref, maps_ref, out_ref, up_ref, norm, map_own, map_send, map_recv, *sems):
    places = pair_places(count)
    me = places[0]
    slots, width = maps_ref.shape[0], up_ref.shape[-1]
    others = [shift(me, k, count) for k in range(1, count)]
    greet([("mlp", place) for place in others])

    def columns(place):
        return maps_ref.at[:, :, :, pl.ds(pl.multiple_of(place * width, 128), width)]

    target = up_ref.at[pl.ds(me * slots, slots)]
    own = pltpu.make_async_copy(columns(me), target, map_own)
    own.start()
    copies = [
        remote(columns(place), target, map_send.at[k], map_recv.at[k], "mlp", place)
        for k, place in enumerate(others)
    ]
    norm[...] = (
        layer_norm(tok_ref[...].astype(jnp.float32)) * (1.0 + scale_ref[...]) + shift_ref[...]
    ).astype(jnp.bfloat16)
    for copy in copies:
        copy.start()
    gather_rows(count, places, norm, out_ref, *sems)
    for copy in copies:
        copy.wait()
    own.wait()


def entry_rows(tokens, scale, shift_rows, maps, count):
    rows, width = tokens.shape
    slots, two, rank, total = maps.shape
    dma = pltpu.SemaphoreType.DMA
    gathered, up = comm_call(
        functools.partial(entry_kernel, count),
        (
            jax.ShapeDtypeStruct((count, rows, width), jnp.bfloat16),
            jax.ShapeDtypeStruct((count * slots, two, rank, total // count), maps.dtype),
        ),
        [VM, VM, VM, ANY],
        (ANY, ANY),
        [pltpu.VMEM((rows, width), jnp.bfloat16), dma(()), dma((count - 1,)), dma((count - 1,))]
        + gather_sems(count),
        0,
        8,
    )(tokens, scale, shift_rows, maps)
    return gathered.reshape(count * rows, width), up


def sum_blocks(count, places, block_of, near, mid, far, ns, nr, fs, fr):
    me, core, sibling, peers, sources = places
    steps = count // PAIR
    order = list(range(1, steps)) + [0]
    pairs = {}
    for k in order:
        other = peers[k] + (PAIR - 1 - 2 * core)
        pairs[k] = remote(block_of(other), near.at[k], ns.at[k], nr.at[k], "mlp", sibling)
        pairs[k].start()
    sends = []
    for k in range(1, steps):
        pairs[k].wait_recv()
        mid[k] = (
            block_of(peers[k])[...].astype(jnp.float32) + near[k].astype(jnp.float32)
        ).astype(jnp.bfloat16)
        sends.append(remote(mid.at[k], far.at[k], fs.at[k], fr.at[k], "mlp", peers[k]))
        sends[-1].start()
    pairs[0].wait_recv()
    total = block_of(me)[...].astype(jnp.float32) + near[0].astype(jnp.float32)
    for k in range(1, steps):
        sends[k - 1].wait_recv()
        total = total + far[k].astype(jnp.float32)
    for k in order:
        pairs[k].wait_send()
    for copy in sends:
        copy.wait_send()
    return total


def sum_scratch(count, extent):
    steps = count // PAIR
    return [pltpu.VMEM((steps,) + extent, jnp.bfloat16)] * 3 + [
        pltpu.SemaphoreType.DMA((steps,))
    ] * 4


def middle_kernel(count, part_ref, base_ref, gate_ref, scale_ref, shift_ref, res_ref, out_ref, near, mid, far, norm, ns, nr, fs, fr, *sems):
    places = pair_places(count)
    greet([("mlp", places[2])] + [("mlp", place) for place in places[3][1:]])
    total = sum_blocks(
        count, places, lambda place: part_ref.at[place], near, mid, far, ns, nr, fs, fr
    )
    res = (base_ref[...].astype(jnp.float32) + gate_ref[...] * total).astype(jnp.bfloat16)
    res_ref[...] = res
    norm[...] = (layer_norm(res.astype(jnp.float32)) * scale_ref[...] + shift_ref[...]).astype(
        jnp.bfloat16
    )
    gather_rows(count, places, norm, out_ref, *sems)


def middle_rows(part, base, gate, scale, shift_rows, count, ident):
    rows, width = base.shape
    scratch = sum_scratch(count, (rows, width))
    res, gathered = comm_call(
        functools.partial(middle_kernel, count),
        (
            jax.ShapeDtypeStruct((rows, width), jnp.bfloat16),
            jax.ShapeDtypeStruct((count, rows, width), jnp.bfloat16),
        ),
        [VM] * 5,
        (VM, ANY),
        scratch[:3] + [pltpu.VMEM((rows, width), jnp.bfloat16)] + scratch[3:] + gather_sems(count),
        ident,
        24,
    )(part.reshape(count, rows, width), base, gate, scale, shift_rows)
    return res, gathered.reshape(count * rows, width)


def small_kernel(count, own_ref, out_ref, slots, send_sem, recv_sem):
    me = lax.axis_index("mlp")
    others = [shift(me, k, count) for k in range(1, count)]
    greet([("mlp", place) for place in others])
    copies = [
        remote(own_ref, slots.at[k], send_sem.at[k], recv_sem.at[k], "mlp", place)
        for k, place in enumerate(others)
    ]
    for copy in copies:
        copy.start()
    total = own_ref[...].astype(jnp.float32)
    for k, copy in enumerate(copies):
        copy.wait_recv()
        total = total + slots[k].astype(jnp.float32)
    out_ref[...] = total
    for copy in copies:
        copy.wait_send()


def small_sum(own, count, ident):
    dma = pltpu.SemaphoreType.DMA((count - 1,))
    return comm_call(
        functools.partial(small_kernel, count),
        jax.ShapeDtypeStruct(own.shape, jnp.float32),
        [VM],
        VM,
        [pltpu.VMEM((count - 1,) + own.shape, own.dtype), dma, dma],
        ident,
    )(own)


def line_kernel(count, own_ref, out_ref, own_sem, rs, rr, ls, lr):
    me = lax.axis_index("req")
    right, left = shift(me, 1, count), shift(me, -1, count)
    greet([("req", right), ("req", left)])
    own = pltpu.make_async_copy(own_ref, out_ref.at[me], own_sem)
    own.start()

    pieces = rs.shape[1]
    rows = own_ref.shape[0] // pieces

    def hop(step, piece, sign):
        block = jnp.clip(me - sign * step, 0, count - 1)
        part = pl.ds(piece * rows, rows)
        source = own_ref.at[part] if step == 0 else out_ref.at[block, part]
        send, recv, place = (rs, rr, right) if sign > 0 else (ls, lr, left)
        return remote(
            source,
            out_ref.at[block, part],
            send.at[step, piece],
            recv.at[step, piece],
            "req",
            place,
        )

    def each(step, work):
        for piece in range(pieces):
            work(step, piece)

    def advance(step, piece):
        if step > 0:

            @pl.when(me >= step)
            def _():
                hop(step - 1, piece, 1).wait_recv()

            @pl.when(me + step < count)
            def _():
                hop(step - 1, piece, -1).wait_recv()

        @pl.when((me >= step) & (me < count - 1))
        def _():
            hop(step, piece, 1).start()

        @pl.when((me + step < count) & (me > 0))
        def _():
            hop(step, piece, -1).start()

    def finish(step, piece):
        @pl.when(me >= count - 1)
        def _():
            hop(step, piece, 1).wait_recv()

        @pl.when(me < 1)
        def _():
            hop(step, piece, -1).wait_recv()

    def drain(step, piece):
        @pl.when((me >= step) & (me < count - 1))
        def _():
            hop(step, piece, 1).wait_send()

        @pl.when((me + step < count) & (me > 0))
        def _():
            hop(step, piece, -1).wait_send()

    for step in range(count - 1):
        each(step, advance)
    each(count - 2, finish)
    for step in range(count - 1):
        each(step, drain)
    own.wait()


def line_gather(own, count, ident):
    dma = pltpu.SemaphoreType.DMA
    return comm_call(
        functools.partial(line_kernel, count),
        jax.ShapeDtypeStruct((count,) + own.shape, own.dtype),
        [ANY],
        ANY,
        [dma(())] + [dma((count - 1, 4))] * 4,
        ident,
    )(own)


def exit_kernel(count, lines, part_ref, out_ref, near, mid, far, final, ns, nr, fs, fr, own_sem, send_sem, recv_sem):
    places = pair_places(count)
    me, core, sibling, peers, _ = places
    steps = count // PAIR
    line = lax.axis_index("req")
    groups = [shift(line, k + 1, lines) for k in range(lines)]
    greet(
        [("mlp", sibling)]
        + [("mlp", place) for place in peers[1:]]
        + [("req", place) for place in groups[:-1]]
    )
    order = list(range(1, steps)) + [0]
    pairs, sends, copies = {}, [], []
    for i, group in enumerate(groups):
        for k in order:
            other = peers[k] + (PAIR - 1 - 2 * core)
            pairs[i, k] = remote(
                part_ref.at[group, other], near.at[i, k], ns.at[i, k], nr.at[i, k], "mlp", sibling
            )
            pairs[i, k].start()
    for i, group in enumerate(groups):
        for k in range(1, steps):
            pairs[i, k].wait_recv()
            mid[i, k] = (
                part_ref[group, peers[k]].astype(jnp.float32) + near[i, k].astype(jnp.float32)
            ).astype(jnp.bfloat16)
            sends.append(
                remote(mid.at[i, k], far.at[i, k], fs.at[i, k], fr.at[i, k], "mlp", peers[k])
            )
            sends[-1].start()
    width = final.shape[-1]
    target = out_ref.at[:, pl.ds(pl.multiple_of(line * width, 128), width)]
    for i, group in enumerate(groups):
        pairs[i, 0].wait_recv()
        total = part_ref[group, me].astype(jnp.float32) + near[i, 0].astype(jnp.float32)
        for k in range(1, steps):
            sends[i * (steps - 1) + k - 1].wait_recv()
            total = total + far[i, k].astype(jnp.float32)
        final[i] = total.astype(jnp.bfloat16)
        if i < lines - 1:
            copies.append(
                remote(final.at[i], target, send_sem.at[i], recv_sem.at[i], "req", group)
            )
        else:
            copies.append(pltpu.make_async_copy(final.at[i], target, own_sem))
        copies[-1].start()
    for copy in list(pairs.values()) + sends:
        copy.wait_send()
    for copy in copies:
        copy.wait()


def exit_rows(part, count, lines, ident):
    groups, _, rows, width = part.shape
    steps = count // PAIR
    dma = pltpu.SemaphoreType.DMA
    return comm_call(
        functools.partial(exit_kernel, count, lines),
        jax.ShapeDtypeStruct((rows, lines * width), jnp.bfloat16),
        [VM],
        VM,
        [pltpu.VMEM((groups, steps, rows, width), jnp.bfloat16)] * 3
        + [pltpu.VMEM((groups, rows, width), jnp.bfloat16)]
        + [dma((groups, steps))] * 4
        + [dma(()), dma((lines - 1,)), dma((lines - 1,))],
        ident,
        24,
    )(part)


def attend_text(queries, text_ref, columns, segment):
    requests = text_ref.shape[1]
    scores = None
    for r in range(requests):
        some = lax.dot_general(
            queries, text_ref[0, r, :, columns], (((1,), (1,)), ((), ())), preferred_element_type=jnp.float32
        )
        scores = some if r == 0 else jnp.where(segment == r, some, scores)
    weights = jnp.exp(scores * (1.0 / math.sqrt(HD)))
    weights = weights * (1.0 / jnp.sum(weights, axis=-1, keepdims=True))
    total = None
    for r in range(requests):
        mine = jnp.where(segment == r, weights, 0.0).astype(jnp.bfloat16)
        some = jnp.dot(mine, text_ref[1, r, :, columns], preferred_element_type=jnp.float32)
        total = some if r == 0 else total + some
    return total.astype(jnp.bfloat16)


def lines_order(lines):
    middle = lines // 2
    return [middle - 1, middle] + [g for g in range(lines) if g not in (middle - 1, middle)]


def dot_tiles(x, w_ref, out_ref, put, tile):
    width = w_ref.shape[1]

    @pl.loop(0, width // tile)
    def _(i):
        columns = pl.ds(pl.multiple_of(i * tile, tile), tile)
        put(columns, jnp.dot(x, w_ref[:, columns], preferred_element_type=jnp.float32))


def ff_kernel(count, lines, parts, query_ref, seg_ref, base_ref, mod_ref, owner_ref, text_hbm, o_hbm, hop_one, hop_two, up_hbm, down_hbm, res, delta_ref,
              text_ref, text_sem, x_ref, o_ref, o_sem, part, near, mid, first_in, second_in, ns, nr, xs, xr, fs, fr, gate, sums,
              up_ref, down_ref, w_sem, norm, act, a_send, a_recv, g_send, g_recv, p_send, p_recv,
              pbuf, from_outer, from_partner, staged, hid, es, er, ts, tr, ho_s, hp_s, h_r,
              dn, near2, mid2, far2, ns2, nr2, fs2, fr2, final, back, bs, br,
              wide_ref, wide_sem, hs, hr, rows_all, acc, zo_s, zp_s, z_r, *sems):
    places = pair_places(count)
    me, core, sibling, peers, sources = places
    steps = count // PAIR
    line = lax.axis_index("req")
    order = lines_order(lines)
    is_mid = (line == 1) | (line == 2)
    outer = jnp.where(line == 1, 0, 3)
    partner = 3 - line
    inner = jnp.where(line == 0, 1, 2)
    adder = QuadSum(parts, part, near, mid, first_in, second_in, ns, nr, xs, xr, fs, fr)
    heads = query_ref.shape[1] // HD
    texts = {}
    for h in range(heads):
        for i in range(2):
            columns = slice(h * HD, (h + 1) * HD)
            texts[i, h] = pltpu.make_async_copy(
                text_hbm.at[i, :, :, columns], text_ref.at[i, :, :, columns], text_sem.at[i, h]
            )
            texts[i, h].start()
    loads_o = {}
    for c in adder.order:
        columns = part_columns(base_ref.shape[1], parts, c)
        loads_o[c] = pltpu.make_async_copy(o_hbm.at[1, :, columns], o_ref.at[:, columns], o_sem.at[c])
        loads_o[c].start()
    friends = (
        [("mlp", sibling)]
        + [("mlp", place) for place in peers[1:]]
        + [("req", shift(line, k, lines)) for k in range(1, lines)]
    )
    hello(friends)
    wide = wide_ref.shape[1]
    weights = [
        pltpu.make_async_copy(up_hbm.at[:, wide:], up_ref, w_sem.at[0]),
        pltpu.make_async_copy(down_hbm, down_ref, w_sem.at[1]),
    ]
    part_width = up_hbm.shape[0]

    def wide_rows(place):
        return wide_ref.at[pl.ds(pl.multiple_of(place * part_width, 128), part_width)]

    hop = LineHop(
        3, lines, hop_two.at[0], hop_two.at[1],
        lambda side, place: wide_rows(jnp.clip(place, 0, lines - 1)), hs, hr,
    )
    sources_w = [(0, up_hbm.at[:, 0:wide])]
    for distance, held in ((1, hop_one), (2, hop_two)):
        sources_w += [(distance, held.at[0]), (-distance, held.at[1])]
    for q in range(lines):
        for distance, source in sources_w:
            @pl.when(line - q == distance)
            def _():
                pltpu.make_async_copy(source, wide_rows(q), wide_sem.at[q]).start()

    def wide_ready(q):
        if q == 0:
            @pl.when(line == lines - 1)
            def _():
                hop.right.wait_recv()

        if q == lines - 1:
            @pl.when(line == 0)
            def _():
                hop.left.wait_recv()

        @pl.when(jnp.abs(line - q) < lines - 1)
        def _():
            pltpu.make_async_copy(hop_one.at[0], wide_rows(q), wide_sem.at[q]).wait()

    for copy in weights:
        copy.start()
    owner = owner_ref[...]
    gate[...] = pick_rows(mod_ref, 5, owner)

    def consume(c, total):
        columns = part_columns(base_ref.shape[1], parts, c)
        value = (base_ref[:, columns].astype(jnp.float32) + total).astype(jnp.bfloat16)
        res[:, columns] = value
        sums[:, columns] = value.astype(jnp.float32)

    segment = seg_ref[...]
    for h in range(heads):
        columns = slice(h * HD, (h + 1) * HD)
        texts[0, h].wait()
        texts[1, h].wait()
        x_ref[:, columns] = attend_text(query_ref[:, columns], text_ref, columns, segment)

    def ready():
        heard(friends)
        hop.start()

    adder.run(part_product(x_ref, o_ref, part, parts, loads_o), consume, ready)
    norm[...] = (
        layer_norm(sums[...]) * (1.0 + pick_rows(mod_ref, 4, owner)) + pick_rows(mod_ref, 3, owner)
    ).astype(jnp.bfloat16)

    rows, width = norm.shape

    def slice_of(place):
        return pl.ds(pl.multiple_of(place * part_width, 128), part_width)

    def spread_to(k):
        place = lax.rem(line + k, lines)
        return remote(
            norm.at[:, slice_of(place)], act.at[line, me], a_send.at[k], a_recv.at[line], "req", place
        )

    gather = QuadGather(parts, norm, rows_all, *sems)
    gather.start()
    for k in (2, 1, 3):
        spread_to(k).start()

    def across(g, k):
        return remote(act.at[g, me], act.at[g, me], g_send.at[g, k], g_recv.at[g, k], "mlp", peers[k])

    def passed(g, k):
        block = act.at[g, sources[k]]
        return remote(block, block, p_send.at[g, k], p_recv.at[g, k], "mlp", sibling)

    def from_sibling(g, k):
        block = act.at[g, sources[k] + PAIR - 1 - 2 * core]
        return remote(block, block, p_send.at[g, k], p_recv.at[g, k], "mlp", sibling)

    def landed(p):
        g = order[p]

        @pl.when(line != g)
        def _():
            remote(norm.at[:, slice_of(g)], act.at[g, me], a_send.at[0], a_recv.at[g], "req", g).wait_recv()

    def opened(p):
        if p < lines:
            g = order[p]
            landed(p)

            @pl.when(line != g)
            def _():
                for k in range(1, steps):
                    across(g, k).start()
                passed(g, 0).start()

    tall = count * rows
    chunks = from_outer.shape[1]
    some = tall // chunks

    def chunk(j):
        return pl.ds(pl.multiple_of(j * some, some), some)

    def to_inner(g, j):
        return remote(pbuf.at[g, chunk(j)], from_outer.at[g, j], es.at[g, j], er.at[g, j], "req", inner)

    def to_partner(g, j):
        return remote(staged.at[g, j], from_partner.at[g, j], ts.at[g, j], tr.at[g, j], "req", partner)

    def out_to(g, j, place, sem):
        block = hid.at[g, chunk(j), wide:]
        return remote(block, block, sem.at[g, j], h_r.at[g, j], "req", place)

    def gathered(p):
        g = order[p]

        @pl.when(line != g)
        def _():
            for k in range(1, steps):
                remote(act.at[g, me], act.at[g, sources[k]], g_send.at[g, k], g_recv.at[g, k], "mlp", peers[k]).wait_recv()
                passed(g, k).start()

        @pl.when(line != g)
        def _():
            for k in range(steps):
                from_sibling(g, k).wait_recv()

    def first_product(p):
        g = order[p]

        def put(columns, value):
            pbuf[g, :, columns] = value.astype(jnp.bfloat16)

        dot_tiles(act[g].reshape(tall, part_width), up_ref, pbuf, put, 256 if up_ref.shape[1] % 256 == 0 else up_ref.shape[1])

        @pl.when(jnp.logical_not(is_mid))
        def _():
            for j in range(chunks):
                to_inner(g, j).start()

    def theirs(g, i):
        j = 2 * i + 2 - line
        to_inner(g, j).wait_recv()
        staged[g, j] = (
            pbuf[g, chunk(j)].astype(jnp.float32) + from_outer[g, j].astype(jnp.float32)
        ).astype(jnp.bfloat16)
        to_partner(g, j).start()

    def mine(g, i):
        j = 2 * i + line - 1
        to_inner(g, j).wait_recv()
        to_partner(g, j).wait_recv()
        value = (
            pbuf[g, chunk(j)].astype(jnp.float32)
            + from_outer[g, j].astype(jnp.float32)
            + from_partner[g, j].astype(jnp.float32)
        )
        hid[g, chunk(j), wide:] = jax.nn.gelu(value, approximate=True).astype(jnp.bfloat16)
        out_to(g, j, partner, hp_s).start()
        out_to(g, j, outer, ho_s).start()

    def forward(g, i):
        j = 2 * i + 2 - line
        out_to(g, j, partner, hp_s).wait_recv()
        out_to(g, j, outer, ho_s).start()

    def at_middle(work, p):
        @pl.when(is_mid)
        def _():
            for i in range(chunks // 2):
                work(order[p], i)

    def all_hidden(p):
        g = order[p]
        @pl.when(jnp.logical_not(is_mid))
        def _():
            for j in range(chunks):
                out_to(g, j, inner, ho_s).wait_recv()

    def pair_copy(g, k):
        other = peers[k] + (PAIR - 1 - 2 * core)
        return remote(dn.at[g, other], near2.at[g, k], ns2.at[g, k], nr2.at[g, k], "mlp", sibling)

    def far_copy(g, k):
        return remote(mid2.at[g, k], far2.at[g, k], fs2.at[g, k], fr2.at[g, k], "mlp", peers[k])

    k_order = list(range(1, steps)) + [0]

    def second_product(p):
        g = order[p]

        def put(columns, value):
            dn[g, :, :, columns] = value.astype(jnp.bfloat16).reshape(count, rows, 256)

        dot_tiles(hid[g], down_ref, dn, put, 256)
        for k in k_order:
            pair_copy(g, k).start()

    def relay(p):
        g = order[p]
        for k in range(1, steps):
            pair_copy(g, k).wait_recv()
            mid2[g, k] = (
                dn[g, peers[k]].astype(jnp.float32) + near2[g, k].astype(jnp.float32)
            ).astype(jnp.bfloat16)
            far_copy(g, k).start()

    def home(g):
        return remote(final.at[g], back.at[line], bs.at[g], br.at[line], "req", g)

    def finish(p):
        g = order[p]
        pair_copy(g, 0).wait_recv()
        value = dn[g, me].astype(jnp.float32) + near2[g, 0].astype(jnp.float32)
        for k in range(1, steps):
            far_copy(g, k).wait_recv()
            value = value + far2[g, k].astype(jnp.float32)
        final[g] = value.astype(jnp.bfloat16)

        @pl.when(line == g)
        def _():
            back[g] = final[g]

        @pl.when(line != g)
        def _():
            home(g).start()

    def along(g, place, sem):
        block = hid.at[g, :, 0:wide]
        return remote(block, block, sem.at[g], z_r.at[g], "req", place)

    def wide_part(c):
        x = rows_all[:, :, part_columns(width, parts, c)].reshape(tall, part_width)
        wide_ready(c)
        value = jnp.dot(x, wide_ref[c * part_width : (c + 1) * part_width], preferred_element_type=jnp.float32)
        acc[...] = value if c == gather.order[0] else acc[...] + value

    def pass_outer():
        @pl.when(is_mid)
        def _():
            along(outer, partner, zp_s).wait_recv()
            along(outer, partner, zp_s).start()

    def pass_partner(g):
        @pl.when(is_mid)
        def _():
            along(g, outer, zo_s).wait_recv()
            along(g, outer, zo_s).start()

    for i in range(parts):
        gather.step(i)
    gather.own.wait()
    for p in range(lines):
        opened(p)
    for k in range(0, parts, 2):
        for c in gather.order[k : k + 2]:
            gather.corner(c)
        for c in gather.order[k : k + 2]:
            gather.whole(c)
            wide_part(c)
    hid[line, :, 0:wide] = jax.nn.gelu(acc[...], approximate=True).astype(jnp.bfloat16)

    @pl.when(is_mid)
    def _():
        along(line, outer, zo_s).start()
        along(line, partner, zp_s).start()

    @pl.when(jnp.logical_not(is_mid))
    def _():
        along(line, inner, zo_s).start()

    act[line] = rows_all[:, :, slice_of(line)]
    weights[0].wait()
    gathered(0)
    first_product(0)
    gathered(1)
    first_product(1)
    at_middle(theirs, 0)
    pass_outer()
    pass_partner(partner)
    gathered(2)
    first_product(2)
    pass_partner(3 - outer)
    at_middle(mine, 0)
    at_middle(theirs, 1)
    gathered(3)
    first_product(3)
    at_middle(forward, 0)
    at_middle(mine, 1)
    at_middle(theirs, 2)
    weights[1].wait()

    @pl.when(jnp.logical_not(is_mid))
    def _():
        for k in range(1, lines):
            along(lax.rem(line + k, lines), inner, zo_s).wait_recv()

    all_hidden(0)
    second_product(0)
    at_middle(forward, 1)
    at_middle(mine, 2)
    at_middle(theirs, 3)
    relay(0)
    all_hidden(1)
    second_product(1)
    at_middle(forward, 2)
    at_middle(mine, 3)
    finish(0)
    relay(1)
    all_hidden(2)
    second_product(2)
    at_middle(forward, 3)
    finish(1)
    relay(2)
    all_hidden(3)
    second_product(3)
    finish(2)
    relay(3)
    finish(3)

    for q in range(lines):
        columns = slice(q * part_width, (q + 1) * part_width)

        @pl.when(line != q)
        def _():
            remote(final.at[q], back.at[q], bs.at[q], br.at[q], "req", q).wait_recv()

        delta_ref[:, columns] = gate[:, columns] * back[q].astype(jnp.float32)

    adder.drain()
    gather.drain()
    hop.sent()
    for k in range(1, lines):
        spread_to(k).wait_send()

    @pl.when(is_mid)
    def _():
        along(outer, partner, zp_s).wait_send()
        along(line, partner, zp_s).wait_send()
        along(line, outer, zo_s).wait_send()
        along(partner, outer, zo_s).wait_send()
        along(3 - outer, outer, zo_s).wait_send()

    @pl.when(jnp.logical_not(is_mid))
    def _():
        along(line, inner, zo_s).wait_send()

    for g in order:
        for k in range(1, steps):
            far_copy(g, k).wait_send()
        for k in range(steps):
            pair_copy(g, k).wait_send()

        @pl.when(line != g)
        def _():
            for k in range(1, steps):
                across(g, k).wait_send()
            for k in range(steps):
                passed(g, k).wait_send()

        @pl.when(line != g)
        def _():
            home(g).wait_send()

        @pl.when(is_mid)
        def _():
            for i in range(chunks // 2):
                to_partner(g, 2 * i + 2 - line).wait_send()
                out_to(g, 2 * i + line - 1, partner, hp_s).wait_send()
            for j in range(chunks):
                out_to(g, j, outer, ho_s).wait_send()

        @pl.when(jnp.logical_not(is_mid))
        def _():
            for j in range(chunks):
                to_inner(g, j).wait_send()


def feed_forward(query, segment, base, modulation, owner, text, out_maps, hop_one, hop_two, up, down, count, lines, ident):
    rows, width = base.shape
    steps = count // PAIR
    depth, units = up.shape
    wide = hop_one.shape[2]
    rest = units - wide
    tall = rows * count
    chunks = 4
    parts = 4
    dma = pltpu.SemaphoreType.DMA
    vm = lambda *extent: pltpu.VMEM(extent, jnp.bfloat16)
    scratch = (
        [vm(*text.shape), dma((2, query.shape[1] // HD)), vm(*query.shape)]
        + [vm(query.shape[1], width), dma((parts,))]
        + quad_sum_scratch(parts, count, rows, width)
        + [pltpu.VMEM((rows, width), jnp.float32)] * 2
        + [vm(depth, rest), vm(units, depth), dma((2,)), vm(rows, width)]
        + [vm(lines, count, rows, depth), dma((lines,)), dma((lines,))]
        + [dma((lines, steps))] * 4
        + [vm(lines, tall, rest)]
        + [vm(lines, chunks, tall // chunks, rest)] * 3
        + [vm(lines, tall, units)]
        + [dma((lines, chunks))] * 7
        + [vm(lines, count, rows, depth)]
        + [vm(lines, steps, rows, depth)] * 3
        + [dma((lines, steps))] * 4
        + [vm(lines, rows, depth)] * 2
        + [dma((lines,))] * 2
        + [vm(width, wide), dma((parts,)), dma((2,)), dma((2,)), vm(count, rows, width), pltpu.VMEM((tall, wide), jnp.float32)]
        + [dma((lines,))] * 3
        + quad_sems(parts)
    )
    return comm_call(
        functools.partial(ff_kernel, count, lines, parts),
        (
            jax.ShapeDtypeStruct((rows, width), jnp.bfloat16),
            jax.ShapeDtypeStruct((rows, width), jnp.float32),
        ),
        [VM] * 5 + [HBM] * 6,
        (VM, VM),
        scratch,
        ident,
        52,
    )(query, segment, base, modulation, owner, *in_hbm(text, out_maps, hop_one, hop_two, up, down))


def layer_norm(values):
    center = values - jnp.mean(values, axis=-1, keepdims=True)
    spread = jnp.mean(center * center, axis=-1, keepdims=True)
    return center * lax.rsqrt(spread + EPSILON)


def rotary_tables(grid):
    half_dim = HD // 2
    spatial = half_dim // 3
    temporal = half_dim - 2 * spatial
    column = jnp.arange(HD, dtype=jnp.int32)
    sign = jnp.where(column < half_dim, -1.0, 1.0).astype(jnp.float32)
    column = column % half_dim
    which_axis = jnp.where(
        column < temporal, 0, jnp.where(column < temporal + spatial, 1, 2)
    ).astype(jnp.int32)
    offset = jnp.where(
        which_axis == 0, 0, jnp.where(which_axis == 1, temporal, temporal + spatial)
    ).astype(jnp.int32)
    span_size = jnp.where(which_axis == 0, temporal, spatial).astype(jnp.float32)
    frequency = jnp.exp(-(column - offset).astype(jnp.float32) / span_size * math.log(10000.0))
    grid = grid.astype(jnp.float32)[:, :, None]
    coordinate = jnp.where(
        which_axis == 0, grid[0], jnp.where(which_axis == 1, grid[1], grid[2])
    )
    angles = coordinate * frequency[None, :]
    return (jnp.cos(angles), jnp.sin(angles) * sign[None, :])


def attend(queries, key_rows, value_rows, allowed):
    scores = lax.dot_general(
        queries, key_rows, (((1,), (1,)), ((), ())), preferred_element_type=jnp.float32
    ) * (1.0 / math.sqrt(HD))
    weights = jnp.exp(jnp.where(allowed, scores, -1e30))
    weights = weights * (1.0 / jnp.sum(weights, axis=-1, keepdims=True))
    return jnp.dot(
        weights.astype(jnp.bfloat16), value_rows, preferred_element_type=jnp.float32
    ).astype(jnp.bfloat16)


def quad():
    me = lax.axis_index("mlp")
    core, x, y = lax.rem(me, 2), lax.rem(lax.div(me, 2), 2), lax.div(me, 4)

    def at(row, column, which):
        return (row * 2 + column) * 2 + which

    return me, at(y, x, 1 - core), at(y, 1 - x, core), at(1 - y, x, core), at(1 - y, 1 - x, core)


def part_columns(width, parts, c):
    return slice(c * (width // parts), (c + 1) * (width // parts))


class QuadGather:
    def __init__(self, parts, own_ref, out_ref, own_sem, xs, xr, ys, yr, fs, fr, ss, sr):
        self.parts, self.own_ref, self.out_ref = parts, own_ref, out_ref
        self.me, self.sib, self.xn, self.yn, self.dg = quad()
        self.sems = (xs, xr, ys, yr, fs, fr, ss, sr)
        self.half = parts // 2
        self.own = pltpu.make_async_copy(own_ref, out_ref.at[self.me], own_sem)
        self.x_order = list(range(parts))
        self.y_order = list(range(self.half, parts)) + list(range(self.half))
        self.order = [c for two in zip(range(self.half), range(self.half, parts)) for c in two]
        self.across, self.up, self.onward, self.passes = {}, {}, {}, {}

    def piece(self, place, c):
        return self.out_ref.at[place, :, part_columns(self.own_ref.shape[1], self.parts, c)]

    def mine(self, c):
        return self.own_ref.at[:, part_columns(self.own_ref.shape[1], self.parts, c)]

    def hand(self, kind, place, c):
        send, recv = self.sems[6].at[kind, c], self.sems[7].at[kind, c]
        source = self.piece(place, c) if kind else self.mine(c)
        self.passes[kind, c] = remote(source, self.piece(place, c), send, recv, "mlp", self.sib)
        self.passes[kind, c].start()

    def start(self):
        xs, xr, ys, yr = self.sems[:4]
        self.own.start()
        for i in range(self.parts):
            c = self.x_order[i]
            self.across[c] = remote(self.mine(c), self.piece(self.me, c), xs.at[c], xr.at[c], "mlp", self.xn)
            self.across[c].start()
            c = self.y_order[i]
            self.up[c] = remote(self.mine(c), self.piece(self.me, c), ys.at[c], yr.at[c], "mlp", self.yn)
            self.up[c].start()
        for c in self.order:
            self.hand(0, self.me, c)

    def send_on(self, place, c, to):
        fs, fr = self.sems[4:6]
        block = self.piece(place, c)
        self.onward[c] = remote(block, block, fs.at[c], fr.at[c], "mlp", to)
        self.onward[c].start()

    def step(self, i):
        c = self.x_order[i]
        self.across[c].wait_recv()
        if c < self.half:
            self.send_on(self.xn, c, self.yn)
        self.hand(1, self.xn, c)
        c = self.y_order[i]
        self.up[c].wait_recv()
        if c >= self.half:
            self.send_on(self.yn, c, self.xn)
        self.hand(2, self.yn, c)

    def corner(self, c):
        self.onward[c].wait_recv()
        self.hand(3, self.dg, c)

    def whole(self, c):
        for kind in range(4):
            self.passes[kind, c].wait_recv()

    def drain(self):
        for group in (self.across, self.up, self.onward, self.passes):
            for copy in group.values():
                copy.wait_send()


def quad_sems(parts):
    dma = pltpu.SemaphoreType.DMA
    return [dma(())] + [dma((parts,))] * 6 + [dma((4, parts))] * 2


def share(own_ref, slots_ref, send_sem, recv_sem, count):
    me = lax.axis_index("mlp")
    copies = [
        remote(own_ref, slots_ref.at[k], send_sem.at[k], recv_sem.at[k], "mlp", shift(me, k, count))
        for k in range(1, count)
    ]
    for copy in copies:
        copy.start()
    return copies


def pick_rows(mod_ref, which, owner):
    chosen = mod_ref[which, 0:1, :]
    for request in range(1, mod_ref.shape[1]):
        chosen = jnp.where(owner == request, mod_ref[which, request : request + 1, :], chosen)
    return chosen


class LineHop:
    def __init__(self, step, lines, from_left, from_right, into, send_sem, recv_sem):
        self.line = lax.axis_index("req")
        self.step, self.lines = step, lines
        right, left = jnp.minimum(self.line + 1, lines - 1), jnp.maximum(self.line - 1, 0)
        self.right = remote(from_left, into(0, self.line + 1 - step), send_sem.at[0], recv_sem.at[0], "req", right)
        self.left = remote(from_right, into(1, self.line - 1 + step), send_sem.at[1], recv_sem.at[1], "req", left)

    def sending(self, work):
        line, step, lines = self.line, self.step, self.lines

        @pl.when((line >= step - 1) & (line < lines - 1))
        def _():
            work(self.right)

        @pl.when((line + step - 1 < lines) & (line > 0))
        def _():
            work(self.left)

    def start(self):
        self.sending(lambda copy: copy.start())

    def landed(self):
        @pl.when(self.line >= self.step)
        def _():
            self.right.wait_recv()

        @pl.when(self.line + self.step < self.lines)
        def _():
            self.left.wait_recv()

    def sent(self):
        self.sending(lambda copy: copy.wait_send())


def line_peers(lines):
    line = lax.axis_index("req")
    return [("req", shift(line, 1, lines)), ("req", shift(line, -1, lines))]


def row_to_column(row, lanes=128):
    return jnp.transpose(jnp.broadcast_to(row, (lanes, row.shape[1])))


def column_to_rows(column, lanes=128):
    return jnp.transpose(jnp.broadcast_to(column, (column.shape[0], lanes)))[0:8]


def enter_kernel(count, lines, parts, tok_ref, mod_ref, owner_ref, seg_ref, pick_ref, down_hbm, maps_hbm, w_hbm, up_hbm,
                 lin_ref, value_ref, scale_ref, hop_ref,
                 down_ref, maps_ref, in_sem, norm, rows_all, w_ref, w_sem, acc, code_acc, code_own, code_slots, cs, cr,
                 chosen, near, mid, far, us, ur, vs, vr, sq_own, sq_slots, qs, qr, hs, hr, *sems):
    me, sib, xn, yn, dg = quad()
    core = lax.rem(me, PAIR)
    flip = 1 - 2 * core
    own_maps = up_hbm.at[:, 0 : hop_ref.shape[2]]
    hop = LineHop(1, lines, own_maps, own_maps, lambda side, _: hop_ref.at[side], hs, hr)
    friends = [("mlp", shift(me, k, count)) for k in range(1, count)] + line_peers(lines)
    hello(friends)
    brought = [
        pltpu.make_async_copy(maps_hbm, maps_ref, in_sem.at[0]),
        pltpu.make_async_copy(down_hbm, down_ref, in_sem.at[1]),
    ]
    for copy in brought:
        copy.start()
    rows, width = tok_ref.shape
    depth = width // parts
    tall = rows * count
    heads = acc.shape[2]
    owner = owner_ref[...]
    norm[...] = (
        layer_norm(tok_ref[...].astype(jnp.float32)) * (1.0 + pick_rows(mod_ref, 1, owner))
        + pick_rows(mod_ref, 0, owner)
    ).astype(jnp.bfloat16)
    gather = QuadGather(parts, norm, rows_all, *sems)
    heard(friends)
    gather.start()
    hop.start()
    loads = {}
    for c in gather.order:
        block = pl.ds(c * depth, depth)
        loads[c] = pltpu.make_async_copy(w_hbm.at[0:3, block], w_ref.at[:, block], w_sem.at[c])
        loads[c].start()

    slots = maps_ref.shape[0]
    requests = mod_ref.shape[1]
    rank = maps_ref.shape[2]

    def choose(r):
        for j in range(2):
            for place in range(count):
                columns = slice(place * heads, (place + 1) * heads)
                total = jnp.zeros((rank, heads), jnp.float32)
                for s in range(slots):
                    total = total + maps_ref[s, j, :, columns].astype(jnp.float32) * pick_ref[
                        r * slots + s : r * slots + s + 1, 0:1
                    ]
                chosen[place, j, r * rank : (r + 1) * rank] = total.astype(jnp.bfloat16)

    dest = [me, xn, yn, dg]
    pair = [
        remote(chosen.at[dest[t] + flip], near.at[t], us.at[t], ur.at[t], "mlp", sib) for t in range(4)
    ]
    out = {
        t: remote(mid.at[t], far.at[t], vs.at[t], vr.at[t], "mlp", dest[t]) for t in (1, 2, 3)
    }

    def code_part(c):
        x = rows_all[:, :, part_columns(width, parts, c)].reshape(tall, depth)
        code_acc[...] += lax.dot_general(
            down_ref[:, part_columns(width, parts, c)], x, (((1,), (1,)), ((), ())),
            preferred_element_type=jnp.float32,
        )

    def product_part(c, fresh):
        loads[c].wait()

        @pl.loop(0, 3)
        def _(i):
            x = rows_all[:, :, part_columns(width, parts, c)].reshape(tall, depth)
            value = jnp.dot(x, w_ref[i, c * depth : (c + 1) * depth], preferred_element_type=jnp.float32)
            acc[i] = value if fresh else acc[i] + value

    code_acc[...] = jnp.zeros_like(code_acc)
    order = gather.order
    brought[0].wait()
    for i in range(max(parts, requests)):
        if i < parts:
            gather.step(i)
        if i < requests:
            choose(i)
    brought[1].wait()
    for copy in pair:
        copy.start()
    for c in order[:2]:
        gather.corner(c)
    for t in (3, 1, 2):
        pair[t].wait_recv()
        mid[t] = chosen[dest[t]] + near[t]
        out[t].start()
    gather.own.wait()
    for c in order[:2]:
        gather.whole(c)
        code_part(c)
        product_part(c, c == order[0])
    for k in range(2, parts, 2):
        for c in order[k : k + 2]:
            gather.corner(c)
        for c in order[k : k + 2]:
            gather.whole(c)
            code_part(c)
    segment = seg_ref[...]
    doubled = 2 * rank
    code = jnp.zeros((doubled, tall), jnp.float32)
    for s in range(slots):
        held = jnp.zeros((1, tall), jnp.float32)
        for r in range(requests):
            held = held + jnp.where(segment == r, pick_ref[r * slots + s : r * slots + s + 1, 0:1], 0.0)
        code = code + held * code_acc[s * doubled : (s + 1) * doubled]
    code_own[...] = code.astype(jnp.bfloat16)
    shared = share(code_own, code_slots, cs, cr, count)
    for c in order[2:]:
        product_part(c, False)
    pair[0].wait_recv()
    up = chosen[me].astype(jnp.float32) + near[0].astype(jnp.float32)
    for t in (1, 2, 3):
        out[t].wait_recv()
        up = up + far[t].astype(jnp.float32)
    up = up.astype(jnp.bfloat16)
    code = code_own[...].astype(jnp.float32)
    for k, copy in enumerate(shared):
        copy.wait_recv()
        code = code + code_slots[k + 1].astype(jnp.float32)

    def adapted(j):
        spread = jnp.concatenate(
            [jnp.where(segment == r, code[j * rank : (j + 1) * rank], 0.0) for r in range(requests)], axis=0
        )
        return jnp.dot(jnp.transpose(spread).astype(jnp.bfloat16), up[j], preferred_element_type=jnp.float32)

    query = acc[0] + adapted(0)
    key = acc[1]
    sq_own[0] = column_to_rows(jnp.sum(query * query, axis=1, keepdims=True))
    sq_own[1] = column_to_rows(jnp.sum(key * key, axis=1, keepdims=True))
    squares = share(sq_own, sq_slots, qs, qr, count)
    lin_ref[0] = query
    lin_ref[1] = key
    value_ref[...] = (acc[2] + adapted(1)).astype(jnp.bfloat16)
    total = sq_own[...]
    for k, copy in enumerate(squares):
        copy.wait_recv()
        total = total + sq_slots[k + 1]
    scale = lax.rsqrt(total / (heads * count) + EPSILON)
    for i in range(2):
        scale_ref[i] = row_to_column(scale[i, 0:1])
    gather.drain()
    hop.landed()
    hop.sent()
    for copy in shared + squares + pair + list(out.values()):
        copy.wait_send()


def enter(tokens, modulation, owner, segment, pick, down, maps, weights, up_maps, wide, count, lines):
    rows, width = tokens.shape
    parts = 4
    heads = weights.shape[2]
    tall = rows * count
    slots, two, rank, _ = maps.shape
    requests = modulation.shape[1]
    dma = pltpu.SemaphoreType.DMA
    vm = lambda *extent: pltpu.VMEM(extent, jnp.bfloat16)
    vf = lambda *extent: pltpu.VMEM(extent, jnp.float32)
    up = (two, requests * rank, heads)
    scratch = (
        [vm(*down.shape), vm(*maps.shape), dma((2,))]
        + [vm(rows, width), vm(count, rows, width), vm(3, width, heads), dma((parts,)), vf(3, tall, heads)]
        + [vf(slots * two * rank, tall), vm(two * rank, tall), vm(count, two * rank, tall), dma((count,)), dma((count,))]
        + [vm(count, *up), vm(4, *up), vm(4, *up), vm(4, *up)]
        + [dma((4,))] * 4
        + [vf(2, 8, tall), vf(count, 2, 8, tall), dma((count,)), dma((count,)), dma((2,)), dma((2,))]
        + quad_sems(parts)
    )
    return comm_call(
        functools.partial(enter_kernel, count, lines, parts),
        (
            jax.ShapeDtypeStruct((2, tall, heads), jnp.float32),
            jax.ShapeDtypeStruct((tall, heads), jnp.bfloat16),
            jax.ShapeDtypeStruct((2, tall, 128), jnp.float32),
            pltpu.HBM((2, up_maps.shape[0], wide), jnp.bfloat16),
        ),
        [VM] * 5 + [HBM] * 4,
        (VM, VM, VM, HBM),
        scratch,
        0,
        48,
    )(tokens, modulation, owner, segment, pick, *in_hbm(down, maps, weights, up_maps))


class QuadSum:
    def __init__(self, parts, part_ref, near, mid, first_in, second_in, ns, nr, xs, xr, fs, fr):
        self.parts, self.part_ref, self.near, self.mid = parts, part_ref, near, mid
        self.first_in, self.second_in = first_in, second_in
        self.sems = (ns, nr, xs, xr, fs, fr)
        self.me, self.sib, self.xn, self.yn, dg = quad()
        self.dest = [self.me, self.xn, self.yn, dg]
        self.flip = 1 - 2 * lax.rem(self.me, PAIR)
        self.half = parts // 2
        self.order = [c for two in zip(range(self.half), range(self.half, parts)) for c in two]
        self.pairs, self.ones, self.twos = {}, {}, {}

    def columns(self, c):
        return part_columns(self.part_ref.shape[2], self.parts, c)

    def ways(self, c):
        return (1, 2) if c < self.half else (2, 1)

    def offer(self, c):
        ns, nr = self.sems[:2]
        columns = self.columns(c)
        for t in (3, 1, 2, 0):
            self.pairs[t, c] = remote(
                self.part_ref.at[self.dest[t] + self.flip, :, columns],
                self.near.at[t, :, columns],
                ns.at[t, c],
                nr.at[t, c],
                "mlp",
                self.sib,
            )
            self.pairs[t, c].start()

    def both(self, t, columns):
        return self.part_ref[self.dest[t], :, columns].astype(jnp.float32) + self.near[
            t, :, columns
        ].astype(jnp.float32)

    def first(self, c):
        xs, xr = self.sems[2:4]
        columns = self.columns(c)
        far, _ = self.ways(c)
        for t, slot in ((3, 1), (far, 0)):
            self.pairs[t, c].wait_recv()
            self.mid[t, :, columns] = self.both(t, columns).astype(jnp.bfloat16)
            self.ones[t, c] = remote(
                self.mid.at[t, :, columns],
                self.first_in.at[slot, :, columns],
                xs.at[slot, c],
                xr.at[slot, c],
                "mlp",
                self.dest[far],
            )
            self.ones[t, c].start()

    def second(self, c):
        fs, fr = self.sems[4:6]
        columns = self.columns(c)
        _, keep = self.ways(c)
        self.pairs[keep, c].wait_recv()
        self.ones[3, c].wait_recv()
        self.mid[keep, :, columns] = (
            self.both(keep, columns) + self.first_in[1, :, columns].astype(jnp.float32)
        ).astype(jnp.bfloat16)
        self.twos[c] = remote(
            self.mid.at[keep, :, columns], self.second_in.at[:, columns], fs.at[c], fr.at[c], "mlp", self.dest[keep]
        )
        self.twos[c].start()

    def total(self, c):
        columns = self.columns(c)
        far, _ = self.ways(c)
        self.pairs[0, c].wait_recv()
        self.ones[far, c].wait_recv()
        self.twos[c].wait_recv()
        return (
            self.both(0, columns)
            + self.first_in[0, :, columns].astype(jnp.float32)
            + self.second_in[:, columns].astype(jnp.float32)
        )

    def run(self, produce, consume, ready):
        order = self.order
        produce(order[0])
        ready()
        self.offer(order[0])
        for i in range(1, self.parts):
            produce(order[i])
            self.offer(order[i])
            self.first(order[i - 1])
        self.first(order[-1])
        for c in order:
            self.second(c)
        for c in order:
            consume(c, self.total(c))

    def drain(self):
        for group in (self.pairs, self.ones, self.twos):
            for copy in group.values():
                copy.wait_send()


def quad_sum_scratch(parts, count, rows, width):
    dma = pltpu.SemaphoreType.DMA
    vm = lambda *extent: pltpu.VMEM(extent, jnp.bfloat16)
    return (
        [vm(count, rows, width), vm(4, rows, width), vm(4, rows, width), vm(2, rows, width), vm(rows, width)]
        + [dma((4, parts))] * 2
        + [dma((2, parts))] * 2
        + [dma((parts,))] * 2
    )


def part_product(x_ref, w_ref, part_ref, parts, loads):
    count, rows, width = part_ref.shape

    def produce(c):
        columns = part_columns(width, parts, c)
        loads[c].wait()
        part_ref[:, :, columns] = (
            jnp.dot(x_ref[...], w_ref[:, columns], preferred_element_type=jnp.float32)
            .astype(jnp.bfloat16)
            .reshape(count, rows, width // parts)
        )

    return produce


def cross_in_kernel(count, lines, parts, att_ref, base_ref, mod_ref, owner_ref, gain_ref, head_gain_ref, o_hbm, q_hbm, held_hbm,
                    res_ref, query_ref, hop_ref,
                    o_ref, o_sem, q_ref, q_sem, sums, norm, rows_all, acc, sq_own, sq_slots, qs, qr, hs, hr, *sems):
    sum_sems, gather_sems_ = sems[:11], sems[11:]
    me = lax.axis_index("mlp")
    rows, width = base_ref.shape
    depth = width // parts
    tall = rows * count
    heads = acc.shape[1]
    adder = QuadSum(parts, *sum_sems)
    loads_o, loads_q = {}, {}
    for c in adder.order:
        columns = part_columns(width, parts, c)
        loads_o[c] = pltpu.make_async_copy(o_hbm.at[0, :, columns], o_ref.at[:, columns], o_sem.at[c])
        loads_o[c].start()
    hop = LineHop(2, lines, held_hbm.at[0], held_hbm.at[1], lambda side, _: hop_ref.at[side], hs, hr)
    friends = [("mlp", shift(me, k, count)) for k in range(1, count)] + line_peers(lines)
    hello(friends)

    def ready():
        heard(friends)
        hop.start()

    for c in adder.order:
        block = pl.ds(c * depth, depth)
        loads_q[c] = pltpu.make_async_copy(q_hbm.at[3, block], q_ref.at[block], q_sem.at[c])
        loads_q[c].start()
    gate = pick_rows(mod_ref, 2, owner_ref[...])

    def consume(c, total):
        columns = part_columns(width, parts, c)
        res = (base_ref[:, columns].astype(jnp.float32) + gate[:, columns] * total).astype(jnp.bfloat16)
        res_ref[:, columns] = res
        sums[:, columns] = res.astype(jnp.float32)

    adder.run(part_product(att_ref, o_ref, sum_sems[0], parts, loads_o), consume, ready)
    norm[...] = (layer_norm(sums[...]) * gain_ref[...]).astype(jnp.bfloat16)
    gather = QuadGather(parts, norm, rows_all, *gather_sems_)
    gather.start()
    order = gather.order

    def product_part(c):
        x = rows_all[:, :, part_columns(width, parts, c)].reshape(tall, depth)
        loads_q[c].wait()
        value = jnp.dot(x, q_ref[c * depth : (c + 1) * depth], preferred_element_type=jnp.float32)
        acc[...] = value if c == order[0] else acc[...] + value

    for i in range(parts):
        gather.step(i)
    gather.own.wait()
    for k in range(0, parts, 2):
        for c in order[k : k + 2]:
            gather.corner(c)
        for c in order[k : k + 2]:
            gather.whole(c)
            product_part(c)
    query = acc[...]
    sq_own[...] = column_to_rows(jnp.sum(query * query, axis=1, keepdims=True))
    squares = share(sq_own, sq_slots, qs, qr, count)
    total = sq_own[...]
    for k, copy in enumerate(squares):
        copy.wait_recv()
        total = total + sq_slots[k + 1]
    scale = row_to_column(lax.rsqrt(total / (heads * count) + EPSILON)[0:1])[:, 0:1]
    query_ref[...] = (acc[...] * scale * head_gain_ref[2:3]).astype(jnp.bfloat16)
    adder.drain()
    gather.drain()
    hop.landed()
    hop.sent()
    for copy in squares:
        copy.wait_send()


def cross_in(attended, base, modulation, owner, gain, head_gain, out_maps, in_maps, held, count, lines):
    rows, width = base.shape
    parts = 4
    tall, heads = attended.shape
    dma = pltpu.SemaphoreType.DMA
    vm = lambda *extent: pltpu.VMEM(extent, jnp.bfloat16)
    vf = lambda *extent: pltpu.VMEM(extent, jnp.float32)
    scratch = (
        [vm(heads, width), dma((parts,)), vm(width, heads), dma((parts,))]
        + [vf(rows, width), vm(rows, width), vm(count, rows, width), vf(tall, heads)]
        + [vf(8, tall), vf(count, 8, tall), dma((count,)), dma((count,)), dma((2,)), dma((2,))]
        + quad_sum_scratch(parts, count, rows, width)
        + quad_sems(parts)
    )
    return comm_call(
        functools.partial(cross_in_kernel, count, lines, parts),
        (
            jax.ShapeDtypeStruct((rows, width), jnp.bfloat16),
            jax.ShapeDtypeStruct((tall, heads), jnp.bfloat16),
            pltpu.HBM(held.shape, held.dtype),
        ),
        [VM] * 6 + [HBM] * 3,
        (VM, VM, HBM),
        scratch,
        3,
        48,
    )(attended, base, modulation, owner, gain, head_gain, *in_hbm(out_maps, in_maps, held))


def self_kernel(page_ref, q_ref, k_ref, v_ref, qs_ref, ks_ref, gain_ref, cos_ref, sin_ref, seg_ref, segs_ref, out_ref, kv_ref):
    cosine, sine = cos_ref[...], sin_ref[...]
    allowed = seg_ref[...] == segs_ref[...]

    def turned(ref, scale, gain, columns):
        rows = ref[:, columns] * scale * gain_ref[gain : gain + 1, columns]
        return (rows * cosine + pltpu.roll(rows, HD // 2, 1) * sine).astype(jnp.bfloat16)

    for head in range(q_ref.shape[1] // HD):
        columns = slice(head * HD, (head + 1) * HD)
        query = turned(q_ref, qs_ref[...], 0, columns)
        key = turned(k_ref, ks_ref[...], 1, columns)
        value = v_ref[:, columns]
        out_ref[:, columns] = attend(query, key, value, allowed)
        for block in range(kv_ref.shape[1]):
            page = page_ref[block]
            rows = slice(block * PAGE, (block + 1) * PAGE)
            kv_ref[0, page, :, columns] = key[rows]
            kv_ref[1, page, :, columns] = value[rows]


def joint_kernel(page_ref, lin_ref, v_ref, scale_ref, gain_ref, cos_ref, sin_ref, seg_ref, segs_ref, out_ref, kv_ref):
    self_kernel(
        page_ref, lin_ref.at[0], lin_ref.at[1], v_ref, scale_ref.at[0, :, 0:1], scale_ref.at[1, :, 0:1],
        gain_ref, cos_ref, sin_ref, seg_ref, segs_ref, out_ref, kv_ref,
    )


def joint_attention(pages, linear, value, scales, gains, cosine, sine, segment):
    _, rows, width = linear.shape
    return pl.pallas_call(
        joint_kernel,
        out_shape=(
            jax.ShapeDtypeStruct((rows, width), jnp.bfloat16),
            jax.ShapeDtypeStruct((2, pages.shape[0], PAGE, width), jnp.bfloat16),
        ),
        in_specs=[pl.BlockSpec(memory_space=pltpu.SMEM)] + [VM] * 8,
        out_specs=(VM, VM),
        compiler_params=pltpu.CompilerParams(vmem_limit_bytes=16 << 20),
    )(pages, linear, value, scales, gains, cosine, sine, segment[:, None], segment[None, :])


def self_attention(pages, query, key, value, query_scale, key_scale, gains, cosine, sine, segment):
    rows, width = query.shape
    return pl.pallas_call(
        self_kernel,
        out_shape=(
            jax.ShapeDtypeStruct((rows, width), jnp.bfloat16),
            jax.ShapeDtypeStruct((2, pages.shape[0], PAGE, width), jnp.bfloat16),
        ),
        in_specs=[pl.BlockSpec(memory_space=pltpu.SMEM)] + [VM] * 10,
        out_specs=(VM, VM),
        compiler_params=pltpu.CompilerParams(vmem_limit_bytes=16 << 20),
    )(
        pages,
        query,
        key,
        value,
        query_scale[:, None],
        key_scale[:, None],
        gains,
        cosine,
        sine,
        segment[:, None],
        segment[None, :],
    )


def cross_kernel(q_ref, k_ref, v_ref, seg_ref, owner_ref, out_ref):
    out_ref[...] = attend(q_ref[...], k_ref[0], v_ref[0], seg_ref[...] == owner_ref[...])


def cross_attention(query, cache, segment, owner):
    rows, width = query.shape
    texts = cache.shape[1]
    head = pl.BlockSpec((rows, HD), lambda h: (0, h))
    return pl.pallas_call(
        cross_kernel,
        out_shape=jax.ShapeDtypeStruct((rows, width), jnp.bfloat16),
        grid=(width // HD,),
        in_specs=[
            head,
            pl.BlockSpec((1, texts, HD), lambda h: (0, 0, h)),
            pl.BlockSpec((1, texts, HD), lambda h: (1, 0, h)),
            pl.BlockSpec((rows, 1), lambda h: (0, 0)),
            pl.BlockSpec((1, texts), lambda h: (0, 0)),
        ],
        out_specs=head,
        compiler_params=pltpu.CompilerParams(vmem_limit_bytes=24 << 20),
    )(query, cache, cache, segment[:, None], owner[None, :])


def product_kernel(act, x_ref, w_ref, out_ref):
    out_ref[0] = act(
        jnp.dot(x_ref[...], w_ref[0], preferred_element_type=jnp.float32)
    ).astype(out_ref.dtype)


def product(rows_in, maps, first, amount, tile, dtype, act=lambda part: part):
    rows, depth = rows_in.shape
    width = maps.shape[2]
    tile = min(tile, width)
    return pl.pallas_call(
        functools.partial(product_kernel, act),
        out_shape=jax.ShapeDtypeStruct((amount, rows, width), dtype),
        grid=(amount, width // tile),
        in_specs=[
            pl.BlockSpec((rows, depth), lambda i, j: (0, 0)),
            pl.BlockSpec((1, depth, tile), lambda i, j: (first + i, 0, j)),
        ],
        out_specs=pl.BlockSpec((1, rows, tile), lambda i, j: (i, 0, j)),
        compiler_params=pltpu.CompilerParams(vmem_limit_bytes=24 << 20),
    )(rows_in, pltpu.with_memory_space_constraint(maps, pltpu.HBM))


def choose_rows(table, segment):
    chosen = jnp.zeros((segment.shape[0],) + table.shape[1:], table.dtype)
    for request in range(table.shape[0]):
        picked = (segment == request).reshape((-1,) + (1,) * (table.ndim - 1))
        chosen = jnp.where(picked, table[request][None], chosen)
    return chosen


def body(
    tokens,
    modulation,
    lengths,
    request_adapter,
    adapter_storage,
    adapter_down_weight,
    adapter_up_maps,
    input_projection,
    query_key_gains,
    positions,
    block_page_lookup,
    output_projection,
    cross_norm_gain,
    text_token_cache,
    feedforward_up,
    feedforward_down,
):
    mlp_count = lax.axis_size("mlp")
    my_index = lax.axis_index("mlp")
    own_count = tokens.shape[0]
    group_rows = own_count * mlp_count
    local_width = input_projection.shape[2]
    entire_width = local_width * mlp_count
    resident_slots = adapter_down_weight.shape[0]
    doubled_rank = adapter_down_weight.shape[2]
    rank_once = doubled_rank // 2

    req_count = lax.axis_size("req")
    slot_total = resident_slots * mlp_count
    tuned = mlp_count == 8 and req_count == 4
    counts = lengths[0]
    index = jnp.arange(counts.shape[0], dtype=jnp.int32)
    bounds = jnp.sum(jnp.where(index[:, None] >= index[None, :], counts[None, :], 0), axis=1)
    position = jnp.arange(group_rows, dtype=jnp.int32)
    segment = jnp.sum((position[:, None] >= bounds[None, :]).astype(jnp.int32), axis=1)
    own_start = my_index * own_count
    own_segment = lax.dynamic_slice_in_dim(segment, own_start, own_count)
    if tuned:
        by_kind = modulation.transpose(1, 0, 2)
        storage = jnp.arange(adapter_storage.shape[0], dtype=jnp.int32)
        request_slot = jnp.sum(
            jnp.where(request_adapter[:, None] == storage[None, :], adapter_storage[None, :], 0), axis=1
        )
        resident = my_index * resident_slots + jnp.arange(resident_slots, dtype=jnp.int32)
        pick = (request_slot[:, None] == resident[None, :]).astype(jnp.float32).reshape(-1, 1)
        linear, value_rows, scales, hop_one = enter(
            tokens,
            by_kind,
            own_segment[:, None],
            segment[None, :],
            jnp.broadcast_to(pick, (pick.shape[0], 128)),
            adapter_down_weight.transpose(0, 2, 1).reshape(resident_slots * doubled_rank, -1),
            adapter_up_maps,
            input_projection,
            feedforward_up,
            feedforward_up.shape[1] * 3 // 8,
            mlp_count,
            req_count,
        )
        cosine, sine = rotary_tables(positions)
        attended, kv_pages = joint_attention(
            block_page_lookup[0], linear, value_rows, scales, query_key_gains, cosine, sine, segment
        )
    else:
        per_token = [choose_rows(modulation[:, which_row, :], own_segment) for which_row in range(6)]
        token_f32 = tokens.astype(jnp.float32)
        rows_in, adapter_up_weight = entry_rows(
            tokens, per_token[1], per_token[0], adapter_up_maps, mlp_count
        )
        request_slot = adapter_storage[request_adapter]
        token_slot = jnp.sum(
            jnp.where(
                segment[:, None] == jnp.arange(request_slot.shape[0], dtype=jnp.int32)[None, :],
                request_slot[None, :],
                0,
            ),
            axis=1,
        )
        resident = my_index * resident_slots + jnp.arange(resident_slots, dtype=jnp.int32)
        held = (token_slot[None, :] == resident[:, None]).astype(jnp.float32)
        code_block = lax.dot_general(
            adapter_down_weight.transpose(0, 2, 1).reshape(resident_slots * doubled_rank, -1),
            rows_in,
            (((1,), (1,)), ((), ())),
            preferred_element_type=jnp.float32,
        ).reshape(resident_slots, doubled_rank, group_rows)
        my_codes = jnp.sum(held[:, None, :] * code_block, axis=0).astype(jnp.bfloat16)
        codes = small_sum(my_codes, mlp_count, 1).astype(jnp.bfloat16)
        slots = jnp.arange(slot_total, dtype=jnp.int32)
        everywhere = token_slot[None, :] == slots[:, None]

        def spread(code_part):
            return jnp.where(everywhere[:, None, :], code_part[None], jnp.bfloat16(0)).reshape(
                slot_total * rank_once, group_rows
            )

        def adapted(code_part, which_map):
            return lax.dot_general(
                spread(code_part),
                adapter_up_weight[:, which_map].reshape(slot_total * rank_once, local_width),
                (((0,), (0,)), ((), ())),
                preferred_element_type=jnp.float32,
            )

        projected = product(rows_in, input_projection, 0, 3, 256, jnp.float32)
        query_linear = projected[0] + adapted(codes[:rank_once], 0)
        key_linear = projected[1]
        value_rows = (projected[2] + adapted(codes[rank_once:], 1)).astype(jnp.bfloat16)
        squares = small_sum(
            jnp.stack(
                [jnp.sum(query_linear * query_linear, axis=1), jnp.sum(key_linear * key_linear, axis=1)]
            ),
            mlp_count,
            2,
        )
        query_square, key_square = squares[0], squares[1]
        query_scale = lax.rsqrt(query_square / entire_width + EPSILON)
        key_scale = lax.rsqrt(key_square / entire_width + EPSILON)
        cosine, sine = rotary_tables(positions)
        attended, kv_pages = self_attention(
            block_page_lookup[0],
            query_linear,
            key_linear,
            value_rows,
            query_scale,
            key_scale,
            query_key_gains,
            cosine,
            sine,
            segment,
        )
    text_owner = (
        jnp.arange(text_token_cache.shape[1] * text_token_cache.shape[2], dtype=jnp.int32)
        // text_token_cache.shape[2]
    )

    def out_rows(rows, which_map):
        return product(rows, output_projection, which_map, 1, 1280, jnp.bfloat16)[0]

    if tuned:
        first_res, cross_query, hop_two = cross_in(
            attended,
            tokens,
            by_kind,
            own_segment[:, None],
            cross_norm_gain[None, :],
            query_key_gains,
            output_projection,
            input_projection,
            hop_one,
            mlp_count,
            req_count,
        )
    else:
        first_res, cross_rows = middle_rows(
            out_rows(attended, 0),
            tokens,
            per_token[2],
            cross_norm_gain[None, :],
            jnp.zeros((1, tokens.shape[1]), jnp.float32),
            mlp_count,
            3,
        )
        cross_linear = product(cross_rows, input_projection, 3, 1, 256, jnp.float32)[0]
        cross_square = small_sum(
            jnp.sum(cross_linear * cross_linear, axis=1)[None, :], mlp_count, 4
        )[0]
        cross_query = (
            cross_linear
            * lax.rsqrt(cross_square / entire_width + EPSILON)[:, None]
            * query_key_gains[2]
        ).astype(jnp.bfloat16)
    if tuned:
        second_res, delta = feed_forward(
            cross_query,
            segment[:, None],
            first_res,
            by_kind,
            own_segment[:, None],
            text_token_cache,
            output_projection,
            hop_one,
            hop_two,
            feedforward_up,
            feedforward_down,
            mlp_count,
            req_count,
            5,
        )
        layer_out = (second_res.astype(jnp.float32) + delta).astype(jnp.bfloat16)
        return (layer_out, kv_pages)
    cross_out = cross_attention(
        cross_query,
        text_token_cache.reshape(2, text_owner.shape[0], local_width),
        segment,
        text_owner,
    )
    up_full = lax.all_gather(feedforward_up, "req", axis=0, tiled=True)
    second_res, mlp_in = middle_rows(
        out_rows(cross_out, 1),
        first_res,
        jnp.ones((1, tokens.shape[1]), jnp.float32),
        1.0 + per_token[4],
        per_token[3],
        mlp_count,
        5,
    )
    hidden = product(
        mlp_in,
        up_full[None],
        0,
        1,
        256,
        jnp.bfloat16,
        functools.partial(jax.nn.gelu, approximate=True),
    )[0]
    hidden_all = line_gather(hidden, req_count, 6)
    units, columns = feedforward_down.shape
    down_part = jnp.dot(
        hidden_all.reshape(req_count * group_rows, units),
        feedforward_down,
        preferred_element_type=jnp.float32,
    ).astype(jnp.bfloat16)
    down_own = exit_rows(
        down_part.reshape(req_count, mlp_count, own_count, columns), mlp_count, req_count, 7
    )
    layer_out = (
        second_res.astype(jnp.float32) + per_token[5] * down_own.astype(jnp.float32)
    ).astype(jnp.bfloat16)
    return (layer_out, kv_pages)


def solution(mesh):
    return jax.shard_map(
        body,
        mesh=mesh,
        in_specs=(
            P(("req", "mlp"), None),
            P("req", None, None),
            P("req", None),
            P("req"),
            P(),
            P("mlp", None, None),
            P("mlp", None, None, None),
            P(None, None, "mlp"),
            P(None, "mlp"),
            P(None, "req"),
            P("req", None),
            P(None, "mlp", None),
            P(),
            P(None, "req", None, "mlp"),
            P("req", "mlp"),
            P("mlp", "req"),
        ),
        out_specs=(P(("req", "mlp"), None), P(None, "req", None, "mlp")),
        check_vma=False,
    )
```

```python
import functools
import math

import jax
import jax.numpy as jnp
from jax import lax
from jax.experimental import pallas as pl
from jax.experimental.pallas import tpu as pltpu
from jax.sharding import PartitionSpec as P

HD = 128
PAGE = 16


EPSILON = 1e-06


PAIR = 2
MESH = pl.DeviceIdType.MESH
ANY = pl.BlockSpec(memory_space=pl.ANY)
VM = pl.BlockSpec(memory_space=pltpu.VMEM)
HBM = pl.BlockSpec(memory_space=pltpu.HBM)


def comm_call(kernel, out_shape, in_specs, out_specs, scratch, ident, room=4):
    return pl.pallas_call(
        kernel,
        out_shape=out_shape,
        in_specs=in_specs,
        out_specs=out_specs,
        scratch_shapes=scratch,
        compiler_params=pltpu.CompilerParams(
            collective_id=ident, has_side_effects=True, vmem_limit_bytes=room << 20
        ),
    )


def remote(source, target, send_sem, recv_sem, axis, place):
    return pltpu.make_async_remote_copy(
        src_ref=source,
        dst_ref=target,
        send_sem=send_sem,
        recv_sem=recv_sem,
        device_id={axis: place},
        device_id_type=MESH,
    )


def shift(me, step, count):
    return lax.rem(me + (step + count) % count, count)


def greet(peers):
    barrier = pltpu.get_barrier_semaphore()
    for axis, place in peers:
        pl.semaphore_signal(barrier, inc=1, device_id={axis: place}, device_id_type=MESH)
    pl.semaphore_wait(barrier, len(peers))


def hello(peers):
    barrier = pltpu.get_barrier_semaphore()
    for axis, place in peers:
        pl.semaphore_signal(barrier, inc=1, device_id={axis: place}, device_id_type=MESH)


def heard(peers):
    pl.semaphore_wait(pltpu.get_barrier_semaphore(), len(peers))


def in_hbm(*arrays):
    return [pltpu.with_memory_space_constraint(array, pltpu.HBM) for array in arrays]


def pair_places(count):
    me = lax.axis_index("mlp")
    outer, core = lax.div(me, PAIR), lax.rem(me, PAIR)
    sibling = outer * PAIR + (PAIR - 1 - core)
    peers = [
        shift(outer, k, count // PAIR) * PAIR + core for k in range(count // PAIR)
    ]
    sources = [
        shift(outer, -k, count // PAIR) * PAIR + core for k in range(count // PAIR)
    ]
    return me, core, sibling, peers, sources


def gather_sems(count):
    steps = count // PAIR
    return [pltpu.SemaphoreType.DMA(())] + [pltpu.SemaphoreType.DMA((steps,))] * 4


def gather_rows(count, places, own_ref, out_ref, own_sem, send_sem, recv_sem, pass_send, pass_recv):
    me, core, sibling, peers, sources = places
    own = pltpu.make_async_copy(own_ref, out_ref.at[me], own_sem)
    sends = [
        remote(own_ref, out_ref.at[me], send_sem.at[k], recv_sem.at[k], "mlp", peers[k])
        for k in range(1, count // PAIR)
    ]
    for copy in sends:
        copy.start()
    passes = [remote(own_ref, out_ref.at[me], pass_send.at[0], pass_recv.at[0], "mlp", sibling)]
    passes[0].start()
    own.start()
    for k in range(1, count // PAIR):
        sends[k - 1].wait_recv()
        block = out_ref.at[sources[k]]
        passes.append(remote(block, block, pass_send.at[k], pass_recv.at[k], "mlp", sibling))
        passes[-1].start()
    for copy in sends:
        copy.wait_send()
    for copy in passes:
        copy.wait()
    own.wait()


def entry_kernel(count, tok_ref, scale_ref, shift_ref, maps_ref, out_ref, up_ref, norm, map_own, map_send, map_recv, *sems):
    places = pair_places(count)
    me = places[0]
    slots, width = maps_ref.shape[0], up_ref.shape[-1]
    others = [shift(me, k, count) for k in range(1, count)]
    greet([("mlp", place) for place in others])

    def columns(place):
        return maps_ref.at[:, :, :, pl.ds(pl.multiple_of(place * width, 128), width)]

    target = up_ref.at[pl.ds(me * slots, slots)]
    own = pltpu.make_async_copy(columns(me), target, map_own)
    own.start()
    copies = [
        remote(columns(place), target, map_send.at[k], map_recv.at[k], "mlp", place)
        for k, place in enumerate(others)
    ]
    norm[...] = (
        layer_norm(tok_ref[...].astype(jnp.float32)) * (1.0 + scale_ref[...]) + shift_ref[...]
    ).astype(jnp.bfloat16)
    for copy in copies:
        copy.start()
    gather_rows(count, places, norm, out_ref, *sems)
    for copy in copies:
        copy.wait()
    own.wait()


def entry_rows(tokens, scale, shift_rows, maps, count):
    rows, width = tokens.shape
    slots, two, rank, total = maps.shape
    dma = pltpu.SemaphoreType.DMA
    gathered, up = comm_call(
        functools.partial(entry_kernel, count),
        (
            jax.ShapeDtypeStruct((count, rows, width), jnp.bfloat16),
            jax.ShapeDtypeStruct((count * slots, two, rank, total // count), maps.dtype),
        ),
        [VM, VM, VM, ANY],
        (ANY, ANY),
        [pltpu.VMEM((rows, width), jnp.bfloat16), dma(()), dma((count - 1,)), dma((count - 1,))]
        + gather_sems(count),
        0,
        8,
    )(tokens, scale, shift_rows, maps)
    return gathered.reshape(count * rows, width), up


def sum_blocks(count, places, block_of, near, mid, far, ns, nr, fs, fr):
    me, core, sibling, peers, sources = places
    steps = count // PAIR
    order = list(range(1, steps)) + [0]
    pairs = {}
    for k in order:
        other = peers[k] + (PAIR - 1 - 2 * core)
        pairs[k] = remote(block_of(other), near.at[k], ns.at[k], nr.at[k], "mlp", sibling)
        pairs[k].start()
    sends = []
    for k in range(1, steps):
        pairs[k].wait_recv()
        mid[k] = (
            block_of(peers[k])[...].astype(jnp.float32) + near[k].astype(jnp.float32)
        ).astype(jnp.bfloat16)
        sends.append(remote(mid.at[k], far.at[k], fs.at[k], fr.at[k], "mlp", peers[k]))
        sends[-1].start()
    pairs[0].wait_recv()
    total = block_of(me)[...].astype(jnp.float32) + near[0].astype(jnp.float32)
    for k in range(1, steps):
        sends[k - 1].wait_recv()
        total = total + far[k].astype(jnp.float32)
    for k in order:
        pairs[k].wait_send()
    for copy in sends:
        copy.wait_send()
    return total


def sum_scratch(count, extent):
    steps = count // PAIR
    return [pltpu.VMEM((steps,) + extent, jnp.bfloat16)] * 3 + [
        pltpu.SemaphoreType.DMA((steps,))
    ] * 4


def middle_kernel(count, part_ref, base_ref, gate_ref, scale_ref, shift_ref, res_ref, out_ref, near, mid, far, norm, ns, nr, fs, fr, *sems):
    places = pair_places(count)
    greet([("mlp", places[2])] + [("mlp", place) for place in places[3][1:]])
    total = sum_blocks(
        count, places, lambda place: part_ref.at[place], near, mid, far, ns, nr, fs, fr
    )
    res = (base_ref[...].astype(jnp.float32) + gate_ref[...] * total).astype(jnp.bfloat16)
    res_ref[...] = res
    norm[...] = (layer_norm(res.astype(jnp.float32)) * scale_ref[...] + shift_ref[...]).astype(
        jnp.bfloat16
    )
    gather_rows(count, places, norm, out_ref, *sems)


def middle_rows(part, base, gate, scale, shift_rows, count, ident):
    rows, width = base.shape
    scratch = sum_scratch(count, (rows, width))
    res, gathered = comm_call(
        functools.partial(middle_kernel, count),
        (
            jax.ShapeDtypeStruct((rows, width), jnp.bfloat16),
            jax.ShapeDtypeStruct((count, rows, width), jnp.bfloat16),
        ),
        [VM] * 5,
        (VM, ANY),
        scratch[:3] + [pltpu.VMEM((rows, width), jnp.bfloat16)] + scratch[3:] + gather_sems(count),
        ident,
        24,
    )(part.reshape(count, rows, width), base, gate, scale, shift_rows)
    return res, gathered.reshape(count * rows, width)


def small_kernel(count, own_ref, out_ref, slots, send_sem, recv_sem):
    me = lax.axis_index("mlp")
    others = [shift(me, k, count) for k in range(1, count)]
    greet([("mlp", place) for place in others])
    copies = [
        remote(own_ref, slots.at[k], send_sem.at[k], recv_sem.at[k], "mlp", place)
        for k, place in enumerate(others)
    ]
    for copy in copies:
        copy.start()
    total = own_ref[...].astype(jnp.float32)
    for k, copy in enumerate(copies):
        copy.wait_recv()
        total = total + slots[k].astype(jnp.float32)
    out_ref[...] = total
    for copy in copies:
        copy.wait_send()


def small_sum(own, count, ident):
    dma = pltpu.SemaphoreType.DMA((count - 1,))
    return comm_call(
        functools.partial(small_kernel, count),
        jax.ShapeDtypeStruct(own.shape, jnp.float32),
        [VM],
        VM,
        [pltpu.VMEM((count - 1,) + own.shape, own.dtype), dma, dma],
        ident,
    )(own)


def line_kernel(count, own_ref, out_ref, own_sem, rs, rr, ls, lr):
    me = lax.axis_index("req")
    right, left = shift(me, 1, count), shift(me, -1, count)
    greet([("req", right), ("req", left)])
    own = pltpu.make_async_copy(own_ref, out_ref.at[me], own_sem)
    own.start()

    pieces = rs.shape[1]
    rows = own_ref.shape[0] // pieces

    def hop(step, piece, sign):
        block = jnp.clip(me - sign * step, 0, count - 1)
        part = pl.ds(piece * rows, rows)
        source = own_ref.at[part] if step == 0 else out_ref.at[block, part]
        send, recv, place = (rs, rr, right) if sign > 0 else (ls, lr, left)
        return remote(
            source,
            out_ref.at[block, part],
            send.at[step, piece],
            recv.at[step, piece],
            "req",
            place,
        )

    def each(step, work):
        for piece in range(pieces):
            work(step, piece)

    def advance(step, piece):
        if step > 0:

            @pl.when(me >= step)
            def _():
                hop(step - 1, piece, 1).wait_recv()

            @pl.when(me + step < count)
            def _():
                hop(step - 1, piece, -1).wait_recv()

        @pl.when((me >= step) & (me < count - 1))
        def _():
            hop(step, piece, 1).start()

        @pl.when((me + step < count) & (me > 0))
        def _():
            hop(step, piece, -1).start()

    def finish(step, piece):
        @pl.when(me >= count - 1)
        def _():
            hop(step, piece, 1).wait_recv()

        @pl.when(me < 1)
        def _():
            hop(step, piece, -1).wait_recv()

    def drain(step, piece):
        @pl.when((me >= step) & (me < count - 1))
        def _():
            hop(step, piece, 1).wait_send()

        @pl.when((me + step < count) & (me > 0))
        def _():
            hop(step, piece, -1).wait_send()

    for step in range(count - 1):
        each(step, advance)
    each(count - 2, finish)
    for step in range(count - 1):
        each(step, drain)
    own.wait()


def line_gather(own, count, ident):
    dma = pltpu.SemaphoreType.DMA
    return comm_call(
        functools.partial(line_kernel, count),
        jax.ShapeDtypeStruct((count,) + own.shape, own.dtype),
        [ANY],
        ANY,
        [dma(())] + [dma((count - 1, 4))] * 4,
        ident,
    )(own)


def exit_kernel(count, lines, part_ref, out_ref, near, mid, far, final, ns, nr, fs, fr, own_sem, send_sem, recv_sem):
    places = pair_places(count)
    me, core, sibling, peers, _ = places
    steps = count // PAIR
    line = lax.axis_index("req")
    groups = [shift(line, k + 1, lines) for k in range(lines)]
    greet(
        [("mlp", sibling)]
        + [("mlp", place) for place in peers[1:]]
        + [("req", place) for place in groups[:-1]]
    )
    order = list(range(1, steps)) + [0]
    pairs, sends, copies = {}, [], []
    for i, group in enumerate(groups):
        for k in order:
            other = peers[k] + (PAIR - 1 - 2 * core)
            pairs[i, k] = remote(
                part_ref.at[group, other], near.at[i, k], ns.at[i, k], nr.at[i, k], "mlp", sibling
            )
            pairs[i, k].start()
    for i, group in enumerate(groups):
        for k in range(1, steps):
            pairs[i, k].wait_recv()
            mid[i, k] = (
                part_ref[group, peers[k]].astype(jnp.float32) + near[i, k].astype(jnp.float32)
            ).astype(jnp.bfloat16)
            sends.append(
                remote(mid.at[i, k], far.at[i, k], fs.at[i, k], fr.at[i, k], "mlp", peers[k])
            )
            sends[-1].start()
    width = final.shape[-1]
    target = out_ref.at[:, pl.ds(pl.multiple_of(line * width, 128), width)]
    for i, group in enumerate(groups):
        pairs[i, 0].wait_recv()
        total = part_ref[group, me].astype(jnp.float32) + near[i, 0].astype(jnp.float32)
        for k in range(1, steps):
            sends[i * (steps - 1) + k - 1].wait_recv()
            total = total + far[i, k].astype(jnp.float32)
        final[i] = total.astype(jnp.bfloat16)
        if i < lines - 1:
            copies.append(
                remote(final.at[i], target, send_sem.at[i], recv_sem.at[i], "req", group)
            )
        else:
            copies.append(pltpu.make_async_copy(final.at[i], target, own_sem))
        copies[-1].start()
    for copy in list(pairs.values()) + sends:
        copy.wait_send()
    for copy in copies:
        copy.wait()


def exit_rows(part, count, lines, ident):
    groups, _, rows, width = part.shape
    steps = count // PAIR
    dma = pltpu.SemaphoreType.DMA
    return comm_call(
        functools.partial(exit_kernel, count, lines),
        jax.ShapeDtypeStruct((rows, lines * width), jnp.bfloat16),
        [VM],
        VM,
        [pltpu.VMEM((groups, steps, rows, width), jnp.bfloat16)] * 3
        + [pltpu.VMEM((groups, rows, width), jnp.bfloat16)]
        + [dma((groups, steps))] * 4
        + [dma(()), dma((lines - 1,)), dma((lines - 1,))],
        ident,
        24,
    )(part)


def attend_text(queries, text_ref, columns, segment):
    requests = text_ref.shape[1]
    scores = None
    for r in range(requests):
        some = lax.dot_general(
            queries, text_ref[0, r, :, columns], (((1,), (1,)), ((), ())), preferred_element_type=jnp.float32
        )
        scores = some if r == 0 else jnp.where(segment == r, some, scores)
    weights = jnp.exp(scores * (1.0 / math.sqrt(HD)))
    weights = weights * (1.0 / jnp.sum(weights, axis=-1, keepdims=True))
    total = None
    for r in range(requests):
        mine = jnp.where(segment == r, weights, 0.0).astype(jnp.bfloat16)
        some = jnp.dot(mine, text_ref[1, r, :, columns], preferred_element_type=jnp.float32)
        total = some if r == 0 else total + some
    return total.astype(jnp.bfloat16)


def lines_order(lines):
    middle = lines // 2
    return [middle - 1, middle] + [g for g in range(lines) if g not in (middle - 1, middle)]


def dot_tiles(x, w_ref, out_ref, put, tile):
    width = w_ref.shape[1]

    @pl.loop(0, width // tile)
    def _(i):
        columns = pl.ds(pl.multiple_of(i * tile, tile), tile)
        put(columns, jnp.dot(x, w_ref[:, columns], preferred_element_type=jnp.float32))


def ff_kernel(count, lines, parts, query_ref, seg_ref, base_ref, mod_ref, owner_ref, text_hbm, o_hbm, hop_one, hop_two, up_hbm, down_hbm, res, delta_ref,
              text_ref, text_sem, x_ref, o_ref, o_sem, part, near, mid, first_in, second_in, ns, nr, xs, xr, fs, fr, gate, sums,
              up_ref, down_ref, w_sem, norm, act, a_send, a_recv, g_send, g_recv, p_send, p_recv,
              pbuf, from_outer, from_partner, staged, hid, es, er, ts, tr, ho_s, hp_s, h_r,
              dn, near2, mid2, far2, ns2, nr2, fs2, fr2, final, back, bs, br,
              wide_ref, wide_sem, hs, hr, rows_all, acc, zo_s, zp_s, z_r, *sems):
    places = pair_places(count)
    me, core, sibling, peers, sources = places
    steps = count // PAIR
    line = lax.axis_index("req")
    order = lines_order(lines)
    is_mid = (line == 1) | (line == 2)
    outer = jnp.where(line == 1, 0, 3)
    partner = 3 - line
    inner = jnp.where(line == 0, 1, 2)
    adder = QuadSum(parts, part, near, mid, first_in, second_in, ns, nr, xs, xr, fs, fr)
    heads = query_ref.shape[1] // HD
    texts = {}
    for h in range(heads):
        for i in range(2):
            columns = slice(h * HD, (h + 1) * HD)
            texts[i, h] = pltpu.make_async_copy(
                text_hbm.at[i, :, :, columns], text_ref.at[i, :, :, columns], text_sem.at[i, h]
            )
            texts[i, h].start()
    loads_o = {}
    for c in adder.order:
        columns = part_columns(base_ref.shape[1], parts, c)
        loads_o[c] = pltpu.make_async_copy(o_hbm.at[1, :, columns], o_ref.at[:, columns], o_sem.at[c])
        loads_o[c].start()
    friends = (
        [("mlp", sibling)]
        + [("mlp", place) for place in peers[1:]]
        + [("req", shift(line, k, lines)) for k in range(1, lines)]
    )
    hello(friends)
    wide = wide_ref.shape[1]
    weights = [
        pltpu.make_async_copy(up_hbm.at[:, wide:], up_ref, w_sem.at[0]),
        pltpu.make_async_copy(down_hbm, down_ref, w_sem.at[1]),
    ]
    part_width = up_hbm.shape[0]

    def wide_rows(place):
        return wide_ref.at[pl.ds(pl.multiple_of(place * part_width, 128), part_width)]

    hop = LineHop(
        3, lines, hop_two.at[0], hop_two.at[1],
        lambda side, place: wide_rows(jnp.clip(place, 0, lines - 1)), hs, hr,
    )
    sources_w = [(0, up_hbm.at[:, 0:wide])]
    for distance, held in ((1, hop_one), (2, hop_two)):
        sources_w += [(distance, held.at[0]), (-distance, held.at[1])]
    for q in range(lines):
        for distance, source in sources_w:
            @pl.when(line - q == distance)
            def _():
                pltpu.make_async_copy(source, wide_rows(q), wide_sem.at[q]).start()

    def wide_ready(q):
        if q == 0:
            @pl.when(line == lines - 1)
            def _():
                hop.right.wait_recv()

        if q == lines - 1:
            @pl.when(line == 0)
            def _():
                hop.left.wait_recv()

        @pl.when(jnp.abs(line - q) < lines - 1)
        def _():
            pltpu.make_async_copy(hop_one.at[0], wide_rows(q), wide_sem.at[q]).wait()

    for copy in weights:
        copy.start()
    owner = owner_ref[...]
    gate[...] = pick_rows(mod_ref, 5, owner)

    def consume(c, total):
        columns = part_columns(base_ref.shape[1], parts, c)
        value = (base_ref[:, columns].astype(jnp.float32) + total).astype(jnp.bfloat16)
        res[:, columns] = value
        sums[:, columns] = value.astype(jnp.float32)

    segment = seg_ref[...]
    for h in range(heads):
        columns = slice(h * HD, (h + 1) * HD)
        texts[0, h].wait()
        texts[1, h].wait()
        x_ref[:, columns] = attend_text(query_ref[:, columns], text_ref, columns, segment)

    def ready():
        heard(friends)
        hop.start()

    adder.run(part_product(x_ref, o_ref, part, parts, loads_o), consume, ready)
    norm[...] = (
        layer_norm(sums[...]) * (1.0 + pick_rows(mod_ref, 4, owner)) + pick_rows(mod_ref, 3, owner)
    ).astype(jnp.bfloat16)

    rows, width = norm.shape

    def slice_of(place):
        return pl.ds(pl.multiple_of(place * part_width, 128), part_width)

    def spread_to(k):
        place = lax.rem(line + k, lines)
        return remote(
            norm.at[:, slice_of(place)], act.at[line, me], a_send.at[k], a_recv.at[line], "req", place
        )

    gather = QuadGather(parts, norm, rows_all, *sems)
    gather.start()
    for k in (2, 1, 3):
        spread_to(k).start()

    def across(g, k):
        return remote(act.at[g, me], act.at[g, me], g_send.at[g, k], g_recv.at[g, k], "mlp", peers[k])

    def passed(g, k):
        block = act.at[g, sources[k]]
        return remote(block, block, p_send.at[g, k], p_recv.at[g, k], "mlp", sibling)

    def from_sibling(g, k):
        block = act.at[g, sources[k] + PAIR - 1 - 2 * core]
        return remote(block, block, p_send.at[g, k], p_recv.at[g, k], "mlp", sibling)

    def landed(p):
        g = order[p]

        @pl.when(line != g)
        def _():
            remote(norm.at[:, slice_of(g)], act.at[g, me], a_send.at[0], a_recv.at[g], "req", g).wait_recv()

    def opened(p):
        if p < lines:
            g = order[p]
            landed(p)

            @pl.when(line != g)
            def _():
                for k in range(1, steps):
                    across(g, k).start()
                passed(g, 0).start()

    tall = count * rows
    chunks = from_outer.shape[1]
    some = tall // chunks

    def chunk(j):
        return pl.ds(pl.multiple_of(j * some, some), some)

    def to_inner(g, j):
        return remote(pbuf.at[g, chunk(j)], from_outer.at[g, j], es.at[g, j], er.at[g, j], "req", inner)

    def to_partner(g, j):
        return remote(staged.at[g, j], from_partner.at[g, j], ts.at[g, j], tr.at[g, j], "req", partner)

    def out_to(g, j, place, sem):
        block = hid.at[g, chunk(j), wide:]
        return remote(block, block, sem.at[g, j], h_r.at[g, j], "req", place)

    def gathered(p):
        g = order[p]

        @pl.when(line != g)
        def _():
            for k in range(1, steps):
                remote(act.at[g, me], act.at[g, sources[k]], g_send.at[g, k], g_recv.at[g, k], "mlp", peers[k]).wait_recv()
                passed(g, k).start()

        @pl.when(line != g)
        def _():
            for k in range(steps):
                from_sibling(g, k).wait_recv()

    def first_product(p):
        g = order[p]

        def put(columns, value):
            pbuf[g, :, columns] = value.astype(jnp.bfloat16)

        dot_tiles(act[g].reshape(tall, part_width), up_ref, pbuf, put, 256 if up_ref.shape[1] % 256 == 0 else up_ref.shape[1])

        @pl.when(jnp.logical_not(is_mid))
        def _():
            for j in range(chunks):
                to_inner(g, j).start()

    def theirs(g, i):
        j = 2 * i + 2 - line
        to_inner(g, j).wait_recv()
        staged[g, j] = (
            pbuf[g, chunk(j)].astype(jnp.float32) + from_outer[g, j].astype(jnp.float32)
        ).astype(jnp.bfloat16)
        to_partner(g, j).start()

    def mine(g, i):
        j = 2 * i + line - 1
        to_inner(g, j).wait_recv()
        to_partner(g, j).wait_recv()
        value = (
            pbuf[g, chunk(j)].astype(jnp.float32)
            + from_outer[g, j].astype(jnp.float32)
            + from_partner[g, j].astype(jnp.float32)
        )
        hid[g, chunk(j), wide:] = jax.nn.gelu(value, approximate=True).astype(jnp.bfloat16)
        out_to(g, j, partner, hp_s).start()
        out_to(g, j, outer, ho_s).start()

    def forward(g, i):
        j = 2 * i + 2 - line
        out_to(g, j, partner, hp_s).wait_recv()
        out_to(g, j, outer, ho_s).start()

    def at_middle(work, p):
        @pl.when(is_mid)
        def _():
            for i in range(chunks // 2):
                work(order[p], i)

    def all_hidden(p):
        g = order[p]
        @pl.when(jnp.logical_not(is_mid))
        def _():
            for j in range(chunks):
                out_to(g, j, inner, ho_s).wait_recv()

    def pair_copy(g, k):
        other = peers[k] + (PAIR - 1 - 2 * core)
        return remote(dn.at[g, other], near2.at[g, k], ns2.at[g, k], nr2.at[g, k], "mlp", sibling)

    def far_copy(g, k):
        return remote(mid2.at[g, k], far2.at[g, k], fs2.at[g, k], fr2.at[g, k], "mlp", peers[k])

    k_order = list(range(1, steps)) + [0]

    def second_product(p):
        g = order[p]

        def put(columns, value):
            dn[g, :, :, columns] = value.astype(jnp.bfloat16).reshape(count, rows, 256)

        dot_tiles(hid[g], down_ref, dn, put, 256)
        for k in k_order:
            pair_copy(g, k).start()

    def relay(p):
        g = order[p]
        for k in range(1, steps):
            pair_copy(g, k).wait_recv()
            mid2[g, k] = (
                dn[g, peers[k]].astype(jnp.float32) + near2[g, k].astype(jnp.float32)
            ).astype(jnp.bfloat16)
            far_copy(g, k).start()

    def home(g):
        return remote(final.at[g], back.at[line], bs.at[g], br.at[line], "req", g)

    def finish(p):
        g = order[p]
        pair_copy(g, 0).wait_recv()
        value = dn[g, me].astype(jnp.float32) + near2[g, 0].astype(jnp.float32)
        for k in range(1, steps):
            far_copy(g, k).wait_recv()
            value = value + far2[g, k].astype(jnp.float32)
        final[g] = value.astype(jnp.bfloat16)

        @pl.when(line == g)
        def _():
            back[g] = final[g]

        @pl.when(line != g)
        def _():
            home(g).start()

    def along(g, place, sem):
        block = hid.at[g, :, 0:wide]
        return remote(block, block, sem.at[g], z_r.at[g], "req", place)

    def wide_part(c):
        x = rows_all[:, :, part_columns(width, parts, c)].reshape(tall, part_width)
        wide_ready(c)
        value = jnp.dot(x, wide_ref[c * part_width : (c + 1) * part_width], preferred_element_type=jnp.float32)
        acc[...] = value if c == gather.order[0] else acc[...] + value

    def pass_outer():
        @pl.when(is_mid)
        def _():
            along(outer, partner, zp_s).wait_recv()
            along(outer, partner, zp_s).start()

    def pass_partner(g):
        @pl.when(is_mid)
        def _():
            along(g, outer, zo_s).wait_recv()
            along(g, outer, zo_s).start()

    for i in range(parts):
        gather.step(i)
    gather.own.wait()
    for p in range(lines):
        opened(p)
    for k in range(0, parts, 2):
        for c in gather.order[k : k + 2]:
            gather.corner(c)
        for c in gather.order[k : k + 2]:
            gather.whole(c)
            wide_part(c)
    hid[line, :, 0:wide] = jax.nn.gelu(acc[...], approximate=True).astype(jnp.bfloat16)

    @pl.when(is_mid)
    def _():
        along(line, outer, zo_s).start()
        along(line, partner, zp_s).start()

    @pl.when(jnp.logical_not(is_mid))
    def _():
        along(line, inner, zo_s).start()

    act[line] = rows_all[:, :, slice_of(line)]
    weights[0].wait()
    gathered(0)
    first_product(0)
    gathered(1)
    first_product(1)
    at_middle(theirs, 0)
    pass_outer()
    pass_partner(partner)
    gathered(2)
    first_product(2)
    pass_partner(3 - outer)
    at_middle(mine, 0)
    at_middle(theirs, 1)
    gathered(3)
    first_product(3)
    at_middle(forward, 0)
    at_middle(mine, 1)
    at_middle(theirs, 2)
    weights[1].wait()

    @pl.when(jnp.logical_not(is_mid))
    def _():
        for k in range(1, lines):
            along(lax.rem(line + k, lines), inner, zo_s).wait_recv()

    all_hidden(0)
    second_product(0)
    at_middle(forward, 1)
    at_middle(mine, 2)
    at_middle(theirs, 3)
    relay(0)
    all_hidden(1)
    second_product(1)
    at_middle(forward, 2)
    at_middle(mine, 3)
    finish(0)
    relay(1)
    all_hidden(2)
    second_product(2)
    at_middle(forward, 3)
    finish(1)
    relay(2)
    all_hidden(3)
    second_product(3)
    finish(2)
    relay(3)
    finish(3)

    for q in range(lines):
        columns = slice(q * part_width, (q + 1) * part_width)

        @pl.when(line != q)
        def _():
            remote(final.at[q], back.at[q], bs.at[q], br.at[q], "req", q).wait_recv()

        delta_ref[:, columns] = gate[:, columns] * back[q].astype(jnp.float32)

    adder.drain()
    gather.drain()
    hop.sent()
    for k in range(1, lines):
        spread_to(k).wait_send()

    @pl.when(is_mid)
    def _():
        along(outer, partner, zp_s).wait_send()
        along(line, partner, zp_s).wait_send()
        along(line, outer, zo_s).wait_send()
        along(partner, outer, zo_s).wait_send()
        along(3 - outer, outer, zo_s).wait_send()

    @pl.when(jnp.logical_not(is_mid))
    def _():
        along(line, inner, zo_s).wait_send()

    for g in order:
        for k in range(1, steps):
            far_copy(g, k).wait_send()
        for k in range(steps):
            pair_copy(g, k).wait_send()

        @pl.when(line != g)
        def _():
            for k in range(1, steps):
                across(g, k).wait_send()
            for k in range(steps):
                passed(g, k).wait_send()

        @pl.when(line != g)
        def _():
            home(g).wait_send()

        @pl.when(is_mid)
        def _():
            for i in range(chunks // 2):
                to_partner(g, 2 * i + 2 - line).wait_send()
                out_to(g, 2 * i + line - 1, partner, hp_s).wait_send()
            for j in range(chunks):
                out_to(g, j, outer, ho_s).wait_send()

        @pl.when(jnp.logical_not(is_mid))
        def _():
            for j in range(chunks):
                to_inner(g, j).wait_send()


def feed_forward(query, segment, base, modulation, owner, text, out_maps, hop_one, hop_two, up, down, count, lines, ident):
    rows, width = base.shape
    steps = count // PAIR
    depth, units = up.shape
    wide = hop_one.shape[2]
    rest = units - wide
    tall = rows * count
    chunks = 4
    parts = 4
    dma = pltpu.SemaphoreType.DMA
    vm = lambda *extent: pltpu.VMEM(extent, jnp.bfloat16)
    scratch = (
        [vm(*text.shape), dma((2, query.shape[1] // HD)), vm(*query.shape)]
        + [vm(query.shape[1], width), dma((parts,))]
        + quad_sum_scratch(parts, count, rows, width)
        + [pltpu.VMEM((rows, width), jnp.float32)] * 2
        + [vm(depth, rest), vm(units, depth), dma((2,)), vm(rows, width)]
        + [vm(lines, count, rows, depth), dma((lines,)), dma((lines,))]
        + [dma((lines, steps))] * 4
        + [vm(lines, tall, rest)]
        + [vm(lines, chunks, tall // chunks, rest)] * 3
        + [vm(lines, tall, units)]
        + [dma((lines, chunks))] * 7
        + [vm(lines, count, rows, depth)]
        + [vm(lines, steps, rows, depth)] * 3
        + [dma((lines, steps))] * 4
        + [vm(lines, rows, depth)] * 2
        + [dma((lines,))] * 2
        + [vm(width, wide), dma((parts,)), dma((2,)), dma((2,)), vm(count, rows, width), pltpu.VMEM((tall, wide), jnp.float32)]
        + [dma((lines,))] * 3
        + quad_sems(parts)
    )
    return comm_call(
        functools.partial(ff_kernel, count, lines, parts),
        (
            jax.ShapeDtypeStruct((rows, width), jnp.bfloat16),
            jax.ShapeDtypeStruct((rows, width), jnp.float32),
        ),
        [VM] * 5 + [HBM] * 6,
        (VM, VM),
        scratch,
        ident,
        52,
    )(query, segment, base, modulation, owner, *in_hbm(text, out_maps, hop_one, hop_two, up, down))


def layer_norm(values):
    center = values - jnp.mean(values, axis=-1, keepdims=True)
    spread = jnp.mean(center * center, axis=-1, keepdims=True)
    return center * lax.rsqrt(spread + EPSILON)


def rotary_tables(grid):
    half_dim = HD // 2
    spatial = half_dim // 3
    temporal = half_dim - 2 * spatial
    column = jnp.arange(HD, dtype=jnp.int32)
    sign = jnp.where(column < half_dim, -1.0, 1.0).astype(jnp.float32)
    column = column % half_dim
    which_axis = jnp.where(
        column < temporal, 0, jnp.where(column < temporal + spatial, 1, 2)
    ).astype(jnp.int32)
    offset = jnp.where(
        which_axis == 0, 0, jnp.where(which_axis == 1, temporal, temporal + spatial)
    ).astype(jnp.int32)
    span_size = jnp.where(which_axis == 0, temporal, spatial).astype(jnp.float32)
    frequency = jnp.exp(-(column - offset).astype(jnp.float32) / span_size * math.log(10000.0))
    grid = grid.astype(jnp.float32)[:, :, None]
    coordinate = jnp.where(
        which_axis == 0, grid[0], jnp.where(which_axis == 1, grid[1], grid[2])
    )
    angles = coordinate * frequency[None, :]
    return (jnp.cos(angles), jnp.sin(angles) * sign[None, :])


def attend(queries, key_rows, value_rows, allowed):
    scores = lax.dot_general(
        queries, key_rows, (((1,), (1,)), ((), ())), preferred_element_type=jnp.float32
    ) * (1.0 / math.sqrt(HD))
    weights = jnp.exp(jnp.where(allowed, scores, -1e30))
    weights = weights * (1.0 / jnp.sum(weights, axis=-1, keepdims=True))
    return jnp.dot(
        weights.astype(jnp.bfloat16), value_rows, preferred_element_type=jnp.float32
    ).astype(jnp.bfloat16)


def quad():
    me = lax.axis_index("mlp")
    core, x, y = lax.rem(me, 2), lax.rem(lax.div(me, 2), 2), lax.div(me, 4)

    def at(row, column, which):
        return (row * 2 + column) * 2 + which

    return me, at(y, x, 1 - core), at(y, 1 - x, core), at(1 - y, x, core), at(1 - y, 1 - x, core)


def part_columns(width, parts, c):
    return slice(c * (width // parts), (c + 1) * (width // parts))


class QuadGather:
    def __init__(self, parts, own_ref, out_ref, own_sem, xs, xr, ys, yr, fs, fr, ss, sr):
        self.parts, self.own_ref, self.out_ref = parts, own_ref, out_ref
        self.me, self.sib, self.xn, self.yn, self.dg = quad()
        self.sems = (xs, xr, ys, yr, fs, fr, ss, sr)
        self.half = parts // 2
        self.own = pltpu.make_async_copy(own_ref, out_ref.at[self.me], own_sem)
        self.x_order = list(range(parts))
        self.y_order = list(range(self.half, parts)) + list(range(self.half))
        self.order = [c for two in zip(range(self.half), range(self.half, parts)) for c in two]
        self.across, self.up, self.onward, self.passes = {}, {}, {}, {}

    def piece(self, place, c):
        return self.out_ref.at[place, :, part_columns(self.own_ref.shape[1], self.parts, c)]

    def mine(self, c):
        return self.own_ref.at[:, part_columns(self.own_ref.shape[1], self.parts, c)]

    def hand(self, kind, place, c):
        send, recv = self.sems[6].at[kind, c], self.sems[7].at[kind, c]
        source = self.piece(place, c) if kind else self.mine(c)
        self.passes[kind, c] = remote(source, self.piece(place, c), send, recv, "mlp", self.sib)
        self.passes[kind, c].start()

    def start(self):
        xs, xr, ys, yr = self.sems[:4]
        self.own.start()
        for i in range(self.parts):
            c = self.x_order[i]
            self.across[c] = remote(self.mine(c), self.piece(self.me, c), xs.at[c], xr.at[c], "mlp", self.xn)
            self.across[c].start()
            c = self.y_order[i]
            self.up[c] = remote(self.mine(c), self.piece(self.me, c), ys.at[c], yr.at[c], "mlp", self.yn)
            self.up[c].start()
        for c in self.order:
            self.hand(0, self.me, c)

    def send_on(self, place, c, to):
        fs, fr = self.sems[4:6]
        block = self.piece(place, c)
        self.onward[c] = remote(block, block, fs.at[c], fr.at[c], "mlp", to)
        self.onward[c].start()

    def step(self, i):
        c = self.x_order[i]
        self.across[c].wait_recv()
        if c < self.half:
            self.send_on(self.xn, c, self.yn)
        self.hand(1, self.xn, c)
        c = self.y_order[i]
        self.up[c].wait_recv()
        if c >= self.half:
            self.send_on(self.yn, c, self.xn)
        self.hand(2, self.yn, c)

    def corner(self, c):
        self.onward[c].wait_recv()
        self.hand(3, self.dg, c)

    def whole(self, c):
        for kind in range(4):
            self.passes[kind, c].wait_recv()

    def drain(self):
        for group in (self.across, self.up, self.onward, self.passes):
            for copy in group.values():
                copy.wait_send()


def quad_sems(parts):
    dma = pltpu.SemaphoreType.DMA
    return [dma(())] + [dma((parts,))] * 6 + [dma((4, parts))] * 2


def share(own_ref, slots_ref, send_sem, recv_sem, count):
    me = lax.axis_index("mlp")
    copies = [
        remote(own_ref, slots_ref.at[k], send_sem.at[k], recv_sem.at[k], "mlp", shift(me, k, count))
        for k in range(1, count)
    ]
    for copy in copies:
        copy.start()
    return copies


def pick_rows(mod_ref, which, owner):
    chosen = mod_ref[which, 0:1, :]
    for request in range(1, mod_ref.shape[1]):
        chosen = jnp.where(owner == request, mod_ref[which, request : request + 1, :], chosen)
    return chosen


class LineHop:
    def __init__(self, step, lines, from_left, from_right, into, send_sem, recv_sem):
        self.line = lax.axis_index("req")
        self.step, self.lines = step, lines
        right, left = jnp.minimum(self.line + 1, lines - 1), jnp.maximum(self.line - 1, 0)
        self.right = remote(from_left, into(0, self.line + 1 - step), send_sem.at[0], recv_sem.at[0], "req", right)
        self.left = remote(from_right, into(1, self.line - 1 + step), send_sem.at[1], recv_sem.at[1], "req", left)

    def sending(self, work):
        line, step, lines = self.line, self.step, self.lines

        @pl.when((line >= step - 1) & (line < lines - 1))
        def _():
            work(self.right)

        @pl.when((line + step - 1 < lines) & (line > 0))
        def _():
            work(self.left)

    def start(self):
        self.sending(lambda copy: copy.start())

    def landed(self):
        @pl.when(self.line >= self.step)
        def _():
            self.right.wait_recv()

        @pl.when(self.line + self.step < self.lines)
        def _():
            self.left.wait_recv()

    def sent(self):
        self.sending(lambda copy: copy.wait_send())


def line_peers(lines):
    line = lax.axis_index("req")
    return [("req", shift(line, 1, lines)), ("req", shift(line, -1, lines))]


def row_to_column(row, lanes=128):
    return jnp.transpose(jnp.broadcast_to(row, (lanes, row.shape[1])))


def column_to_rows(column, lanes=128):
    return jnp.transpose(jnp.broadcast_to(column, (column.shape[0], lanes)))[0:8]


def enter_kernel(count, lines, parts, owner_ref, seg_ref, pick_ref, tok_hbm, mod_hbm, down_hbm, maps_hbm, w_hbm, up_hbm,
                 lin_ref, value_ref, scale_ref, hop_ref,
                 tok_ref, mod_ref, down_ref, maps_ref, in_sem, norm, rows_all, w_ref, w_sem, acc, code_acc, code_own, code_slots, cs, cr,
                 chosen, near, mid, far, us, ur, vs, vr, sq_own, sq_slots, qs, qr, hs, hr, *sems):
    me, sib, xn, yn, dg = quad()
    core = lax.rem(me, PAIR)
    flip = 1 - 2 * core
    own_maps = up_hbm.at[:, 0 : hop_ref.shape[2]]
    hop = LineHop(1, lines, own_maps, own_maps, lambda side, _: hop_ref.at[side], hs, hr)
    friends = [("mlp", shift(me, k, count)) for k in range(1, count)] + line_peers(lines)
    hello(friends)
    early = [
        pltpu.make_async_copy(tok_hbm, tok_ref, in_sem.at[2]),
        pltpu.make_async_copy(mod_hbm.at[0:2], mod_ref, in_sem.at[3]),
    ]
    for copy in early:
        copy.start()
    brought = [
        pltpu.make_async_copy(maps_hbm, maps_ref, in_sem.at[0]),
        pltpu.make_async_copy(down_hbm, down_ref, in_sem.at[1]),
    ]
    for copy in brought:
        copy.start()
    for copy in early:
        copy.wait()
    rows, width = tok_ref.shape
    depth = width // parts
    tall = rows * count
    heads = acc.shape[2]
    owner = owner_ref[...]
    norm[...] = (
        layer_norm(tok_ref[...].astype(jnp.float32)) * (1.0 + pick_rows(mod_ref, 1, owner))
        + pick_rows(mod_ref, 0, owner)
    ).astype(jnp.bfloat16)
    gather = QuadGather(parts, norm, rows_all, *sems)
    heard(friends)
    gather.start()
    hop.start()
    loads = {}
    for c in gather.order:
        block = pl.ds(c * depth, depth)
        loads[c] = pltpu.make_async_copy(w_hbm.at[0:3, block], w_ref.at[:, block], w_sem.at[c])
        loads[c].start()

    slots = maps_ref.shape[0]
    requests = mod_ref.shape[1]
    rank = maps_ref.shape[2]

    def choose(r):
        for j in range(2):
            for place in range(count):
                columns = slice(place * heads, (place + 1) * heads)
                total = jnp.zeros((rank, heads), jnp.float32)
                for s in range(slots):
                    total = total + maps_ref[s, j, :, columns].astype(jnp.float32) * pick_ref[
                        r * slots + s : r * slots + s + 1, 0:1
                    ]
                chosen[place, j, r * rank : (r + 1) * rank] = total.astype(jnp.bfloat16)

    dest = [me, xn, yn, dg]
    pair = [
        remote(chosen.at[dest[t] + flip], near.at[t], us.at[t], ur.at[t], "mlp", sib) for t in range(4)
    ]
    out = {
        t: remote(mid.at[t], far.at[t], vs.at[t], vr.at[t], "mlp", dest[t]) for t in (1, 2, 3)
    }

    def code_part(c):
        x = rows_all[:, :, part_columns(width, parts, c)].reshape(tall, depth)
        code_acc[...] += lax.dot_general(
            down_ref[:, part_columns(width, parts, c)], x, (((1,), (1,)), ((), ())),
            preferred_element_type=jnp.float32,
        )

    def product_part(c, fresh):
        loads[c].wait()

        @pl.loop(0, 3)
        def _(i):
            x = rows_all[:, :, part_columns(width, parts, c)].reshape(tall, depth)
            value = jnp.dot(x, w_ref[i, c * depth : (c + 1) * depth], preferred_element_type=jnp.float32)
            acc[i] = value if fresh else acc[i] + value

    code_acc[...] = jnp.zeros_like(code_acc)
    order = gather.order
    brought[0].wait()
    for i in range(max(parts, requests)):
        if i < parts:
            gather.step(i)
        if i < requests:
            choose(i)
    brought[1].wait()
    for copy in pair:
        copy.start()
    for c in order[:2]:
        gather.corner(c)
    for t in (3, 1, 2):
        pair[t].wait_recv()
        mid[t] = chosen[dest[t]] + near[t]
        out[t].start()
    gather.own.wait()
    for c in order[:2]:
        gather.whole(c)
        code_part(c)
        product_part(c, c == order[0])
    for k in range(2, parts, 2):
        for c in order[k : k + 2]:
            gather.corner(c)
        for c in order[k : k + 2]:
            gather.whole(c)
            code_part(c)
    segment = seg_ref[...]
    doubled = 2 * rank
    code = jnp.zeros((doubled, tall), jnp.float32)
    for s in range(slots):
        held = jnp.zeros((1, tall), jnp.float32)
        for r in range(requests):
            held = held + jnp.where(segment == r, pick_ref[r * slots + s : r * slots + s + 1, 0:1], 0.0)
        code = code + held * code_acc[s * doubled : (s + 1) * doubled]
    code_own[...] = code.astype(jnp.bfloat16)
    shared = share(code_own, code_slots, cs, cr, count)
    for c in order[2:]:
        product_part(c, False)
    pair[0].wait_recv()
    up = chosen[me].astype(jnp.float32) + near[0].astype(jnp.float32)
    for t in (1, 2, 3):
        out[t].wait_recv()
        up = up + far[t].astype(jnp.float32)
    up = up.astype(jnp.bfloat16)
    code = code_own[...].astype(jnp.float32)
    for k, copy in enumerate(shared):
        copy.wait_recv()
        code = code + code_slots[k + 1].astype(jnp.float32)

    def adapted(j):
        spread = jnp.concatenate(
            [jnp.where(segment == r, code[j * rank : (j + 1) * rank], 0.0) for r in range(requests)], axis=0
        )
        return jnp.dot(jnp.transpose(spread).astype(jnp.bfloat16), up[j], preferred_element_type=jnp.float32)

    query = acc[0] + adapted(0)
    key = acc[1]
    sq_own[0] = column_to_rows(jnp.sum(query * query, axis=1, keepdims=True))
    sq_own[1] = column_to_rows(jnp.sum(key * key, axis=1, keepdims=True))
    squares = share(sq_own, sq_slots, qs, qr, count)
    lin_ref[0] = query
    lin_ref[1] = key
    value_ref[...] = (acc[2] + adapted(1)).astype(jnp.bfloat16)
    total = sq_own[...]
    for k, copy in enumerate(squares):
        copy.wait_recv()
        total = total + sq_slots[k + 1]
    scale = lax.rsqrt(total / (heads * count) + EPSILON)
    for i in range(2):
        scale_ref[i] = row_to_column(scale[i, 0:1])
    gather.drain()
    hop.landed()
    hop.sent()
    for copy in shared + squares + pair + list(out.values()):
        copy.wait_send()


def enter(tokens, modulation, owner, segment, pick, down, maps, weights, up_maps, wide, count, lines):
    rows, width = tokens.shape
    parts = 4
    heads = weights.shape[2]
    tall = rows * count
    slots, two, rank, _ = maps.shape
    requests = modulation.shape[1]
    dma = pltpu.SemaphoreType.DMA
    vm = lambda *extent: pltpu.VMEM(extent, jnp.bfloat16)
    vf = lambda *extent: pltpu.VMEM(extent, jnp.float32)
    up = (two, requests * rank, heads)
    scratch = (
        [vm(rows, width), vf(2, *modulation.shape[1:]), vm(*down.shape), vm(*maps.shape), dma((4,))]
        + [vm(rows, width), vm(count, rows, width), vm(3, width, heads), dma((parts,)), vf(3, tall, heads)]
        + [vf(slots * two * rank, tall), vm(two * rank, tall), vm(count, two * rank, tall), dma((count,)), dma((count,))]
        + [vm(count, *up), vm(4, *up), vm(4, *up), vm(4, *up)]
        + [dma((4,))] * 4
        + [vf(2, 8, tall), vf(count, 2, 8, tall), dma((count,)), dma((count,)), dma((2,)), dma((2,))]
        + quad_sems(parts)
    )
    return comm_call(
        functools.partial(enter_kernel, count, lines, parts),
        (
            jax.ShapeDtypeStruct((2, tall, heads), jnp.float32),
            jax.ShapeDtypeStruct((tall, heads), jnp.bfloat16),
            jax.ShapeDtypeStruct((2, tall, 128), jnp.float32),
            pltpu.HBM((2, up_maps.shape[0], wide), jnp.bfloat16),
        ),
        [VM] * 3 + [HBM] * 6,
        (VM, VM, VM, HBM),
        scratch,
        0,
        48,
    )(owner, segment, pick, *in_hbm(tokens, modulation, down, maps, weights, up_maps))


class QuadSum:
    def __init__(self, parts, part_ref, near, mid, first_in, second_in, ns, nr, xs, xr, fs, fr):
        self.parts, self.part_ref, self.near, self.mid = parts, part_ref, near, mid
        self.first_in, self.second_in = first_in, second_in
        self.sems = (ns, nr, xs, xr, fs, fr)
        self.me, self.sib, self.xn, self.yn, dg = quad()
        self.dest = [self.me, self.xn, self.yn, dg]
        self.flip = 1 - 2 * lax.rem(self.me, PAIR)
        self.half = parts // 2
        self.order = [c for two in zip(range(self.half), range(self.half, parts)) for c in two]
        self.pairs, self.ones, self.twos = {}, {}, {}

    def columns(self, c):
        return part_columns(self.part_ref.shape[2], self.parts, c)

    def ways(self, c):
        return (1, 2) if c < self.half else (2, 1)

    def offer(self, c):
        ns, nr = self.sems[:2]
        columns = self.columns(c)
        for t in (3, 1, 2, 0):
            self.pairs[t, c] = remote(
                self.part_ref.at[self.dest[t] + self.flip, :, columns],
                self.near.at[t, :, columns],
                ns.at[t, c],
                nr.at[t, c],
                "mlp",
                self.sib,
            )
            self.pairs[t, c].start()

    def both(self, t, columns):
        return self.part_ref[self.dest[t], :, columns].astype(jnp.float32) + self.near[
            t, :, columns
        ].astype(jnp.float32)

    def first(self, c):
        xs, xr = self.sems[2:4]
        columns = self.columns(c)
        far, _ = self.ways(c)
        for t, slot in ((3, 1), (far, 0)):
            self.pairs[t, c].wait_recv()
            self.mid[t, :, columns] = self.both(t, columns).astype(jnp.bfloat16)
            self.ones[t, c] = remote(
                self.mid.at[t, :, columns],
                self.first_in.at[slot, :, columns],
                xs.at[slot, c],
                xr.at[slot, c],
                "mlp",
                self.dest[far],
            )
            self.ones[t, c].start()

    def second(self, c):
        fs, fr = self.sems[4:6]
        columns = self.columns(c)
        _, keep = self.ways(c)
        self.pairs[keep, c].wait_recv()
        self.ones[3, c].wait_recv()
        self.mid[keep, :, columns] = (
            self.both(keep, columns) + self.first_in[1, :, columns].astype(jnp.float32)
        ).astype(jnp.bfloat16)
        self.twos[c] = remote(
            self.mid.at[keep, :, columns], self.second_in.at[:, columns], fs.at[c], fr.at[c], "mlp", self.dest[keep]
        )
        self.twos[c].start()

    def total(self, c):
        columns = self.columns(c)
        far, _ = self.ways(c)
        self.pairs[0, c].wait_recv()
        self.ones[far, c].wait_recv()
        self.twos[c].wait_recv()
        return (
            self.both(0, columns)
            + self.first_in[0, :, columns].astype(jnp.float32)
            + self.second_in[:, columns].astype(jnp.float32)
        )

    def run(self, produce, consume, ready):
        order = self.order
        produce(order[0])
        ready()
        self.offer(order[0])
        for i in range(1, self.parts):
            produce(order[i])
            self.offer(order[i])
            self.first(order[i - 1])
        self.first(order[-1])
        for c in order:
            self.second(c)
        for c in order:
            consume(c, self.total(c))

    def drain(self):
        for group in (self.pairs, self.ones, self.twos):
            for copy in group.values():
                copy.wait_send()


def quad_sum_scratch(parts, count, rows, width):
    dma = pltpu.SemaphoreType.DMA
    vm = lambda *extent: pltpu.VMEM(extent, jnp.bfloat16)
    return (
        [vm(count, rows, width), vm(4, rows, width), vm(4, rows, width), vm(2, rows, width), vm(rows, width)]
        + [dma((4, parts))] * 2
        + [dma((2, parts))] * 2
        + [dma((parts,))] * 2
    )


def part_product(x_ref, w_ref, part_ref, parts, loads):
    count, rows, width = part_ref.shape

    def produce(c):
        columns = part_columns(width, parts, c)
        loads[c].wait()
        part_ref[:, :, columns] = (
            jnp.dot(x_ref[...], w_ref[:, columns], preferred_element_type=jnp.float32)
            .astype(jnp.bfloat16)
            .reshape(count, rows, width // parts)
        )

    return produce


def cross_in_kernel(count, lines, parts, att_ref, base_ref, mod_ref, owner_ref, gain_ref, head_gain_ref, o_hbm, q_hbm, held_hbm,
                    res_ref, query_ref, hop_ref,
                    o_ref, o_sem, q_ref, q_sem, sums, norm, rows_all, acc, sq_own, sq_slots, qs, qr, hs, hr, *sems):
    sum_sems, gather_sems_ = sems[:11], sems[11:]
    me = lax.axis_index("mlp")
    rows, width = base_ref.shape
    depth = width // parts
    tall = rows * count
    heads = acc.shape[1]
    adder = QuadSum(parts, *sum_sems)
    loads_o, loads_q = {}, {}
    for c in adder.order:
        columns = part_columns(width, parts, c)
        loads_o[c] = pltpu.make_async_copy(o_hbm.at[0, :, columns], o_ref.at[:, columns], o_sem.at[c])
        loads_o[c].start()
    hop = LineHop(2, lines, held_hbm.at[0], held_hbm.at[1], lambda side, _: hop_ref.at[side], hs, hr)
    friends = [("mlp", shift(me, k, count)) for k in range(1, count)] + line_peers(lines)
    hello(friends)

    def ready():
        heard(friends)
        hop.start()

    for c in adder.order:
        block = pl.ds(c * depth, depth)
        loads_q[c] = pltpu.make_async_copy(q_hbm.at[3, block], q_ref.at[block], q_sem.at[c])
        loads_q[c].start()
    gate = pick_rows(mod_ref, 2, owner_ref[...])

    def consume(c, total):
        columns = part_columns(width, parts, c)
        res = (base_ref[:, columns].astype(jnp.float32) + gate[:, columns] * total).astype(jnp.bfloat16)
        res_ref[:, columns] = res
        sums[:, columns] = res.astype(jnp.float32)

    adder.run(part_product(att_ref, o_ref, sum_sems[0], parts, loads_o), consume, ready)
    norm[...] = (layer_norm(sums[...]) * gain_ref[...]).astype(jnp.bfloat16)
    gather = QuadGather(parts, norm, rows_all, *gather_sems_)
    gather.start()
    order = gather.order

    def product_part(c):
        x = rows_all[:, :, part_columns(width, parts, c)].reshape(tall, depth)
        loads_q[c].wait()
        value = jnp.dot(x, q_ref[c * depth : (c + 1) * depth], preferred_element_type=jnp.float32)
        acc[...] = value if c == order[0] else acc[...] + value

    for i in range(parts):
        gather.step(i)
    gather.own.wait()
    for k in range(0, parts, 2):
        for c in order[k : k + 2]:
            gather.corner(c)
        for c in order[k : k + 2]:
            gather.whole(c)
            product_part(c)
    query = acc[...]
    sq_own[...] = column_to_rows(jnp.sum(query * query, axis=1, keepdims=True))
    squares = share(sq_own, sq_slots, qs, qr, count)
    total = sq_own[...]
    for k, copy in enumerate(squares):
        copy.wait_recv()
        total = total + sq_slots[k + 1]
    scale = row_to_column(lax.rsqrt(total / (heads * count) + EPSILON)[0:1])[:, 0:1]
    query_ref[...] = (acc[...] * scale * head_gain_ref[2:3]).astype(jnp.bfloat16)
    adder.drain()
    gather.drain()
    hop.landed()
    hop.sent()
    for copy in squares:
        copy.wait_send()


def cross_in(attended, base, modulation, owner, gain, head_gain, out_maps, in_maps, held, count, lines):
    rows, width = base.shape
    parts = 4
    tall, heads = attended.shape
    dma = pltpu.SemaphoreType.DMA
    vm = lambda *extent: pltpu.VMEM(extent, jnp.bfloat16)
    vf = lambda *extent: pltpu.VMEM(extent, jnp.float32)
    scratch = (
        [vm(heads, width), dma((parts,)), vm(width, heads), dma((parts,))]
        + [vf(rows, width), vm(rows, width), vm(count, rows, width), vf(tall, heads)]
        + [vf(8, tall), vf(count, 8, tall), dma((count,)), dma((count,)), dma((2,)), dma((2,))]
        + quad_sum_scratch(parts, count, rows, width)
        + quad_sems(parts)
    )
    return comm_call(
        functools.partial(cross_in_kernel, count, lines, parts),
        (
            jax.ShapeDtypeStruct((rows, width), jnp.bfloat16),
            jax.ShapeDtypeStruct((tall, heads), jnp.bfloat16),
            pltpu.HBM(held.shape, held.dtype),
        ),
        [VM] * 6 + [HBM] * 3,
        (VM, VM, HBM),
        scratch,
        3,
        48,
    )(attended, base, modulation, owner, gain, head_gain, *in_hbm(out_maps, in_maps, held))


def self_kernel(page_ref, q_ref, k_ref, v_ref, qs_ref, ks_ref, gain_ref, cos_ref, sin_ref, seg_ref, segs_ref, out_ref, kv_ref):
    cosine, sine = cos_ref[...], sin_ref[...]
    allowed = seg_ref[...] == segs_ref[...]

    def turned(ref, scale, gain, columns):
        rows = ref[:, columns] * scale * gain_ref[gain : gain + 1, columns]
        return (rows * cosine + pltpu.roll(rows, HD // 2, 1) * sine).astype(jnp.bfloat16)

    for head in range(q_ref.shape[1] // HD):
        columns = slice(head * HD, (head + 1) * HD)
        query = turned(q_ref, qs_ref[...], 0, columns)
        key = turned(k_ref, ks_ref[...], 1, columns)
        value = v_ref[:, columns]
        out_ref[:, columns] = attend(query, key, value, allowed)
        for block in range(kv_ref.shape[1]):
            page = page_ref[block]
            rows = slice(block * PAGE, (block + 1) * PAGE)
            kv_ref[0, page, :, columns] = key[rows]
            kv_ref[1, page, :, columns] = value[rows]


def joint_kernel(page_ref, lin_ref, v_ref, scale_ref, gain_ref, cos_ref, sin_ref, seg_ref, segs_ref, out_ref, kv_ref):
    self_kernel(
        page_ref, lin_ref.at[0], lin_ref.at[1], v_ref, scale_ref.at[0, :, 0:1], scale_ref.at[1, :, 0:1],
        gain_ref, cos_ref, sin_ref, seg_ref, segs_ref, out_ref, kv_ref,
    )


def joint_attention(pages, linear, value, scales, gains, cosine, sine, segment):
    _, rows, width = linear.shape
    return pl.pallas_call(
        joint_kernel,
        out_shape=(
            jax.ShapeDtypeStruct((rows, width), jnp.bfloat16),
            jax.ShapeDtypeStruct((2, pages.shape[0], PAGE, width), jnp.bfloat16),
        ),
        in_specs=[pl.BlockSpec(memory_space=pltpu.SMEM)] + [VM] * 8,
        out_specs=(VM, VM),
        compiler_params=pltpu.CompilerParams(vmem_limit_bytes=16 << 20),
    )(pages, linear, value, scales, gains, cosine, sine, segment[:, None], segment[None, :])


def self_attention(pages, query, key, value, query_scale, key_scale, gains, cosine, sine, segment):
    rows, width = query.shape
    return pl.pallas_call(
        self_kernel,
        out_shape=(
            jax.ShapeDtypeStruct((rows, width), jnp.bfloat16),
            jax.ShapeDtypeStruct((2, pages.shape[0], PAGE, width), jnp.bfloat16),
        ),
        in_specs=[pl.BlockSpec(memory_space=pltpu.SMEM)] + [VM] * 10,
        out_specs=(VM, VM),
        compiler_params=pltpu.CompilerParams(vmem_limit_bytes=16 << 20),
    )(
        pages,
        query,
        key,
        value,
        query_scale[:, None],
        key_scale[:, None],
        gains,
        cosine,
        sine,
        segment[:, None],
        segment[None, :],
    )


def cross_kernel(q_ref, k_ref, v_ref, seg_ref, owner_ref, out_ref):
    out_ref[...] = attend(q_ref[...], k_ref[0], v_ref[0], seg_ref[...] == owner_ref[...])


def cross_attention(query, cache, segment, owner):
    rows, width = query.shape
    texts = cache.shape[1]
    head = pl.BlockSpec((rows, HD), lambda h: (0, h))
    return pl.pallas_call(
        cross_kernel,
        out_shape=jax.ShapeDtypeStruct((rows, width), jnp.bfloat16),
        grid=(width // HD,),
        in_specs=[
            head,
            pl.BlockSpec((1, texts, HD), lambda h: (0, 0, h)),
            pl.BlockSpec((1, texts, HD), lambda h: (1, 0, h)),
            pl.BlockSpec((rows, 1), lambda h: (0, 0)),
            pl.BlockSpec((1, texts), lambda h: (0, 0)),
        ],
        out_specs=head,
        compiler_params=pltpu.CompilerParams(vmem_limit_bytes=24 << 20),
    )(query, cache, cache, segment[:, None], owner[None, :])


def product_kernel(act, x_ref, w_ref, out_ref):
    out_ref[0] = act(
        jnp.dot(x_ref[...], w_ref[0], preferred_element_type=jnp.float32)
    ).astype(out_ref.dtype)


def product(rows_in, maps, first, amount, tile, dtype, act=lambda part: part):
    rows, depth = rows_in.shape
    width = maps.shape[2]
    tile = min(tile, width)
    return pl.pallas_call(
        functools.partial(product_kernel, act),
        out_shape=jax.ShapeDtypeStruct((amount, rows, width), dtype),
        grid=(amount, width // tile),
        in_specs=[
            pl.BlockSpec((rows, depth), lambda i, j: (0, 0)),
            pl.BlockSpec((1, depth, tile), lambda i, j: (first + i, 0, j)),
        ],
        out_specs=pl.BlockSpec((1, rows, tile), lambda i, j: (i, 0, j)),
        compiler_params=pltpu.CompilerParams(vmem_limit_bytes=24 << 20),
    )(rows_in, pltpu.with_memory_space_constraint(maps, pltpu.HBM))


def choose_rows(table, segment):
    chosen = jnp.zeros((segment.shape[0],) + table.shape[1:], table.dtype)
    for request in range(table.shape[0]):
        picked = (segment == request).reshape((-1,) + (1,) * (table.ndim - 1))
        chosen = jnp.where(picked, table[request][None], chosen)
    return chosen


def body(
    tokens,
    modulation,
    lengths,
    request_adapter,
    adapter_storage,
    adapter_down_weight,
    adapter_up_maps,
    input_projection,
    query_key_gains,
    positions,
    block_page_lookup,
    output_projection,
    cross_norm_gain,
    text_token_cache,
    feedforward_up,
    feedforward_down,
):
    mlp_count = lax.axis_size("mlp")
    my_index = lax.axis_index("mlp")
    own_count = tokens.shape[0]
    group_rows = own_count * mlp_count
    local_width = input_projection.shape[2]
    entire_width = local_width * mlp_count
    resident_slots = adapter_down_weight.shape[0]
    doubled_rank = adapter_down_weight.shape[2]
    rank_once = doubled_rank // 2

    req_count = lax.axis_size("req")
    slot_total = resident_slots * mlp_count
    tuned = mlp_count == 8 and req_count == 4
    counts = lengths[0]
    index = jnp.arange(counts.shape[0], dtype=jnp.int32)
    bounds = jnp.sum(jnp.where(index[:, None] >= index[None, :], counts[None, :], 0), axis=1)
    position = jnp.arange(group_rows, dtype=jnp.int32)
    segment = jnp.sum((position[:, None] >= bounds[None, :]).astype(jnp.int32), axis=1)
    own_start = my_index * own_count
    own_segment = lax.dynamic_slice_in_dim(segment, own_start, own_count)
    if tuned:
        by_kind = modulation.transpose(1, 0, 2)
        storage = jnp.arange(adapter_storage.shape[0], dtype=jnp.int32)
        request_slot = jnp.sum(
            jnp.where(request_adapter[:, None] == storage[None, :], adapter_storage[None, :], 0), axis=1
        )
        resident = my_index * resident_slots + jnp.arange(resident_slots, dtype=jnp.int32)
        pick = (request_slot[:, None] == resident[None, :]).astype(jnp.float32).reshape(-1, 1)
        linear, value_rows, scales, hop_one = enter(
            tokens,
            by_kind,
            own_segment[:, None],
            segment[None, :],
            jnp.broadcast_to(pick, (pick.shape[0], 128)),
            adapter_down_weight.transpose(0, 2, 1).reshape(resident_slots * doubled_rank, -1),
            adapter_up_maps,
            input_projection,
            feedforward_up,
            feedforward_up.shape[1] * 3 // 8,
            mlp_count,
            req_count,
        )
        cosine, sine = rotary_tables(positions)
        attended, kv_pages = joint_attention(
            block_page_lookup[0], linear, value_rows, scales, query_key_gains, cosine, sine, segment
        )
    else:
        per_token = [choose_rows(modulation[:, which_row, :], own_segment) for which_row in range(6)]
        token_f32 = tokens.astype(jnp.float32)
        rows_in, adapter_up_weight = entry_rows(
            tokens, per_token[1], per_token[0], adapter_up_maps, mlp_count
        )
        request_slot = adapter_storage[request_adapter]
        token_slot = jnp.sum(
            jnp.where(
                segment[:, None] == jnp.arange(request_slot.shape[0], dtype=jnp.int32)[None, :],
                request_slot[None, :],
                0,
            ),
            axis=1,
        )
        resident = my_index * resident_slots + jnp.arange(resident_slots, dtype=jnp.int32)
        held = (token_slot[None, :] == resident[:, None]).astype(jnp.float32)
        code_block = lax.dot_general(
            adapter_down_weight.transpose(0, 2, 1).reshape(resident_slots * doubled_rank, -1),
            rows_in,
            (((1,), (1,)), ((), ())),
            preferred_element_type=jnp.float32,
        ).reshape(resident_slots, doubled_rank, group_rows)
        my_codes = jnp.sum(held[:, None, :] * code_block, axis=0).astype(jnp.bfloat16)
        codes = small_sum(my_codes, mlp_count, 1).astype(jnp.bfloat16)
        slots = jnp.arange(slot_total, dtype=jnp.int32)
        everywhere = token_slot[None, :] == slots[:, None]

        def spread(code_part):
            return jnp.where(everywhere[:, None, :], code_part[None], jnp.bfloat16(0)).reshape(
                slot_total * rank_once, group_rows
            )

        def adapted(code_part, which_map):
            return lax.dot_general(
                spread(code_part),
                adapter_up_weight[:, which_map].reshape(slot_total * rank_once, local_width),
                (((0,), (0,)), ((), ())),
                preferred_element_type=jnp.float32,
            )

        projected = product(rows_in, input_projection, 0, 3, 256, jnp.float32)
        query_linear = projected[0] + adapted(codes[:rank_once], 0)
        key_linear = projected[1]
        value_rows = (projected[2] + adapted(codes[rank_once:], 1)).astype(jnp.bfloat16)
        squares = small_sum(
            jnp.stack(
                [jnp.sum(query_linear * query_linear, axis=1), jnp.sum(key_linear * key_linear, axis=1)]
            ),
            mlp_count,
            2,
        )
        query_square, key_square = squares[0], squares[1]
        query_scale = lax.rsqrt(query_square / entire_width + EPSILON)
        key_scale = lax.rsqrt(key_square / entire_width + EPSILON)
        cosine, sine = rotary_tables(positions)
        attended, kv_pages = self_attention(
            block_page_lookup[0],
            query_linear,
            key_linear,
            value_rows,
            query_scale,
            key_scale,
            query_key_gains,
            cosine,
            sine,
            segment,
        )
    text_owner = (
        jnp.arange(text_token_cache.shape[1] * text_token_cache.shape[2], dtype=jnp.int32)
        // text_token_cache.shape[2]
    )

    def out_rows(rows, which_map):
        return product(rows, output_projection, which_map, 1, 1280, jnp.bfloat16)[0]

    if tuned:
        first_res, cross_query, hop_two = cross_in(
            attended,
            tokens,
            by_kind,
            own_segment[:, None],
            cross_norm_gain[None, :],
            query_key_gains,
            output_projection,
            input_projection,
            hop_one,
            mlp_count,
            req_count,
        )
    else:
        first_res, cross_rows = middle_rows(
            out_rows(attended, 0),
            tokens,
            per_token[2],
            cross_norm_gain[None, :],
            jnp.zeros((1, tokens.shape[1]), jnp.float32),
            mlp_count,
            3,
        )
        cross_linear = product(cross_rows, input_projection, 3, 1, 256, jnp.float32)[0]
        cross_square = small_sum(
            jnp.sum(cross_linear * cross_linear, axis=1)[None, :], mlp_count, 4
        )[0]
        cross_query = (
            cross_linear
            * lax.rsqrt(cross_square / entire_width + EPSILON)[:, None]
            * query_key_gains[2]
        ).astype(jnp.bfloat16)
    if tuned:
        second_res, delta = feed_forward(
            cross_query,
            segment[:, None],
            first_res,
            by_kind,
            own_segment[:, None],
            text_token_cache,
            output_projection,
            hop_one,
            hop_two,
            feedforward_up,
            feedforward_down,
            mlp_count,
            req_count,
            5,
        )
        layer_out = (second_res.astype(jnp.float32) + delta).astype(jnp.bfloat16)
        return (layer_out, kv_pages)
    cross_out = cross_attention(
        cross_query,
        text_token_cache.reshape(2, text_owner.shape[0], local_width),
        segment,
        text_owner,
    )
    up_full = lax.all_gather(feedforward_up, "req", axis=0, tiled=True)
    second_res, mlp_in = middle_rows(
        out_rows(cross_out, 1),
        first_res,
        jnp.ones((1, tokens.shape[1]), jnp.float32),
        1.0 + per_token[4],
        per_token[3],
        mlp_count,
        5,
    )
    hidden = product(
        mlp_in,
        up_full[None],
        0,
        1,
        256,
        jnp.bfloat16,
        functools.partial(jax.nn.gelu, approximate=True),
    )[0]
    hidden_all = line_gather(hidden, req_count, 6)
    units, columns = feedforward_down.shape
    down_part = jnp.dot(
        hidden_all.reshape(req_count * group_rows, units),
        feedforward_down,
        preferred_element_type=jnp.float32,
    ).astype(jnp.bfloat16)
    down_own = exit_rows(
        down_part.reshape(req_count, mlp_count, own_count, columns), mlp_count, req_count, 7
    )
    layer_out = (
        second_res.astype(jnp.float32) + per_token[5] * down_own.astype(jnp.float32)
    ).astype(jnp.bfloat16)
    return (layer_out, kv_pages)


def solution(mesh):
    return jax.shard_map(
        body,
        mesh=mesh,
        in_specs=(
            P(("req", "mlp"), None),
            P("req", None, None),
            P("req", None),
            P("req"),
            P(),
            P("mlp", None, None),
            P("mlp", None, None, None),
            P(None, None, "mlp"),
            P(None, "mlp"),
            P(None, "req"),
            P("req", None),
            P(None, "mlp", None),
            P(),
            P(None, "req", None, "mlp"),
            P("req", "mlp"),
            P("mlp", "req"),
        ),
        out_specs=(P(("req", "mlp"), None), P(None, "req", None, "mlp")),
        check_vma=False,
    )
```
